32 devices in a mesh: rows: 8 (over z, y), wide: 4 (over x, core).
Axes of the slice: x: 2, y: 2, z: 4, core: 2. Of those that a mesh axis runs over, the one named last changes fastest.
Arguments:
- tokens: bfloat16 [16, 1024, 1024], P('rows', 'wide'), may hold values from -6 to 6
- doc_ids: int32 [16, 1024], P('rows'), may hold values from 0 to 5, never falling along the last dimension, each value on 1 to 512 neighbouring positions
- factor_weight: bfloat16 [1024, 800], replicated, may hold values from -0.3125 to 0.3125
- output_weight: bfloat16 [1024, 1024], replicated, may hold values from -0.5 to 0.5
- norm_one: float32 [1024], replicated, may hold values from 0.5 to 1.5
- norm_two: float32 [1024], replicated, may hold values from 0.5 to 1.5
- gate_weight: bfloat16 [1024, 2816], P(None, 'wide'), may hold values from -0.1875 to 0.1875
- up_weight: bfloat16 [1024, 2816], P(None, 'wide'), may hold values from -0.1875 to 0.1875
- down_weight: bfloat16 [2816, 1024], P('wide'), may hold values from -0.15625 to 0.15625
- cotangent: bfloat16 [16, 1024, 1024], P('rows', 'wide'), may hold values from -6 to 6
Outputs:
- output: bfloat16 [16, 1024, 1024], P('rows', 'wide')
- input_grad: bfloat16 [16, 1024, 1024], P('rows', 'wide')
- grad_factors: float32 [1024, 800], replicated
- grad_out: float32 [1024, 1024], replicated
- grad_norm_one: float32 [1024], replicated
- grad_norm_two: float32 [1024], replicated
- grad_gate: float32 [1024, 2816], P(None, 'wide')
- up_weight_gradient: float32 [1024, 2816], P(None, 'wide')
- down_weight_gradient: float32 [2816, 1024], P('wide')
The draws below stay inside these ranges and needn't reach their ends.
Inputs may be any that keep to these rules, and one draw needn't show every extreme that they name: `doc_ids`: in each sequence the ids never fall along the positions; a document holds 1 to 512 positions, and one document of every sequence holds exactly 512.
All inputs are finite; a program needn't handle non-finite values.
Results may differ from the reference program's by a relative error of at most 0.017.
The reference program's roundings to bfloat16 on the way count: a program that leaves them out, or rounds other values in their place, can miss the bound.
Values may be sent and summed in bfloat16 or wider, within the bound.
A program may use at most 256 MiB of HBM per device.

```python
import math
import jax
import jax.numpy as jnp
import numpy as np
from jax import lax

D = 1024
H = 16
DH = 64
RQ = 6
RK = 2
FF = 2816
LEN = 1024
DOCS = 6
SEQ_BLOCK = 2
NSEQ = 16
FAC = 800


def levels(own_key, dims, shards, least, largest):
    def one(dim, blocks):
        heights = jax.random.uniform(jax.random.fold_in(jax.random.fold_in(own_key, 6), dim), (blocks,), jnp.float32, least / len(shards), largest / len(shards))
        return jnp.repeat(jnp.exp(heights), dims[dim] // blocks).reshape((-1,) + (1,) * (len(dims) - dim - 1))

    level = one(*shards[0])
    for cut in shards[1:]:
        level = level * one(*cut)
    return level


def profile(amount, total, bound, slope):
    weights = [(1 << 20) // math.isqrt(rank ** slope) + 1 for rank in range(2, amount + 1)]
    spare, given = total - bound - (amount - 1), [1] * (amount - 1)
    while spare > 0:
        candidates = [i for i in range(amount - 1) if given[i] < bound]
        pool, left = sum([weights[i] for i in candidates]), spare
        for i in candidates:
            extra = min(bound - given[i], max(1, left * weights[i] // pool), spare)
            given[i] = given[i] + extra
            spare = spare - extra
    return np.array([bound] + given)


def ragged(rng, amount, total, reach, lean):
    if amount == 2:
        one = jax.random.randint(rng, (), max(1, total - reach), min(reach, total - 1) + 1)
        return jnp.stack([one, total - one])
    lengths = jnp.asarray(profile(amount, total, reach, lean), jnp.int32)
    pairs = (amount - 1) // 2
    giver, taker = lengths[1:1 + 2 * pairs:2], lengths[2:2 + 2 * pairs:2]
    slack = jnp.minimum(giver - 1, reach - taker)
    passed = jax.random.randint(jax.random.fold_in(rng, 1), (pairs,), 0, 1 << 20) % (slack + 1)
    lengths = lengths.at[1:1 + 2 * pairs:2].set(giver - passed).at[2:2 + 2 * pairs:2].set(taker + passed)
    return lengths[jax.random.permutation(jax.random.fold_in(rng, 2), amount)]


def centred(stream_key, extent, scale, bound, pieces=(), held_as=jnp.bfloat16):
    array = jax.random.normal(stream_key, extent, jnp.float32) * scale
    if len(pieces) > 0:
        array = levels(stream_key, extent, pieces, -0.22, 0.18) * array
    return jnp.clip(array, min=-bound, max=bound).astype(held_as)


def setup_inputs(seed: int = 0) -> dict:
    keys = jax.random.split(jax.random.key(seed), 11)
    tokens = centred(keys[0], (NSEQ, LEN, D), 1.0, 6.0, ((0, 8), (1, 4)))
    doc_ids = jax.vmap(lambda own: jnp.searchsorted(jnp.cumsum(ragged(own, DOCS, LEN, LEN // 2, 1)), jnp.arange(LEN), side="right"))(jax.random.split(keys[1], NSEQ)).reshape((NSEQ, LEN)).astype(jnp.int32)
    factor_weight = centred(keys[2], (D, FAC), (D // 3) ** -0.5, 0.3125)
    output_weight = centred(keys[3], (D, D), (D // 8) ** -0.5, 0.5)
    norm_one = jnp.clip(1.0 + 0.1 * jax.random.normal(keys[4], (D,), jnp.float32), 0.5, 1.5)
    norm_two = jnp.clip(1.0 + 0.1 * jax.random.normal(keys[5], (D,), jnp.float32), 0.5, 1.5)
    gate_weight = centred(keys[6], (D, FF), D ** -0.5, 0.1875, ((1, 4),))
    up_weight = centred(keys[7], (D, FF), D ** -0.5, 0.1875, ((1, 4),))
    down_weight = centred(keys[8], (FF, D), (FF // 2) ** -0.5, 0.15625, ((0, 4),))
    cotangent = centred(keys[9], (NSEQ, LEN, D), 1.0, 6.0, ((0, 8), (1, 4)))
    return dict(tokens=tokens, doc_ids=doc_ids, factor_weight=factor_weight, output_weight=output_weight, norm_one=norm_one, norm_two=norm_two, gate_weight=gate_weight, up_weight=up_weight, down_weight=down_weight, cotangent=cotangent)


EPS = 1e-06
NEG = -1000000000.0
MATMUL_EXACTNESS = lax.Precision.HIGHEST

@jax.custom_vjp
def reduced_copy(v):
    return lax.optimization_barrier(v.astype(jnp.bfloat16)).astype(jnp.float32)

@jax.custom_vjp
def reduced_backward(v):
    return v

def low_keep(v):
    return (reduced_copy(v), None)

def low_pass(kept, grad):
    return (grad,)

def back_keep(v):
    return (v, None)

def back_low(kept, grad):
    return (reduced_copy(grad),)
reduced_copy.defvjp(low_keep, low_pass)
reduced_backward.defvjp(back_keep, back_low)

def rms_norm(values, gain):
    scaling = lax.rsqrt(lax.optimization_barrier(jnp.mean(values * values, axis=-1, keepdims=True)) + EPS)
    return values * scaling * gain

def expand(part_a, part_b, heads, rank):
    leading = part_a.shape[:-1]
    left_part = part_a.reshape(leading + (heads, rank))
    right_part = part_b.reshape(leading + (rank, -1))
    return jnp.einsum('...hr,...rd->...hd', left_part, right_part, precision=MATMUL_EXACTNESS) / rank

def attend(block_parts):
    queries, key_heads, value_heads, doc_block = block_parts
    length = doc_block.shape[1]
    key_pos = lax.broadcasted_iota(jnp.int32, (length, length), 1)
    query_pos = lax.broadcasted_iota(jnp.int32, (length, length), 0)
    allowed = (doc_block[:, :, None] == doc_block[:, None, :]) & (key_pos <= query_pos)[None]
    scores = jnp.einsum('bqhd,bkhd->bhqk', queries, key_heads, precision=MATMUL_EXACTNESS) * DH ** (-0.5)
    scores = reduced_backward(scores)
    scores = jnp.where(allowed[:, None], scores, NEG)
    attn_probs = reduced_copy(jax.nn.softmax(scores, axis=-1))
    return jnp.einsum('bhqk,bkhd->bqhd', attn_probs, value_heads, precision=MATMUL_EXACTNESS)

def grouped(array_in):
    return array_in.reshape((array_in.shape[0] // SEQ_BLOCK, SEQ_BLOCK) + array_in.shape[1:])

def forward(tokens, factor_weight, output_weight, norm_one, norm_two, gate_weight, up_weight, down_weight, doc_ids):
    seq_count, length, _unused = tokens.shape
    cut_one = H * RQ
    cut_two = cut_one + RQ * DH
    cut_three = cut_two + H * RK
    cut_four = cut_three + RK * DH
    cut_five = cut_four + H * RK
    first_normalized = reduced_copy(rms_norm(tokens, norm_one))
    factor_rows = reduced_backward(reduced_copy(jnp.einsum('cnx,xo->cno', first_normalized, factor_weight, precision=MATMUL_EXACTNESS)))
    queries = reduced_copy(expand(factor_rows[..., :cut_one], factor_rows[..., cut_one:cut_two], H, RQ))
    key_heads = reduced_copy(expand(factor_rows[..., cut_two:cut_three], factor_rows[..., cut_three:cut_four], H, RK))
    value_heads = reduced_copy(expand(factor_rows[..., cut_four:cut_five], factor_rows[..., cut_five:], H, RK))
    mixed_out = lax.map(jax.checkpoint(attend), (grouped(queries), grouped(key_heads), grouped(value_heads), grouped(doc_ids)))
    attention_result = reduced_backward(reduced_copy(mixed_out.reshape(seq_count, length, H * DH)))
    hidden_middle = tokens + reduced_backward(jnp.einsum('trq,qx->trx', attention_result, output_weight, precision=MATMUL_EXACTNESS))
    second_normalized = reduced_copy(rms_norm(hidden_middle, norm_two))
    gate_logits = reduced_backward(jnp.einsum('cnx,xo->cno', second_normalized, gate_weight, precision=MATMUL_EXACTNESS))
    up_activation = reduced_backward(jnp.einsum('cnx,xo->cno', second_normalized, up_weight, precision=MATMUL_EXACTNESS))
    feedforward_hidden = reduced_copy(jax.nn.silu(gate_logits) * up_activation)
    return hidden_middle + reduced_backward(jnp.einsum('gxk,km->gxm', feedforward_hidden, down_weight, precision=MATMUL_EXACTNESS))

def reference(tokens, doc_ids, factor_weight, output_weight, norm_one, norm_two, gate_weight, up_weight, down_weight, cotangent):
    floats = [array_in.astype(jnp.float32) for array_in in (tokens, factor_weight, output_weight, norm_one, norm_two, gate_weight, up_weight, down_weight)]

    def wrapped(*input_rows_total):
        return forward(*input_rows_total, doc_ids)
    result, pullback = jax.vjp(wrapped, *floats)
    gradients = pullback(cotangent.astype(jnp.float32))
    return (result.astype(jnp.bfloat16), gradients[0].astype(jnp.bfloat16), gradients[1], gradients[2], gradients[3], gradients[4], gradients[5], gradients[6], gradients[7])
```

```python
import functools

import jax
import jax.numpy as jnp
from jax import lax
from jax.experimental import pallas as pl
from jax.experimental.pallas import tpu as pltpu
from jax.sharding import PartitionSpec as P

H = 16
DH = 64
RQ = 6
RK = 2
MAX_DOC = 512
EPS = 1e-06
NEG = -1000000000.0
BIG = 3.0e38

QA = H * RQ
QCOLS = QA + RQ * DH
KA = H * RK
KCOLS = KA + RK * DH
KV = 2 * KCOLS
QPAD = 512
KPAD = 384
PAIRS = H // 2

F32 = jnp.float32
BF16 = jnp.bfloat16

NN = (((1,), (0,)), ((), ()))
NT = (((1,), (1,)), ((), ()))
TN = (((0,), (0,)), ((), ()))


def mm(a, b, dims=NN):
    return lax.dot_general(a, b, dims, preferred_element_type=F32)


def params(vmem_mb=60):
    return pltpu.CompilerParams(vmem_limit_bytes=vmem_mb << 20)


def cost(flops, nbytes):
    return pl.CostEstimate(flops=int(flops), bytes_accessed=int(nbytes), transcendentals=0)


def selection(shape, rule):
    row = lax.broadcasted_iota(jnp.int32, shape, 0)
    col = lax.broadcasted_iota(jnp.int32, shape, 1)
    return jnp.where(rule(row, col), 1.0, 0.0).astype(BF16)


def head_spread(pair, base, rank, shape):
    def rule(row, col):
        r = col // 128
        lane = col - r * 128
        head = 2 * pair + jnp.where(lane >= DH, 1, 0)
        return row == base + head * rank + r

    return selection(shape, rule)


def rank_tile(base, shape):
    def rule(row, col):
        r = col // 128
        lane = col - r * 128
        return row == base + r * DH + jnp.where(lane >= DH, lane - DH, lane)

    return selection(shape, rule)


def front_kernel(x_ref, w_ref, g_ref, n_ref, q_ref, kv_ref):
    x = x_ref[...].astype(F32)
    r = lax.rsqrt(jnp.mean(x * x, axis=-1, keepdims=True) + EPS)
    n = (x * r * g_ref[...]).astype(BF16)
    n_ref[...] = n
    f = mm(n, w_ref[...]).astype(BF16)
    q_ref[...] = f[:, :QPAD]
    kv_ref[:, :KV] = f[:, QCOLS:]
    kv_ref[:, KV:] = jnp.zeros((f.shape[0], KPAD - KV), BF16)


def front(x, w, gain):
    rows, d = x.shape
    blk = 256 if rows % 256 == 0 else rows
    return pl.pallas_call(
        front_kernel,
        grid=(rows // blk,),
        in_specs=[
            pl.BlockSpec((blk, d), lambda i: (i, 0)),
            pl.BlockSpec(w.shape, lambda i: (0, 0)),
            pl.BlockSpec((1, d), lambda i: (0, 0)),
        ],
        out_specs=[
            pl.BlockSpec((blk, d), lambda i: (i, 0)),
            pl.BlockSpec((blk, QPAD), lambda i: (i, 0)),
            pl.BlockSpec((blk, KPAD), lambda i: (i, 0)),
        ],
        out_shape=[
            jax.ShapeDtypeStruct((rows, d), BF16),
            jax.ShapeDtypeStruct((rows, QPAD), BF16),
            jax.ShapeDtypeStruct((rows, KPAD), BF16),
        ],
        compiler_params=params(),
        cost_estimate=cost(2 * rows * d * 800, rows * d * 6 + d * 1600),
        name="front",
    )(x, w, gain)


def make_cap(s_ref, dq_ref, dk_ref, cap_ref, nblk, own):
    dq = dq_ref[...]
    for i in range(nblk):
        rows = pl.ds(i * own, own)
        key = lax.broadcasted_iota(jnp.int32, (own, own), 0)
        query = lax.broadcasted_iota(jnp.int32, (own, own), 1) + s_ref[1 + i]
        ok = (dk_ref[rows, :] == dq) & (key <= query)
        cap_ref[rows, :] = jnp.where(ok, BIG, NEG)


def stacked(x):
    lane = lax.broadcasted_iota(jnp.int32, x.shape, 1)
    zero = jnp.zeros_like(x)
    return jnp.concatenate(
        [jnp.where(lane < DH, x, zero), jnp.where(lane >= DH, x, zero)], axis=0
    )


def unstacked(xt, own):
    pair = jnp.concatenate([xt[:DH, :own], xt[DH:, own:]], axis=0)
    return pair.T


def key_parts(kvf_ref, pair):
    ek = head_spread(pair, 0, RK, (128, RK * 128))
    ev = head_spread(pair, KCOLS - 128, RK, (128, RK * 128))
    ke = mm(kvf_ref[:, :128], ek)
    ve = mm(kvf_ref[:, 128:256], ev)
    return ke, ve


def tile_keys(kvf_ref, bk_ref, bv_ref):
    bk_ref[...] = mm(kvf_ref[:, :256], rank_tile(KA, (256, RK * 128)))
    bv_ref[...] = mm(kvf_ref[:, 128:384], rank_tile(KCOLS + KA - 128, (256, RK * 128)))


def attend_kernel(
    nblk, s_ref, qf_ref, kvg_ref, dq_ref, dk_ref, x_ref, wo_ref, g_ref,
    att_ref, q_ref, k_ref, v_ref, lse_ref, hm_ref, n_ref, kvw_ref,
    bq_ref, bk_ref, bv_ref, cap_ref, full_ref,
):
    pair = pl.program_id(0)
    own = qf_ref.shape[0]

    @pl.when(pair == 0)
    def _():
        for i in range(nblk):
            kvw_ref[pl.ds(i * own, own), :] = kvg_ref[s_ref[1 + nblk + i]]
        bq_ref[...] = mm(qf_ref[...], rank_tile(QA, (QPAD, RQ * 128)))
        tile_keys(kvw_ref, bk_ref, bv_ref)
        make_cap(s_ref, dq_ref, dk_ref, cap_ref, nblk, own)

    qe = mm(qf_ref[:, :128], head_spread(pair, 0, RQ, (128, RQ * 128)))
    qsum = qe[:, :128] * bq_ref[:, :128]
    for r in range(1, RQ):
        cols = slice(r * 128, (r + 1) * 128)
        qsum = qsum + qe[:, cols] * bq_ref[:, cols]
    q = (qsum * (1.0 / RQ)).astype(BF16)
    ke, ve = key_parts(kvw_ref, pair)
    k = ((ke[:, :128] * bk_ref[:, :128] + ke[:, 128:] * bk_ref[:, 128:]) * (1.0 / RK)).astype(BF16)
    v = ((ve[:, :128] * bv_ref[:, :128] + ve[:, 128:] * bv_ref[:, 128:]) * (1.0 / RK)).astype(BF16)
    q = q * jnp.asarray(DH ** (-0.5), BF16)
    q_ref[...] = q
    k_ref[...] = k
    v_ref[...] = v
    cap = cap_ref[...]
    st = jnp.minimum(mm(k, stacked(q), NT), jnp.concatenate([cap, cap], axis=1))
    top = jnp.max(st, axis=0, keepdims=True)
    e = jnp.exp(st - top)
    total = jnp.sum(e, axis=0, keepdims=True)
    p = (e * (1.0 / total)).astype(BF16)
    lse_ref[0] = top + jnp.log(total)
    att = unstacked(mm(v, p, TN), own).astype(BF16)
    att_ref[...] = att
    full_ref[pair] = att

    @pl.when(pair == pl.num_programs(0) - 1)
    def _():
        hm = x_ref[...].astype(F32)
        att_all = jnp.concatenate([full_ref[i] for i in range(PAIRS)], axis=1)
        hm = hm + mm(att_all, wo_ref[...])
        hm_ref[...] = hm
        r = lax.rsqrt(jnp.mean(hm * hm, axis=-1, keepdims=True) + EPS)
        n_ref[...] = (hm * r * g_ref[...]).astype(BF16)


def attend(nblk, scalars, qf, kvg, dq, dk, x, wo, gain):
    own, d = x.shape
    win = nblk * own
    whole = lambda a: pl.BlockSpec(a.shape, lambda p, a=a: (0,) * a.ndim)
    col = lambda rows: pl.BlockSpec((rows, 128), lambda p: (0, p))
    return pl.pallas_call(
        functools.partial(attend_kernel, nblk),
        grid=(PAIRS,),
        in_specs=[pl.BlockSpec(memory_space=pltpu.SMEM)]
        + [whole(a) for a in (qf, kvg, dq, dk, x, wo, gain)],
        out_specs=[
            col(own), col(own), col(win), col(win),
            pl.BlockSpec((1, 1, 2 * own), lambda p: (p, 0, 0)),
            pl.BlockSpec((own, d), lambda p: (0, 0)),
            pl.BlockSpec((own, d), lambda p: (0, 0)),
            pl.BlockSpec((win, KPAD), lambda p: (0, 0)),
        ],
        out_shape=[
            jax.ShapeDtypeStruct((own, d), BF16),
            jax.ShapeDtypeStruct((own, d), BF16),
            jax.ShapeDtypeStruct((win, d), BF16),
            jax.ShapeDtypeStruct((win, d), BF16),
            jax.ShapeDtypeStruct((PAIRS, 1, 2 * own), F32),
            jax.ShapeDtypeStruct((own, d), F32),
            jax.ShapeDtypeStruct((own, d), BF16),
            jax.ShapeDtypeStruct((win, KPAD), BF16),
        ],
        scratch_shapes=[
            pltpu.VMEM((own, RQ * 128), F32),
            pltpu.VMEM((win, RK * 128), F32),
            pltpu.VMEM((win, RK * 128), F32),
            pltpu.VMEM((win, own), F32),
            pltpu.VMEM((PAIRS, own, 128), BF16),
        ],
        compiler_params=params(),
        cost_estimate=cost(12e9, 12e6),
        name="attend",
    )(scalars, qf, kvg, dq, dk, x, wo, gain)


def ffn_kernel(has_prev, bf16_out, *refs):
    if has_prev:
        n_ref, c_ref, wg_ref, wu_ref, wd_ref, pg_ref, pu_ref, pd_ref = refs[:8]
        refs = refs[8:]
    else:
        n_ref, c_ref, wg_ref, wu_ref, wd_ref = refs[:5]
        refs = refs[5:]
    o_ref, dn_ref, og_ref, ou_ref, od_ref = refs[:5]
    if bf16_out:
        ag_ref, au_ref, ad_ref = refs[5:]
    else:
        ag_ref, au_ref, ad_ref = og_ref, ou_ref, od_ref
    step = pl.program_id(0)

    @pl.when(step == 0)
    def _():
        if has_prev:
            ag_ref[...] = pg_ref[...]
            au_ref[...] = pu_ref[...]
            ad_ref[...] = pd_ref[...]
        else:
            ag_ref[...] = jnp.zeros_like(ag_ref)
            au_ref[...] = jnp.zeros_like(au_ref)
            ad_ref[...] = jnp.zeros_like(ad_ref)

    n = n_ref[0]
    c = c_ref[0]
    wg, wu, wd = wg_ref[...], wu_ref[...], wd_ref[...]
    g = mm(n, wg)
    u = mm(n, wu)
    dh = mm(c, wd, NT)
    s = 1.0 / (1.0 + jnp.exp(-g))
    gs = g * s
    hid = (gs * u).astype(BF16)
    dg = (dh * u * (s * (1.0 + g * (1.0 - s)))).astype(BF16)
    du = (dh * gs).astype(BF16)
    o_ref[0] = mm(hid, wd).astype(BF16)
    dn_ref[0] = (mm(dg, wg, NT) + mm(du, wu, NT)).astype(BF16)
    ag_ref[...] += mm(n, dg, TN)
    au_ref[...] += mm(n, du, TN)
    ad_ref[...] += mm(hid, c, TN)
    if bf16_out:

        @pl.when(step == pl.num_programs(0) - 1)
        def _():
            og_ref[...] = ag_ref[...].astype(BF16)
            ou_ref[...] = au_ref[...].astype(BF16)
            od_ref[...] = ad_ref[...].astype(BF16)


def ffn(n, c, wg, wu, wd, prev, last):
    w, own, d = n.shape
    ff = wg.shape[1]
    one = lambda a: pl.BlockSpec(
        a.shape, lambda i, a=a: (0,) * a.ndim, pipeline_mode=pl.Buffered(1)
    )
    blk = pl.BlockSpec((1, own, d), lambda i: (i, 0, 0))
    dt = BF16 if last else F32
    args = [n, c, wg, wu, wd] + list(prev or [])
    shapes = [(d, ff), (d, ff), (ff, d)]
    return pl.pallas_call(
        functools.partial(ffn_kernel, bool(prev), last),
        grid=(w,),
        in_specs=[blk, blk] + [one(a) for a in args[2:]],
        out_specs=[blk, blk] + [
            pl.BlockSpec(s, lambda i: (0, 0), pipeline_mode=pl.Buffered(1)) for s in shapes
        ],
        out_shape=[jax.ShapeDtypeStruct(n.shape, BF16)] * 2
        + [jax.ShapeDtypeStruct(s, dt) for s in shapes],
        scratch_shapes=[pltpu.VMEM(s, F32) for s in shapes] if last else [],
        compiler_params=params(),
        cost_estimate=cost(18 * w * own * d * ff, 20 * w * own * d),
        name="ffn",
    )(*args)


def back_kernel(
    nblk, s_ref, q_ref, k_ref, v_ref, lse_ref, dq_ref, dk_ref, qf_ref, kvw_ref,
    dn_ref, hm_ref, c_ref, wo_ref, g_ref,
    dm_ref, dl_ref, gain_ref, gq_ref, gkv_ref,
    bq_ref, bk_ref, bv_ref, cap_ref, da_ref, aq_ref, ak_ref, av_ref, tq_ref, tk_ref, tv_ref,
):
    pair = pl.program_id(0)
    own = q_ref.shape[0]
    last = pl.num_programs(0) - 1

    @pl.when(pair == 0)
    def _():
        hm = hm_ref[...]
        dn = dn_ref[...].astype(F32)
        r = lax.rsqrt(jnp.mean(hm * hm, axis=-1, keepdims=True) + EPS)
        z = dn * g_ref[...]
        gain_ref[...] = jnp.sum(dn * hm * r, axis=0, keepdims=True)
        dm = (
            c_ref[...].astype(F32)
            + r * z
            - hm * (r * r * r) * jnp.mean(z * hm, axis=-1, keepdims=True)
        )
        dm_ref[...] = dm
        low = dm.astype(BF16)
        dl_ref[...] = low
        da = mm(low, wo_ref[...], NT).astype(BF16)
        for i in range(PAIRS):
            da_ref[i] = da[:, i * 128:(i + 1) * 128]
        bq_ref[...] = mm(qf_ref[...], rank_tile(QA, (QPAD, RQ * 128)))
        tile_keys(kvw_ref, bk_ref, bv_ref)
        make_cap(s_ref, dq_ref, dk_ref, cap_ref, nblk, own)
        for ref in (aq_ref, ak_ref, av_ref, tq_ref, tk_ref, tv_ref):
            ref[...] = jnp.zeros_like(ref)

    q = q_ref[...]
    k = k_ref[...]
    v = v_ref[...]
    qs = stacked(q)
    ds_ = stacked(da_ref[pair])
    cap = cap_ref[...]
    st = jnp.minimum(mm(k, qs, NT), jnp.concatenate([cap, cap], axis=1))
    p = jnp.exp(st - lse_ref[0])
    dp = mm(v, ds_, NT)
    delta = jnp.sum(p * dp, axis=0, keepdims=True)
    ds = (p * (dp - delta)).astype(BF16)
    dv = mm(p.astype(BF16), ds_)
    dk = mm(ds, qs)
    dq = unstacked(mm(k, ds, TN), own) * (DH ** (-0.5))

    eq = head_spread(pair, 0, RQ, (128, RQ * 128))
    qe = mm(qf_ref[:, :128], eq)
    dq6 = jnp.concatenate([dq] * RQ, axis=1)
    tq_ref[...] += dq6 * qe
    aq_ref[...] += mm((dq6 * bq_ref[...]).astype(BF16), eq, NT)
    ek = head_spread(pair, 0, RK, (128, RK * 128))
    ev = head_spread(pair, KCOLS - 128, RK, (128, RK * 128))
    ke = mm(kvw_ref[:, :128], ek)
    ve = mm(kvw_ref[:, 128:256], ev)
    dk2 = jnp.concatenate([dk] * RK, axis=1)
    dv2 = jnp.concatenate([dv] * RK, axis=1)
    tk_ref[...] += dk2 * ke
    tv_ref[...] += dv2 * ve
    ak_ref[...] += mm((dk2 * bk_ref[...]).astype(BF16), ek, NT)
    av_ref[...] += mm((dv2 * bv_ref[...]).astype(BF16), ev, NT)

    @pl.when(pair == last)
    def _():
        def fold(x, t):
            hi = x.astype(BF16)
            lo = (x - hi.astype(F32)).astype(BF16)
            return mm(hi, t, NT) + mm(lo, t, NT)

        gq = fold(tq_ref[...], rank_tile(QA, (QPAD, RQ * 128)))
        gq_ref[:, :128] = ((gq[:, :128] + aq_ref[...]) * (1.0 / RQ)).astype(BF16)
        gq_ref[:, 128:] = (gq[:, 128:] * (1.0 / RQ)).astype(BF16)
        gk = fold(tk_ref[...], rank_tile(KA, (KPAD, RK * 128)))
        gv = fold(tv_ref[...], rank_tile(KCOLS + KA, (KPAD, RK * 128)))
        gkv = gk + gv
        first = ((gkv[:, :128] + ak_ref[...]) * (1.0 / RK)).astype(BF16)
        second = ((gkv[:, 128:256] + av_ref[...]) * (1.0 / RK)).astype(BF16)
        third = (gkv[:, 256:] * (1.0 / RK)).astype(BF16)
        gkv_ref[...] = jnp.zeros_like(gkv_ref)
        for i in range(nblk):
            rows = slice(i * own, (i + 1) * own)
            slot = s_ref[1 + nblk + i]
            gkv_ref[slot, :, :128] = first[rows]
            gkv_ref[slot, :, 128:256] = second[rows]
            gkv_ref[slot, :, 256:] = third[rows]


def back(nblk, width, scalars, q, k, v, lse, dq, dk, qf, kvw, dn, hm, c, wo, gain):
    own, d = q.shape
    win = nblk * own
    whole = lambda a: pl.BlockSpec(a.shape, lambda p, a=a: (0,) * a.ndim)
    col = lambda rows: pl.BlockSpec((rows, 128), lambda p: (0, p))
    fixed = lambda *s: pl.BlockSpec(s, lambda p: (0,) * len(s))
    return pl.pallas_call(
        functools.partial(back_kernel, nblk),
        grid=(PAIRS,),
        in_specs=[
            pl.BlockSpec(memory_space=pltpu.SMEM), col(own), col(win), col(win),
            pl.BlockSpec((1, 1, 2 * own), lambda p: (p, 0, 0)),
        ] + [whole(a) for a in (dq, dk, qf, kvw, dn, hm, c, wo, gain)],
        out_specs=[
            fixed(own, d), fixed(own, d), fixed(1, d), fixed(own, QPAD),
            fixed(width, own, KPAD),
        ],
        out_shape=[
            jax.ShapeDtypeStruct((own, d), F32),
            jax.ShapeDtypeStruct((own, d), BF16),
            jax.ShapeDtypeStruct((1, d), F32),
            jax.ShapeDtypeStruct((own, QPAD), BF16),
            jax.ShapeDtypeStruct((width, own, KPAD), BF16),
        ],
        scratch_shapes=[
            pltpu.VMEM((own, RQ * 128), F32),
            pltpu.VMEM((win, RK * 128), F32),
            pltpu.VMEM((win, RK * 128), F32),
            pltpu.VMEM((win, own), F32),
            pltpu.VMEM((PAIRS, own, 128), BF16),
            pltpu.VMEM((own, 128), F32),
            pltpu.VMEM((win, 128), F32),
            pltpu.VMEM((win, 128), F32),
            pltpu.VMEM((own, RQ * 128), F32),
            pltpu.VMEM((win, RK * 128), F32),
            pltpu.VMEM((win, RK * 128), F32),
        ],
        compiler_params=params(),
        cost_estimate=cost(30e9, 15e6),
        name="back",
    )(scalars, q, k, v, lse, dq, dk, qf, kvw, dn, hm, c, wo, gain)


def swap(x, axis, size, bit):
    return lax.ppermute(x, axis, [(i, i ^ bit) for i in range(size)])


def steps_of(size):
    bits, b = [], size // 2
    while b:
        bits.append(b)
        b //= 2
    return bits


def gather(x, size):
    buf = x[None]
    for bit in steps_of(size):
        buf = jnp.concatenate([buf, swap(buf, "wide", size, bit)], axis=0)
    return buf


def order_of(size):
    order = [0]
    for bit in steps_of(size):
        order = order + [o ^ bit for o in order]
    return order


def scatter(parts, size):
    for bit in reversed(steps_of(size)):
        half = parts.shape[0] // 2
        got = swap(parts[half:], "wide", size, bit)
        total = parts[:half].astype(F32) + got.astype(F32)
        parts = total if half == 1 else total.astype(BF16)
    return parts[0]


def body(
    tokens, doc_ids, factor_weight, output_weight, norm_one, norm_two,
    gate_weight, up_weight, down_weight, cotangent,
):
    seqs, own, d = tokens.shape
    full_len = doc_ids.shape[1]
    size = full_len // own
    me = lax.axis_index("wide")
    left = min(-(-(MAX_DOC - 1) // own), size - 1)
    nblk = left + 1
    start = jnp.maximum(me - left, 0)
    order = order_of(size)
    slot_of = [order.index(j) for j in range(size)]
    slots = jnp.asarray(slot_of, jnp.int32)
    blocks = start + jnp.arange(nblk, dtype=jnp.int32)
    scalars = jnp.concatenate(
        [me[None].astype(jnp.int32), (me - blocks) * own, slots[me ^ blocks]]
    ).astype(jnp.int32)
    g1 = norm_one[None]
    g2 = norm_two[None]

    n1, qf, kvf = front(tokens.reshape(seqs * own, d), factor_weight, g1)
    qf = qf.reshape(seqs, own, QPAD)
    kvg = gather(kvf.reshape(seqs, own, KPAD), size)
    doc_query = lax.dynamic_slice_in_dim(doc_ids, me * own, own, 1)
    doc_key = lax.dynamic_slice_in_dim(doc_ids, start * own, nblk * own, 1)
    cots = [gather(cotangent[s], size) for s in range(seqs)]

    fwd = []
    for s in range(seqs):
        dq = doc_query[s][None, :]
        dk = doc_key[s][:, None]
        fwd.append(
            (dq, dk)
            + tuple(attend(nblk, scalars, qf[s], kvg[:, s], dq, dk, tokens[s], output_weight, g2))
        )
    prev = None
    outs, dns = [], []
    for s in range(seqs):
        n2 = gather(fwd[s][8], size)
        res = ffn(n2, cots[s], gate_weight, up_weight, down_weight, prev, s == seqs - 1)
        outs.append(res[0])
        dns.append(res[1])
        prev = res[2:]
    grads = [lax.psum(g, "rows").astype(F32) for g in prev]

    output, mids, lows, gain_two, gqs, gkvs = [], [], [], 0.0, [], []
    for s in range(seqs):
        dq, dk, att, q, k, v, lse, hm, n2, kvw = fwd[s]
        dn = scatter(dns[s], size)
        dm, low, gain, gq, gkv = back(
            nblk, size, scalars, q, k, v, lse, dq, dk, qf[s], kvw, dn, hm,
            cotangent[s], output_weight, g2,
        )
        output.append((hm + scatter(outs[s], size)).astype(BF16))
        mids.append(dm)
        lows.append(low)
        gqs.append(gq)
        gkvs.append(gkv)
        gain_two = gain_two + gain
    att_all = jnp.stack([f[2] for f in fwd]).reshape(seqs * own, d)
    grad_out = mm(att_all, jnp.stack(lows).reshape(seqs * own, d), TN)
    gkv = scatter(jnp.stack(gkvs, axis=1), size).astype(BF16)
    dfac = jnp.concatenate([jnp.stack(gqs)[..., :QCOLS], gkv[..., :KV]], axis=-1)
    dfac = dfac.reshape(seqs * own, -1)
    grad_factors = mm(n1, dfac, TN)
    dn1 = mm(dfac, factor_weight, NT)
    hin = tokens.reshape(seqs * own, d).astype(F32)
    r1 = lax.rsqrt(jnp.mean(hin * hin, axis=-1, keepdims=True) + EPS)
    z1 = dn1 * g1
    gain_one = jnp.sum(dn1 * hin * r1, axis=0)
    grad_norm = r1 * z1 - hin * (r1 * r1 * r1) * jnp.mean(z1 * hin, axis=-1, keepdims=True)
    input_grad = (jnp.stack(mids).reshape(seqs * own, d) + grad_norm).astype(BF16)
    packed = jnp.concatenate(
        [grad_out, jnp.pad(grad_factors.T, ((0, 0), (0, 0))), gain_one[None], gain_two], axis=0
    )
    packed = lax.psum(packed.astype(BF16), ("rows", "wide")).astype(F32)
    fac = grad_factors.shape[1]
    return (
        jnp.stack(output),
        input_grad.reshape(seqs, own, d),
        packed[d:d + fac].T,
        packed[:d],
        packed[d + fac],
        packed[d + fac + 1],
        grads[0],
        grads[1],
        grads[2],
    )


def solution(mesh):
    placed = (
        P("rows", "wide", None), P("rows", None), P(), P(), P(), P(),
        P(None, "wide"), P(None, "wide"), P("wide", None), P("rows", "wide", None),
    )
    return jax.shard_map(
        body,
        mesh=mesh,
        in_specs=placed,
        out_specs=(
            P("rows", "wide", None), P("rows", "wide", None), P(), P(), P(), P(),
            P(None, "wide"), P(None, "wide"), P("wide", None),
        ),
        check_vma=False,
    )
```

```python
import functools

import jax
import jax.numpy as jnp
from jax import lax
from jax.experimental import pallas as pl
from jax.experimental.pallas import tpu as pltpu
from jax.sharding import PartitionSpec as P

H = 16
DH = 64
RQ = 6
RK = 2
MAX_DOC = 512
EPS = 1e-06
NEG = -1000000000.0
BIG = 3.0e38

QA = H * RQ
QCOLS = QA + RQ * DH
KA = H * RK
KCOLS = KA + RK * DH
KV = 2 * KCOLS
QPAD = 512
KPAD = 384
PAIRS = H // 2

F32 = jnp.float32
BF16 = jnp.bfloat16

NN = (((1,), (0,)), ((), ()))
NT = (((1,), (1,)), ((), ()))
TN = (((0,), (0,)), ((), ()))


def mm(a, b, dims=NN):
    return lax.dot_general(a, b, dims, preferred_element_type=F32)


def params(vmem_mb=60):
    return pltpu.CompilerParams(vmem_limit_bytes=vmem_mb << 20)


def cost(flops, nbytes):
    return pl.CostEstimate(flops=int(flops), bytes_accessed=int(nbytes), transcendentals=0)


def selection(shape, rule):
    row = lax.broadcasted_iota(jnp.int32, shape, 0)
    col = lax.broadcasted_iota(jnp.int32, shape, 1)
    return jnp.where(rule(row, col), 1.0, 0.0).astype(BF16)


def head_spread(pair, base, rank, shape):
    def rule(row, col):
        r = col // 128
        lane = col - r * 128
        head = 2 * pair + jnp.where(lane >= DH, 1, 0)
        return row == base + head * rank + r

    return selection(shape, rule)


def rank_tile(base, shape):
    def rule(row, col):
        r = col // 128
        lane = col - r * 128
        return row == base + r * DH + jnp.where(lane >= DH, lane - DH, lane)

    return selection(shape, rule)


def front_kernel(x_ref, w_ref, g_ref, n_ref, q_ref, kv_ref):
    x = x_ref[...].astype(F32)
    r = lax.rsqrt(jnp.mean(x * x, axis=-1, keepdims=True) + EPS)
    n = (x * r * g_ref[...]).astype(BF16)
    n_ref[...] = n
    f = mm(n, w_ref[...]).astype(BF16)
    q_ref[...] = f[:, :QPAD]
    kv_ref[:, :KV] = f[:, QCOLS:]
    kv_ref[:, KV:] = jnp.zeros((f.shape[0], KPAD - KV), BF16)


def front(x, w, gain):
    rows, d = x.shape
    blk = 256 if rows % 256 == 0 else rows
    return pl.pallas_call(
        front_kernel,
        grid=(rows // blk,),
        in_specs=[
            pl.BlockSpec((blk, d), lambda i: (i, 0)),
            pl.BlockSpec(w.shape, lambda i: (0, 0)),
            pl.BlockSpec((1, d), lambda i: (0, 0)),
        ],
        out_specs=[
            pl.BlockSpec((blk, d), lambda i: (i, 0)),
            pl.BlockSpec((blk, QPAD), lambda i: (i, 0)),
            pl.BlockSpec((blk, KPAD), lambda i: (i, 0)),
        ],
        out_shape=[
            jax.ShapeDtypeStruct((rows, d), BF16),
            jax.ShapeDtypeStruct((rows, QPAD), BF16),
            jax.ShapeDtypeStruct((rows, KPAD), BF16),
        ],
        compiler_params=params(),
        cost_estimate=cost(2 * rows * d * 800, rows * d * 6 + d * 1600),
        name="front",
    )(x, w, gain)


def make_cap(s_ref, dq_ref, dk_ref, cap_ref, nblk, own):
    dq = dq_ref[...]
    for i in range(nblk):
        rows = pl.ds(i * own, own)
        key = lax.broadcasted_iota(jnp.int32, (own, own), 0)
        query = lax.broadcasted_iota(jnp.int32, (own, own), 1) + s_ref[1 + i]
        ok = (dk_ref[rows, :] == dq) & (key <= query)
        cap_ref[rows, :] = jnp.where(ok, BIG, NEG)


def stacked(x):
    lane = lax.broadcasted_iota(jnp.int32, x.shape, 1)
    zero = jnp.zeros_like(x)
    return jnp.concatenate(
        [jnp.where(lane < DH, x, zero), jnp.where(lane >= DH, x, zero)], axis=0
    )


def unstacked(xt, own):
    pair = jnp.concatenate([xt[:DH, :own], xt[DH:, own:]], axis=0)
    return pair.T


def key_parts(kvf_ref, pair):
    ek = head_spread(pair, 0, RK, (128, RK * 128))
    ev = head_spread(pair, KCOLS - 128, RK, (128, RK * 128))
    ke = mm(kvf_ref[:, :128], ek)
    ve = mm(kvf_ref[:, 128:256], ev)
    return ke, ve


def tile_keys(kvf_ref, bk_ref, bv_ref):
    bk_ref[...] = mm(kvf_ref[:, :256], rank_tile(KA, (256, RK * 128)))
    bv_ref[...] = mm(kvf_ref[:, 128:384], rank_tile(KCOLS + KA - 128, (256, RK * 128)))


def attend_kernel(
    nblk, s_ref, qf_ref, kvg_ref, dq_ref, dk_ref, x_ref, wo_ref, g_ref,
    att_ref, q_ref, k_ref, v_ref, lse_ref, hm_ref, n_ref, kvw_ref,
    bq_ref, bk_ref, bv_ref, cap_ref, full_ref,
):
    pair = pl.program_id(0)
    own = qf_ref.shape[0]

    @pl.when(pair == 0)
    def _():
        for i in range(nblk):
            kvw_ref[pl.ds(i * own, own), :] = kvg_ref[s_ref[1 + nblk + i]]
        bq_ref[...] = mm(qf_ref[...], rank_tile(QA, (QPAD, RQ * 128)))
        tile_keys(kvw_ref, bk_ref, bv_ref)
        make_cap(s_ref, dq_ref, dk_ref, cap_ref, nblk, own)

    qe = mm(qf_ref[:, :128], head_spread(pair, 0, RQ, (128, RQ * 128)))
    qsum = qe[:, :128] * bq_ref[:, :128]
    for r in range(1, RQ):
        cols = slice(r * 128, (r + 1) * 128)
        qsum = qsum + qe[:, cols] * bq_ref[:, cols]
    q = (qsum * (1.0 / RQ)).astype(BF16)
    ke, ve = key_parts(kvw_ref, pair)
    k = ((ke[:, :128] * bk_ref[:, :128] + ke[:, 128:] * bk_ref[:, 128:]) * (1.0 / RK)).astype(BF16)
    v = ((ve[:, :128] * bv_ref[:, :128] + ve[:, 128:] * bv_ref[:, 128:]) * (1.0 / RK)).astype(BF16)
    q = q * jnp.asarray(DH ** (-0.5), BF16)
    q_ref[...] = q
    k_ref[...] = k
    v_ref[...] = v
    cap = cap_ref[...]
    st = jnp.minimum(mm(k, stacked(q), NT), jnp.concatenate([cap, cap], axis=1))
    top = jnp.max(st, axis=0, keepdims=True)
    e = jnp.exp(st - top)
    total = jnp.sum(e, axis=0, keepdims=True)
    p = (e * (1.0 / total)).astype(BF16)
    lse_ref[0] = top + jnp.log(total)
    att = unstacked(mm(v, p, TN), own).astype(BF16)
    att_ref[...] = att
    full_ref[pair] = att

    @pl.when(pair == pl.num_programs(0) - 1)
    def _():
        hm = x_ref[...].astype(F32)
        att_all = jnp.concatenate([full_ref[i] for i in range(PAIRS)], axis=1)
        hm = hm + mm(att_all, wo_ref[...])
        hm_ref[...] = hm
        r = lax.rsqrt(jnp.mean(hm * hm, axis=-1, keepdims=True) + EPS)
        n_ref[...] = (hm * r * g_ref[...]).astype(BF16)


def attend(nblk, scalars, qf, kvg, dq, dk, x, wo, gain):
    own, d = x.shape
    win = nblk * own
    whole = lambda a: pl.BlockSpec(a.shape, lambda p, a=a: (0,) * a.ndim)
    col = lambda rows: pl.BlockSpec((rows, 128), lambda p: (0, p))
    return pl.pallas_call(
        functools.partial(attend_kernel, nblk),
        grid=(PAIRS,),
        in_specs=[pl.BlockSpec(memory_space=pltpu.SMEM)]
        + [whole(a) for a in (qf, kvg, dq, dk, x, wo, gain)],
        out_specs=[
            col(own), col(own), col(win), col(win),
            pl.BlockSpec((1, 1, 2 * own), lambda p: (p, 0, 0)),
            pl.BlockSpec((own, d), lambda p: (0, 0)),
            pl.BlockSpec((own, d), lambda p: (0, 0)),
            pl.BlockSpec((win, KPAD), lambda p: (0, 0)),
        ],
        out_shape=[
            jax.ShapeDtypeStruct((own, d), BF16),
            jax.ShapeDtypeStruct((own, d), BF16),
            jax.ShapeDtypeStruct((win, d), BF16),
            jax.ShapeDtypeStruct((win, d), BF16),
            jax.ShapeDtypeStruct((PAIRS, 1, 2 * own), F32),
            jax.ShapeDtypeStruct((own, d), F32),
            jax.ShapeDtypeStruct((own, d), BF16),
            jax.ShapeDtypeStruct((win, KPAD), BF16),
        ],
        scratch_shapes=[
            pltpu.VMEM((own, RQ * 128), F32),
            pltpu.VMEM((win, RK * 128), F32),
            pltpu.VMEM((win, RK * 128), F32),
            pltpu.VMEM((win, own), F32),
            pltpu.VMEM((PAIRS, own, 128), BF16),
        ],
        compiler_params=params(),
        cost_estimate=cost(12e9, 12e6),
        name="attend",
    )(scalars, qf, kvg, dq, dk, x, wo, gain)


def ffn_kernel(has_prev, bf16_out, *refs):
    if has_prev:
        n_ref, c_ref, wg_ref, wu_ref, wd_ref, pg_ref, pu_ref, pd_ref = refs[:8]
        refs = refs[8:]
    else:
        n_ref, c_ref, wg_ref, wu_ref, wd_ref = refs[:5]
        refs = refs[5:]
    o_ref, dn_ref, og_ref, ou_ref, od_ref = refs[:5]
    if bf16_out:
        ag_ref, au_ref, ad_ref = refs[5:]
    else:
        ag_ref, au_ref, ad_ref = og_ref, ou_ref, od_ref
    step = pl.program_id(0)

    @pl.when(step == 0)
    def _():
        if has_prev:
            ag_ref[...] = pg_ref[...]
            au_ref[...] = pu_ref[...]
            ad_ref[...] = pd_ref[...]
        else:
            ag_ref[...] = jnp.zeros_like(ag_ref)
            au_ref[...] = jnp.zeros_like(au_ref)
            ad_ref[...] = jnp.zeros_like(ad_ref)

    n = n_ref[0]
    c = c_ref[0]
    wg, wu, wd = wg_ref[...], wu_ref[...], wd_ref[...]
    g = mm(n, wg)
    u = mm(n, wu)
    dh = mm(c, wd, NT)
    s = 1.0 / (1.0 + jnp.exp(-g))
    gs = g * s
    hid = (gs * u).astype(BF16)
    dg = (dh * u * (s * (1.0 + g * (1.0 - s)))).astype(BF16)
    du = (dh * gs).astype(BF16)
    o_ref[0] = mm(hid, wd).astype(BF16)
    dn_ref[0] = (mm(dg, wg, NT) + mm(du, wu, NT)).astype(BF16)
    ag_ref[...] += mm(n, dg, TN)
    au_ref[...] += mm(n, du, TN)
    ad_ref[...] += mm(hid, c, TN)
    if bf16_out:

        @pl.when(step == pl.num_programs(0) - 1)
        def _():
            og_ref[...] = ag_ref[...].astype(BF16)
            ou_ref[...] = au_ref[...].astype(BF16)
            od_ref[...] = ad_ref[...].astype(BF16)


def ffn(n, c, wg, wu, wd, prev, last):
    w, own, d = n.shape
    ff = wg.shape[1]
    one = lambda a: pl.BlockSpec(
        a.shape, lambda i, a=a: (0,) * a.ndim, pipeline_mode=pl.Buffered(1)
    )
    blk = pl.BlockSpec((1, own, d), lambda i: (i, 0, 0))
    dt = BF16 if last else F32
    args = [n, c, wg, wu, wd] + list(prev or [])
    shapes = [(d, ff), (d, ff), (ff, d)]
    return pl.pallas_call(
        functools.partial(ffn_kernel, bool(prev), last),
        grid=(w,),
        in_specs=[blk, blk] + [one(a) for a in args[2:]],
        out_specs=[blk, blk] + [
            pl.BlockSpec(s, lambda i: (0, 0), pipeline_mode=pl.Buffered(1)) for s in shapes
        ],
        out_shape=[jax.ShapeDtypeStruct(n.shape, BF16)] * 2
        + [jax.ShapeDtypeStruct(s, dt) for s in shapes],
        scratch_shapes=[pltpu.VMEM(s, F32) for s in shapes] if last else [],
        compiler_params=params(),
        cost_estimate=cost(18 * w * own * d * ff, 20 * w * own * d),
        name="ffn",
    )(*args)


def back_kernel(
    nblk, s_ref, q_ref, k_ref, v_ref, lse_ref, dq_ref, dk_ref, qf_ref, kvw_ref,
    dn_ref, hm_ref, c_ref, wo_ref, g_ref,
    dm_ref, dl_ref, gain_ref, gq_ref, gkv_ref,
    bq_ref, bk_ref, bv_ref, cap_ref, da_ref, aq_ref, ak_ref, av_ref, tq_ref, tk_ref, tv_ref,
):
    pair = pl.program_id(0)
    own = q_ref.shape[0]
    last = pl.num_programs(0) - 1

    @pl.when(pair == 0)
    def _():
        hm = hm_ref[...]
        dn = dn_ref[...].astype(F32)
        r = lax.rsqrt(jnp.mean(hm * hm, axis=-1, keepdims=True) + EPS)
        z = dn * g_ref[...]
        gain_ref[...] = jnp.sum(dn * hm * r, axis=0, keepdims=True)
        dm = (
            c_ref[...].astype(F32)
            + r * z
            - hm * (r * r * r) * jnp.mean(z * hm, axis=-1, keepdims=True)
        )
        dm_ref[...] = dm
        low = dm.astype(BF16)
        dl_ref[...] = low
        da = mm(low, wo_ref[...], NT).astype(BF16)
        for i in range(PAIRS):
            da_ref[i] = da[:, i * 128:(i + 1) * 128]
        bq_ref[...] = mm(qf_ref[...], rank_tile(QA, (QPAD, RQ * 128)))
        tile_keys(kvw_ref, bk_ref, bv_ref)
        make_cap(s_ref, dq_ref, dk_ref, cap_ref, nblk, own)
        for ref in (aq_ref, ak_ref, av_ref, tq_ref, tk_ref, tv_ref):
            ref[...] = jnp.zeros_like(ref)

    q = q_ref[...]
    k = k_ref[...]
    v = v_ref[...]
    qs = stacked(q)
    ds_ = stacked(da_ref[pair])
    cap = cap_ref[...]
    st = jnp.minimum(mm(k, qs, NT), jnp.concatenate([cap, cap], axis=1))
    p = jnp.exp(st - lse_ref[0])
    dp = mm(v, ds_, NT)
    delta = jnp.sum(p * dp, axis=0, keepdims=True)
    ds = (p * (dp - delta)).astype(BF16)
    dv = mm(p.astype(BF16), ds_)
    dk = mm(ds, qs)
    dq = unstacked(mm(k, ds, TN), own) * (DH ** (-0.5))

    eq = head_spread(pair, 0, RQ, (128, RQ * 128))
    qe = mm(qf_ref[:, :128], eq)
    dq6 = jnp.concatenate([dq] * RQ, axis=1)
    tq_ref[...] += dq6 * qe
    aq_ref[...] += mm((dq6 * bq_ref[...]).astype(BF16), eq, NT)
    ek = head_spread(pair, 0, RK, (128, RK * 128))
    ev = head_spread(pair, KCOLS - 128, RK, (128, RK * 128))
    ke = mm(kvw_ref[:, :128], ek)
    ve = mm(kvw_ref[:, 128:256], ev)
    dk2 = jnp.concatenate([dk] * RK, axis=1)
    dv2 = jnp.concatenate([dv] * RK, axis=1)
    tk_ref[...] += dk2 * ke
    tv_ref[...] += dv2 * ve
    ak_ref[...] += mm((dk2 * bk_ref[...]).astype(BF16), ek, NT)
    av_ref[...] += mm((dv2 * bv_ref[...]).astype(BF16), ev, NT)

    @pl.when(pair == last)
    def _():
        def fold(x, t):
            hi = x.astype(BF16)
            lo = (x - hi.astype(F32)).astype(BF16)
            return mm(hi, t, NT) + mm(lo, t, NT)

        gq = fold(tq_ref[...], rank_tile(QA, (QPAD, RQ * 128)))
        gq_ref[:, :128] = ((gq[:, :128] + aq_ref[...]) * (1.0 / RQ)).astype(BF16)
        gq_ref[:, 128:] = (gq[:, 128:] * (1.0 / RQ)).astype(BF16)
        gk = fold(tk_ref[...], rank_tile(KA, (KPAD, RK * 128)))
        gv = fold(tv_ref[...], rank_tile(KCOLS + KA, (KPAD, RK * 128)))
        gkv = gk + gv
        first = ((gkv[:, :128] + ak_ref[...]) * (1.0 / RK)).astype(BF16)
        second = ((gkv[:, 128:256] + av_ref[...]) * (1.0 / RK)).astype(BF16)
        third = (gkv[:, 256:] * (1.0 / RK)).astype(BF16)
        gkv_ref[...] = jnp.zeros_like(gkv_ref)
        for i in range(nblk):
            rows = slice(i * own, (i + 1) * own)
            slot = s_ref[1 + nblk + i]
            gkv_ref[slot, :, :128] = first[rows]
            gkv_ref[slot, :, 128:256] = second[rows]
            gkv_ref[slot, :, 256:] = third[rows]


def back(nblk, width, scalars, q, k, v, lse, dq, dk, qf, kvw, dn, hm, c, wo, gain):
    own, d = q.shape
    win = nblk * own
    whole = lambda a: pl.BlockSpec(a.shape, lambda p, a=a: (0,) * a.ndim)
    col = lambda rows: pl.BlockSpec((rows, 128), lambda p: (0, p))
    fixed = lambda *s: pl.BlockSpec(s, lambda p: (0,) * len(s))
    return pl.pallas_call(
        functools.partial(back_kernel, nblk),
        grid=(PAIRS,),
        in_specs=[
            pl.BlockSpec(memory_space=pltpu.SMEM), col(own), col(win), col(win),
            pl.BlockSpec((1, 1, 2 * own), lambda p: (p, 0, 0)),
        ] + [whole(a) for a in (dq, dk, qf, kvw, dn, hm, c, wo, gain)],
        out_specs=[
            fixed(own, d), fixed(own, d), fixed(1, d), fixed(own, QPAD),
            fixed(width, own, KPAD),
        ],
        out_shape=[
            jax.ShapeDtypeStruct((own, d), F32),
            jax.ShapeDtypeStruct((own, d), BF16),
            jax.ShapeDtypeStruct((1, d), F32),
            jax.ShapeDtypeStruct((own, QPAD), BF16),
            jax.ShapeDtypeStruct((width, own, KPAD), BF16),
        ],
        scratch_shapes=[
            pltpu.VMEM((own, RQ * 128), F32),
            pltpu.VMEM((win, RK * 128), F32),
            pltpu.VMEM((win, RK * 128), F32),
            pltpu.VMEM((win, own), F32),
            pltpu.VMEM((PAIRS, own, 128), BF16),
            pltpu.VMEM((own, 128), F32),
            pltpu.VMEM((win, 128), F32),
            pltpu.VMEM((win, 128), F32),
            pltpu.VMEM((own, RQ * 128), F32),
            pltpu.VMEM((win, RK * 128), F32),
            pltpu.VMEM((win, RK * 128), F32),
        ],
        compiler_params=params(),
        cost_estimate=cost(30e9, 15e6),
        name="back",
    )(scalars, q, k, v, lse, dq, dk, qf, kvw, dn, hm, c, wo, gain)


def flip(index, bit):
    digit = (index // bit) % 2
    return index + bit - 2 * bit * digit


class Butterfly:
    def __init__(self, buf, got, res, send, recv, partners):
        self.buf, self.got, self.res, self.send, self.recv = buf, got, res, send, recv
        self.partners = partners
        self.slots = 2 ** len(partners)

    def halve(self, i):
        half = self.slots >> (i + 1)
        offset = self.slots - 2 * half
        return pltpu.make_async_remote_copy(
            src_ref=self.buf.at[pl.ds(half, half)],
            dst_ref=self.got.at[pl.ds(offset, half)],
            send_sem=self.send.at[i],
            recv_sem=self.recv.at[i],
            device_id=self.partners[i],
            device_id_type=pl.DeviceIdType.MESH,
        )

    def add(self, i):
        half = self.slots >> (i + 1)
        offset = self.slots - 2 * half
        self.halve(i).wait()

        def one(j, carry):
            total = self.buf[j].astype(F32) + self.got[offset + j].astype(F32)
            into = self.res if half == 1 else self.buf
            into[j] = total.astype(BF16)
            return carry

        lax.fori_loop(0, half, one, 0)

    def double(self, i):
        half = self.slots >> (i + 1)
        k = len(self.partners) + i
        return pltpu.make_async_remote_copy(
            src_ref=self.res.at[pl.ds(0, half)],
            dst_ref=self.res.at[pl.ds(half, half)],
            send_sem=self.send.at[k],
            recv_sem=self.recv.at[k],
            device_id=self.partners[i],
            device_id_type=pl.DeviceIdType.MESH,
        )


AXES = {"c": ("wide", 1), "x": ("wide", 2), "y": ("rows", 1), "n": ("rows", 2), "f": ("rows", 4)}
ORDERS = ("cxynf", "cynfx", "cnfxy")


def enter(names):
    barrier = pltpu.get_barrier_semaphore()
    for name in names:
        pl.semaphore_signal(
            barrier, inc=1, device_id=partner(name), device_id_type=pl.DeviceIdType.MESH
        )
    pl.semaphore_wait(barrier, len(names))


def partner(name):
    axis, bit = AXES[name]
    return {axis: flip(lax.axis_index(axis), bit)}


def digit(name):
    axis, bit = AXES[name]
    return (lax.axis_index(axis) // bit) % 2


def chunk_of(slot, names):
    n = len(names)
    weight = {name: 2 ** k for k, name in enumerate(sorted(names))}
    total = 0
    for i, name in enumerate(names):
        turned = (slot >> (n - 1 - i)) & 1
        d = digit(name)
        total = total + weight[name] * ((1 - d) if turned else d)
    return total


def total_kernel(parts, x_ref, o_ref, *refs):
    count = len(parts)
    bufs, gots, ress = refs[:count], refs[count:2 * count], refs[2 * count:3 * count]
    send, recv = refs[3 * count:]
    flies = []
    base = 0
    places = []
    for g, rows in enumerate(parts):
        names = ORDERS[g]
        flies.append(
            Butterfly(bufs[g], gots[g], ress[g], send.at[g], recv.at[g], [partner(n) for n in names])
        )
        spots = []
        for t in range(32):
            c = chunk_of(t, names)
            row = pl.multiple_of(base + (c // 8) * rows, 16)
            col = pl.multiple_of((c % 8) * 128, 128)
            spots.append((pl.ds(row, rows), pl.ds(col, 128)))
        places.append(spots)
        base += 4 * rows
    enter("cxynf")
    for half in (range(16, 32), range(16)):
        for g in range(count):
            for t in half:
                bufs[g][t] = x_ref[places[g][t]]
            if half[0] == 16:
                flies[g].halve(0).start()
    for i in range(5):
        for fly in flies:
            fly.add(i)
            if i < 4:
                fly.halve(i + 1).start()
            else:
                fly.double(4).start()
    for i in range(4, -1, -1):
        for g, fly in enumerate(flies):
            fly.double(i).wait()
            if i > 0:
                fly.double(i - 1).start()
            half = 32 >> (i + 1)
            for t in range(half, 2 * half):
                o_ref[places[g][t]] = ress[g][t]
            if i == 4:
                o_ref[places[g][0]] = ress[g][0]


def total(x):
    rows, d = x.shape
    unit = rows // 64
    parts = [16 * (unit // 3 + (1 if g < unit % 3 else 0)) for g in range(3)]
    return pl.pallas_call(
        functools.partial(total_kernel, parts),
        in_specs=[pl.BlockSpec(memory_space=pltpu.VMEM)],
        out_specs=pl.BlockSpec(memory_space=pltpu.VMEM),
        out_shape=jax.ShapeDtypeStruct((rows, d), BF16),
        scratch_shapes=[pltpu.VMEM((32, r, 128), BF16) for r in parts]
        + [pltpu.VMEM((31, r, 128), BF16) for r in parts]
        + [pltpu.VMEM((32, r, 128), BF16) for r in parts]
        + [pltpu.SemaphoreType.DMA((3, 10)), pltpu.SemaphoreType.DMA((3, 10))],
        compiler_params=pltpu.CompilerParams(
            vmem_limit_bytes=60 << 20, collective_id=0, has_side_effects=True
        ),
        cost_estimate=cost(1e6, 8 * rows * d),
        name="total",
    )(x)


def swap(x, axis, size, bit):
    return lax.ppermute(x, axis, [(i, i ^ bit) for i in range(size)])


def steps_of(size):
    bits, b = [], size // 2
    while b:
        bits.append(b)
        b //= 2
    return bits


def gather(x, size):
    buf = x[None]
    for bit in steps_of(size):
        buf = jnp.concatenate([buf, swap(buf, "wide", size, bit)], axis=0)
    return buf


def order_of(size):
    order = [0]
    for bit in steps_of(size):
        order = order + [o ^ bit for o in order]
    return order


def scatter(parts, size):
    for bit in reversed(steps_of(size)):
        half = parts.shape[0] // 2
        got = swap(parts[half:], "wide", size, bit)
        total = parts[:half].astype(F32) + got.astype(F32)
        parts = total if half == 1 else total.astype(BF16)
    return parts[0]


def body(
    small, tokens, doc_ids, factor_weight, output_weight, norm_one, norm_two,
    gate_weight, up_weight, down_weight, cotangent,
):
    seqs, own, d = tokens.shape
    full_len = doc_ids.shape[1]
    size = full_len // own
    me = lax.axis_index("wide")
    left = min(-(-(MAX_DOC - 1) // own), size - 1)
    nblk = left + 1
    start = jnp.maximum(me - left, 0)
    order = order_of(size)
    slot_of = [order.index(j) for j in range(size)]
    slots = jnp.asarray(slot_of, jnp.int32)
    blocks = start + jnp.arange(nblk, dtype=jnp.int32)
    scalars = jnp.concatenate(
        [me[None].astype(jnp.int32), (me - blocks) * own, slots[me ^ blocks]]
    ).astype(jnp.int32)
    g1 = norm_one[None]
    g2 = norm_two[None]

    n1, qf, kvf = front(tokens.reshape(seqs * own, d), factor_weight, g1)
    qf = qf.reshape(seqs, own, QPAD)
    kvg = gather(kvf.reshape(seqs, own, KPAD), size)
    doc_query = lax.dynamic_slice_in_dim(doc_ids, me * own, own, 1)
    doc_key = lax.dynamic_slice_in_dim(doc_ids, start * own, nblk * own, 1)
    cots = [gather(cotangent[s], size) for s in range(seqs)]

    fwd = []
    for s in range(seqs):
        dq = doc_query[s][None, :]
        dk = doc_key[s][:, None]
        fwd.append(
            (dq, dk)
            + tuple(attend(nblk, scalars, qf[s], kvg[:, s], dq, dk, tokens[s], output_weight, g2))
        )
    prev = None
    outs, dns = [], []
    for s in range(seqs):
        n2 = gather(fwd[s][8], size)
        res = ffn(n2, cots[s], gate_weight, up_weight, down_weight, prev, s == seqs - 1)
        outs.append(res[0])
        dns.append(res[1])
        prev = res[2:]
    grads = [lax.psum(g, "rows").astype(F32) for g in prev]

    output, mids, lows, gain_two, gqs, gkvs = [], [], [], 0.0, [], []
    for s in range(seqs):
        dq, dk, att, q, k, v, lse, hm, n2, kvw = fwd[s]
        dn = scatter(dns[s], size)
        dm, low, gain, gq, gkv = back(
            nblk, size, scalars, q, k, v, lse, dq, dk, qf[s], kvw, dn, hm,
            cotangent[s], output_weight, g2,
        )
        output.append((hm + scatter(outs[s], size)).astype(BF16))
        mids.append(dm)
        lows.append(low)
        gqs.append(gq)
        gkvs.append(gkv)
        gain_two = gain_two + gain
    att_all = jnp.stack([f[2] for f in fwd]).reshape(seqs * own, d)
    grad_out = mm(att_all, jnp.stack(lows).reshape(seqs * own, d), TN)
    gkv = scatter(jnp.stack(gkvs, axis=1), size).astype(BF16)
    dfac = jnp.concatenate([jnp.stack(gqs)[..., :QCOLS], gkv[..., :KV]], axis=-1)
    dfac = dfac.reshape(seqs * own, -1)
    grad_factors = mm(n1, dfac, TN)
    dn1 = mm(dfac, factor_weight, NT)
    hin = tokens.reshape(seqs * own, d).astype(F32)
    r1 = lax.rsqrt(jnp.mean(hin * hin, axis=-1, keepdims=True) + EPS)
    z1 = dn1 * g1
    gain_one = jnp.sum(dn1 * hin * r1, axis=0)
    grad_norm = r1 * z1 - hin * (r1 * r1 * r1) * jnp.mean(z1 * hin, axis=-1, keepdims=True)
    input_grad = (jnp.stack(mids).reshape(seqs * own, d) + grad_norm).astype(BF16)
    parts = [grad_out, grad_factors.T, gain_one[None], gain_two]
    packed = jnp.concatenate([p.astype(BF16) for p in parts], axis=0)
    packed = jnp.pad(packed, ((0, -packed.shape[0] % 64), (0, 0)))
    if small:
        packed = total(packed).astype(F32)
    else:
        packed = lax.psum(packed, ("rows", "wide")).astype(F32)
    fac = grad_factors.shape[1]
    return (
        jnp.stack(output),
        input_grad.reshape(seqs, own, d),
        packed[d:d + fac].T,
        packed[:d],
        packed[d + fac],
        packed[d + fac + 1],
        grads[0],
        grads[1],
        grads[2],
    )


def solution(mesh):
    placed = (
        P("rows", "wide", None), P("rows", None), P(), P(), P(), P(),
        P(None, "wide"), P(None, "wide"), P("wide", None), P("rows", "wide", None),
    )
    small = mesh.shape["rows"] == 8 and mesh.shape["wide"] == 4
    return jax.shard_map(
        functools.partial(body, small),
        mesh=mesh,
        in_specs=placed,
        out_specs=(
            P("rows", "wide", None), P("rows", "wide", None), P(), P(), P(), P(),
            P(None, "wide"), P(None, "wide"), P("wide", None),
        ),
        check_vma=False,
    )
```

```python
import functools

import jax
import jax.numpy as jnp
from jax import lax
from jax.experimental import pallas as pl
from jax.experimental.pallas import tpu as pltpu
from jax.sharding import PartitionSpec as P

H = 16
DH = 64
RQ = 6
RK = 2
MAX_DOC = 512
EPS = 1e-06
NEG = -1000000000.0
BIG = 3.0e38

QA = H * RQ
QCOLS = QA + RQ * DH
KA = H * RK
KCOLS = KA + RK * DH
KV = 2 * KCOLS
QPAD = 512
KPAD = 384
PAIRS = H // 2

F32 = jnp.float32
BF16 = jnp.bfloat16

NN = (((1,), (0,)), ((), ()))
NT = (((1,), (1,)), ((), ()))
TN = (((0,), (0,)), ((), ()))


def mm(a, b, dims=NN):
    return lax.dot_general(a, b, dims, preferred_element_type=F32)


def params(vmem_mb=60):
    return pltpu.CompilerParams(vmem_limit_bytes=vmem_mb << 20)


def cost(flops, nbytes):
    return pl.CostEstimate(flops=int(flops), bytes_accessed=int(nbytes), transcendentals=0)


def selection(shape, rule):
    row = lax.broadcasted_iota(jnp.int32, shape, 0)
    col = lax.broadcasted_iota(jnp.int32, shape, 1)
    return jnp.where(rule(row, col), 1.0, 0.0).astype(BF16)


def head_spread(pair, base, rank, shape):
    def rule(row, col):
        r = col // 128
        lane = col - r * 128
        head = 2 * pair + jnp.where(lane >= DH, 1, 0)
        return row == base + head * rank + r

    return selection(shape, rule)


def rank_tile(base, shape):
    def rule(row, col):
        r = col // 128
        lane = col - r * 128
        return row == base + r * DH + jnp.where(lane >= DH, lane - DH, lane)

    return selection(shape, rule)


def front_kernel(x_ref, w_ref, g_ref, n_ref, q_ref, kv_ref):
    x = x_ref[...].astype(F32)
    r = lax.rsqrt(jnp.mean(x * x, axis=-1, keepdims=True) + EPS)
    n = (x * r * g_ref[...]).astype(BF16)
    n_ref[...] = n
    f = mm(n, w_ref[...]).astype(BF16)
    q_ref[...] = f[:, :QPAD]
    kv_ref[:, :KV] = f[:, QCOLS:]
    kv_ref[:, KV:] = jnp.zeros((f.shape[0], KPAD - KV), BF16)


def front(x, w, gain):
    rows, d = x.shape
    blk = 256 if rows % 256 == 0 else rows
    return pl.pallas_call(
        front_kernel,
        grid=(rows // blk,),
        in_specs=[
            pl.BlockSpec((blk, d), lambda i: (i, 0)),
            pl.BlockSpec(w.shape, lambda i: (0, 0)),
            pl.BlockSpec((1, d), lambda i: (0, 0)),
        ],
        out_specs=[
            pl.BlockSpec((blk, d), lambda i: (i, 0)),
            pl.BlockSpec((blk, QPAD), lambda i: (i, 0)),
            pl.BlockSpec((blk, KPAD), lambda i: (i, 0)),
        ],
        out_shape=[
            jax.ShapeDtypeStruct((rows, d), BF16),
            jax.ShapeDtypeStruct((rows, QPAD), BF16),
            jax.ShapeDtypeStruct((rows, KPAD), BF16),
        ],
        compiler_params=params(),
        cost_estimate=cost(2 * rows * d * 800, rows * d * 6 + d * 1600),
        name="front",
    )(x, w, gain)


def make_cap(s_ref, dq_ref, dk_ref, cap_ref, nblk, own):
    dq = dq_ref[...]
    for i in range(nblk):
        rows = pl.ds(i * own, own)
        key = lax.broadcasted_iota(jnp.int32, (own, own), 0)
        query = lax.broadcasted_iota(jnp.int32, (own, own), 1) + s_ref[1 + i]
        ok = (dk_ref[rows, :] == dq) & (key <= query)
        cap_ref[rows, :] = jnp.where(ok, BIG, NEG)


def stacked(x):
    lane = lax.broadcasted_iota(jnp.int32, x.shape, 1)
    zero = jnp.zeros_like(x)
    return jnp.concatenate(
        [jnp.where(lane < DH, x, zero), jnp.where(lane >= DH, x, zero)], axis=0
    )


def unstacked(xt, own):
    pair = jnp.concatenate([xt[:DH, :own], xt[DH:, own:]], axis=0)
    return pair.T


def key_parts(kvf_ref, pair):
    ek = head_spread(pair, 0, RK, (128, RK * 128))
    ev = head_spread(pair, KCOLS - 128, RK, (128, RK * 128))
    ke = mm(kvf_ref[:, :128], ek)
    ve = mm(kvf_ref[:, 128:256], ev)
    return ke, ve


def tile_keys(kvf_ref, bk_ref, bv_ref):
    bk_ref[...] = mm(kvf_ref[:, :256], rank_tile(KA, (256, RK * 128)))
    bv_ref[...] = mm(kvf_ref[:, 128:384], rank_tile(KCOLS + KA - 128, (256, RK * 128)))


def attend_kernel(
    nblk, s_ref, qf_ref, kvg_ref, dq_ref, dk_ref, x_ref, wo_ref, g_ref,
    att_ref, q_ref, k_ref, v_ref, lse_ref, hm_ref, n_ref, kvw_ref,
    bq_ref, bk_ref, bv_ref, cap_ref, full_ref,
):
    pair = pl.program_id(0)
    own = qf_ref.shape[0]

    @pl.when(pair == 0)
    def _():
        for i in range(nblk):
            kvw_ref[pl.ds(i * own, own), :] = kvg_ref[s_ref[1 + nblk + i]]
        bq_ref[...] = mm(qf_ref[...], rank_tile(QA, (QPAD, RQ * 128)))
        tile_keys(kvw_ref, bk_ref, bv_ref)
        make_cap(s_ref, dq_ref, dk_ref, cap_ref, nblk, own)

    qe = mm(qf_ref[:, :128], head_spread(pair, 0, RQ, (128, RQ * 128)))
    qsum = qe[:, :128] * bq_ref[:, :128]
    for r in range(1, RQ):
        cols = slice(r * 128, (r + 1) * 128)
        qsum = qsum + qe[:, cols] * bq_ref[:, cols]
    q = (qsum * (1.0 / RQ)).astype(BF16)
    ke, ve = key_parts(kvw_ref, pair)
    k = ((ke[:, :128] * bk_ref[:, :128] + ke[:, 128:] * bk_ref[:, 128:]) * (1.0 / RK)).astype(BF16)
    v = ((ve[:, :128] * bv_ref[:, :128] + ve[:, 128:] * bv_ref[:, 128:]) * (1.0 / RK)).astype(BF16)
    q = q * jnp.asarray(DH ** (-0.5), BF16)
    q_ref[...] = q
    k_ref[...] = k
    v_ref[...] = v
    cap = cap_ref[...]
    st = jnp.minimum(mm(k, stacked(q), NT), jnp.concatenate([cap, cap], axis=1))
    top = jnp.max(st, axis=0, keepdims=True)
    e = jnp.exp(st - top)
    total = jnp.sum(e, axis=0, keepdims=True)
    p = (e * (1.0 / total)).astype(BF16)
    lse_ref[0] = top + jnp.log(total)
    att = unstacked(mm(v, p, TN), own).astype(BF16)
    att_ref[...] = att
    full_ref[pair] = att

    @pl.when(pair == pl.num_programs(0) - 1)
    def _():
        hm = x_ref[...].astype(F32)
        att_all = jnp.concatenate([full_ref[i] for i in range(PAIRS)], axis=1)
        hm = hm + mm(att_all, wo_ref[...])
        hm_ref[...] = hm
        r = lax.rsqrt(jnp.mean(hm * hm, axis=-1, keepdims=True) + EPS)
        n_ref[...] = (hm * r * g_ref[...]).astype(BF16)


def attend(nblk, scalars, qf, kvg, dq, dk, x, wo, gain):
    own, d = x.shape
    win = nblk * own
    whole = lambda a: pl.BlockSpec(a.shape, lambda p, a=a: (0,) * a.ndim)
    col = lambda rows: pl.BlockSpec((rows, 128), lambda p: (0, p))
    return pl.pallas_call(
        functools.partial(attend_kernel, nblk),
        grid=(PAIRS,),
        in_specs=[pl.BlockSpec(memory_space=pltpu.SMEM)]
        + [whole(a) for a in (qf, kvg, dq, dk, x, wo, gain)],
        out_specs=[
            col(own), col(own), col(win), col(win),
            pl.BlockSpec((1, 1, 2 * own), lambda p: (p, 0, 0)),
            pl.BlockSpec((own, d), lambda p: (0, 0)),
            pl.BlockSpec((own, d), lambda p: (0, 0)),
            pl.BlockSpec((win, KPAD), lambda p: (0, 0)),
        ],
        out_shape=[
            jax.ShapeDtypeStruct((own, d), BF16),
            jax.ShapeDtypeStruct((own, d), BF16),
            jax.ShapeDtypeStruct((win, d), BF16),
            jax.ShapeDtypeStruct((win, d), BF16),
            jax.ShapeDtypeStruct((PAIRS, 1, 2 * own), F32),
            jax.ShapeDtypeStruct((own, d), F32),
            jax.ShapeDtypeStruct((own, d), BF16),
            jax.ShapeDtypeStruct((win, KPAD), BF16),
        ],
        scratch_shapes=[
            pltpu.VMEM((own, RQ * 128), F32),
            pltpu.VMEM((win, RK * 128), F32),
            pltpu.VMEM((win, RK * 128), F32),
            pltpu.VMEM((win, own), F32),
            pltpu.VMEM((PAIRS, own, 128), BF16),
        ],
        compiler_params=params(),
        cost_estimate=cost(12e9, 12e6),
        name="attend",
    )(scalars, qf, kvg, dq, dk, x, wo, gain)


def ffn_kernel(has_prev, bf16_out, *refs):
    if has_prev:
        n_ref, c_ref, wg_ref, wu_ref, wd_ref, pg_ref, pu_ref, pd_ref = refs[:8]
        refs = refs[8:]
    else:
        n_ref, c_ref, wg_ref, wu_ref, wd_ref = refs[:5]
        refs = refs[5:]
    o_ref, dn_ref, og_ref, ou_ref, od_ref = refs[:5]
    if bf16_out:
        ag_ref, au_ref, ad_ref = refs[5:]
    else:
        ag_ref, au_ref, ad_ref = og_ref, ou_ref, od_ref
    step = pl.program_id(0)

    @pl.when(step == 0)
    def _():
        if has_prev:
            ag_ref[...] = pg_ref[...]
            au_ref[...] = pu_ref[...]
            ad_ref[...] = pd_ref[...]
        else:
            ag_ref[...] = jnp.zeros_like(ag_ref)
            au_ref[...] = jnp.zeros_like(au_ref)
            ad_ref[...] = jnp.zeros_like(ad_ref)

    n = n_ref[0]
    c = c_ref[0]
    wg, wu, wd = wg_ref[...], wu_ref[...], wd_ref[...]
    g = mm(n, wg)
    u = mm(n, wu)
    dh = mm(c, wd, NT)
    s = 1.0 / (1.0 + jnp.exp(-g))
    gs = g * s
    hid = (gs * u).astype(BF16)
    dg = (dh * u * (s * (1.0 + g * (1.0 - s)))).astype(BF16)
    du = (dh * gs).astype(BF16)
    o_ref[0] = mm(hid, wd).astype(BF16)
    dn_ref[0] = (mm(dg, wg, NT) + mm(du, wu, NT)).astype(BF16)
    ag_ref[...] += mm(n, dg, TN)
    au_ref[...] += mm(n, du, TN)
    ad_ref[...] += mm(hid, c, TN)
    if bf16_out:

        @pl.when(step == pl.num_programs(0) - 1)
        def _():
            og_ref[...] = ag_ref[...].astype(BF16)
            ou_ref[...] = au_ref[...].astype(BF16)
            od_ref[...] = ad_ref[...].astype(BF16)


def ffn(n, c, wg, wu, wd, prev, last):
    w, own, d = n.shape
    ff = wg.shape[1]
    one = lambda a: pl.BlockSpec(
        a.shape, lambda i, a=a: (0,) * a.ndim, pipeline_mode=pl.Buffered(1)
    )
    blk = pl.BlockSpec((1, own, d), lambda i: (i, 0, 0))
    dt = BF16 if last else F32
    args = [n, c, wg, wu, wd] + list(prev or [])
    shapes = [(d, ff), (d, ff), (ff, d)]
    return pl.pallas_call(
        functools.partial(ffn_kernel, bool(prev), last),
        grid=(w,),
        in_specs=[blk, blk] + [one(a) for a in args[2:]],
        out_specs=[blk, blk] + [
            pl.BlockSpec(s, lambda i: (0, 0), pipeline_mode=pl.Buffered(1)) for s in shapes
        ],
        out_shape=[jax.ShapeDtypeStruct(n.shape, BF16)] * 2
        + [jax.ShapeDtypeStruct(s, dt) for s in shapes],
        scratch_shapes=[pltpu.VMEM(s, F32) for s in shapes] if last else [],
        compiler_params=params(),
        cost_estimate=cost(18 * w * own * d * ff, 20 * w * own * d),
        name="ffn",
    )(*args)


def back_kernel(
    nblk, s_ref, q_ref, k_ref, v_ref, lse_ref, dq_ref, dk_ref, qf_ref, kvw_ref,
    dn_ref, hm_ref, c_ref, wo_ref, g_ref,
    dm_ref, dl_ref, gain_ref, gq_ref, gkv_ref,
    bq_ref, bk_ref, bv_ref, cap_ref, da_ref, aq_ref, ak_ref, av_ref, tq_ref, tk_ref, tv_ref,
):
    pair = pl.program_id(0)
    own = q_ref.shape[0]
    last = pl.num_programs(0) - 1

    @pl.when(pair == 0)
    def _():
        hm = hm_ref[...]
        dn = dn_ref[...].astype(F32)
        r = lax.rsqrt(jnp.mean(hm * hm, axis=-1, keepdims=True) + EPS)
        z = dn * g_ref[...]
        gain_ref[...] = jnp.sum(dn * hm * r, axis=0, keepdims=True)
        dm = (
            c_ref[...].astype(F32)
            + r * z
            - hm * (r * r * r) * jnp.mean(z * hm, axis=-1, keepdims=True)
        )
        dm_ref[...] = dm
        low = dm.astype(BF16)
        dl_ref[...] = low
        da = mm(low, wo_ref[...], NT).astype(BF16)
        for i in range(PAIRS):
            da_ref[i] = da[:, i * 128:(i + 1) * 128]
        bq_ref[...] = mm(qf_ref[...], rank_tile(QA, (QPAD, RQ * 128)))
        tile_keys(kvw_ref, bk_ref, bv_ref)
        make_cap(s_ref, dq_ref, dk_ref, cap_ref, nblk, own)
        for ref in (aq_ref, ak_ref, av_ref, tq_ref, tk_ref, tv_ref):
            ref[...] = jnp.zeros_like(ref)

    q = q_ref[...]
    k = k_ref[...]
    v = v_ref[...]
    qs = stacked(q)
    ds_ = stacked(da_ref[pair])
    cap = cap_ref[...]
    st = jnp.minimum(mm(k, qs, NT), jnp.concatenate([cap, cap], axis=1))
    p = jnp.exp(st - lse_ref[0])
    dp = mm(v, ds_, NT)
    delta = jnp.sum(p * dp, axis=0, keepdims=True)
    ds = (p * (dp - delta)).astype(BF16)
    dv = mm(p.astype(BF16), ds_)
    dk = mm(ds, qs)
    dq = unstacked(mm(k, ds, TN), own) * (DH ** (-0.5))

    eq = head_spread(pair, 0, RQ, (128, RQ * 128))
    qe = mm(qf_ref[:, :128], eq)
    dq6 = jnp.concatenate([dq] * RQ, axis=1)
    tq_ref[...] += dq6 * qe
    aq_ref[...] += mm((dq6 * bq_ref[...]).astype(BF16), eq, NT)
    ek = head_spread(pair, 0, RK, (128, RK * 128))
    ev = head_spread(pair, KCOLS - 128, RK, (128, RK * 128))
    ke = mm(kvw_ref[:, :128], ek)
    ve = mm(kvw_ref[:, 128:256], ev)
    dk2 = jnp.concatenate([dk] * RK, axis=1)
    dv2 = jnp.concatenate([dv] * RK, axis=1)
    tk_ref[...] += dk2 * ke
    tv_ref[...] += dv2 * ve
    ak_ref[...] += mm((dk2 * bk_ref[...]).astype(BF16), ek, NT)
    av_ref[...] += mm((dv2 * bv_ref[...]).astype(BF16), ev, NT)

    @pl.when(pair == last)
    def _():
        def fold(x, t):
            hi = x.astype(BF16)
            lo = (x - hi.astype(F32)).astype(BF16)
            return mm(hi, t, NT) + mm(lo, t, NT)

        gq = fold(tq_ref[...], rank_tile(QA, (QPAD, RQ * 128)))
        gq_ref[:, :128] = ((gq[:, :128] + aq_ref[...]) * (1.0 / RQ)).astype(BF16)
        gq_ref[:, 128:] = (gq[:, 128:] * (1.0 / RQ)).astype(BF16)
        gk = fold(tk_ref[...], rank_tile(KA, (KPAD, RK * 128)))
        gv = fold(tv_ref[...], rank_tile(KCOLS + KA, (KPAD, RK * 128)))
        gkv = gk + gv
        first = ((gkv[:, :128] + ak_ref[...]) * (1.0 / RK)).astype(BF16)
        second = ((gkv[:, 128:256] + av_ref[...]) * (1.0 / RK)).astype(BF16)
        third = (gkv[:, 256:] * (1.0 / RK)).astype(BF16)
        gkv_ref[...] = jnp.zeros_like(gkv_ref)
        for i in range(nblk):
            rows = slice(i * own, (i + 1) * own)
            slot = s_ref[1 + nblk + i]
            gkv_ref[slot, :, :128] = first[rows]
            gkv_ref[slot, :, 128:256] = second[rows]
            gkv_ref[slot, :, 256:] = third[rows]


def back(nblk, width, scalars, q, k, v, lse, dq, dk, qf, kvw, dn, hm, c, wo, gain):
    own, d = q.shape
    win = nblk * own
    whole = lambda a: pl.BlockSpec(a.shape, lambda p, a=a: (0,) * a.ndim)
    col = lambda rows: pl.BlockSpec((rows, 128), lambda p: (0, p))
    fixed = lambda *s: pl.BlockSpec(s, lambda p: (0,) * len(s))
    return pl.pallas_call(
        functools.partial(back_kernel, nblk),
        grid=(PAIRS,),
        in_specs=[
            pl.BlockSpec(memory_space=pltpu.SMEM), col(own), col(win), col(win),
            pl.BlockSpec((1, 1, 2 * own), lambda p: (p, 0, 0)),
        ] + [whole(a) for a in (dq, dk, qf, kvw, dn, hm, c, wo, gain)],
        out_specs=[
            fixed(own, d), fixed(own, d), fixed(1, d), fixed(own, QPAD),
            fixed(width, own, KPAD),
        ],
        out_shape=[
            jax.ShapeDtypeStruct((own, d), F32),
            jax.ShapeDtypeStruct((own, d), BF16),
            jax.ShapeDtypeStruct((1, d), F32),
            jax.ShapeDtypeStruct((own, QPAD), BF16),
            jax.ShapeDtypeStruct((width, own, KPAD), BF16),
        ],
        scratch_shapes=[
            pltpu.VMEM((own, RQ * 128), F32),
            pltpu.VMEM((win, RK * 128), F32),
            pltpu.VMEM((win, RK * 128), F32),
            pltpu.VMEM((win, own), F32),
            pltpu.VMEM((PAIRS, own, 128), BF16),
            pltpu.VMEM((own, 128), F32),
            pltpu.VMEM((win, 128), F32),
            pltpu.VMEM((win, 128), F32),
            pltpu.VMEM((own, RQ * 128), F32),
            pltpu.VMEM((win, RK * 128), F32),
            pltpu.VMEM((win, RK * 128), F32),
        ],
        compiler_params=params(),
        cost_estimate=cost(30e9, 15e6),
        name="back",
    )(scalars, q, k, v, lse, dq, dk, qf, kvw, dn, hm, c, wo, gain)


def flip(index, bit):
    digit = (index // bit) % 2
    return index + bit - 2 * bit * digit


AXES = {"c": ("wide", 1), "x": ("wide", 2), "y": ("rows", 1), "n": ("rows", 2), "f": ("rows", 4)}


def enter(names):
    barrier = pltpu.get_barrier_semaphore()
    for name in names:
        pl.semaphore_signal(
            barrier, inc=1, device_id=partner(name), device_id_type=pl.DeviceIdType.MESH
        )
    pl.semaphore_wait(barrier, len(names))


def partner(name):
    axis, bit = AXES[name]
    return {axis: flip(lax.axis_index(axis), bit)}


def digit(name):
    axis, bit = AXES[name]
    return (lax.axis_index(axis) // bit) % 2


def wide_digits(index):
    return index // 2, index % 2


def slot_for(me, block):
    mx, mc = wide_digits(me)
    bx, bc = wide_digits(block)
    return 2 * ((mc + bc) % 2) + (mx + bx) % 2


def send_to(name, src, dst, send, recv):
    return pltpu.make_async_remote_copy(
        src_ref=src, dst_ref=dst, send_sem=send, recv_sem=recv,
        device_id=partner(name), device_id_type=pl.DeviceIdType.MESH,
    )


class Gather:
    def __init__(self, ref, send, recv):
        self.x = send_to("x", ref.at[0], ref.at[1], send.at[0], recv.at[0])
        self.c = send_to("c", ref.at[0], ref.at[2], send.at[1], recv.at[1])
        self.r = send_to("c", ref.at[1], ref.at[3], send.at[2], recv.at[2])

    def first(self):
        self.x.start()
        self.c.start()

    def relay(self):
        self.x.wait()
        self.r.start()

    def done(self):
        self.c.wait()
        self.r.wait()


class Scatter:
    def __init__(self, part, got, last, send, recv):
        self.part, self.got, self.last = part, got, last
        self.c = send_to("c", part.at[pl.ds(2, 2)], got, send.at[0], recv.at[0])
        if last is not None:
            self.x = send_to("x", part.at[1], last, send.at[1], recv.at[1])

    def core(self):
        self.c.start()

    def kept(self, i):
        return self.part[i].astype(F32) + self.got[i].astype(F32)

    def cross(self):
        self.c.wait()
        self.part[1] = self.kept(1).astype(BF16)
        self.x.start()
        self.part[0] = self.kept(0).astype(BF16)

    def total(self):
        self.x.wait()
        return self.part[0].astype(F32) + self.last[...].astype(F32)


class Sum:
    def __init__(self, names, unit, src, base, acc, got, res, rbase, send, recv, local=None):
        self.names, self.unit, self.n = names, unit, len(names)
        self.src, self.base, self.acc, self.got = src, base, acc, got
        self.res, self.rbase, self.send, self.recv = res, rbase, send, recv
        self.local = local

    def low(self, i, skip=0):
        total = 0
        for j in range(skip, i):
            total = total + digit(self.names[j]) * 2 ** (self.n - 1 - j)
        return total

    def span(self, ref, base, chunk, count):
        return ref.at[pl.ds(base + chunk * self.unit, count * self.unit)]

    def keep(self):
        half = 2 ** (self.n - 1)
        return pltpu.make_async_copy(
            self.span(self.src, self.base, self.low(1), half), self.acc, self.local
        )

    def halve(self, i):
        half = 2 ** (self.n - 1 - i)
        away = (1 - digit(self.names[i])) * half
        if i == 0:
            src = self.span(self.src, self.base, away, half)
        else:
            src = self.span(self.acc, 0, self.low(i, 1) + away, half)
        dst = self.span(self.got, 0, 2 ** self.n - 2 * half, half)
        return send_to(self.names[i], src, dst, self.send.at[i], self.recv.at[i])

    def begin(self):
        self.halve(0).start()
        if self.local is not None:
            self.keep().start()

    def double(self, i):
        half = 2 ** (self.n - 1 - i)
        held = self.span(self.res, self.rbase, self.low(i + 1), half)
        k = self.n + i
        return send_to(self.names[i], held, held, self.send.at[k], self.recv.at[k])

    def add(self, i):
        half = 2 ** (self.n - 1 - i)
        offset = (2 ** self.n - 2 * half) * self.unit
        self.halve(i).wait()
        kept = self.low(i + 1, 1) * self.unit
        first = i == 0 and self.local is None
        if i == 0 and self.local is not None:
            self.keep().wait()
        own = self.base + self.low(1) * self.unit
        last = i == self.n - 1
        place = self.rbase + self.low(self.n) * self.unit

        def one(j, carry):
            mine = self.src[own + j] if first else self.acc[kept + j]
            value = (mine.astype(F32) + self.got[offset + j].astype(F32)).astype(BF16)
            if last:
                self.res[place + j] = value
            else:
                self.acc[kept + j] = value
            return carry

        lax.fori_loop(0, half * self.unit, one, 0)

    def step(self, k):
        n = self.n
        if k < n:
            self.add(k)
            if k < n - 1:
                self.halve(k + 1).start()
            else:
                self.double(n - 1).start()
        else:
            i = 2 * n - 1 - k
            self.double(i).wait()
            if i > 0:
                self.double(i - 1).start()


def fill_cap(me, first, dq, dk, cap_ref, nblk, own):
    for i in range(nblk):
        rows = pl.ds(i * own, own)
        key = lax.broadcasted_iota(jnp.int32, (own, own), 0)
        query = lax.broadcasted_iota(jnp.int32, (own, own), 1) + (me - first - i) * own
        ok = (dk[i * own:(i + 1) * own, :] == dq) & (key <= query)
        cap_ref[rows, :] = jnp.where(ok, BIG, NEG)


def fore_kernel(
    nblk, x_ref, wt_ref, wo_ref, g1_ref, g2_ref, dq_ref, dk_ref, c_ref,
    n1_ref, qf_ref, kvw_ref, att_ref, q_ref, k_ref, v_ref, lse_ref, hm_ref, ng_ref, cg_ref,
    kvg_ref, bq_ref, bk_ref, bv_ref, cap_ref, full_ref, send, recv,
):
    seqs, own, d = x_ref.shape
    me = lax.axis_index("wide")
    first = me // 3
    kvs = [Gather(kvg_ref.at[s], send.at[s], recv.at[s]) for s in range(seqs)]
    cots = [Gather(cg_ref.at[s], send.at[2 + s], recv.at[2 + s]) for s in range(seqs)]
    norms = [Gather(ng_ref.at[s], send.at[4 + s], recv.at[4 + s]) for s in range(seqs)]
    for s in range(seqs):
        cg_ref[s, 0] = c_ref[s]
    for s in range(seqs):
        x = x_ref[s].astype(F32)
        r = lax.rsqrt(jnp.mean(x * x, axis=-1, keepdims=True) + EPS)
        n = (x * r * g1_ref[...]).astype(BF16)
        n1_ref[s] = n
        f = mm(n, wt_ref[...], NT).astype(BF16)
        qf_ref[s] = f[:, :QPAD]
        kvg_ref[s, 0, :, :KV] = f[:, QCOLS:]
        kvg_ref[s, 0, :, KV:] = jnp.zeros((own, KPAD - KV), BF16)
        if s == 0:
            enter("cx")
        kvs[s].first()
    cots[0].first()
    kvs[0].relay()
    kvs[0].done()

    def step(t, carry):
        s = t // PAIRS
        pair = t % PAIRS

        @pl.when(t == PAIRS)
        def _():
            kvs[1].done()

        @pl.when(pair == 0)
        def _():
            for i in range(nblk):
                kvw_ref[s, pl.ds(i * own, own), :] = kvg_ref[s, slot_for(me, first + i)]
            bq_ref[...] = mm(qf_ref[s], rank_tile(QA, (QPAD, RQ * 128)))
            bk_ref[...] = mm(kvw_ref[s, :, :256], rank_tile(KA, (256, RK * 128)))
            bv_ref[...] = mm(kvw_ref[s, :, 128:384], rank_tile(KCOLS + KA - 128, (256, RK * 128)))
            fill_cap(me, first, dq_ref[s], dk_ref[s], cap_ref, nblk, own)

        qe = mm(qf_ref[s, :, :128], head_spread(pair, 0, RQ, (128, RQ * 128)))
        qsum = qe[:, :128] * bq_ref[:, :128]
        for r in range(1, RQ):
            cols = slice(r * 128, (r + 1) * 128)
            qsum = qsum + qe[:, cols] * bq_ref[:, cols]
        q = (qsum * (1.0 / RQ)).astype(BF16)
        ke = mm(kvw_ref[s, :, :128], head_spread(pair, 0, RK, (128, RK * 128)))
        ve = mm(kvw_ref[s, :, 128:256], head_spread(pair, KCOLS - 128, RK, (128, RK * 128)))
        k = ((ke[:, :128] * bk_ref[:, :128] + ke[:, 128:] * bk_ref[:, 128:]) * (1.0 / RK)).astype(BF16)
        v = ((ve[:, :128] * bv_ref[:, :128] + ve[:, 128:] * bv_ref[:, 128:]) * (1.0 / RK)).astype(BF16)
        q = q * jnp.asarray(DH ** (-0.5), BF16)
        q_ref[s, pair] = q
        k_ref[s, pair] = k
        v_ref[s, pair] = v
        cap = cap_ref[...]
        st = jnp.minimum(mm(k, stacked(q), NT), jnp.concatenate([cap, cap], axis=1))
        top = jnp.max(st, axis=0, keepdims=True)
        e = jnp.exp(st - top)
        total = jnp.sum(e, axis=0, keepdims=True)
        p = (e * (1.0 / total)).astype(BF16)
        lse_ref[s, pair] = top + jnp.log(total)
        full_ref[pair] = unstacked(mm(v, p, TN), own).astype(BF16)

        @pl.when(pair == PAIRS - 1)
        def _():
            att = jnp.concatenate([full_ref[i] for i in range(PAIRS)], axis=1)
            att_ref[s] = att
            hm = x_ref[s].astype(F32) + mm(att, wo_ref[...])
            hm_ref[s] = hm
            r = lax.rsqrt(jnp.mean(hm * hm, axis=-1, keepdims=True) + EPS)
            ng_ref[s, 0] = (hm * r * g2_ref[...]).astype(BF16)

        @pl.when(t == 2)
        def _():
            kvs[1].relay()

        @pl.when(t == 6)
        def _():
            cots[0].relay()
            cots[1].first()

        @pl.when(t == PAIRS - 1)
        def _():
            norms[0].first()

        @pl.when(t == 11)
        def _():
            cots[1].relay()

        @pl.when(t == 14)
        def _():
            norms[0].relay()

        return carry

    lax.fori_loop(0, seqs * PAIRS, step, 0)
    norms[1].first()
    for s in range(seqs):
        cots[s].done()
    norms[0].done()
    norms[1].relay()
    norms[1].done()


def vmem():
    return pl.BlockSpec(memory_space=pltpu.VMEM)


def hbm():
    return pl.BlockSpec(memory_space=pl.ANY)


def fused(ident, limit=63):
    return pltpu.CompilerParams(
        vmem_limit_bytes=limit << 20, collective_id=ident, has_side_effects=True
    )


def fore(nblk, x, wt, wo, g1, g2, dq, dk, c):
    seqs, own, d = x.shape
    win = nblk * own
    shape = jax.ShapeDtypeStruct
    return pl.pallas_call(
        functools.partial(fore_kernel, nblk),
        in_specs=[vmem()] * 8,
        out_specs=[vmem()] * 11,
        out_shape=[
            shape((seqs, own, d), BF16), shape((seqs, own, QPAD), BF16),
            shape((seqs, win, KPAD), BF16), shape((seqs, own, d), BF16),
            shape((seqs, PAIRS, own, 128), BF16), shape((seqs, PAIRS, win, 128), BF16),
            shape((seqs, PAIRS, win, 128), BF16), shape((seqs, PAIRS, 1, 2 * own), F32),
            shape((seqs, own, d), F32), shape((seqs, 4, own, d), BF16),
            shape((seqs, 4, own, d), BF16),
        ],
        scratch_shapes=[
            pltpu.VMEM((seqs, 4, own, KPAD), BF16),
            pltpu.VMEM((own, RQ * 128), F32),
            pltpu.VMEM((win, RK * 128), F32),
            pltpu.VMEM((win, RK * 128), F32),
            pltpu.VMEM((win, own), F32),
            pltpu.VMEM((PAIRS, own, 128), BF16),
            pltpu.SemaphoreType.DMA((6, 3)),
            pltpu.SemaphoreType.DMA((6, 3)),
        ],
        compiler_params=fused(0),
        cost_estimate=cost(30e9, 30e6),
        name="fore",
    )(x, wt, wo, g1, g2, dq, dk, c)


def middle_kernel(
    n_ref, c_ref, wg_ref, wu_ref, wd_ref,
    dn_ref, ok_ref, os_ref, gw_ref,
    hid_ref, dg_ref, du_ref, dp_ref, op_ref, dc_ref, dx_ref, oc_ref, send, recv,
):
    seqs, size, own, d = n_ref.shape
    ff = wd_ref.shape[0]
    downs = [
        Scatter(dp_ref.at[s], dc_ref.at[s], dx_ref.at[s], send.at[s], recv.at[s])
        for s in range(seqs)
    ]
    ups = [
        Scatter(op_ref.at[s], oc_ref.at[s], None, send.at[seqs + s], recv.at[seqs + s])
        for s in range(seqs)
    ]
    enter("cx")

    def step(t, carry):
        s = t // size
        b = size - 1 - t % size
        n = n_ref[s, b]
        c = c_ref[s, b]
        g = mm(wg_ref[...], n, NT)
        u = mm(wu_ref[...], n, NT)
        dh = mm(wd_ref[...], c, NT)
        sg = 1.0 / (1.0 + jnp.exp(-g))
        gs = g * sg
        hid = (gs * u).astype(BF16)
        dg = (dh * u * (sg * (1.0 + g * (1.0 - sg)))).astype(BF16)
        du = (dh * gs).astype(BF16)
        cols = pl.ds(pl.multiple_of((s * size + b) * own, 128), own)
        hid_ref[:, cols] = hid
        dg_ref[:, cols] = dg
        du_ref[:, cols] = du
        op_ref[s, b] = mm(hid, wd_ref[...], TN).astype(BF16)
        dp_ref[s, b] = (mm(dg, wg_ref[...], TN) + mm(du, wu_ref[...], TN)).astype(BF16)
        for i in range(seqs):

            @pl.when(t == i * size + 1)
            def _(i=i):
                downs[i].core()
                ups[i].core()

            @pl.when(t == i * size + size - 1)
            def _(i=i):
                downs[i].cross()

        return carry

    lax.fori_loop(0, seqs * size, step, 0)
    units = ff // 16
    half = units // 2
    rows = half * 16
    gw_ref[pl.ds(3 * units, gw_ref.shape[0] - 3 * units)] = jnp.zeros(
        (gw_ref.shape[0] - 3 * units, 16, d), BF16
    )
    for m, (a_ref, b_ref) in enumerate(((dg_ref, n_ref), (du_ref, n_ref), (hid_ref, c_ref))):

        def part(i, carry, m=m, a_ref=a_ref, b_ref=b_ref):
            a = a_ref[pl.ds(pl.multiple_of(i * rows, 16), rows), :]
            w = mm(a, b_ref[...].reshape(seqs * size * own, d))
            gw_ref[pl.ds(m * units + i * half, half)] = w.astype(BF16).reshape(half, 16, d)
            return carry

        lax.fori_loop(0, 2, part, 0)
    for s in range(seqs):
        ups[s].c.wait()
        ok_ref[s] = ups[s].kept(0).astype(BF16)
        os_ref[s] = ups[s].kept(1).astype(BF16)
    for s in range(seqs):
        dn_ref[s] = downs[s].total()


def middle(n, c, wg, wu, wd, units):
    seqs, size, own, d = n.shape
    ff = wd.shape[0]
    shape = jax.ShapeDtypeStruct
    flat = (ff, seqs * size * own)
    return pl.pallas_call(
        middle_kernel,
        in_specs=[vmem()] * 5,
        out_specs=[vmem()] * 4,
        out_shape=[
            shape((seqs, own, d), F32), shape((seqs, own, d), BF16),
            shape((seqs, own, d), BF16), shape((units, 16, d), BF16),
        ],
        scratch_shapes=[pltpu.VMEM(flat, BF16)] * 3
        + [pltpu.VMEM((seqs, size, own, d), BF16)] * 2
        + [
            pltpu.VMEM((seqs, 2, own, d), BF16),
            pltpu.VMEM((seqs, own, d), BF16),
            pltpu.VMEM((seqs, 2, own, d), BF16),
            pltpu.SemaphoreType.DMA((2 * seqs, 2)),
            pltpu.SemaphoreType.DMA((2 * seqs, 2)),
        ],
        compiler_params=fused(1),
        cost_estimate=cost(27e9, 30e6),
        name="middle",
    )(n, c, wg, wu, wd)


PARTS = (("ynf", 4), ("ynf", 4), ("ynf", 4), ("nfy", 5))
UNITS = 8 * sum(u for _, u in PARTS)
OUT_PARTS = (("cxynf", 128), ("cxnfy", 128))
FAC_PARTS = (("cxynf", 80), ("cynfx", 64), ("cnfxy", 64))
FAC_ROWS = 4 * sum(r for _, r in FAC_PARTS)


def cut(value, parts, bufs, only):
    m = sum(r for _, r in parts)
    at = 0
    for g, (_, r) in enumerate(parts):
        if g in only:
            for i in range(32):
                row = m * (i // 8) + at
                bufs[g][i] = value[row:row + r, 128 * (i % 8):128 * (i % 8) + 128]
        at += r


def joined(results, parts):
    cols = [r.reshape(4, 8, rows, 128) for r, (_, rows) in zip(results, parts)]
    whole = jnp.concatenate(cols, axis=2)
    return whole.transpose(0, 2, 1, 3).reshape(-1, 1024).astype(F32)


def after_kernel(
    nblk, gw_ref, dn_ref, ok_ref, os_ref, q_ref, k_ref, v_ref, lse_ref, dq_ref, dk_ref,
    qf_ref, kvw_ref, hm_ref, c_ref, wo_ref, g1_ref, g2_ref, att_ref, n1_ref, x_ref, wt_ref,
    out_ref, ig_ref, gr_ref, *refs,
):
    n_out, n_fac = len(OUT_PARTS), len(FAC_PARTS)
    or_refs, refs = refs[:n_out], refs[n_out:]
    fr_refs, refs = refs[:n_fac], refs[n_fac:]
    (bq_ref, bk_ref, bv_ref, cap_ref, da_ref, aq_ref, ak_ref, av_ref, tq_ref, tk_ref, tv_ref,
     dm_ref, late_ref, gq_ref, gkp_ref, gkc_ref, gkx_ref, ox_ref, kb_ref, vb_ref) = refs[:20]
    refs = refs[20:]
    gots, refs = refs[:len(PARTS)], refs[len(PARTS):]
    accs, refs = refs[:len(PARTS)], refs[len(PARTS):]
    ob, refs = refs[:n_out], refs[n_out:]
    og, refs = refs[:n_out], refs[n_out:]
    oa, refs = refs[:n_out], refs[n_out:]
    fb, refs = refs[:n_fac], refs[n_fac:]
    fg, refs = refs[:n_fac], refs[n_fac:]
    fa, refs = refs[:n_fac], refs[n_fac:]
    send, recv, loc, gs, gr, kvsem, wsem = refs
    seqs, own, d = hm_ref.shape
    me = lax.axis_index("wide")
    first = me // 3

    sums, base = [], 0
    for p, (names, u) in enumerate(PARTS):
        sums.append(Sum(
            names, u, gw_ref, base, accs[p], gots[p], gr_ref, base, send.at[p], recv.at[p],
            loc.at[p],
        ))
        base += 8 * u
    k0 = len(PARTS)
    outs = [
        Sum(names, 1, ob[g], 0, oa[g], og[g], or_refs[g], 0, send.at[k0 + g], recv.at[k0 + g])
        for g, (names, _) in enumerate(OUT_PARTS)
    ]
    k1 = k0 + n_out
    facs = [
        Sum(names, 1, fb[g], 0, fa[g], fg[g], fr_refs[g], 0, send.at[k1 + g], recv.at[k1 + g])
        for g, (names, _) in enumerate(FAC_PARTS)
    ]
    keys = [
        Scatter(gkp_ref.at[s], gkc_ref.at[s], gkx_ref.at[s], gs.at[s], gr.at[s])
        for s in range(seqs)
    ]
    crosses = [
        send_to("x", os_ref.at[s], ox_ref.at[s], gs.at[2 + s, 0], gr.at[2 + s, 0])
        for s in range(seqs)
    ]

    def fetch(t):
        return [
            pltpu.make_async_copy(a.at[t // PAIRS, t % PAIRS], b.at[t % 2], kvsem.at[i, t % 2])
            for i, (a, b) in enumerate(((k_ref, kb_ref), (v_ref, vb_ref)))
        ]

    for copy in fetch(0):
        copy.start()
    loads = [
        pltpu.make_async_copy(dn_ref, dm_ref, wsem.at[0]),
        pltpu.make_async_copy(c_ref, late_ref, wsem.at[1]),
    ]
    for copy in loads:
        copy.start()
    enter("cxynf")
    for part in sums:
        part.begin()
    for cross in crosses:
        cross.start()

    for copy in loads:
        copy.wait()
    gain_two = jnp.zeros((1, d), F32)
    for s in range(seqs):
        hm = hm_ref[s]
        dn = dm_ref[s]
        r = lax.rsqrt(jnp.mean(hm * hm, axis=-1, keepdims=True) + EPS)
        z = dn * g2_ref[...]
        gain_two = gain_two + jnp.sum(dn * hm * r, axis=0, keepdims=True)
        dm = (
            late_ref[s].astype(F32)
            + r * z
            - hm * (r * r * r) * jnp.mean(z * hm, axis=-1, keepdims=True)
        )
        dm_ref[s] = dm
        low = dm.astype(BF16)
        late_ref[s] = low
        da = mm(low, wo_ref[...], NT).astype(BF16)
        for i in range(PAIRS):
            da_ref[s, i] = da[:, i * 128:(i + 1) * 128]
    go = mm(att_ref[...].reshape(seqs * own, d), late_ref[...].reshape(seqs * own, d), TN)
    cut(go.astype(BF16), OUT_PARTS, ob, range(n_out))
    for part in outs:
        part.begin()
    load_x = pltpu.make_async_copy(x_ref, late_ref, wsem.at[2])
    load_x.start()

    def finish(s):
        def fold(x, t):
            hi = x.astype(BF16)
            lo = (x - hi.astype(F32)).astype(BF16)
            return mm(hi, t, NT) + mm(lo, t, NT)

        gq = fold(tq_ref[...], rank_tile(QA, (QPAD, RQ * 128)))
        gq_ref[s, :, :128] = ((gq[:, :128] + aq_ref[...]) * (1.0 / RQ)).astype(BF16)
        gq_ref[s, :, 128:] = (gq[:, 128:] * (1.0 / RQ)).astype(BF16)
        gk = fold(tk_ref[...], rank_tile(KA, (KPAD, RK * 128)))
        gv = fold(tv_ref[...], rank_tile(KCOLS + KA, (KPAD, RK * 128)))
        gkv = gk + gv
        one = ((gkv[:, :128] + ak_ref[...]) * (1.0 / RK)).astype(BF16)
        two = ((gkv[:, 128:256] + av_ref[...]) * (1.0 / RK)).astype(BF16)
        three = (gkv[:, 256:] * (1.0 / RK)).astype(BF16)
        gkp_ref[s] = jnp.zeros_like(gkp_ref[s])
        for i in range(nblk):
            rows = slice(i * own, (i + 1) * own)
            slot = slot_for(me, first + i)
            gkp_ref[s, slot, :, :128] = one[rows]
            gkp_ref[s, slot, :, 128:256] = two[rows]
            gkp_ref[s, slot, :, 256:] = three[rows]

    def emit(s):
        crosses[s].wait()
        total = hm_ref[s] + (ok_ref[s].astype(F32) + ox_ref[s].astype(F32))
        out_ref[s] = total.astype(BF16)

    events = {t: [] for t in range(2 * PAIRS)}
    rest = []

    def at(t, call):
        (events[t] if t < 2 * PAIRS else rest).append(call)

    for part, times in zip(sums, (
        (1, 3, 5, 7, 9, 12), (4, 6, 8, 10, 12, 16), (8, 10, 12, 13, 16, 18), (1, 5, 6, 8, 11, 15),
    )):
        for k, t in enumerate(times):
            at(t, functools.partial(part.step, k))
    for g, part in enumerate(outs):
        for k in range(10):
            at(2 + g + k + (k // 5), functools.partial(part.step, k))
    at(6, functools.partial(emit, 0))
    at(8, functools.partial(emit, 1))
    at(PAIRS + 1, keys[0].cross)

    def step(t, carry):
        s = t // PAIRS
        pair = t % PAIRS
        slot = t % 2

        @pl.when(t < seqs * PAIRS - 1)
        def _():
            for copy in fetch(t + 1):
                copy.start()

        @pl.when(pair == 0)
        def _():
            bq_ref[...] = mm(qf_ref[s], rank_tile(QA, (QPAD, RQ * 128)))
            bk_ref[...] = mm(kvw_ref[s, :, :256], rank_tile(KA, (256, RK * 128)))
            bv_ref[...] = mm(kvw_ref[s, :, 128:384], rank_tile(KCOLS + KA - 128, (256, RK * 128)))
            fill_cap(me, first, dq_ref[s], dk_ref[s], cap_ref, nblk, own)
            for ref in (aq_ref, ak_ref, av_ref, tq_ref, tk_ref, tv_ref):
                ref[...] = jnp.zeros_like(ref)

        for copy in fetch(t):
            copy.wait()
        q = q_ref[s, pair]
        k = kb_ref[slot]
        v = vb_ref[slot]
        qs = stacked(q)
        da = stacked(da_ref[s, pair])
        cap = cap_ref[...]
        st = jnp.minimum(mm(k, qs, NT), jnp.concatenate([cap, cap], axis=1))
        p = jnp.exp(st - lse_ref[s, pair])
        dp = mm(v, da, NT)
        delta = jnp.sum(p * dp, axis=0, keepdims=True)
        ds = (p * (dp - delta)).astype(BF16)
        dv = mm(p.astype(BF16), da)
        dk = mm(ds, qs)
        dq = unstacked(mm(k, ds, TN), own) * (DH ** (-0.5))

        eq = head_spread(pair, 0, RQ, (128, RQ * 128))
        qe = mm(qf_ref[s, :, :128], eq)
        dq6 = jnp.concatenate([dq] * RQ, axis=1)
        tq_ref[...] += dq6 * qe
        aq_ref[...] += mm((dq6 * bq_ref[...]).astype(BF16), eq, NT)
        ek = head_spread(pair, 0, RK, (128, RK * 128))
        ev = head_spread(pair, KCOLS - 128, RK, (128, RK * 128))
        ke = mm(kvw_ref[s, :, :128], ek)
        ve = mm(kvw_ref[s, :, 128:256], ev)
        dk2 = jnp.concatenate([dk] * RK, axis=1)
        dv2 = jnp.concatenate([dv] * RK, axis=1)
        tk_ref[...] += dk2 * ke
        tv_ref[...] += dv2 * ve
        ak_ref[...] += mm((dk2 * bk_ref[...]).astype(BF16), ek, NT)
        av_ref[...] += mm((dv2 * bv_ref[...]).astype(BF16), ev, NT)

        @pl.when(pair == PAIRS - 1)
        def _():
            finish(s)

        @pl.when(t == PAIRS - 1)
        def _():
            keys[0].core()

        for when, calls in events.items():
            if calls:

                @pl.when(t == when)
                def _(calls=calls):
                    for call in calls:
                        call()

        return carry

    lax.fori_loop(0, seqs * PAIRS, step, 0)
    keys[1].core()
    n1 = n1_ref[...].reshape(seqs * own, d)
    gq = gq_ref[...].reshape(seqs * own, QPAD)
    gfq = mm(gq, n1, TN)[:QCOLS]
    dn1 = mm(gq[:, :QCOLS], wt_ref[:QCOLS, :])
    keys[1].cross()
    gkv0 = keys[0].total().astype(BF16)
    gkv = jnp.concatenate([gkv0, keys[1].total().astype(BF16)], axis=0)
    gfk = mm(gkv, n1, TN)[:KV]
    tail = jnp.zeros((FAC_ROWS - QCOLS - KV, d), F32)
    gf = jnp.concatenate([gfq, gfk, tail], axis=0).astype(BF16)
    cut(gf, FAC_PARTS, fb, range(n_fac - 1))
    for part in facs[:-1]:
        part.begin()
    dn1 = dn1 + mm(gkv[:, :KV], wt_ref[QCOLS:, :])
    load_x.wait()
    hin = late_ref[...].reshape(seqs * own, d).astype(F32)
    r1 = lax.rsqrt(jnp.mean(hin * hin, axis=-1, keepdims=True) + EPS)
    z1 = dn1 * g1_ref[...]
    gain_one = jnp.sum(dn1 * hin * r1, axis=0, keepdims=True)
    gains = jnp.concatenate(
        [gain_one, gain_two, jnp.zeros((FAC_ROWS - QCOLS - KV - 2, d), F32)], axis=0
    )
    gf = jnp.concatenate([gfq, gfk, gains], axis=0).astype(BF16)
    cut(gf, FAC_PARTS, fb, (n_fac - 1,))
    facs[-1].begin()
    grad = r1 * z1 - hin * (r1 * r1 * r1) * jnp.mean(z1 * hin, axis=-1, keepdims=True)
    ig_ref[...] = (dm_ref[...].reshape(seqs * own, d) + grad).astype(BF16).reshape(seqs, own, d)
    tails = [functools.partial(part.step, k) for k in range(10) for part in facs]
    while tails or rest:
        for call in tails[:n_fac]:
            call()
        tails = tails[n_fac:]
        for call in rest[:2]:
            call()
        rest = rest[2:]


def after(nblk, gw, dn, ok, os, q, k, v, lse, dq, dk, qf, kvw, hm, c, wo, g1, g2, att, n1, x, wt):
    seqs, own, d = hm.shape
    win = nblk * own
    shape = jax.ShapeDtypeStruct
    far = (0, 1, 3, 5, 6, 13, 19)
    results = [shape((32, r, 128), BF16) for _, r in OUT_PARTS + FAC_PARTS]
    total = len(PARTS) + len(OUT_PARTS) + len(FAC_PARTS)
    args = (gw, dn, ok, os, q, k, v, lse, dq, dk, qf, kvw, hm, c, wo, g1, g2, att, n1, x, wt)
    res = pl.pallas_call(
        functools.partial(after_kernel, nblk),
        in_specs=[hbm() if i in far else vmem() for i in range(len(args))],
        out_specs=[vmem()] * (3 + len(results)),
        out_shape=[
            shape((seqs, own, d), BF16), shape((seqs, own, d), BF16), shape(gw.shape, BF16),
        ] + results,
        scratch_shapes=[
            pltpu.VMEM((own, RQ * 128), F32),
            pltpu.VMEM((win, RK * 128), F32),
            pltpu.VMEM((win, RK * 128), F32),
            pltpu.VMEM((win, own), F32),
            pltpu.VMEM((seqs, PAIRS, own, 128), BF16),
            pltpu.VMEM((own, 128), F32),
            pltpu.VMEM((win, 128), F32),
            pltpu.VMEM((win, 128), F32),
            pltpu.VMEM((own, RQ * 128), F32),
            pltpu.VMEM((win, RK * 128), F32),
            pltpu.VMEM((win, RK * 128), F32),
            pltpu.VMEM((seqs, own, d), F32),
            pltpu.VMEM((seqs, own, d), BF16),
            pltpu.VMEM((seqs, own, QPAD), BF16),
            pltpu.VMEM((seqs, 4, own, KPAD), BF16),
            pltpu.VMEM((seqs, 2, own, KPAD), BF16),
            pltpu.VMEM((seqs, own, KPAD), BF16),
            pltpu.VMEM((seqs, own, d), BF16),
            pltpu.VMEM((2, win, 128), BF16),
            pltpu.VMEM((2, win, 128), BF16),
        ]
        + [pltpu.VMEM((7 * u, 16, d), BF16) for _, u in PARTS]
        + [pltpu.VMEM((4 * u, 16, d), BF16) for _, u in PARTS]
        + [pltpu.VMEM((n, r, 128), BF16) for n in (32, 31, 16) for _, r in OUT_PARTS]
        + [pltpu.VMEM((n, r, 128), BF16) for n in (32, 31, 16) for _, r in FAC_PARTS]
        + [
            pltpu.SemaphoreType.DMA((total, 10)),
            pltpu.SemaphoreType.DMA((total, 10)),
            pltpu.SemaphoreType.DMA((len(PARTS),)),
            pltpu.SemaphoreType.DMA((4, 2)),
            pltpu.SemaphoreType.DMA((4, 2)),
            pltpu.SemaphoreType.DMA((2, 2)),
            pltpu.SemaphoreType.DMA((3,)),
        ],
        compiler_params=fused(2),
        cost_estimate=cost(60e9, 60e6),
        name="after",
    )(*args)
    n = 3 + len(OUT_PARTS)
    return res[0], res[1], res[2], res[3:n], res[n:]


def fused_body(
    tokens, doc_ids, factor_weight, output_weight, norm_one, norm_two,
    gate_weight, up_weight, down_weight, cotangent,
):
    seqs, own, d = tokens.shape
    me = lax.axis_index("wide")
    nblk = -(-(MAX_DOC - 1) // own) + 1
    first = me // 3
    g1 = norm_one[None]
    g2 = norm_two[None]
    dq = lax.dynamic_slice_in_dim(doc_ids, me * own, own, 1)[:, None, :]
    dk = lax.dynamic_slice_in_dim(doc_ids, first * own, nblk * own, 1)[:, :, None]
    wt = factor_weight.T
    n1, qf, kvw, att, q, k, v, lse, hm, ng, cg = fore(
        nblk, tokens, wt, output_weight, g1, g2, dq, dk, cotangent
    )
    dn, ok, os, gw = middle(ng, cg, gate_weight.T, up_weight.T, down_weight, UNITS)
    output, input_grad, gr, go, gf = after(
        nblk, gw, dn, ok, os, q, k, v, lse, dq, dk, qf, kvw, hm, cotangent, output_weight,
        g1, g2, att, n1, tokens, wt,
    )
    ff = down_weight.shape[0]
    gr = gr.reshape(-1, d)
    grad_out = joined(go, OUT_PARTS)
    fac = joined(gf, FAC_PARTS)
    cols = factor_weight.shape[1]
    return (
        output, input_grad, fac[:cols].T, grad_out, fac[cols], fac[cols + 1],
        gr[:ff].astype(F32).T, gr[ff:2 * ff].astype(F32).T, gr[2 * ff:3 * ff].astype(F32),
    )


def swap(x, axis, size, bit):
    return lax.ppermute(x, axis, [(i, i ^ bit) for i in range(size)])


def steps_of(size):
    bits, b = [], size // 2
    while b:
        bits.append(b)
        b //= 2
    return bits


def gather(x, size):
    buf = x[None]
    for bit in steps_of(size):
        buf = jnp.concatenate([buf, swap(buf, "wide", size, bit)], axis=0)
    return buf


def order_of(size):
    order = [0]
    for bit in steps_of(size):
        order = order + [o ^ bit for o in order]
    return order


def scatter(parts, size):
    for bit in reversed(steps_of(size)):
        half = parts.shape[0] // 2
        got = swap(parts[half:], "wide", size, bit)
        total = parts[:half].astype(F32) + got.astype(F32)
        parts = total if half == 1 else total.astype(BF16)
    return parts[0]


def body(
    tokens, doc_ids, factor_weight, output_weight, norm_one, norm_two,
    gate_weight, up_weight, down_weight, cotangent,
):
    seqs, own, d = tokens.shape
    full_len = doc_ids.shape[1]
    size = full_len // own
    me = lax.axis_index("wide")
    left = min(-(-(MAX_DOC - 1) // own), size - 1)
    nblk = left + 1
    start = jnp.maximum(me - left, 0)
    order = order_of(size)
    slot_of = [order.index(j) for j in range(size)]
    slots = jnp.asarray(slot_of, jnp.int32)
    blocks = start + jnp.arange(nblk, dtype=jnp.int32)
    scalars = jnp.concatenate(
        [me[None].astype(jnp.int32), (me - blocks) * own, slots[me ^ blocks]]
    ).astype(jnp.int32)
    g1 = norm_one[None]
    g2 = norm_two[None]

    n1, qf, kvf = front(tokens.reshape(seqs * own, d), factor_weight, g1)
    qf = qf.reshape(seqs, own, QPAD)
    kvg = gather(kvf.reshape(seqs, own, KPAD), size)
    doc_query = lax.dynamic_slice_in_dim(doc_ids, me * own, own, 1)
    doc_key = lax.dynamic_slice_in_dim(doc_ids, start * own, nblk * own, 1)
    cots = [gather(cotangent[s], size) for s in range(seqs)]

    fwd = []
    for s in range(seqs):
        dq = doc_query[s][None, :]
        dk = doc_key[s][:, None]
        fwd.append(
            (dq, dk)
            + tuple(attend(nblk, scalars, qf[s], kvg[:, s], dq, dk, tokens[s], output_weight, g2))
        )
    prev = None
    outs, dns = [], []
    for s in range(seqs):
        n2 = gather(fwd[s][8], size)
        res = ffn(n2, cots[s], gate_weight, up_weight, down_weight, prev, s == seqs - 1)
        outs.append(res[0])
        dns.append(res[1])
        prev = res[2:]
    grads = [lax.psum(g, "rows").astype(F32) for g in prev]

    output, mids, lows, gain_two, gqs, gkvs = [], [], [], 0.0, [], []
    for s in range(seqs):
        dq, dk, att, q, k, v, lse, hm, n2, kvw = fwd[s]
        dn = scatter(dns[s], size)
        dm, low, gain, gq, gkv = back(
            nblk, size, scalars, q, k, v, lse, dq, dk, qf[s], kvw, dn, hm,
            cotangent[s], output_weight, g2,
        )
        output.append((hm + scatter(outs[s], size)).astype(BF16))
        mids.append(dm)
        lows.append(low)
        gqs.append(gq)
        gkvs.append(gkv)
        gain_two = gain_two + gain
    att_all = jnp.stack([f[2] for f in fwd]).reshape(seqs * own, d)
    grad_out = mm(att_all, jnp.stack(lows).reshape(seqs * own, d), TN)
    gkv = scatter(jnp.stack(gkvs, axis=1), size).astype(BF16)
    dfac = jnp.concatenate([jnp.stack(gqs)[..., :QCOLS], gkv[..., :KV]], axis=-1)
    dfac = dfac.reshape(seqs * own, -1)
    grad_factors = mm(n1, dfac, TN)
    dn1 = mm(dfac, factor_weight, NT)
    hin = tokens.reshape(seqs * own, d).astype(F32)
    r1 = lax.rsqrt(jnp.mean(hin * hin, axis=-1, keepdims=True) + EPS)
    z1 = dn1 * g1
    gain_one = jnp.sum(dn1 * hin * r1, axis=0)
    grad_norm = r1 * z1 - hin * (r1 * r1 * r1) * jnp.mean(z1 * hin, axis=-1, keepdims=True)
    input_grad = (jnp.stack(mids).reshape(seqs * own, d) + grad_norm).astype(BF16)
    parts = [grad_out, grad_factors.T, gain_one[None], gain_two]
    packed = jnp.concatenate([p.astype(BF16) for p in parts], axis=0)
    packed = lax.psum(packed, ("rows", "wide")).astype(F32)
    fac = grad_factors.shape[1]
    return (
        jnp.stack(output),
        input_grad.reshape(seqs, own, d),
        packed[d:d + fac].T,
        packed[:d],
        packed[d + fac],
        packed[d + fac + 1],
        grads[0],
        grads[1],
        grads[2],
    )


def solution(mesh):
    placed = (
        P("rows", "wide", None), P("rows", None), P(), P(), P(), P(),
        P(None, "wide"), P(None, "wide"), P("wide", None), P("rows", "wide", None),
    )
    small = mesh.shape["rows"] == 8 and mesh.shape["wide"] == 4
    return jax.shard_map(
        fused_body if small else body,
        mesh=mesh,
        in_specs=placed,
        out_specs=(
            P("rows", "wide", None), P("rows", "wide", None), P(), P(), P(), P(),
            P(None, "wide"), P(None, "wide"), P("wide", None),
        ),
        check_vma=False,
    )
```

```python
import functools

import jax
import jax.numpy as jnp
from jax import lax
from jax.experimental import pallas as pl
from jax.experimental.pallas import tpu as pltpu
from jax.sharding import PartitionSpec as P

H = 16
DH = 64
RQ = 6
RK = 2
MAX_DOC = 512
EPS = 1e-06
NEG = -1000000000.0
BIG = 3.0e38

QA = H * RQ
QCOLS = QA + RQ * DH
KA = H * RK
KCOLS = KA + RK * DH
KV = 2 * KCOLS
QPAD = 512
KPAD = 384
PAIRS = H // 2

F32 = jnp.float32
BF16 = jnp.bfloat16

NN = (((1,), (0,)), ((), ()))
NT = (((1,), (1,)), ((), ()))
TN = (((0,), (0,)), ((), ()))


def mm(a, b, dims=NN):
    return lax.dot_general(a, b, dims, preferred_element_type=F32)


def params(vmem_mb=60):
    return pltpu.CompilerParams(vmem_limit_bytes=vmem_mb << 20)


def cost(flops, nbytes):
    return pl.CostEstimate(flops=int(flops), bytes_accessed=int(nbytes), transcendentals=0)


def selection(shape, rule):
    row = lax.broadcasted_iota(jnp.int32, shape, 0)
    col = lax.broadcasted_iota(jnp.int32, shape, 1)
    return jnp.where(rule(row, col), 1.0, 0.0).astype(BF16)


def head_spread(pair, base, rank, shape):
    def rule(row, col):
        r = col // 128
        lane = col - r * 128
        head = 2 * pair + jnp.where(lane >= DH, 1, 0)
        return row == base + head * rank + r

    return selection(shape, rule)


def rank_tile(base, shape):
    def rule(row, col):
        r = col // 128
        lane = col - r * 128
        return row == base + r * DH + jnp.where(lane >= DH, lane - DH, lane)

    return selection(shape, rule)


def front_kernel(x_ref, w_ref, g_ref, n_ref, q_ref, kv_ref):
    x = x_ref[...].astype(F32)
    r = lax.rsqrt(jnp.mean(x * x, axis=-1, keepdims=True) + EPS)
    n = (x * r * g_ref[...]).astype(BF16)
    n_ref[...] = n
    f = mm(n, w_ref[...]).astype(BF16)
    q_ref[...] = f[:, :QPAD]
    kv_ref[:, :KV] = f[:, QCOLS:]
    kv_ref[:, KV:] = jnp.zeros((f.shape[0], KPAD - KV), BF16)


def front(x, w, gain):
    rows, d = x.shape
    blk = 256 if rows % 256 == 0 else rows
    return pl.pallas_call(
        front_kernel,
        grid=(rows // blk,),
        in_specs=[
            pl.BlockSpec((blk, d), lambda i: (i, 0)),
            pl.BlockSpec(w.shape, lambda i: (0, 0)),
            pl.BlockSpec((1, d), lambda i: (0, 0)),
        ],
        out_specs=[
            pl.BlockSpec((blk, d), lambda i: (i, 0)),
            pl.BlockSpec((blk, QPAD), lambda i: (i, 0)),
            pl.BlockSpec((blk, KPAD), lambda i: (i, 0)),
        ],
        out_shape=[
            jax.ShapeDtypeStruct((rows, d), BF16),
            jax.ShapeDtypeStruct((rows, QPAD), BF16),
            jax.ShapeDtypeStruct((rows, KPAD), BF16),
        ],
        compiler_params=params(),
        cost_estimate=cost(2 * rows * d * 800, rows * d * 6 + d * 1600),
        name="front",
    )(x, w, gain)


def make_cap(s_ref, dq_ref, dk_ref, cap_ref, nblk, own):
    dq = dq_ref[...]
    for i in range(nblk):
        rows = pl.ds(i * own, own)
        key = lax.broadcasted_iota(jnp.int32, (own, own), 0)
        query = lax.broadcasted_iota(jnp.int32, (own, own), 1) + s_ref[1 + i]
        ok = (dk_ref[rows, :] == dq) & (key <= query)
        cap_ref[rows, :] = jnp.where(ok, BIG, NEG)


def stacked(x):
    lane = lax.broadcasted_iota(jnp.int32, x.shape, 1)
    zero = jnp.zeros_like(x)
    return jnp.concatenate(
        [jnp.where(lane < DH, x, zero), jnp.where(lane >= DH, x, zero)], axis=0
    )


def unstacked(xt, own):
    pair = jnp.concatenate([xt[:DH, :own], xt[DH:, own:]], axis=0)
    return pair.T


def key_parts(kvf_ref, pair):
    ek = head_spread(pair, 0, RK, (128, RK * 128))
    ev = head_spread(pair, KCOLS - 128, RK, (128, RK * 128))
    ke = mm(kvf_ref[:, :128], ek)
    ve = mm(kvf_ref[:, 128:256], ev)
    return ke, ve


def tile_keys(kvf_ref, bk_ref, bv_ref):
    bk_ref[...] = mm(kvf_ref[:, :256], rank_tile(KA, (256, RK * 128)))
    bv_ref[...] = mm(kvf_ref[:, 128:384], rank_tile(KCOLS + KA - 128, (256, RK * 128)))


def attend_kernel(
    nblk, s_ref, qf_ref, kvg_ref, dq_ref, dk_ref, x_ref, wo_ref, g_ref,
    att_ref, q_ref, k_ref, v_ref, lse_ref, hm_ref, n_ref, kvw_ref,
    bq_ref, bk_ref, bv_ref, cap_ref, full_ref,
):
    pair = pl.program_id(0)
    own = qf_ref.shape[0]

    @pl.when(pair == 0)
    def _():
        for i in range(nblk):
            kvw_ref[pl.ds(i * own, own), :] = kvg_ref[s_ref[1 + nblk + i]]
        bq_ref[...] = mm(qf_ref[...], rank_tile(QA, (QPAD, RQ * 128)))
        tile_keys(kvw_ref, bk_ref, bv_ref)
        make_cap(s_ref, dq_ref, dk_ref, cap_ref, nblk, own)

    qe = mm(qf_ref[:, :128], head_spread(pair, 0, RQ, (128, RQ * 128)))
    qsum = qe[:, :128] * bq_ref[:, :128]
    for r in range(1, RQ):
        cols = slice(r * 128, (r + 1) * 128)
        qsum = qsum + qe[:, cols] * bq_ref[:, cols]
    q = (qsum * (1.0 / RQ)).astype(BF16)
    ke, ve = key_parts(kvw_ref, pair)
    k = ((ke[:, :128] * bk_ref[:, :128] + ke[:, 128:] * bk_ref[:, 128:]) * (1.0 / RK)).astype(BF16)
    v = ((ve[:, :128] * bv_ref[:, :128] + ve[:, 128:] * bv_ref[:, 128:]) * (1.0 / RK)).astype(BF16)
    q = q * jnp.asarray(DH ** (-0.5), BF16)
    q_ref[...] = q
    k_ref[...] = k
    v_ref[...] = v
    cap = cap_ref[...]
    st = jnp.minimum(mm(k, stacked(q), NT), jnp.concatenate([cap, cap], axis=1))
    top = jnp.max(st, axis=0, keepdims=True)
    e = jnp.exp(st - top)
    total = jnp.sum(e, axis=0, keepdims=True)
    p = (e * (1.0 / total)).astype(BF16)
    lse_ref[0] = top + jnp.log(total)
    att = unstacked(mm(v, p, TN), own).astype(BF16)
    att_ref[...] = att
    full_ref[pair] = att

    @pl.when(pair == pl.num_programs(0) - 1)
    def _():
        hm = x_ref[...].astype(F32)
        att_all = jnp.concatenate([full_ref[i] for i in range(PAIRS)], axis=1)
        hm = hm + mm(att_all, wo_ref[...])
        hm_ref[...] = hm
        r = lax.rsqrt(jnp.mean(hm * hm, axis=-1, keepdims=True) + EPS)
        n_ref[...] = (hm * r * g_ref[...]).astype(BF16)


def attend(nblk, scalars, qf, kvg, dq, dk, x, wo, gain):
    own, d = x.shape
    win = nblk * own
    whole = lambda a: pl.BlockSpec(a.shape, lambda p, a=a: (0,) * a.ndim)
    col = lambda rows: pl.BlockSpec((rows, 128), lambda p: (0, p))
    return pl.pallas_call(
        functools.partial(attend_kernel, nblk),
        grid=(PAIRS,),
        in_specs=[pl.BlockSpec(memory_space=pltpu.SMEM)]
        + [whole(a) for a in (qf, kvg, dq, dk, x, wo, gain)],
        out_specs=[
            col(own), col(own), col(win), col(win),
            pl.BlockSpec((1, 1, 2 * own), lambda p: (p, 0, 0)),
            pl.BlockSpec((own, d), lambda p: (0, 0)),
            pl.BlockSpec((own, d), lambda p: (0, 0)),
            pl.BlockSpec((win, KPAD), lambda p: (0, 0)),
        ],
        out_shape=[
            jax.ShapeDtypeStruct((own, d), BF16),
            jax.ShapeDtypeStruct((own, d), BF16),
            jax.ShapeDtypeStruct((win, d), BF16),
            jax.ShapeDtypeStruct((win, d), BF16),
            jax.ShapeDtypeStruct((PAIRS, 1, 2 * own), F32),
            jax.ShapeDtypeStruct((own, d), F32),
            jax.ShapeDtypeStruct((own, d), BF16),
            jax.ShapeDtypeStruct((win, KPAD), BF16),
        ],
        scratch_shapes=[
            pltpu.VMEM((own, RQ * 128), F32),
            pltpu.VMEM((win, RK * 128), F32),
            pltpu.VMEM((win, RK * 128), F32),
            pltpu.VMEM((win, own), F32),
            pltpu.VMEM((PAIRS, own, 128), BF16),
        ],
        compiler_params=params(),
        cost_estimate=cost(12e9, 12e6),
        name="attend",
    )(scalars, qf, kvg, dq, dk, x, wo, gain)


def ffn_kernel(has_prev, bf16_out, *refs):
    if has_prev:
        n_ref, c_ref, wg_ref, wu_ref, wd_ref, pg_ref, pu_ref, pd_ref = refs[:8]
        refs = refs[8:]
    else:
        n_ref, c_ref, wg_ref, wu_ref, wd_ref = refs[:5]
        refs = refs[5:]
    o_ref, dn_ref, og_ref, ou_ref, od_ref = refs[:5]
    if bf16_out:
        ag_ref, au_ref, ad_ref = refs[5:]
    else:
        ag_ref, au_ref, ad_ref = og_ref, ou_ref, od_ref
    step = pl.program_id(0)

    @pl.when(step == 0)
    def _():
        if has_prev:
            ag_ref[...] = pg_ref[...]
            au_ref[...] = pu_ref[...]
            ad_ref[...] = pd_ref[...]
        else:
            ag_ref[...] = jnp.zeros_like(ag_ref)
            au_ref[...] = jnp.zeros_like(au_ref)
            ad_ref[...] = jnp.zeros_like(ad_ref)

    n = n_ref[0]
    c = c_ref[0]
    wg, wu, wd = wg_ref[...], wu_ref[...], wd_ref[...]
    g = mm(n, wg)
    u = mm(n, wu)
    dh = mm(c, wd, NT)
    s = 1.0 / (1.0 + jnp.exp(-g))
    gs = g * s
    hid = (gs * u).astype(BF16)
    dg = (dh * u * (s * (1.0 + g * (1.0 - s)))).astype(BF16)
    du = (dh * gs).astype(BF16)
    o_ref[0] = mm(hid, wd).astype(BF16)
    dn_ref[0] = (mm(dg, wg, NT) + mm(du, wu, NT)).astype(BF16)
    ag_ref[...] += mm(n, dg, TN)
    au_ref[...] += mm(n, du, TN)
    ad_ref[...] += mm(hid, c, TN)
    if bf16_out:

        @pl.when(step == pl.num_programs(0) - 1)
        def _():
            og_ref[...] = ag_ref[...].astype(BF16)
            ou_ref[...] = au_ref[...].astype(BF16)
            od_ref[...] = ad_ref[...].astype(BF16)


def ffn(n, c, wg, wu, wd, prev, last):
    w, own, d = n.shape
    ff = wg.shape[1]
    one = lambda a: pl.BlockSpec(
        a.shape, lambda i, a=a: (0,) * a.ndim, pipeline_mode=pl.Buffered(1)
    )
    blk = pl.BlockSpec((1, own, d), lambda i: (i, 0, 0))
    dt = BF16 if last else F32
    args = [n, c, wg, wu, wd] + list(prev or [])
    shapes = [(d, ff), (d, ff), (ff, d)]
    return pl.pallas_call(
        functools.partial(ffn_kernel, bool(prev), last),
        grid=(w,),
        in_specs=[blk, blk] + [one(a) for a in args[2:]],
        out_specs=[blk, blk] + [
            pl.BlockSpec(s, lambda i: (0, 0), pipeline_mode=pl.Buffered(1)) for s in shapes
        ],
        out_shape=[jax.ShapeDtypeStruct(n.shape, BF16)] * 2
        + [jax.ShapeDtypeStruct(s, dt) for s in shapes],
        scratch_shapes=[pltpu.VMEM(s, F32) for s in shapes] if last else [],
        compiler_params=params(),
        cost_estimate=cost(18 * w * own * d * ff, 20 * w * own * d),
        name="ffn",
    )(*args)


def back_kernel(
    nblk, s_ref, q_ref, k_ref, v_ref, lse_ref, dq_ref, dk_ref, qf_ref, kvw_ref,
    dn_ref, hm_ref, c_ref, wo_ref, g_ref,
    dm_ref, dl_ref, gain_ref, gq_ref, gkv_ref,
    bq_ref, bk_ref, bv_ref, cap_ref, da_ref, aq_ref, ak_ref, av_ref, tq_ref, tk_ref, tv_ref,
):
    pair = pl.program_id(0)
    own = q_ref.shape[0]
    last = pl.num_programs(0) - 1

    @pl.when(pair == 0)
    def _():
        hm = hm_ref[...]
        dn = dn_ref[...].astype(F32)
        r = lax.rsqrt(jnp.mean(hm * hm, axis=-1, keepdims=True) + EPS)
        z = dn * g_ref[...]
        gain_ref[...] = jnp.sum(dn * hm * r, axis=0, keepdims=True)
        dm = (
            c_ref[...].astype(F32)
            + r * z
            - hm * (r * r * r) * jnp.mean(z * hm, axis=-1, keepdims=True)
        )
        dm_ref[...] = dm
        low = dm.astype(BF16)
        dl_ref[...] = low
        da = mm(low, wo_ref[...], NT).astype(BF16)
        for i in range(PAIRS):
            da_ref[i] = da[:, i * 128:(i + 1) * 128]
        bq_ref[...] = mm(qf_ref[...], rank_tile(QA, (QPAD, RQ * 128)))
        tile_keys(kvw_ref, bk_ref, bv_ref)
        make_cap(s_ref, dq_ref, dk_ref, cap_ref, nblk, own)
        for ref in (aq_ref, ak_ref, av_ref, tq_ref, tk_ref, tv_ref):
            ref[...] = jnp.zeros_like(ref)

    q = q_ref[...]
    k = k_ref[...]
    v = v_ref[...]
    qs = stacked(q)
    ds_ = stacked(da_ref[pair])
    cap = cap_ref[...]
    st = jnp.minimum(mm(k, qs, NT), jnp.concatenate([cap, cap], axis=1))
    p = jnp.exp(st - lse_ref[0])
    dp = mm(v, ds_, NT)
    delta = jnp.sum(p * dp, axis=0, keepdims=True)
    ds = (p * (dp - delta)).astype(BF16)
    dv = mm(p.astype(BF16), ds_)
    dk = mm(ds, qs)
    dq = unstacked(mm(k, ds, TN), own) * (DH ** (-0.5))

    eq = head_spread(pair, 0, RQ, (128, RQ * 128))
    qe = mm(qf_ref[:, :128], eq)
    dq6 = jnp.concatenate([dq] * RQ, axis=1)
    tq_ref[...] += dq6 * qe
    aq_ref[...] += mm((dq6 * bq_ref[...]).astype(BF16), eq, NT)
    ek = head_spread(pair, 0, RK, (128, RK * 128))
    ev = head_spread(pair, KCOLS - 128, RK, (128, RK * 128))
    ke = mm(kvw_ref[:, :128], ek)
    ve = mm(kvw_ref[:, 128:256], ev)
    dk2 = jnp.concatenate([dk] * RK, axis=1)
    dv2 = jnp.concatenate([dv] * RK, axis=1)
    tk_ref[...] += dk2 * ke
    tv_ref[...] += dv2 * ve
    ak_ref[...] += mm((dk2 * bk_ref[...]).astype(BF16), ek, NT)
    av_ref[...] += mm((dv2 * bv_ref[...]).astype(BF16), ev, NT)

    @pl.when(pair == last)
    def _():
        def fold(x, t):
            hi = x.astype(BF16)
            lo = (x - hi.astype(F32)).astype(BF16)
            return mm(hi, t, NT) + mm(lo, t, NT)

        gq = fold(tq_ref[...], rank_tile(QA, (QPAD, RQ * 128)))
        gq_ref[:, :128] = ((gq[:, :128] + aq_ref[...]) * (1.0 / RQ)).astype(BF16)
        gq_ref[:, 128:] = (gq[:, 128:] * (1.0 / RQ)).astype(BF16)
        gk = fold(tk_ref[...], rank_tile(KA, (KPAD, RK * 128)))
        gv = fold(tv_ref[...], rank_tile(KCOLS + KA, (KPAD, RK * 128)))
        gkv = gk + gv
        first = ((gkv[:, :128] + ak_ref[...]) * (1.0 / RK)).astype(BF16)
        second = ((gkv[:, 128:256] + av_ref[...]) * (1.0 / RK)).astype(BF16)
        third = (gkv[:, 256:] * (1.0 / RK)).astype(BF16)
        gkv_ref[...] = jnp.zeros_like(gkv_ref)
        for i in range(nblk):
            rows = slice(i * own, (i + 1) * own)
            slot = s_ref[1 + nblk + i]
            gkv_ref[slot, :, :128] = first[rows]
            gkv_ref[slot, :, 128:256] = second[rows]
            gkv_ref[slot, :, 256:] = third[rows]


def back(nblk, width, scalars, q, k, v, lse, dq, dk, qf, kvw, dn, hm, c, wo, gain):
    own, d = q.shape
    win = nblk * own
    whole = lambda a: pl.BlockSpec(a.shape, lambda p, a=a: (0,) * a.ndim)
    col = lambda rows: pl.BlockSpec((rows, 128), lambda p: (0, p))
    fixed = lambda *s: pl.BlockSpec(s, lambda p: (0,) * len(s))
    return pl.pallas_call(
        functools.partial(back_kernel, nblk),
        grid=(PAIRS,),
        in_specs=[
            pl.BlockSpec(memory_space=pltpu.SMEM), col(own), col(win), col(win),
            pl.BlockSpec((1, 1, 2 * own), lambda p: (p, 0, 0)),
        ] + [whole(a) for a in (dq, dk, qf, kvw, dn, hm, c, wo, gain)],
        out_specs=[
            fixed(own, d), fixed(own, d), fixed(1, d), fixed(own, QPAD),
            fixed(width, own, KPAD),
        ],
        out_shape=[
            jax.ShapeDtypeStruct((own, d), F32),
            jax.ShapeDtypeStruct((own, d), BF16),
            jax.ShapeDtypeStruct((1, d), F32),
            jax.ShapeDtypeStruct((own, QPAD), BF16),
            jax.ShapeDtypeStruct((width, own, KPAD), BF16),
        ],
        scratch_shapes=[
            pltpu.VMEM((own, RQ * 128), F32),
            pltpu.VMEM((win, RK * 128), F32),
            pltpu.VMEM((win, RK * 128), F32),
            pltpu.VMEM((win, own), F32),
            pltpu.VMEM((PAIRS, own, 128), BF16),
            pltpu.VMEM((own, 128), F32),
            pltpu.VMEM((win, 128), F32),
            pltpu.VMEM((win, 128), F32),
            pltpu.VMEM((own, RQ * 128), F32),
            pltpu.VMEM((win, RK * 128), F32),
            pltpu.VMEM((win, RK * 128), F32),
        ],
        compiler_params=params(),
        cost_estimate=cost(30e9, 15e6),
        name="back",
    )(scalars, q, k, v, lse, dq, dk, qf, kvw, dn, hm, c, wo, gain)


def flip(index, bit):
    digit = (index // bit) % 2
    return index + bit - 2 * bit * digit


AXES = {"c": ("wide", 1), "x": ("wide", 2), "y": ("rows", 1), "n": ("rows", 2), "f": ("rows", 4)}


def enter(names):
    barrier = pltpu.get_barrier_semaphore()
    for name in names:
        pl.semaphore_signal(
            barrier, inc=1, device_id=partner(name), device_id_type=pl.DeviceIdType.MESH
        )
    pl.semaphore_wait(barrier, len(names))


def partner(name):
    axis, bit = AXES[name]
    return {axis: flip(lax.axis_index(axis), bit)}


def digit(name):
    axis, bit = AXES[name]
    return (lax.axis_index(axis) // bit) % 2


def wide_digits(index):
    return index // 2, index % 2


def slot_for(me, block):
    mx, mc = wide_digits(me)
    bx, bc = wide_digits(block)
    return 2 * ((mc + bc) % 2) + (mx + bx) % 2


def send_to(name, src, dst, send, recv):
    return pltpu.make_async_remote_copy(
        src_ref=src, dst_ref=dst, send_sem=send, recv_sem=recv,
        device_id=partner(name), device_id_type=pl.DeviceIdType.MESH,
    )


class Gather:
    def __init__(self, ref, send, recv):
        self.x = send_to("x", ref.at[0], ref.at[1], send.at[0], recv.at[0])
        self.c = send_to("c", ref.at[0], ref.at[2], send.at[1], recv.at[1])
        self.r = send_to("c", ref.at[1], ref.at[3], send.at[2], recv.at[2])

    def first(self):
        self.x.start()
        self.c.start()

    def relay(self):
        self.x.wait()
        self.r.start()

    def done(self):
        self.c.wait()
        self.r.wait()


class Scatter:
    def __init__(self, part, got, last, send, recv):
        self.part, self.got, self.last = part, got, last
        self.c = send_to("c", part.at[pl.ds(2, 2)], got, send.at[0], recv.at[0])
        if last is not None:
            self.x = send_to("x", part.at[1], last, send.at[1], recv.at[1])

    def core(self):
        self.c.start()

    def kept(self, i):
        return self.part[i].astype(F32) + self.got[i].astype(F32)

    def cross(self):
        self.c.wait()
        self.part[1] = self.kept(1).astype(BF16)
        self.x.start()
        self.part[0] = self.kept(0).astype(BF16)

    def total(self):
        self.x.wait()
        return self.part[0].astype(F32) + self.last[...].astype(F32)


class Sum:
    def __init__(self, names, unit, src, base, acc, got, res, rbase, send, recv,
                 local=None, top=None, flat=False):
        self.names, self.unit, self.n = names, unit, len(names)
        self.src, self.base, self.acc, self.got = src, base, acc, got
        self.res, self.rbase, self.send, self.recv = res, rbase, send, recv
        self.local, self.flat = local, flat
        self.top = unit * 2 ** (self.n - 1) if top is None else top

    def low(self, i, skip=0):
        total = 0
        for j in range(skip, i):
            total = total + digit(self.names[j]) * 2 ** (self.n - 1 - j)
        return total

    def span(self, ref, base, chunk, count):
        return ref.at[pl.ds(base + chunk * self.unit, count * self.unit)]

    def keep(self):
        half = 2 ** (self.n - 1)
        return pltpu.make_async_copy(
            self.span(self.src, self.base, self.low(1), half), self.acc, self.local
        )

    def halve(self, i):
        half = 2 ** (self.n - 1 - i)
        away = (1 - digit(self.names[i])) * half
        if i == 0:
            src = self.span(self.src, self.base, away, half)
        else:
            src = self.span(self.acc, 0, self.low(i, 1) + away, half)
        dst = self.span(self.got, 0, 2 ** self.n - 2 * half, half)
        return send_to(self.names[i], src, dst, self.send.at[i], self.recv.at[i])

    def begin(self):
        self.halve(0).start()
        if self.local is not None:
            self.keep().start()

    def place(self, i):
        if self.flat:
            return self.rbase
        return self.rbase + digit(self.names[0]) * self.top + self.low(i, 1) * self.unit

    def double(self, i):
        half = 2 ** (self.n - 1 - i)
        held = self.res.at[pl.ds(self.place(i + 1), half * self.unit)]
        k = self.n + i
        return send_to(self.names[i], held, held, self.send.at[k], self.recv.at[k])

    def resume(self, own, at):
        place = self.place(self.n)
        for j in range(self.unit):
            self.res[place + j] = own[at + j]
        self.double(self.n - 1).start()

    def add(self, i):
        half = 2 ** (self.n - 1 - i)
        offset = (2 ** self.n - 2 * half) * self.unit
        self.halve(i).wait()
        kept = self.low(i + 1, 1) * self.unit
        first = i == 0 and self.local is None
        if i == 0 and self.local is not None:
            self.keep().wait()
        own = self.base + self.low(1) * self.unit
        last = i == self.n - 1
        place = self.place(self.n)

        def one(j, carry):
            mine = self.src[own + j] if first else self.acc[kept + j]
            value = (mine.astype(F32) + self.got[offset + j].astype(F32)).astype(BF16)
            if last:
                self.res[place + j] = value
            else:
                self.acc[kept + j] = value
            return carry

        lax.fori_loop(0, half * self.unit, one, 0)

    def step(self, k):
        n = self.n
        if k < n:
            self.add(k)
            if k < n - 1:
                self.halve(k + 1).start()
            elif not self.flat:
                self.double(n - 1).start()
        else:
            i = 2 * n - 1 - k
            self.double(i).wait()
            if i > 0:
                self.double(i - 1).start()


def fill_cap(me, first, dq, dk, cap_ref, nblk, own):
    for i in range(nblk):
        rows = pl.ds(i * own, own)
        key = lax.broadcasted_iota(jnp.int32, (own, own), 0)
        query = lax.broadcasted_iota(jnp.int32, (own, own), 1) + (me - first - i) * own
        ok = (dk[i * own:(i + 1) * own, :] == dq) & (key <= query)
        cap_ref[rows, :] = jnp.where(ok, BIG, NEG)


def fore_kernel(
    nblk, x_ref, wt_ref, wo_ref, g1_ref, g2_ref, dq_ref, dk_ref, c_ref,
    n1_ref, qf_ref, kvw_ref, att_ref, q_ref, k_ref, v_ref, lse_ref, hm_ref, ng_ref, cg_ref,
    kvg_ref, bq_ref, bk_ref, bv_ref, cap_ref, full_ref, send, recv,
):
    seqs, own, d = x_ref.shape
    me = lax.axis_index("wide")
    first = me // 3
    kvs = [Gather(kvg_ref.at[s], send.at[s], recv.at[s]) for s in range(seqs)]
    cots = [Gather(cg_ref.at[s], send.at[2 + s], recv.at[2 + s]) for s in range(seqs)]
    norms = [Gather(ng_ref.at[s], send.at[4 + s], recv.at[4 + s]) for s in range(seqs)]
    for s in range(seqs):
        cg_ref[s, 0] = c_ref[s]
    for s in range(seqs):
        x = x_ref[s].astype(F32)
        r = lax.rsqrt(jnp.mean(x * x, axis=-1, keepdims=True) + EPS)
        n = (x * r * g1_ref[...]).astype(BF16)
        n1_ref[s] = n
        f = mm(n, wt_ref[...], NT).astype(BF16)
        qf_ref[s] = f[:, :QPAD]
        kvg_ref[s, 0, :, :KV] = f[:, QCOLS:]
        kvg_ref[s, 0, :, KV:] = jnp.zeros((own, KPAD - KV), BF16)
        if s == 0:
            enter("cx")
        kvs[s].first()
    kvs[0].relay()
    for s in range(seqs):
        cots[s].first()
    kvs[0].done()

    def step(t, carry):
        s = t // PAIRS
        pair = t % PAIRS

        @pl.when(t == PAIRS)
        def _():
            kvs[1].done()

        @pl.when(pair == 0)
        def _():
            for i in range(nblk):
                kvw_ref[s, pl.ds(i * own, own), :] = kvg_ref[s, slot_for(me, first + i)]
            bq_ref[...] = mm(qf_ref[s], rank_tile(QA, (QPAD, RQ * 128)))
            bk_ref[...] = mm(kvw_ref[s, :, :256], rank_tile(KA, (256, RK * 128)))
            bv_ref[...] = mm(kvw_ref[s, :, 128:384], rank_tile(KCOLS + KA - 128, (256, RK * 128)))
            fill_cap(me, first, dq_ref[s], dk_ref[s], cap_ref, nblk, own)

        qe = mm(qf_ref[s, :, :128], head_spread(pair, 0, RQ, (128, RQ * 128)))
        qsum = qe[:, :128] * bq_ref[:, :128]
        for r in range(1, RQ):
            cols = slice(r * 128, (r + 1) * 128)
            qsum = qsum + qe[:, cols] * bq_ref[:, cols]
        q = (qsum * (1.0 / RQ)).astype(BF16)
        ke = mm(kvw_ref[s, :, :128], head_spread(pair, 0, RK, (128, RK * 128)))
        ve = mm(kvw_ref[s, :, 128:256], head_spread(pair, KCOLS - 128, RK, (128, RK * 128)))
        k = ((ke[:, :128] * bk_ref[:, :128] + ke[:, 128:] * bk_ref[:, 128:]) * (1.0 / RK)).astype(BF16)
        v = ((ve[:, :128] * bv_ref[:, :128] + ve[:, 128:] * bv_ref[:, 128:]) * (1.0 / RK)).astype(BF16)
        q = q * jnp.asarray(DH ** (-0.5), BF16)
        q_ref[s, pair] = q
        k_ref[s, pair] = k
        v_ref[s, pair] = v
        cap = cap_ref[...]
        st = jnp.minimum(mm(k, stacked(q), NT), jnp.concatenate([cap, cap], axis=1))
        top = jnp.max(st, axis=0, keepdims=True)
        e = jnp.exp(st - top)
        total = jnp.sum(e, axis=0, keepdims=True)
        p = (e * (1.0 / total)).astype(BF16)
        lse_ref[s, pair] = top + jnp.log(total)
        full_ref[pair] = unstacked(mm(v, p, TN), own).astype(BF16)

        @pl.when(pair == PAIRS - 1)
        def _():
            att = jnp.concatenate([full_ref[i] for i in range(PAIRS)], axis=1)
            att_ref[s] = att
            hm = x_ref[s].astype(F32) + mm(att, wo_ref[...])
            hm_ref[s] = hm
            r = lax.rsqrt(jnp.mean(hm * hm, axis=-1, keepdims=True) + EPS)
            ng_ref[s, 0] = (hm * r * g2_ref[...]).astype(BF16)

        @pl.when(t == 2)
        def _():
            kvs[1].relay()

        @pl.when(t == 6)
        def _():
            cots[0].relay()

        @pl.when(t == PAIRS - 1)
        def _():
            norms[0].first()

        @pl.when(t == 13)
        def _():
            cots[1].relay()

        return carry

    lax.fori_loop(0, seqs * PAIRS, step, 0)
    norms[1].first()
    norms[0].relay()
    for s in range(seqs):
        cots[s].done()
    norms[0].done()
    norms[1].relay()
    norms[1].done()


def vmem():
    return pl.BlockSpec(memory_space=pltpu.VMEM)


def hbm():
    return pl.BlockSpec(memory_space=pl.ANY)


def fused(ident, limit=63):
    return pltpu.CompilerParams(
        vmem_limit_bytes=limit << 20, collective_id=ident, has_side_effects=True
    )


def fore(nblk, x, wt, wo, g1, g2, dq, dk, c):
    seqs, own, d = x.shape
    win = nblk * own
    shape = jax.ShapeDtypeStruct
    return pl.pallas_call(
        functools.partial(fore_kernel, nblk),
        in_specs=[vmem()] * 8,
        out_specs=[vmem()] * 11,
        out_shape=[
            shape((seqs, own, d), BF16), shape((seqs, own, QPAD), BF16),
            shape((seqs, win, KPAD), BF16), shape((seqs, own, d), BF16),
            shape((seqs, PAIRS, own, 128), BF16), shape((seqs, PAIRS, win, 128), BF16),
            shape((seqs, PAIRS, win, 128), BF16), shape((seqs, PAIRS, 1, 2 * own), F32),
            shape((seqs, own, d), F32), shape((seqs, 4, own, d), BF16),
            shape((seqs, 4, own, d), BF16),
        ],
        scratch_shapes=[
            pltpu.VMEM((seqs, 4, own, KPAD), BF16),
            pltpu.VMEM((own, RQ * 128), F32),
            pltpu.VMEM((win, RK * 128), F32),
            pltpu.VMEM((win, RK * 128), F32),
            pltpu.VMEM((win, own), F32),
            pltpu.VMEM((PAIRS, own, 128), BF16),
            pltpu.SemaphoreType.DMA((6, 3)),
            pltpu.SemaphoreType.DMA((6, 3)),
        ],
        compiler_params=fused(0),
        cost_estimate=cost(30e9, 30e6),
        name="fore",
    )(x, wt, wo, g1, g2, dq, dk, c)


SPLITS = ((0, 192), (192, 256), (448, 256))
EARLY = len(SPLITS) - 1
LANES = 512
FFN_NAMES = (("ynf", "ynf", "nyf"), ("ynf", "nyf", "ynf"), ("ynf", "nyf", "ynf"))


def chunk_units(h):
    return SPLITS[h][1] // 16 * (1024 // LANES) // 8


def own_at(h, m):
    return 3 * sum(chunk_units(i) for i in range(h)) + m * chunk_units(h)


MIDDLE_EVENTS = {
    (1, 5): ((0, 0, 0),),
    (1, "m0"): ((0, 2, 0),),
    (1, "m1"): ((0, 1, 0), (0, 0, 1),),
    (2, 1): ((0, 0, 2), (1, 0, 0),),
    (2, 2): ((1, 1, 0), (0, 2, 1),),
    (2, 3): ((0, 1, 1),),
    (2, 5): ((0, 2, 2), (1, 0, 1), (1, 2, 0),),
    (2, 6): ((0, 1, 2),),
    (2, 7): ((1, 1, 1),),
    (2, "m0"): ((1, 0, 2), (1, 2, 1),),
    (2, "m2"): ((1, 1, 2),),
    "end": ((1, 2, 2),),
}


def middle_kernel(
    n_ref, c_ref, wg_ref, wu_ref, wd_ref,
    dn_ref, ds_ref, ok_ref, os_ref, gw_ref, own_ref,
    hid_ref, dg_ref, du_ref, oa_ref, da_ref, op_ref, dp_ref, xs_ref, oc_ref, dc_ref, dx_ref, *refs,
):
    seqs, size, own, d = n_ref.shape
    srcs, refs = refs[:EARLY], refs[EARLY:]
    accs, refs = refs[:3 * EARLY], refs[3 * EARLY:]
    gots, refs = refs[:3 * EARLY], refs[3 * EARLY:]
    send, recv, xsend, xrecv = refs
    downs = [
        send_to("c", dp_ref.at[s], dc_ref.at[s], xsend.at[0, s], xrecv.at[0, s]) for s in range(seqs)
    ]
    ups = [
        send_to("c", op_ref.at[s], oc_ref.at[s], xsend.at[1, s], xrecv.at[1, s]) for s in range(seqs)
    ]
    cross = send_to("x", xs_ref, dx_ref, xsend.at[2, 0], xrecv.at[2, 0])
    parts = {}
    for h in range(EARLY):
        for m in range(3):
            i = 3 * h + m
            u = chunk_units(h)
            parts[h, m] = Sum(
                FFN_NAMES[h][m], u, srcs[h], 8 * u * m, accs[i], gots[i], own_ref, own_at(h, m),
                send.at[i], recv.at[i], flat=True,
            )
    enter("cxynf")

    def run(point):
        for h, m, k in MIDDLE_EVENTS.get(point, ()):
            parts[h, m].step(k)

    for h, (off, rows) in enumerate(SPLITS):
        last = h == EARLY

        def step(t, carry, h=h, off=off, rows=rows, last=last):
            s = t // size
            b = size - 1 - t % size
            n = n_ref[s, b]
            c = c_ref[s, b]
            span = slice(off, off + rows)
            g = mm(wg_ref[span, :], n, NT)
            u = mm(wu_ref[span, :], n, NT)
            dh = mm(wd_ref[span, :], c, NT)
            sg = 1.0 / (1.0 + jnp.exp(-g))
            gs = g * sg
            cols = pl.ds(pl.multiple_of((s * size + b) * own, 128), own)
            hid_ref[span, cols] = (gs * u).astype(BF16)
            dg_ref[span, cols] = (dh * u * (sg * (1.0 + g * (1.0 - sg)))).astype(BF16)
            du_ref[span, cols] = (dh * gs).astype(BF16)
            if last:
                o = mm(hid_ref[:, cols], wd_ref[...], TN)
                dn = mm(dg_ref[:, cols], wg_ref[...], TN) + mm(du_ref[:, cols], wu_ref[...], TN)

                @pl.when(b >= 2)
                def _():
                    op_ref[s, b - 2] = o.astype(BF16)
                    dp_ref[s, b - 2] = dn.astype(BF16)

                @pl.when(b < 2)
                def _():
                    oa_ref[s, b] = o.astype(BF16)
                    da_ref[s, b] = dn

                for i in range(seqs):

                    @pl.when(t == i * size + 1)
                    def _(i=i):
                        downs[i].start()
                        ups[i].start()

                @pl.when(t == size - 1)
                def _():
                    downs[0].wait()
                    xs_ref[...] = (da_ref[0, 1] + dc_ref[0, 1].astype(F32)).astype(BF16)
                    cross.start()

            for j in range(seqs * size):
                if (h, j) in MIDDLE_EVENTS:

                    @pl.when(t == j)
                    def _(j=j):
                        run((h, j))

            return carry

        lax.fori_loop(0, seqs * size, step, 0)
        count = rows // 16
        for m, (a_ref, b_ref) in enumerate(((dg_ref, n_ref), (du_ref, n_ref), (hid_ref, c_ref))):
            w = mm(a_ref[off:off + rows, :], b_ref[...].reshape(seqs * size * own, d)).astype(BF16)
            to = gw_ref if last else srcs[h]
            for i in range(d // LANES):
                at = (m * (d // LANES) + i) * count
                piece = w[:, i * LANES:(i + 1) * LANES]
                to[pl.ds(at, count)] = piece.reshape(count, 16, LANES)
            if not last:
                parts[h, m].begin()
            run((h, "m%d" % m))
    for s in range(seqs):
        ups[s].wait()
        ok_ref[s] = (oa_ref[s, 0].astype(F32) + oc_ref[s, 0].astype(F32)).astype(BF16)
        os_ref[s] = (oa_ref[s, 1].astype(F32) + oc_ref[s, 1].astype(F32)).astype(BF16)
    downs[1].wait()
    dn_ref[1] = da_ref[1, 0] + dc_ref[1, 0].astype(F32)
    ds_ref[...] = (da_ref[1, 1] + dc_ref[1, 1].astype(F32)).astype(BF16)
    run("end")
    cross.wait()
    dn_ref[0] = da_ref[0, 0] + dc_ref[0, 0].astype(F32) + dx_ref[...].astype(F32)


def middle(n, c, wg, wu, wd):
    seqs, size, own, d = n.shape
    shape = jax.ShapeDtypeStruct
    flat = (wd.shape[0], seqs * size * own)
    u = [chunk_units(h) for h in range(EARLY) for _ in range(3)]
    unit = lambda k: pltpu.VMEM((k, 16, LANES), BF16)
    return pl.pallas_call(
        middle_kernel,
        in_specs=[vmem()] * 5,
        out_specs=[vmem()] * 6,
        out_shape=[
            shape((seqs, own, d), F32), shape((own, d), BF16), shape((seqs, own, d), BF16),
            shape((seqs, own, d), BF16), shape((24 * chunk_units(EARLY), 16, LANES), BF16),
            shape((own_at(EARLY, 0), 16, LANES), BF16),
        ],
        scratch_shapes=[pltpu.VMEM(flat, BF16)] * 3
        + [pltpu.VMEM((seqs, 2, own, d), BF16), pltpu.VMEM((seqs, 2, own, d), F32)]
        + [pltpu.VMEM((seqs, 2, own, d), BF16)] * 2
        + [pltpu.VMEM((own, d), BF16)]
        + [pltpu.VMEM((seqs, 2, own, d), BF16)] * 2
        + [pltpu.VMEM((own, d), BF16)]
        + [unit(24 * chunk_units(h)) for h in range(EARLY)]
        + [unit(4 * k) for k in u]
        + [unit(7 * k) for k in u]
        + [
            pltpu.SemaphoreType.DMA((3 * EARLY, 3)),
            pltpu.SemaphoreType.DMA((3 * EARLY, 3)),
            pltpu.SemaphoreType.DMA((3, seqs)),
            pltpu.SemaphoreType.DMA((3, seqs)),
        ],
        compiler_params=fused(1),
        cost_estimate=cost(27e9, 30e6),
        name="middle",
    )(n, c, wg, wu, wd)


FFN_UNITS = 3 * sum(r for _, r in SPLITS) // 16
AFTER_EVENTS = {
    0: (("F00", 3), ("F01", 3), ("F20", 0),),
    1: (("F02", 3),),
    2: (("second", 0), ("F10", 3), ("F22", 0), ("F11", 3), ("F02", 4), ("F12", 3),),
    4: (("F21", 0), ("O0", 0), ("F11", 4), ("F00", 4), ("O1", 0),),
    5: (("cross", 0), ("F01", 4),),
    6: (("F20", 1), ("F21", 1),),
    7: (("F10", 4), ("O1", 1), ("F22", 1), ("O0", 1),),
    8: (("F20", 2), ("F02", 5), ("F00", 5), ("F21", 2),),
    9: (("cross", 1), ("key", 0), ("F12", 4), ("F22", 2),),
    10: (("F01", 5), ("F20", 3), ("emit", 0),),
    11: (("O0", 2), ("F11", 5), ("F21", 3), ("F10", 5),),
    12: (("F22", 3),),
    13: (("O1", 2), ("F12", 5),),
    14: (("F21", 4),),
    15: (("O1", 3), ("F20", 4), ("emit", 1),),
    "T0": (("O0", 3),),
    "T1": (("F22", 4), ("O1", 4), ("K0", 0), ("K1", 0), ("O0", 4), ("F20", 5), ("O1", 5), ("F21", 5),),
    "T2": (("O0", 5), ("K0", 1), ("K2", 0), ("F22", 5), ("K3", 0), ("K1", 1), ("O1", 6),),
    "T3": (("K4", 0), ("O0", 6), ("K0", 2), ("K2", 1), ("K3", 1), ("O1", 7), ("K1", 2), ("K2", 2), ("K4", 1), ("O0", 7), ("K0", 3), ("K3", 2), ("K2", 3), ("K1", 3), ("K4", 2), ("K0", 4), ("K3", 3), ("K2", 4), ("O1", 8), ("K1", 4), ("K4", 3), ("K3", 4), ("O0", 8), ("K0", 5), ("K1", 5), ("K4", 4), ("K2", 5), ("O1", 9), ("K3", 5), ("K0", 6), ("K4", 5), ("K2", 6), ("O0", 9), ("K1", 6), ("K4", 6), ("K3", 6), ("K0", 7), ("K2", 7), ("K1", 7), ("K3", 7), ("K4", 7), ("K0", 8), ("K3", 8), ("K2", 8), ("K1", 8), ("K0", 9), ("K3", 9), ("K4", 8), ("K2", 9), ("K1", 9), ("K4", 9),),
}
OUT_PARTS = (("cyxnf", 128), ("cxnyf", 128))
Q_PARTS = (("cxynf", 64), ("cnyfx", 64))
K_PARTS = (("cxynf", 32), ("cynfx", 32), ("cnfxy", 32))
K_ROWS = 4 * sum(r for _, r in K_PARTS)
GAIN_ROW = 352


def cut(value, parts, bufs, only):
    m = sum(r for _, r in parts)
    at = 0
    for g, (_, r) in enumerate(parts):
        if g in only:
            for i in range(32):
                row = m * (i // 8) + at
                bufs[g][i] = value[row:row + r, 128 * (i % 8):128 * (i % 8) + 128]
        at += r


def joined(results, parts):
    cols = [r.reshape(4, 8, rows, 128) for r, (_, rows) in zip(results, parts)]
    whole = jnp.concatenate(cols, axis=2)
    return whole.transpose(0, 2, 1, 3).reshape(-1, 1024).astype(F32)


def after_kernel(
    nblk, gw_ref, own_ref, dn_ref, ds_ref, ok_ref, os_ref, q_ref, k_ref, v_ref, lse_ref, dq_ref, dk_ref,
    qf_ref, kvw_ref, hm_ref, c_ref, wo_ref, g1_ref, g2_ref, att_ref, n1_ref, x_ref, wt_ref,
    out_ref, ig_ref, gr_ref, *refs,
):
    n_out, n_q = len(OUT_PARTS), len(Q_PARTS)
    n_fac = n_q + len(K_PARTS)
    or_refs, refs = refs[:n_out], refs[n_out:]
    fr_refs, refs = refs[:n_fac], refs[n_fac:]
    (bq_ref, bk_ref, bv_ref, cap_ref, da_ref, aq_ref, ak_ref, av_ref, tq_ref, tk_ref, tv_ref,
     dm_ref, late_ref, gq_ref, gkp_ref, gkc_ref, gkx_ref, ox_ref, kb_ref, vb_ref, dx_ref, gain_ref) = refs[:22]
    refs = refs[22:]
    gots, refs = refs[:3], refs[3:]
    accs, refs = refs[:3], refs[3:]
    ob, refs = refs[:n_out], refs[n_out:]
    og, refs = refs[:n_out], refs[n_out:]
    oa, refs = refs[:n_out], refs[n_out:]
    fb, refs = refs[:n_fac], refs[n_fac:]
    fg, refs = refs[:n_fac], refs[n_fac:]
    fa, refs = refs[:n_fac], refs[n_fac:]
    send, recv, loc, gs, gr, kvsem, wsem = refs
    seqs, own, d = hm_ref.shape
    me = lax.axis_index("wide")
    first = me // 3

    sums = {}
    half = gr_ref.shape[0] // 2
    for h, (off, rows) in enumerate(SPLITS):
        for m in range(3):
            i = 3 * h + m
            u = chunk_units(h)
            late = h == EARLY
            sums[h, m] = Sum(
                FFN_NAMES[h][m], u, gw_ref if late else None, 8 * u * m,
                accs[m] if late else None, gots[m] if late else None,
                gr_ref, m * (half // 3) + off // 16, send.at[i], recv.at[i],
                local=loc.at[m] if late else None, top=half,
            )
    k0 = len(sums)
    outs = [
        Sum(names, 1, ob[g], 0, oa[g], og[g], or_refs[g], 0, send.at[k0 + g], recv.at[k0 + g])
        for g, (names, _) in enumerate(OUT_PARTS)
    ]
    k1 = k0 + n_out
    facs = [
        Sum(names, 1, fb[g], 0, fa[g], fg[g], fr_refs[g], 0, send.at[k1 + g], recv.at[k1 + g])
        for g, (names, _) in enumerate(Q_PARTS + K_PARTS)
    ]
    keys = [
        Scatter(gkp_ref.at[s], gkc_ref.at[s], gkx_ref.at[s], gs.at[s], gr.at[s])
        for s in range(seqs)
    ]
    crosses = [
        send_to("x", os_ref.at[s], ox_ref.at[s], gs.at[2 + s, 0], gr.at[2 + s, 0])
        for s in range(seqs)
    ]

    def fetch(t):
        return [
            pltpu.make_async_copy(a.at[t // PAIRS, t % PAIRS], b.at[t % 2], kvsem.at[i, t % 2])
            for i, (a, b) in enumerate(((k_ref, kb_ref), (v_ref, vb_ref)))
        ]

    for copy in fetch(0):
        copy.start()
    loads = [
        pltpu.make_async_copy(dn_ref, dm_ref, wsem.at[0]),
        pltpu.make_async_copy(c_ref, late_ref, wsem.at[1]),
    ]
    for copy in loads:
        copy.start()
    enter("cxynf")
    for h, m in sums:
        if h == EARLY:
            sums[h, m].begin()
        else:
            sums[h, m].resume(own_ref, own_at(h, m))

    for copy in loads:
        copy.wait()
    down = send_to("x", ds_ref, dx_ref, gs.at[4, 0], gr.at[4, 0])
    down.start()
    gain_ref[...] = jnp.zeros((1, d), F32)

    def mids(s):
        if s == 1:
            down.wait()
            dm_ref[1] += dx_ref[...].astype(F32)
        hm = hm_ref[s]
        dn = dm_ref[s]
        r = lax.rsqrt(jnp.mean(hm * hm, axis=-1, keepdims=True) + EPS)
        z = dn * g2_ref[...]
        gain_ref[...] += jnp.sum(dn * hm * r, axis=0, keepdims=True)
        dm = (
            late_ref[s].astype(F32)
            + r * z
            - hm * (r * r * r) * jnp.mean(z * hm, axis=-1, keepdims=True)
        )
        dm_ref[s] = dm
        low = dm.astype(BF16)
        late_ref[s] = low
        da = mm(low, wo_ref[...], NT).astype(BF16)
        for i in range(PAIRS):
            da_ref[s, i] = da[:, i * 128:(i + 1) * 128]

    load_x = pltpu.make_async_copy(x_ref, late_ref, wsem.at[2])

    def second():
        mids(1)
        go = mm(att_ref[...].reshape(seqs * own, d), late_ref[...].reshape(seqs * own, d), TN)
        cut(go.astype(BF16), OUT_PARTS, ob, range(n_out))
        for part in outs:
            part.begin()
        load_x.start()

    mids(0)

    def finish(s):
        def fold(x, t):
            hi = x.astype(BF16)
            lo = (x - hi.astype(F32)).astype(BF16)
            return mm(hi, t, NT) + mm(lo, t, NT)

        gq = fold(tq_ref[...], rank_tile(QA, (QPAD, RQ * 128)))
        gq_ref[s, :, :128] = ((gq[:, :128] + aq_ref[...]) * (1.0 / RQ)).astype(BF16)
        gq_ref[s, :, 128:] = (gq[:, 128:] * (1.0 / RQ)).astype(BF16)
        gk = fold(tk_ref[...], rank_tile(KA, (KPAD, RK * 128)))
        gv = fold(tv_ref[...], rank_tile(KCOLS + KA, (KPAD, RK * 128)))
        gkv = gk + gv
        one = ((gkv[:, :128] + ak_ref[...]) * (1.0 / RK)).astype(BF16)
        two = ((gkv[:, 128:256] + av_ref[...]) * (1.0 / RK)).astype(BF16)
        three = (gkv[:, 256:] * (1.0 / RK)).astype(BF16)
        gkp_ref[s] = jnp.zeros_like(gkp_ref[s])
        for i in range(nblk):
            rows = slice(i * own, (i + 1) * own)
            slot = slot_for(me, first + i)
            gkp_ref[s, slot, :, :128] = one[rows]
            gkp_ref[s, slot, :, 128:256] = two[rows]
            gkp_ref[s, slot, :, 256:] = three[rows]

    def emit(s):
        crosses[s].wait()
        total = hm_ref[s] + (ok_ref[s].astype(F32) + ox_ref[s].astype(F32))
        out_ref[s] = total.astype(BF16)

    named = {"F%d%d" % key: part for key, part in sums.items()}
    named.update({"O%d" % g: part for g, part in enumerate(outs)})
    named.update({"K%d" % g: part for g, part in enumerate(facs)})

    def run(point):
        for name, k in AFTER_EVENTS.get(point, ()):
            if name == "cross":
                crosses[k].start()
            elif name == "emit":
                emit(k)
            elif name == "key":
                keys[k].cross()
            elif name == "second":
                second()
            else:
                named[name].step(k)

    def step(t, carry):
        s = t // PAIRS
        pair = t % PAIRS
        slot = t % 2

        @pl.when(t < seqs * PAIRS - 1)
        def _():
            for copy in fetch(t + 1):
                copy.start()

        @pl.when(pair == 0)
        def _():
            bq_ref[...] = mm(qf_ref[s], rank_tile(QA, (QPAD, RQ * 128)))
            bk_ref[...] = mm(kvw_ref[s, :, :256], rank_tile(KA, (256, RK * 128)))
            bv_ref[...] = mm(kvw_ref[s, :, 128:384], rank_tile(KCOLS + KA - 128, (256, RK * 128)))
            fill_cap(me, first, dq_ref[s], dk_ref[s], cap_ref, nblk, own)
            for ref in (aq_ref, ak_ref, av_ref, tq_ref, tk_ref, tv_ref):
                ref[...] = jnp.zeros_like(ref)

        for copy in fetch(t):
            copy.wait()
        q = q_ref[s, pair]
        k = kb_ref[slot]
        v = vb_ref[slot]
        qs = stacked(q)
        da = stacked(da_ref[s, pair])
        cap = cap_ref[...]
        st = jnp.minimum(mm(k, qs, NT), jnp.concatenate([cap, cap], axis=1))
        p = jnp.exp(st - lse_ref[s, pair])
        dp = mm(v, da, NT)
        delta = jnp.sum(p * dp, axis=0, keepdims=True)
        ds = (p * (dp - delta)).astype(BF16)
        dv = mm(p.astype(BF16), da)
        dk = mm(ds, qs)
        dq = unstacked(mm(k, ds, TN), own) * (DH ** (-0.5))

        eq = head_spread(pair, 0, RQ, (128, RQ * 128))
        qe = mm(qf_ref[s, :, :128], eq)
        dq6 = jnp.concatenate([dq] * RQ, axis=1)
        tq_ref[...] += dq6 * qe
        aq_ref[...] += mm((dq6 * bq_ref[...]).astype(BF16), eq, NT)
        ek = head_spread(pair, 0, RK, (128, RK * 128))
        ev = head_spread(pair, KCOLS - 128, RK, (128, RK * 128))
        ke = mm(kvw_ref[s, :, :128], ek)
        ve = mm(kvw_ref[s, :, 128:256], ev)
        dk2 = jnp.concatenate([dk] * RK, axis=1)
        dv2 = jnp.concatenate([dv] * RK, axis=1)
        tk_ref[...] += dk2 * ke
        tv_ref[...] += dv2 * ve
        ak_ref[...] += mm((dk2 * bk_ref[...]).astype(BF16), ek, NT)
        av_ref[...] += mm((dv2 * bv_ref[...]).astype(BF16), ev, NT)

        @pl.when(pair == PAIRS - 1)
        def _():
            finish(s)

        @pl.when(t == PAIRS - 1)
        def _():
            keys[0].core()

        for when in range(seqs * PAIRS):
            if when in AFTER_EVENTS:

                @pl.when(t == when)
                def _(when=when):
                    run(when)

        return carry

    lax.fori_loop(0, seqs * PAIRS, step, 0)
    keys[1].core()
    n1 = n1_ref[...].reshape(seqs * own, d)
    gq = gq_ref[...].reshape(seqs * own, QPAD)
    cut(mm(gq, n1, TN).astype(BF16), Q_PARTS, fb[:n_q], range(n_q))
    for part in facs[:n_q]:
        part.begin()
    dn1 = mm(gq[:, :QCOLS], wt_ref[:QCOLS, :])
    run("T0")
    keys[1].cross()
    run("T1")
    gkv0 = keys[0].total().astype(BF16)
    gkv = jnp.concatenate([gkv0, keys[1].total().astype(BF16)], axis=0)
    gf = mm(gkv, n1, TN)
    cut(gf.astype(BF16), K_PARTS, fb[n_q:], range(len(K_PARTS) - 1))
    for part in facs[n_q:-1]:
        part.begin()
    dn1 = dn1 + mm(gkv[:, :KV], wt_ref[QCOLS:, :])
    load_x.wait()
    hin = late_ref[...].reshape(seqs * own, d).astype(F32)
    r1 = lax.rsqrt(jnp.mean(hin * hin, axis=-1, keepdims=True) + EPS)
    z1 = dn1 * g1_ref[...]
    gain_one = jnp.sum(dn1 * hin * r1, axis=0, keepdims=True)
    gf = jnp.concatenate(
        [gf[:GAIN_ROW], gain_one, gain_ref[...], gf[GAIN_ROW + 2:]], axis=0
    )
    cut(gf.astype(BF16), K_PARTS, fb[n_q:], (len(K_PARTS) - 1,))
    facs[-1].begin()
    run("T2")
    grad = r1 * z1 - hin * (r1 * r1 * r1) * jnp.mean(z1 * hin, axis=-1, keepdims=True)
    ig_ref[...] = (dm_ref[...].reshape(seqs * own, d) + grad).astype(BF16).reshape(seqs, own, d)
    run("T3")


def after(nblk, gw, own_sums, dn, ds, ok, os, q, k, v, lse, dq, dk, qf, kvw, hm, c, wo, g1, g2, att, n1, x, wt):
    seqs, own, d = hm.shape
    win = nblk * own
    shape = jax.ShapeDtypeStruct
    far = (0, 2, 3, 5, 7, 8, 15, 21)
    results = [shape((32, r, 128), BF16) for _, r in OUT_PARTS + Q_PARTS + K_PARTS]
    total = 3 * len(SPLITS) + len(results)
    args = (gw, own_sums, dn, ds, ok, os, q, k, v, lse, dq, dk, qf, kvw, hm, c, wo, g1, g2, att, n1, x, wt)
    res = pl.pallas_call(
        functools.partial(after_kernel, nblk),
        in_specs=[hbm() if i in far else vmem() for i in range(len(args))],
        out_specs=[vmem()] * (3 + len(results)),
        out_shape=[
            shape((seqs, own, d), BF16), shape((seqs, own, d), BF16),
            shape((2 * FFN_UNITS, 16, LANES), BF16),
        ] + results,
        scratch_shapes=[
            pltpu.VMEM((own, RQ * 128), F32),
            pltpu.VMEM((win, RK * 128), F32),
            pltpu.VMEM((win, RK * 128), F32),
            pltpu.VMEM((win, own), F32),
            pltpu.VMEM((seqs, PAIRS, own, 128), BF16),
            pltpu.VMEM((own, 128), F32),
            pltpu.VMEM((win, 128), F32),
            pltpu.VMEM((win, 128), F32),
            pltpu.VMEM((own, RQ * 128), F32),
            pltpu.VMEM((win, RK * 128), F32),
            pltpu.VMEM((win, RK * 128), F32),
            pltpu.VMEM((seqs, own, d), F32),
            pltpu.VMEM((seqs, own, d), BF16),
            pltpu.VMEM((seqs, own, QPAD), BF16),
            pltpu.VMEM((seqs, 4, own, KPAD), BF16),
            pltpu.VMEM((seqs, 2, own, KPAD), BF16),
            pltpu.VMEM((seqs, own, KPAD), BF16),
            pltpu.VMEM((seqs, own, d), BF16),
            pltpu.VMEM((2, win, 128), BF16),
            pltpu.VMEM((2, win, 128), BF16),
            pltpu.VMEM((own, d), BF16),
            pltpu.VMEM((1, d), F32),
        ]
        + [pltpu.VMEM((7 * chunk_units(EARLY), 16, LANES), BF16)] * 3
        + [pltpu.VMEM((4 * chunk_units(EARLY), 16, LANES), BF16)] * 3
        + [pltpu.VMEM((n, r, 128), BF16) for n in (32, 31, 16) for _, r in OUT_PARTS]
        + [pltpu.VMEM((n, r, 128), BF16) for n in (32, 31, 16) for _, r in Q_PARTS + K_PARTS]
        + [
            pltpu.SemaphoreType.DMA((total, 10)),
            pltpu.SemaphoreType.DMA((total, 10)),
            pltpu.SemaphoreType.DMA((3,)),
            pltpu.SemaphoreType.DMA((5, 2)),
            pltpu.SemaphoreType.DMA((5, 2)),
            pltpu.SemaphoreType.DMA((2, 2)),
            pltpu.SemaphoreType.DMA((3,)),
        ],
        compiler_params=fused(2),
        cost_estimate=cost(60e9, 60e6),
        name="after",
    )(*args)
    n = 3 + len(OUT_PARTS)
    return res[0], res[1], res[2], res[3:n], res[n:]


def fused_body(
    tokens, doc_ids, factor_weight, output_weight, norm_one, norm_two,
    gate_weight, up_weight, down_weight, cotangent,
):
    seqs, own, d = tokens.shape
    me = lax.axis_index("wide")
    nblk = -(-(MAX_DOC - 1) // own) + 1
    first = me // 3
    g1 = norm_one[None]
    g2 = norm_two[None]
    dq = lax.dynamic_slice_in_dim(doc_ids, me * own, own, 1)[:, None, :]
    dk = lax.dynamic_slice_in_dim(doc_ids, first * own, nblk * own, 1)[:, :, None]
    wt = factor_weight.T
    n1, qf, kvw, att, q, k, v, lse, hm, ng, cg = fore(
        nblk, tokens, wt, output_weight, g1, g2, dq, dk, cotangent
    )
    dn, ds, ok, os, gw, own_sums = middle(ng, cg, gate_weight.T, up_weight.T, down_weight)
    output, input_grad, gr, go, gf = after(
        nblk, gw, own_sums, dn, ds, ok, os, q, k, v, lse, dq, dk, qf, kvw, hm, cotangent, output_weight,
        g1, g2, att, n1, tokens, wt,
    )
    ff = down_weight.shape[0]
    gr = gr.reshape(2, 3, ff, LANES)
    gr = [jnp.concatenate([gr[0, m], gr[1, m]], axis=1).astype(F32) for m in range(3)]
    grad_out = joined(go, OUT_PARTS)
    n_q = len(Q_PARTS)
    fac = joined(gf[n_q:], K_PARTS)
    gain = fac[GAIN_ROW:GAIN_ROW + 2]
    fac = jnp.concatenate([joined(gf[:n_q], Q_PARTS)[:QCOLS], fac[:KV]], axis=0)
    return (
        output, input_grad, fac.T, grad_out, gain[0], gain[1], gr[0].T, gr[1].T, gr[2],
    )


def swap(x, axis, size, bit):
    return lax.ppermute(x, axis, [(i, i ^ bit) for i in range(size)])


def steps_of(size):
    bits, b = [], size // 2
    while b:
        bits.append(b)
        b //= 2
    return bits


def gather(x, size):
    buf = x[None]
    for bit in steps_of(size):
        buf = jnp.concatenate([buf, swap(buf, "wide", size, bit)], axis=0)
    return buf


def order_of(size):
    order = [0]
    for bit in steps_of(size):
        order = order + [o ^ bit for o in order]
    return order


def scatter(parts, size):
    for bit in reversed(steps_of(size)):
        half = parts.shape[0] // 2
        got = swap(parts[half:], "wide", size, bit)
        total = parts[:half].astype(F32) + got.astype(F32)
        parts = total if half == 1 else total.astype(BF16)
    return parts[0]


def body(
    tokens, doc_ids, factor_weight, output_weight, norm_one, norm_two,
    gate_weight, up_weight, down_weight, cotangent,
):
    seqs, own, d = tokens.shape
    full_len = doc_ids.shape[1]
    size = full_len // own
    me = lax.axis_index("wide")
    left = min(-(-(MAX_DOC - 1) // own), size - 1)
    nblk = left + 1
    start = jnp.maximum(me - left, 0)
    order = order_of(size)
    slot_of = [order.index(j) for j in range(size)]
    slots = jnp.asarray(slot_of, jnp.int32)
    blocks = start + jnp.arange(nblk, dtype=jnp.int32)
    scalars = jnp.concatenate(
        [me[None].astype(jnp.int32), (me - blocks) * own, slots[me ^ blocks]]
    ).astype(jnp.int32)
    g1 = norm_one[None]
    g2 = norm_two[None]

    n1, qf, kvf = front(tokens.reshape(seqs * own, d), factor_weight, g1)
    qf = qf.reshape(seqs, own, QPAD)
    kvg = gather(kvf.reshape(seqs, own, KPAD), size)
    doc_query = lax.dynamic_slice_in_dim(doc_ids, me * own, own, 1)
    doc_key = lax.dynamic_slice_in_dim(doc_ids, start * own, nblk * own, 1)
    cots = [gather(cotangent[s], size) for s in range(seqs)]

    fwd = []
    for s in range(seqs):
        dq = doc_query[s][None, :]
        dk = doc_key[s][:, None]
        fwd.append(
            (dq, dk)
            + tuple(attend(nblk, scalars, qf[s], kvg[:, s], dq, dk, tokens[s], output_weight, g2))
        )
    prev = None
    outs, dns = [], []
    for s in range(seqs):
        n2 = gather(fwd[s][8], size)
        res = ffn(n2, cots[s], gate_weight, up_weight, down_weight, prev, s == seqs - 1)
        outs.append(res[0])
        dns.append(res[1])
        prev = res[2:]
    grads = [lax.psum(g, "rows").astype(F32) for g in prev]

    output, mids, lows, gain_two, gqs, gkvs = [], [], [], 0.0, [], []
    for s in range(seqs):
        dq, dk, att, q, k, v, lse, hm, n2, kvw = fwd[s]
        dn = scatter(dns[s], size)
        dm, low, gain, gq, gkv = back(
            nblk, size, scalars, q, k, v, lse, dq, dk, qf[s], kvw, dn, hm,
            cotangent[s], output_weight, g2,
        )
        output.append((hm + scatter(outs[s], size)).astype(BF16))
        mids.append(dm)
        lows.append(low)
        gqs.append(gq)
        gkvs.append(gkv)
        gain_two = gain_two + gain
    att_all = jnp.stack([f[2] for f in fwd]).reshape(seqs * own, d)
    grad_out = mm(att_all, jnp.stack(lows).reshape(seqs * own, d), TN)
    gkv = scatter(jnp.stack(gkvs, axis=1), size).astype(BF16)
    dfac = jnp.concatenate([jnp.stack(gqs)[..., :QCOLS], gkv[..., :KV]], axis=-1)
    dfac = dfac.reshape(seqs * own, -1)
    grad_factors = mm(n1, dfac, TN)
    dn1 = mm(dfac, factor_weight, NT)
    hin = tokens.reshape(seqs * own, d).astype(F32)
    r1 = lax.rsqrt(jnp.mean(hin * hin, axis=-1, keepdims=True) + EPS)
    z1 = dn1 * g1
    gain_one = jnp.sum(dn1 * hin * r1, axis=0)
    grad_norm = r1 * z1 - hin * (r1 * r1 * r1) * jnp.mean(z1 * hin, axis=-1, keepdims=True)
    input_grad = (jnp.stack(mids).reshape(seqs * own, d) + grad_norm).astype(BF16)
    parts = [grad_out, grad_factors.T, gain_one[None], gain_two]
    packed = jnp.concatenate([p.astype(BF16) for p in parts], axis=0)
    packed = lax.psum(packed, ("rows", "wide")).astype(F32)
    fac = grad_factors.shape[1]
    return (
        jnp.stack(output),
        input_grad.reshape(seqs, own, d),
        packed[d:d + fac].T,
        packed[:d],
        packed[d + fac],
        packed[d + fac + 1],
        grads[0],
        grads[1],
        grads[2],
    )


def solution(mesh):
    placed = (
        P("rows", "wide", None), P("rows", None), P(), P(), P(), P(),
        P(None, "wide"), P(None, "wide"), P("wide", None), P("rows", "wide", None),
    )
    small = mesh.shape["rows"] == 8 and mesh.shape["wide"] == 4
    return jax.shard_map(
        fused_body if small else body,
        mesh=mesh,
        in_specs=placed,
        out_specs=(
            P("rows", "wide", None), P("rows", "wide", None), P(), P(), P(), P(),
            P(None, "wide"), P(None, "wide"), P("wide", None),
        ),
        check_vma=False,
    )
```

```python
import functools

import jax
import jax.numpy as jnp
from jax import lax
from jax.experimental import pallas as pl
from jax.experimental.pallas import tpu as pltpu
from jax.sharding import PartitionSpec as P

H = 16
DH = 64
RQ = 6
RK = 2
MAX_DOC = 512
EPS = 1e-06
NEG = -1000000000.0
BIG = 3.0e38

QA = H * RQ
QCOLS = QA + RQ * DH
KA = H * RK
KCOLS = KA + RK * DH
KV = 2 * KCOLS
QPAD = 512
KPAD = 384
PAIRS = H // 2

F32 = jnp.float32
BF16 = jnp.bfloat16

NN = (((1,), (0,)), ((), ()))
NT = (((1,), (1,)), ((), ()))
TN = (((0,), (0,)), ((), ()))


def mm(a, b, dims=NN):
    return lax.dot_general(a, b, dims, preferred_element_type=F32)


def params(vmem_mb=60):
    return pltpu.CompilerParams(vmem_limit_bytes=vmem_mb << 20)


def cost(flops, nbytes):
    return pl.CostEstimate(flops=int(flops), bytes_accessed=int(nbytes), transcendentals=0)


def selection(shape, rule):
    row = lax.broadcasted_iota(jnp.int32, shape, 0)
    col = lax.broadcasted_iota(jnp.int32, shape, 1)
    return jnp.where(rule(row, col), 1.0, 0.0).astype(BF16)


def head_spread(pair, base, rank, shape):
    def rule(row, col):
        r = col // 128
        lane = col - r * 128
        head = 2 * pair + jnp.where(lane >= DH, 1, 0)
        return row == base + head * rank + r

    return selection(shape, rule)


def rank_tile(base, shape):
    def rule(row, col):
        r = col // 128
        lane = col - r * 128
        return row == base + r * DH + jnp.where(lane >= DH, lane - DH, lane)

    return selection(shape, rule)


def front_kernel(x_ref, w_ref, g_ref, n_ref, q_ref, kv_ref):
    x = x_ref[...].astype(F32)
    r = lax.rsqrt(jnp.mean(x * x, axis=-1, keepdims=True) + EPS)
    n = (x * r * g_ref[...]).astype(BF16)
    n_ref[...] = n
    f = mm(n, w_ref[...]).astype(BF16)
    q_ref[...] = f[:, :QPAD]
    kv_ref[:, :KV] = f[:, QCOLS:]
    kv_ref[:, KV:] = jnp.zeros((f.shape[0], KPAD - KV), BF16)


def front(x, w, gain):
    rows, d = x.shape
    blk = 256 if rows % 256 == 0 else rows
    return pl.pallas_call(
        front_kernel,
        grid=(rows // blk,),
        in_specs=[
            pl.BlockSpec((blk, d), lambda i: (i, 0)),
            pl.BlockSpec(w.shape, lambda i: (0, 0)),
            pl.BlockSpec((1, d), lambda i: (0, 0)),
        ],
        out_specs=[
            pl.BlockSpec((blk, d), lambda i: (i, 0)),
            pl.BlockSpec((blk, QPAD), lambda i: (i, 0)),
            pl.BlockSpec((blk, KPAD), lambda i: (i, 0)),
        ],
        out_shape=[
            jax.ShapeDtypeStruct((rows, d), BF16),
            jax.ShapeDtypeStruct((rows, QPAD), BF16),
            jax.ShapeDtypeStruct((rows, KPAD), BF16),
        ],
        compiler_params=params(),
        cost_estimate=cost(2 * rows * d * 800, rows * d * 6 + d * 1600),
        name="front",
    )(x, w, gain)


def make_cap(s_ref, dq_ref, dk_ref, cap_ref, nblk, own):
    dq = dq_ref[...]
    for i in range(nblk):
        rows = pl.ds(i * own, own)
        key = lax.broadcasted_iota(jnp.int32, (own, own), 0)
        query = lax.broadcasted_iota(jnp.int32, (own, own), 1) + s_ref[1 + i]
        ok = (dk_ref[rows, :] == dq) & (key <= query)
        cap_ref[rows, :] = jnp.where(ok, BIG, NEG)


def stacked(x):
    lane = lax.broadcasted_iota(jnp.int32, x.shape, 1)
    zero = jnp.zeros_like(x)
    return jnp.concatenate(
        [jnp.where(lane < DH, x, zero), jnp.where(lane >= DH, x, zero)], axis=0
    )


def unstacked(xt, own):
    pair = jnp.concatenate([xt[:DH, :own], xt[DH:, own:]], axis=0)
    return pair.T


def key_parts(kvf_ref, pair):
    ek = head_spread(pair, 0, RK, (128, RK * 128))
    ev = head_spread(pair, KCOLS - 128, RK, (128, RK * 128))
    ke = mm(kvf_ref[:, :128], ek)
    ve = mm(kvf_ref[:, 128:256], ev)
    return ke, ve


def tile_keys(kvf_ref, bk_ref, bv_ref):
    bk_ref[...] = mm(kvf_ref[:, :256], rank_tile(KA, (256, RK * 128)))
    bv_ref[...] = mm(kvf_ref[:, 128:384], rank_tile(KCOLS + KA - 128, (256, RK * 128)))


def attend_kernel(
    nblk, s_ref, qf_ref, kvg_ref, dq_ref, dk_ref, x_ref, wo_ref, g_ref,
    att_ref, q_ref, k_ref, v_ref, lse_ref, hm_ref, n_ref, kvw_ref,
    bq_ref, bk_ref, bv_ref, cap_ref, full_ref,
):
    pair = pl.program_id(0)
    own = qf_ref.shape[0]

    @pl.when(pair == 0)
    def _():
        for i in range(nblk):
            kvw_ref[pl.ds(i * own, own), :] = kvg_ref[s_ref[1 + nblk + i]]
        bq_ref[...] = mm(qf_ref[...], rank_tile(QA, (QPAD, RQ * 128)))
        tile_keys(kvw_ref, bk_ref, bv_ref)
        make_cap(s_ref, dq_ref, dk_ref, cap_ref, nblk, own)

    qe = mm(qf_ref[:, :128], head_spread(pair, 0, RQ, (128, RQ * 128)))
    qsum = qe[:, :128] * bq_ref[:, :128]
    for r in range(1, RQ):
        cols = slice(r * 128, (r + 1) * 128)
        qsum = qsum + qe[:, cols] * bq_ref[:, cols]
    q = (qsum * (1.0 / RQ)).astype(BF16)
    ke, ve = key_parts(kvw_ref, pair)
    k = ((ke[:, :128] * bk_ref[:, :128] + ke[:, 128:] * bk_ref[:, 128:]) * (1.0 / RK)).astype(BF16)
    v = ((ve[:, :128] * bv_ref[:, :128] + ve[:, 128:] * bv_ref[:, 128:]) * (1.0 / RK)).astype(BF16)
    q = q * jnp.asarray(DH ** (-0.5), BF16)
    q_ref[...] = q
    k_ref[...] = k
    v_ref[...] = v
    cap = cap_ref[...]
    st = jnp.minimum(mm(k, stacked(q), NT), jnp.concatenate([cap, cap], axis=1))
    top = jnp.max(st, axis=0, keepdims=True)
    e = jnp.exp(st - top)
    total = jnp.sum(e, axis=0, keepdims=True)
    p = (e * (1.0 / total)).astype(BF16)
    lse_ref[0] = top + jnp.log(total)
    att = unstacked(mm(v, p, TN), own).astype(BF16)
    att_ref[...] = att
    full_ref[pair] = att

    @pl.when(pair == pl.num_programs(0) - 1)
    def _():
        hm = x_ref[...].astype(F32)
        att_all = jnp.concatenate([full_ref[i] for i in range(PAIRS)], axis=1)
        hm = hm + mm(att_all, wo_ref[...])
        hm_ref[...] = hm
        r = lax.rsqrt(jnp.mean(hm * hm, axis=-1, keepdims=True) + EPS)
        n_ref[...] = (hm * r * g_ref[...]).astype(BF16)


def attend(nblk, scalars, qf, kvg, dq, dk, x, wo, gain):
    own, d = x.shape
    win = nblk * own
    whole = lambda a: pl.BlockSpec(a.shape, lambda p, a=a: (0,) * a.ndim)
    col = lambda rows: pl.BlockSpec((rows, 128), lambda p: (0, p))
    return pl.pallas_call(
        functools.partial(attend_kernel, nblk),
        grid=(PAIRS,),
        in_specs=[pl.BlockSpec(memory_space=pltpu.SMEM)]
        + [whole(a) for a in (qf, kvg, dq, dk, x, wo, gain)],
        out_specs=[
            col(own), col(own), col(win), col(win),
            pl.BlockSpec((1, 1, 2 * own), lambda p: (p, 0, 0)),
            pl.BlockSpec((own, d), lambda p: (0, 0)),
            pl.BlockSpec((own, d), lambda p: (0, 0)),
            pl.BlockSpec((win, KPAD), lambda p: (0, 0)),
        ],
        out_shape=[
            jax.ShapeDtypeStruct((own, d), BF16),
            jax.ShapeDtypeStruct((own, d), BF16),
            jax.ShapeDtypeStruct((win, d), BF16),
            jax.ShapeDtypeStruct((win, d), BF16),
            jax.ShapeDtypeStruct((PAIRS, 1, 2 * own), F32),
            jax.ShapeDtypeStruct((own, d), F32),
            jax.ShapeDtypeStruct((own, d), BF16),
            jax.ShapeDtypeStruct((win, KPAD), BF16),
        ],
        scratch_shapes=[
            pltpu.VMEM((own, RQ * 128), F32),
            pltpu.VMEM((win, RK * 128), F32),
            pltpu.VMEM((win, RK * 128), F32),
            pltpu.VMEM((win, own), F32),
            pltpu.VMEM((PAIRS, own, 128), BF16),
        ],
        compiler_params=params(),
        cost_estimate=cost(12e9, 12e6),
        name="attend",
    )(scalars, qf, kvg, dq, dk, x, wo, gain)


def ffn_kernel(has_prev, bf16_out, *refs):
    if has_prev:
        n_ref, c_ref, wg_ref, wu_ref, wd_ref, pg_ref, pu_ref, pd_ref = refs[:8]
        refs = refs[8:]
    else:
        n_ref, c_ref, wg_ref, wu_ref, wd_ref = refs[:5]
        refs = refs[5:]
    o_ref, dn_ref, og_ref, ou_ref, od_ref = refs[:5]
    if bf16_out:
        ag_ref, au_ref, ad_ref = refs[5:]
    else:
        ag_ref, au_ref, ad_ref = og_ref, ou_ref, od_ref
    step = pl.program_id(0)

    @pl.when(step == 0)
    def _():
        if has_prev:
            ag_ref[...] = pg_ref[...]
            au_ref[...] = pu_ref[...]
            ad_ref[...] = pd_ref[...]
        else:
            ag_ref[...] = jnp.zeros_like(ag_ref)
            au_ref[...] = jnp.zeros_like(au_ref)
            ad_ref[...] = jnp.zeros_like(ad_ref)

    n = n_ref[0]
    c = c_ref[0]
    wg, wu, wd = wg_ref[...], wu_ref[...], wd_ref[...]
    g = mm(n, wg)
    u = mm(n, wu)
    dh = mm(c, wd, NT)
    s = 1.0 / (1.0 + jnp.exp(-g))
    gs = g * s
    hid = (gs * u).astype(BF16)
    dg = (dh * u * (s * (1.0 + g * (1.0 - s)))).astype(BF16)
    du = (dh * gs).astype(BF16)
    o_ref[0] = mm(hid, wd).astype(BF16)
    dn_ref[0] = (mm(dg, wg, NT) + mm(du, wu, NT)).astype(BF16)
    ag_ref[...] += mm(n, dg, TN)
    au_ref[...] += mm(n, du, TN)
    ad_ref[...] += mm(hid, c, TN)
    if bf16_out:

        @pl.when(step == pl.num_programs(0) - 1)
        def _():
            og_ref[...] = ag_ref[...].astype(BF16)
            ou_ref[...] = au_ref[...].astype(BF16)
            od_ref[...] = ad_ref[...].astype(BF16)


def ffn(n, c, wg, wu, wd, prev, last):
    w, own, d = n.shape
    ff = wg.shape[1]
    one = lambda a: pl.BlockSpec(
        a.shape, lambda i, a=a: (0,) * a.ndim, pipeline_mode=pl.Buffered(1)
    )
    blk = pl.BlockSpec((1, own, d), lambda i: (i, 0, 0))
    dt = BF16 if last else F32
    args = [n, c, wg, wu, wd] + list(prev or [])
    shapes = [(d, ff), (d, ff), (ff, d)]
    return pl.pallas_call(
        functools.partial(ffn_kernel, bool(prev), last),
        grid=(w,),
        in_specs=[blk, blk] + [one(a) for a in args[2:]],
        out_specs=[blk, blk] + [
            pl.BlockSpec(s, lambda i: (0, 0), pipeline_mode=pl.Buffered(1)) for s in shapes
        ],
        out_shape=[jax.ShapeDtypeStruct(n.shape, BF16)] * 2
        + [jax.ShapeDtypeStruct(s, dt) for s in shapes],
        scratch_shapes=[pltpu.VMEM(s, F32) for s in shapes] if last else [],
        compiler_params=params(),
        cost_estimate=cost(18 * w * own * d * ff, 20 * w * own * d),
        name="ffn",
    )(*args)


def back_kernel(
    nblk, s_ref, q_ref, k_ref, v_ref, lse_ref, dq_ref, dk_ref, qf_ref, kvw_ref,
    dn_ref, hm_ref, c_ref, wo_ref, g_ref,
    dm_ref, dl_ref, gain_ref, gq_ref, gkv_ref,
    bq_ref, bk_ref, bv_ref, cap_ref, da_ref, aq_ref, ak_ref, av_ref, tq_ref, tk_ref, tv_ref,
):
    pair = pl.program_id(0)
    own = q_ref.shape[0]
    last = pl.num_programs(0) - 1

    @pl.when(pair == 0)
    def _():
        hm = hm_ref[...]
        dn = dn_ref[...].astype(F32)
        r = lax.rsqrt(jnp.mean(hm * hm, axis=-1, keepdims=True) + EPS)
        z = dn * g_ref[...]
        gain_ref[...] = jnp.sum(dn * hm * r, axis=0, keepdims=True)
        dm = (
            c_ref[...].astype(F32)
            + r * z
            - hm * (r * r * r) * jnp.mean(z * hm, axis=-1, keepdims=True)
        )
        dm_ref[...] = dm
        low = dm.astype(BF16)
        dl_ref[...] = low
        da = mm(low, wo_ref[...], NT).astype(BF16)
        for i in range(PAIRS):
            da_ref[i] = da[:, i * 128:(i + 1) * 128]
        bq_ref[...] = mm(qf_ref[...], rank_tile(QA, (QPAD, RQ * 128)))
        tile_keys(kvw_ref, bk_ref, bv_ref)
        make_cap(s_ref, dq_ref, dk_ref, cap_ref, nblk, own)
        for ref in (aq_ref, ak_ref, av_ref, tq_ref, tk_ref, tv_ref):
            ref[...] = jnp.zeros_like(ref)

    q = q_ref[...]
    k = k_ref[...]
    v = v_ref[...]
    qs = stacked(q)
    ds_ = stacked(da_ref[pair])
    cap = cap_ref[...]
    st = jnp.minimum(mm(k, qs, NT), jnp.concatenate([cap, cap], axis=1))
    p = jnp.exp(st - lse_ref[0])
    dp = mm(v, ds_, NT)
    delta = jnp.sum(p * dp, axis=0, keepdims=True)
    ds = (p * (dp - delta)).astype(BF16)
    dv = mm(p.astype(BF16), ds_)
    dk = mm(ds, qs)
    dq = unstacked(mm(k, ds, TN), own) * (DH ** (-0.5))

    eq = head_spread(pair, 0, RQ, (128, RQ * 128))
    qe = mm(qf_ref[:, :128], eq)
    dq6 = jnp.concatenate([dq] * RQ, axis=1)
    tq_ref[...] += dq6 * qe
    aq_ref[...] += mm((dq6 * bq_ref[...]).astype(BF16), eq, NT)
    ek = head_spread(pair, 0, RK, (128, RK * 128))
    ev = head_spread(pair, KCOLS - 128, RK, (128, RK * 128))
    ke = mm(kvw_ref[:, :128], ek)
    ve = mm(kvw_ref[:, 128:256], ev)
    dk2 = jnp.concatenate([dk] * RK, axis=1)
    dv2 = jnp.concatenate([dv] * RK, axis=1)
    tk_ref[...] += dk2 * ke
    tv_ref[...] += dv2 * ve
    ak_ref[...] += mm((dk2 * bk_ref[...]).astype(BF16), ek, NT)
    av_ref[...] += mm((dv2 * bv_ref[...]).astype(BF16), ev, NT)

    @pl.when(pair == last)
    def _():
        def fold(x, t):
            hi = x.astype(BF16)
            lo = (x - hi.astype(F32)).astype(BF16)
            return mm(hi, t, NT) + mm(lo, t, NT)

        gq = fold(tq_ref[...], rank_tile(QA, (QPAD, RQ * 128)))
        gq_ref[:, :128] = ((gq[:, :128] + aq_ref[...]) * (1.0 / RQ)).astype(BF16)
        gq_ref[:, 128:] = (gq[:, 128:] * (1.0 / RQ)).astype(BF16)
        gk = fold(tk_ref[...], rank_tile(KA, (KPAD, RK * 128)))
        gv = fold(tv_ref[...], rank_tile(KCOLS + KA, (KPAD, RK * 128)))
        gkv = gk + gv
        first = ((gkv[:, :128] + ak_ref[...]) * (1.0 / RK)).astype(BF16)
        second = ((gkv[:, 128:256] + av_ref[...]) * (1.0 / RK)).astype(BF16)
        third = (gkv[:, 256:] * (1.0 / RK)).astype(BF16)
        gkv_ref[...] = jnp.zeros_like(gkv_ref)
        for i in range(nblk):
            rows = slice(i * own, (i + 1) * own)
            slot = s_ref[1 + nblk + i]
            gkv_ref[slot, :, :128] = first[rows]
            gkv_ref[slot, :, 128:256] = second[rows]
            gkv_ref[slot, :, 256:] = third[rows]


def back(nblk, width, scalars, q, k, v, lse, dq, dk, qf, kvw, dn, hm, c, wo, gain):
    own, d = q.shape
    win = nblk * own
    whole = lambda a: pl.BlockSpec(a.shape, lambda p, a=a: (0,) * a.ndim)
    col = lambda rows: pl.BlockSpec((rows, 128), lambda p: (0, p))
    fixed = lambda *s: pl.BlockSpec(s, lambda p: (0,) * len(s))
    return pl.pallas_call(
        functools.partial(back_kernel, nblk),
        grid=(PAIRS,),
        in_specs=[
            pl.BlockSpec(memory_space=pltpu.SMEM), col(own), col(win), col(win),
            pl.BlockSpec((1, 1, 2 * own), lambda p: (p, 0, 0)),
        ] + [whole(a) for a in (dq, dk, qf, kvw, dn, hm, c, wo, gain)],
        out_specs=[
            fixed(own, d), fixed(own, d), fixed(1, d), fixed(own, QPAD),
            fixed(width, own, KPAD),
        ],
        out_shape=[
            jax.ShapeDtypeStruct((own, d), F32),
            jax.ShapeDtypeStruct((own, d), BF16),
            jax.ShapeDtypeStruct((1, d), F32),
            jax.ShapeDtypeStruct((own, QPAD), BF16),
            jax.ShapeDtypeStruct((width, own, KPAD), BF16),
        ],
        scratch_shapes=[
            pltpu.VMEM((own, RQ * 128), F32),
            pltpu.VMEM((win, RK * 128), F32),
            pltpu.VMEM((win, RK * 128), F32),
            pltpu.VMEM((win, own), F32),
            pltpu.VMEM((PAIRS, own, 128), BF16),
            pltpu.VMEM((own, 128), F32),
            pltpu.VMEM((win, 128), F32),
            pltpu.VMEM((win, 128), F32),
            pltpu.VMEM((own, RQ * 128), F32),
            pltpu.VMEM((win, RK * 128), F32),
            pltpu.VMEM((win, RK * 128), F32),
        ],
        compiler_params=params(),
        cost_estimate=cost(30e9, 15e6),
        name="back",
    )(scalars, q, k, v, lse, dq, dk, qf, kvw, dn, hm, c, wo, gain)


def flip(index, bit):
    digit = (index // bit) % 2
    return index + bit - 2 * bit * digit


AXES = {"c": ("wide", 1), "x": ("wide", 2), "y": ("rows", 1), "n": ("rows", 2), "f": ("rows", 4)}


def enter(names):
    barrier = pltpu.get_barrier_semaphore()
    for name in names:
        pl.semaphore_signal(
            barrier, inc=1, device_id=partner(name), device_id_type=pl.DeviceIdType.MESH
        )
    pl.semaphore_wait(barrier, len(names))


def partner(name):
    axis, bit = AXES[name]
    return {axis: flip(lax.axis_index(axis), bit)}


def digit(name):
    axis, bit = AXES[name]
    return (lax.axis_index(axis) // bit) % 2


def wide_digits(index):
    return index // 2, index % 2


def slot_for(me, block):
    mx, mc = wide_digits(me)
    bx, bc = wide_digits(block)
    return 2 * ((mc + bc) % 2) + (mx + bx) % 2


def send_to(name, src, dst, send, recv):
    return pltpu.make_async_remote_copy(
        src_ref=src, dst_ref=dst, send_sem=send, recv_sem=recv,
        device_id=partner(name), device_id_type=pl.DeviceIdType.MESH,
    )


class Gather:
    def __init__(self, ref, send, recv, rows=None):
        at = [ref.at[i] if rows is None else ref.at[i, rows] for i in range(4)]
        self.x = send_to("x", at[0], at[1], send.at[0], recv.at[0])
        self.c = send_to("c", at[0], at[2], send.at[1], recv.at[1])
        self.r = send_to("c", at[1], at[3], send.at[2], recv.at[2])

    def first(self):
        self.x.start()
        self.c.start()

    def relay(self):
        self.x.wait()
        self.r.start()

    def done(self):
        self.c.wait()
        self.r.wait()


class Scatter:
    def __init__(self, part, got, last, send, recv):
        self.part, self.got, self.last = part, got, last
        self.c = send_to("c", part.at[pl.ds(2, 2)], got, send.at[0], recv.at[0])
        if last is not None:
            self.x = send_to("x", part.at[1], last, send.at[1], recv.at[1])

    def core(self):
        self.c.start()

    def kept(self, i):
        return self.part[i].astype(F32) + self.got[i].astype(F32)

    def cross(self):
        self.c.wait()
        self.part[1] = self.kept(1).astype(BF16)
        self.x.start()
        self.part[0] = self.kept(0).astype(BF16)

    def total(self):
        self.x.wait()
        return self.part[0].astype(F32) + self.last[...].astype(F32)


class Sum:
    def __init__(self, names, unit, src, base, acc, got, res, rbase, send, recv,
                 local=None, top=None, flat=False):
        self.names, self.unit, self.n = names, unit, len(names)
        self.src, self.base, self.acc, self.got = src, base, acc, got
        self.res, self.rbase, self.send, self.recv = res, rbase, send, recv
        self.local, self.flat = local, flat
        self.top = unit * 2 ** (self.n - 1) if top is None else top

    def low(self, i, skip=0):
        total = 0
        for j in range(skip, i):
            total = total + digit(self.names[j]) * 2 ** (self.n - 1 - j)
        return total

    def span(self, ref, base, chunk, count):
        return ref.at[pl.ds(base + chunk * self.unit, count * self.unit)]

    def keep(self):
        half = 2 ** (self.n - 1)
        return pltpu.make_async_copy(
            self.span(self.src, self.base, self.low(1), half), self.acc, self.local
        )

    def halve(self, i):
        half = 2 ** (self.n - 1 - i)
        away = (1 - digit(self.names[i])) * half
        if i == 0:
            src = self.span(self.src, self.base, away, half)
        else:
            src = self.span(self.acc, 0, self.low(i, 1) + away, half)
        dst = self.span(self.got, 0, 2 ** self.n - 2 * half, half)
        return send_to(self.names[i], src, dst, self.send.at[i], self.recv.at[i])

    def begin(self):
        self.halve(0).start()
        if self.local is not None:
            self.keep().start()

    def place(self, i):
        if self.flat:
            return self.rbase
        return self.rbase + digit(self.names[0]) * self.top + self.low(i, 1) * self.unit

    def double(self, i):
        half = 2 ** (self.n - 1 - i)
        held = self.res.at[pl.ds(self.place(i + 1), half * self.unit)]
        k = self.n + i
        return send_to(self.names[i], held, held, self.send.at[k], self.recv.at[k])

    def resume(self, own, at):
        place = self.place(self.n)
        for j in range(self.unit):
            self.res[place + j] = own[at + j]
        self.double(self.n - 1).start()

    def add(self, i):
        half = 2 ** (self.n - 1 - i)
        offset = (2 ** self.n - 2 * half) * self.unit
        self.halve(i).wait()
        kept = self.low(i + 1, 1) * self.unit
        first = i == 0 and self.local is None
        if i == 0 and self.local is not None:
            self.keep().wait()
        own = self.base + self.low(1) * self.unit
        last = i == self.n - 1
        place = self.place(self.n)

        count = self.unit if self.unit > 1 else min(half, 4)

        def some(i, carry):
            j = i * count
            mine = self.src[pl.ds(own + j, count)] if first else self.acc[pl.ds(kept + j, count)]
            value = (mine.astype(F32) + self.got[pl.ds(offset + j, count)].astype(F32)).astype(BF16)
            if last:
                self.res[pl.ds(place + j, count)] = value
            else:
                self.acc[pl.ds(kept + j, count)] = value
            return carry

        lax.fori_loop(0, half * self.unit // count, some, 0)

    def step(self, k):
        n = self.n
        if k < n:
            self.add(k)
            if k < n - 1:
                self.halve(k + 1).start()
            elif not self.flat:
                self.double(n - 1).start()
        else:
            i = 2 * n - 1 - k
            self.double(i).wait()
            if i > 0:
                self.double(i - 1).start()


def fill_cap(me, first, dq, dk, cap_ref, nblk, own):
    for i in range(nblk):
        rows = pl.ds(i * own, own)
        key = lax.broadcasted_iota(jnp.int32, (own, own), 0)
        query = lax.broadcasted_iota(jnp.int32, (own, own), 1) + (me - first - i) * own
        ok = (dk[i * own:(i + 1) * own, :] == dq) & (key <= query)
        cap_ref[rows, :] = jnp.where(ok, BIG, NEG)


def fore_kernel(
    nblk, x_ref, wt_ref, wo_ref, g1_ref, g2_ref, dq_ref, dk_ref, c_ref,
    n1_ref, qf_ref, kvw_ref, att_ref, q_ref, k_ref, v_ref, lse_ref, hm_ref, ng_ref, cg_ref,
    kvg_ref, bq_ref, bk_ref, bv_ref, cap_ref, full_ref, send, recv,
):
    seqs, own, d = x_ref.shape
    me = lax.axis_index("wide")
    first = me // 3
    kvs = [Gather(kvg_ref.at[s], send.at[s], recv.at[s]) for s in range(seqs)]
    cots = [Gather(cg_ref.at[s], send.at[2 + s], recv.at[2 + s]) for s in range(seqs)]
    norms = [Gather(ng_ref.at[0], send.at[4], recv.at[4])]
    norms += [
        Gather(ng_ref.at[1], send.at[5 + i], recv.at[5 + i], pl.ds(i * (own // 4), own // 4))
        for i in range(4)
    ]
    for s in range(seqs):
        cg_ref[s, 0] = c_ref[s]
    for s in range(seqs):
        x = x_ref[s].astype(F32)
        r = lax.rsqrt(jnp.mean(x * x, axis=-1, keepdims=True) + EPS)
        n = (x * r * g1_ref[...]).astype(BF16)
        n1_ref[s] = n
        f = mm(n, wt_ref[...], NT).astype(BF16)
        qf_ref[s] = f[:, :QPAD]
        kvg_ref[s, 0, :, :KV] = f[:, QCOLS:]
        kvg_ref[s, 0, :, KV:] = jnp.zeros((own, KPAD - KV), BF16)
        if s == 0:
            enter("cx")
        kvs[s].first()
    kvs[0].relay()
    for s in range(seqs):
        cots[s].first()
    kvs[0].done()

    def step(t, carry):
        s = t // PAIRS
        pair = t % PAIRS

        @pl.when(t == PAIRS)
        def _():
            kvs[1].done()

        @pl.when(pair == 0)
        def _():
            for i in range(nblk):
                kvw_ref[s, pl.ds(i * own, own), :] = kvg_ref[s, slot_for(me, first + i)]
            bq_ref[...] = mm(qf_ref[s], rank_tile(QA, (QPAD, RQ * 128)))
            bk_ref[...] = mm(kvw_ref[s, :, :256], rank_tile(KA, (256, RK * 128)))
            bv_ref[...] = mm(kvw_ref[s, :, 128:384], rank_tile(KCOLS + KA - 128, (256, RK * 128)))
            fill_cap(me, first, dq_ref[s], dk_ref[s], cap_ref, nblk, own)

        qe = mm(qf_ref[s, :, :128], head_spread(pair, 0, RQ, (128, RQ * 128)))
        qsum = qe[:, :128] * bq_ref[:, :128]
        for r in range(1, RQ):
            cols = slice(r * 128, (r + 1) * 128)
            qsum = qsum + qe[:, cols] * bq_ref[:, cols]
        q = (qsum * (1.0 / RQ)).astype(BF16)
        ke = mm(kvw_ref[s, :, :128], head_spread(pair, 0, RK, (128, RK * 128)))
        ve = mm(kvw_ref[s, :, 128:256], head_spread(pair, KCOLS - 128, RK, (128, RK * 128)))
        k = ((ke[:, :128] * bk_ref[:, :128] + ke[:, 128:] * bk_ref[:, 128:]) * (1.0 / RK)).astype(BF16)
        v = ((ve[:, :128] * bv_ref[:, :128] + ve[:, 128:] * bv_ref[:, 128:]) * (1.0 / RK)).astype(BF16)
        q = q * jnp.asarray(DH ** (-0.5), BF16)
        q_ref[s, pair] = q
        k_ref[s, pair] = k
        v_ref[s, pair] = v
        cap = cap_ref[...]
        st = jnp.minimum(mm(k, stacked(q), NT), jnp.concatenate([cap, cap], axis=1))
        top = jnp.max(st, axis=0, keepdims=True)
        e = jnp.exp(st - top)
        total = jnp.sum(e, axis=0, keepdims=True)
        p = (e * (1.0 / total)).astype(BF16)
        lse_ref[s, pair] = top + jnp.log(total)
        full_ref[pair] = unstacked(mm(v, p, TN), own).astype(BF16)

        @pl.when(pair == PAIRS - 1)
        def _():
            att = jnp.concatenate([full_ref[i] for i in range(PAIRS)], axis=1)
            att_ref[s] = att
            hm = x_ref[s].astype(F32) + mm(att, wo_ref[...])
            hm_ref[s] = hm
            r = lax.rsqrt(jnp.mean(hm * hm, axis=-1, keepdims=True) + EPS)
            ng_ref[s, 0] = (hm * r * g2_ref[...]).astype(BF16)

        @pl.when(t == 2)
        def _():
            kvs[1].relay()

        @pl.when(t == 6)
        def _():
            cots[0].relay()

        @pl.when(t == PAIRS - 1)
        def _():
            norms[0].first()

        @pl.when(t == 13)
        def _():
            cots[1].relay()

        return carry

    lax.fori_loop(0, seqs * PAIRS, step, 0)
    for norm in norms[1:]:
        norm.first()
    for norm in norms:
        norm.relay()
    for each in cots + norms:
        each.done()


def vmem():
    return pl.BlockSpec(memory_space=pltpu.VMEM)


def hbm():
    return pl.BlockSpec(memory_space=pl.ANY)


def fused(ident, limit=63):
    return pltpu.CompilerParams(
        vmem_limit_bytes=limit << 20, collective_id=ident, has_side_effects=True
    )


def fore(nblk, x, wt, wo, g1, g2, dq, dk, c):
    seqs, own, d = x.shape
    win = nblk * own
    shape = jax.ShapeDtypeStruct
    return pl.pallas_call(
        functools.partial(fore_kernel, nblk),
        in_specs=[vmem()] * 8,
        out_specs=[vmem()] * 11,
        out_shape=[
            shape((seqs, own, d), BF16), shape((seqs, own, QPAD), BF16),
            shape((seqs, win, KPAD), BF16), shape((seqs, own, d), BF16),
            shape((seqs, PAIRS, own, 128), BF16), shape((seqs, PAIRS, win, 128), BF16),
            shape((seqs, PAIRS, win, 128), BF16), shape((seqs, PAIRS, 1, 2 * own), F32),
            shape((seqs, own, d), F32), shape((seqs, 4, own, d), BF16),
            shape((seqs, 4, own, d), BF16),
        ],
        scratch_shapes=[
            pltpu.VMEM((seqs, 4, own, KPAD), BF16),
            pltpu.VMEM((own, RQ * 128), F32),
            pltpu.VMEM((win, RK * 128), F32),
            pltpu.VMEM((win, RK * 128), F32),
            pltpu.VMEM((win, own), F32),
            pltpu.VMEM((PAIRS, own, 128), BF16),
            pltpu.SemaphoreType.DMA((9, 3)),
            pltpu.SemaphoreType.DMA((9, 3)),
        ],
        compiler_params=fused(0),
        cost_estimate=cost(30e9, 30e6),
        name="fore",
    )(x, wt, wo, g1, g2, dq, dk, c)


SPLITS = ((0, 192), (192, 256), (448, 256))
EARLY = len(SPLITS) - 1
LANES = 512
FFN_NAMES = (("ynf", "ynf", "nyf"), ("ynf", "nyf", "ynf"), ("ynf", "nyf", "ynf"))


def chunk_units(h):
    return SPLITS[h][1] // 16 * (1024 // LANES) // 8


def own_at(h, m):
    return 3 * sum(chunk_units(i) for i in range(h)) + m * chunk_units(h)


MIDDLE_EVENTS = {
    (1, 5): ((0, 0, 0),),
    (1, "m0"): ((0, 2, 0),),
    (1, "m1"): ((0, 1, 0), (0, 0, 1),),
    (2, 1): ((0, 0, 2), (1, 0, 0),),
    (2, 2): ((1, 1, 0), (0, 2, 1),),
    (2, 3): ((0, 1, 1),),
    (2, 5): ((0, 2, 2), (1, 0, 1), (1, 2, 0),),
    (2, 6): ((0, 1, 2),),
    (2, 7): ((1, 1, 1),),
    (2, "m0"): ((1, 0, 2), (1, 2, 1),),
    (2, "m2"): ((1, 1, 2),),
    "end": ((1, 2, 2),),
}


def middle_kernel(
    n_ref, c_ref, wg_ref, wu_ref, wd_ref,
    dn_ref, ds_ref, ok_ref, os_ref, gw_ref, own_ref,
    hid_ref, dg_ref, du_ref, oa_ref, da_ref, op_ref, dp_ref, xs_ref, oc_ref, dc_ref, dx_ref, *refs,
):
    seqs, size, own, d = n_ref.shape
    srcs, refs = refs[:EARLY], refs[EARLY:]
    accs, refs = refs[:3 * EARLY], refs[3 * EARLY:]
    gots, refs = refs[:3 * EARLY], refs[3 * EARLY:]
    send, recv, xsend, xrecv = refs
    downs = [
        send_to("c", dp_ref.at[s], dc_ref.at[s], xsend.at[0, s], xrecv.at[0, s]) for s in range(seqs)
    ]
    ups = [
        send_to("c", op_ref.at[s], oc_ref.at[s], xsend.at[1, s], xrecv.at[1, s]) for s in range(seqs)
    ]
    cross = send_to("x", xs_ref, dx_ref, xsend.at[2, 0], xrecv.at[2, 0])
    parts = {}
    for h in range(EARLY):
        for m in range(3):
            i = 3 * h + m
            u = chunk_units(h)
            parts[h, m] = Sum(
                FFN_NAMES[h][m], u, srcs[h], 8 * u * m, accs[i], gots[i], own_ref, own_at(h, m),
                send.at[i], recv.at[i], flat=True,
            )
    enter("cxynf")

    def run(point):
        for h, m, k in MIDDLE_EVENTS.get(point, ()):
            parts[h, m].step(k)

    for h, (off, rows) in enumerate(SPLITS):
        last = h == EARLY

        def step(t, carry, h=h, off=off, rows=rows, last=last):
            s = t // size
            b = size - 1 - t % size
            n = n_ref[s, b]
            c = c_ref[s, b]
            span = slice(off, off + rows)
            g = mm(wg_ref[span, :], n, NT)
            u = mm(wu_ref[span, :], n, NT)
            dh = mm(wd_ref[span, :], c, NT)
            sg = 1.0 / (1.0 + jnp.exp(-g))
            gs = g * sg
            cols = pl.ds(pl.multiple_of((s * size + b) * own, 128), own)
            hid_ref[span, cols] = (gs * u).astype(BF16)
            dg_ref[span, cols] = (dh * u * (sg * (1.0 + g * (1.0 - sg)))).astype(BF16)
            du_ref[span, cols] = (dh * gs).astype(BF16)
            if last:
                o = mm(hid_ref[:, cols], wd_ref[...], TN)
                dn = mm(dg_ref[:, cols], wg_ref[...], TN) + mm(du_ref[:, cols], wu_ref[...], TN)

                @pl.when(b >= 2)
                def _():
                    op_ref[s, b - 2] = o.astype(BF16)
                    dp_ref[s, b - 2] = dn.astype(BF16)

                @pl.when(b < 2)
                def _():
                    oa_ref[s, b] = o.astype(BF16)
                    da_ref[s, b] = dn

                for i in range(seqs):

                    @pl.when(t == i * size + 1)
                    def _(i=i):
                        downs[i].start()
                        ups[i].start()

                @pl.when(t == size - 1)
                def _():
                    downs[0].wait()
                    xs_ref[...] = (da_ref[0, 1] + dc_ref[0, 1].astype(F32)).astype(BF16)
                    cross.start()

            for j in range(seqs * size):
                if (h, j) in MIDDLE_EVENTS:

                    @pl.when(t == j)
                    def _(j=j):
                        run((h, j))

            return carry

        lax.fori_loop(0, seqs * size, step, 0)
        count = rows // 16
        for m, (a_ref, b_ref) in enumerate(((dg_ref, n_ref), (du_ref, n_ref), (hid_ref, c_ref))):
            w = mm(a_ref[off:off + rows, :], b_ref[...].reshape(seqs * size * own, d)).astype(BF16)
            to = gw_ref if last else srcs[h]
            for i in range(d // LANES):
                at = (m * (d // LANES) + i) * count
                piece = w[:, i * LANES:(i + 1) * LANES]
                to[pl.ds(at, count)] = piece.reshape(count, 16, LANES)
            if not last:
                parts[h, m].begin()
            run((h, "m%d" % m))
    for s in range(seqs):
        ups[s].wait()
        ok_ref[s] = (oa_ref[s, 0].astype(F32) + oc_ref[s, 0].astype(F32)).astype(BF16)
        os_ref[s] = (oa_ref[s, 1].astype(F32) + oc_ref[s, 1].astype(F32)).astype(BF16)
    downs[1].wait()
    dn_ref[1] = da_ref[1, 0] + dc_ref[1, 0].astype(F32)
    ds_ref[...] = (da_ref[1, 1] + dc_ref[1, 1].astype(F32)).astype(BF16)
    run("end")
    cross.wait()
    dn_ref[0] = da_ref[0, 0] + dc_ref[0, 0].astype(F32) + dx_ref[...].astype(F32)


def middle(n, c, wg, wu, wd):
    seqs, size, own, d = n.shape
    shape = jax.ShapeDtypeStruct
    flat = (wd.shape[0], seqs * size * own)
    u = [chunk_units(h) for h in range(EARLY) for _ in range(3)]
    unit = lambda k: pltpu.VMEM((k, 16, LANES), BF16)
    return pl.pallas_call(
        middle_kernel,
        in_specs=[vmem()] * 5,
        out_specs=[vmem()] * 6,
        out_shape=[
            shape((seqs, own, d), F32), shape((own, d), BF16), shape((seqs, own, d), BF16),
            shape((seqs, own, d), BF16), shape((24 * chunk_units(EARLY), 16, LANES), BF16),
            shape((own_at(EARLY, 0), 16, LANES), BF16),
        ],
        scratch_shapes=[pltpu.VMEM(flat, BF16)] * 3
        + [pltpu.VMEM((seqs, 2, own, d), BF16), pltpu.VMEM((seqs, 2, own, d), F32)]
        + [pltpu.VMEM((seqs, 2, own, d), BF16)] * 2
        + [pltpu.VMEM((own, d), BF16)]
        + [pltpu.VMEM((seqs, 2, own, d), BF16)] * 2
        + [pltpu.VMEM((own, d), BF16)]
        + [unit(24 * chunk_units(h)) for h in range(EARLY)]
        + [unit(4 * k) for k in u]
        + [unit(7 * k) for k in u]
        + [
            pltpu.SemaphoreType.DMA((3 * EARLY, 3)),
            pltpu.SemaphoreType.DMA((3 * EARLY, 3)),
            pltpu.SemaphoreType.DMA((3, seqs)),
            pltpu.SemaphoreType.DMA((3, seqs)),
        ],
        compiler_params=fused(1),
        cost_estimate=cost(27e9, 30e6),
        name="middle",
    )(n, c, wg, wu, wd)


FFN_UNITS = 3 * sum(r for _, r in SPLITS) // 16
SECOND = 3
AFTER_EVENTS = {
    0: (("F00", 3), ("F01", 3), ("F20", 0),),
    1: (("F02", 3),),
    2: (("F10", 3), ("F22", 0), ("F11", 3), ("F02", 4), ("F12", 3),),
    4: (("F21", 0), ("O0", 0), ("F11", 4), ("F00", 4), ("O1", 0),),
    5: (("cross", 0), ("F01", 4),),
    6: (("F20", 1), ("F21", 1),),
    7: (("F10", 4), ("O1", 1), ("F22", 1), ("O0", 1),),
    8: (("F20", 2), ("F02", 5), ("F00", 5), ("F21", 2),),
    9: (("cross", 1), ("key", 0), ("F12", 4), ("F22", 2),),
    10: (("F01", 5), ("F20", 3), ("emit", 0),),
    11: (("O0", 2), ("F11", 5), ("F21", 3), ("F10", 5),),
    12: (("F22", 3),),
    13: (("O1", 2), ("F12", 5),),
    14: (("F21", 4),),
    15: (("O1", 3), ("F20", 4), ("emit", 1),),
    "T0": (("O0", 3),),
    "T1": (("F22", 4), ("O1", 4), ("K0", 0), ("K1", 0), ("O0", 4), ("F20", 5), ("O1", 5), ("F21", 5),),
    "T2": (("O0", 5), ("K0", 1), ("K2", 0), ("F22", 5), ("K3", 0), ("K1", 1), ("O1", 6),),
    "T3": (("K4", 0), ("O0", 6), ("K0", 2), ("K2", 1), ("K3", 1), ("O1", 7), ("K1", 2), ("K2", 2), ("K4", 1), ("O0", 7), ("K0", 3), ("K3", 2), ("K2", 3), ("K1", 3), ("K4", 2), ("K0", 4), ("K3", 3), ("K2", 4), ("O1", 8), ("K1", 4), ("K4", 3), ("K3", 4), ("O0", 8), ("K0", 5), ("K1", 5), ("K4", 4), ("K2", 5), ("O1", 9), ("K3", 5), ("K0", 6), ("K4", 5), ("K2", 6), ("O0", 9), ("K1", 6), ("K4", 6), ("K3", 6), ("K0", 7), ("K2", 7), ("K1", 7), ("K3", 7), ("K4", 7), ("K0", 8), ("K3", 8), ("K2", 8), ("K1", 8), ("K0", 9), ("K3", 9), ("K4", 8), ("K2", 9), ("K1", 9), ("K4", 9),),
}
OUT_PARTS = ("cyxnf", "cxnyf")
Q_PARTS = ("cxynf", "cnyfx")
K_PARTS = ("cxynf", "cynfx", "cnfxy")
K_LANES = 256
GAIN_ROW = 352


def attention_parts():
    return [(n, 1024) for n in OUT_PARTS] + [(n, 512) for n in Q_PARTS] + [(n, K_LANES) for n in K_PARTS]


def after_kernel(
    nblk, gw_ref, own_ref, dn_ref, ds_ref, ok_ref, os_ref, q_ref, k_ref, v_ref, lse_ref, dq_ref, dk_ref,
    qf_ref, kvw_ref, hm_ref, c_ref, wo_ref, g1_ref, g2_ref, att_ref, n1_ref, x_ref, wt_ref,
    out_ref, ig_ref, gr_ref, *refs,
):
    n_out, n_q = len(OUT_PARTS), len(Q_PARTS)
    n_fac = n_q + len(K_PARTS)
    or_refs, refs = refs[:n_out], refs[n_out:]
    fr_refs, refs = refs[:n_fac], refs[n_fac:]
    (bq_ref, bk_ref, bv_ref, cap_ref, da_ref, aq_ref, ak_ref, av_ref, tq_ref, tk_ref, tv_ref,
     dm_ref, late_ref, gq_ref, gkp_ref, gkc_ref, gkx_ref, ox_ref, kb_ref, vb_ref, dx_ref, gain_ref) = refs[:22]
    refs = refs[22:]
    gots, refs = refs[:3], refs[3:]
    accs, refs = refs[:3], refs[3:]
    ob, refs = refs[:n_out], refs[n_out:]
    og, refs = refs[:n_out], refs[n_out:]
    oa, refs = refs[:n_out], refs[n_out:]
    fb, refs = refs[:n_fac], refs[n_fac:]
    fg, refs = refs[:n_fac], refs[n_fac:]
    fa, refs = refs[:n_fac], refs[n_fac:]
    send, recv, loc, gs, gr, kvsem, wsem = refs
    seqs, own, d = hm_ref.shape
    me = lax.axis_index("wide")
    first = me // 3

    sums = {}
    half = gr_ref.shape[0] // 2
    for h, (off, rows) in enumerate(SPLITS):
        for m in range(3):
            i = 3 * h + m
            u = chunk_units(h)
            late = h == EARLY
            sums[h, m] = Sum(
                FFN_NAMES[h][m], u, gw_ref if late else None, 8 * u * m,
                accs[m] if late else None, gots[m] if late else None,
                gr_ref, m * (half // 3) + off // 16, send.at[i], recv.at[i],
                local=loc.at[m] if late else None, top=half,
            )
    k0 = len(sums)
    outs = [
        Sum(names, 1, ob[g], 0, oa[g], og[g], or_refs[g], 0, send.at[k0 + g], recv.at[k0 + g])
        for g, names in enumerate(OUT_PARTS)
    ]
    k1 = k0 + n_out
    facs = [
        Sum(names, 1, fb[g], 0, fa[g], fg[g], fr_refs[g], 0, send.at[k1 + g], recv.at[k1 + g])
        for g, names in enumerate(Q_PARTS + K_PARTS)
    ]
    keys = [
        Scatter(gkp_ref.at[s], gkc_ref.at[s], gkx_ref.at[s], gs.at[s], gr.at[s])
        for s in range(seqs)
    ]
    crosses = [
        send_to("x", os_ref.at[s], ox_ref.at[s], gs.at[2 + s, 0], gr.at[2 + s, 0])
        for s in range(seqs)
    ]

    def fetch(t):
        return [
            pltpu.make_async_copy(a.at[t // PAIRS, t % PAIRS], b.at[t % 2], kvsem.at[i, t % 2])
            for i, (a, b) in enumerate(((k_ref, kb_ref), (v_ref, vb_ref)))
        ]

    for copy in fetch(0):
        copy.start()
    loads = [
        pltpu.make_async_copy(dn_ref, dm_ref, wsem.at[0]),
        pltpu.make_async_copy(c_ref, late_ref, wsem.at[1]),
    ]
    for copy in loads:
        copy.start()
    enter("cxynf")
    for h, m in sums:
        if h == EARLY:
            sums[h, m].begin()
        else:
            sums[h, m].resume(own_ref, own_at(h, m))

    for copy in loads:
        copy.wait()
    down = send_to("x", ds_ref, dx_ref, gs.at[4, 0], gr.at[4, 0])
    down.start()
    gain_ref[...] = jnp.zeros((1, d), F32)

    def mids(s):
        hm = hm_ref[s]
        dn = dm_ref[s]
        r = lax.rsqrt(jnp.mean(hm * hm, axis=-1, keepdims=True) + EPS)
        z = dn * g2_ref[...]
        gain_ref[...] += jnp.sum(dn * hm * r, axis=0, keepdims=True)
        dm = (
            late_ref[s].astype(F32)
            + r * z
            - hm * (r * r * r) * jnp.mean(z * hm, axis=-1, keepdims=True)
        )
        dm_ref[s] = dm
        low = dm.astype(BF16)
        late_ref[s] = low
        da = mm(low, wo_ref[...], NT).astype(BF16)
        for i in range(PAIRS):
            da_ref[s, i] = da[:, i * 128:(i + 1) * 128]

    load_x = pltpu.make_async_copy(x_ref, late_ref, wsem.at[2])

    def second():
        for g in range(n_out):

            def rows(j, carry, g=g):
                cols = pl.ds(pl.multiple_of(g * 512 + j * 256, 128), 256)
                a = att_ref[:, :, cols].reshape(seqs * own, 256)
                w = mm(a, late_ref[...].reshape(seqs * own, d), TN).astype(BF16)
                ob[g][pl.ds(j * 16, 16)] = w.reshape(16, 16, d)
                return carry

            lax.fori_loop(0, 2, rows, 0)
            outs[g].begin()
        load_x.start()

    def finish(s):
        def fold(x, t):
            hi = x.astype(BF16)
            lo = (x - hi.astype(F32)).astype(BF16)
            return mm(hi, t, NT) + mm(lo, t, NT)

        gq = fold(tq_ref[...], rank_tile(QA, (QPAD, RQ * 128)))
        gq_ref[s, :, :128] = ((gq[:, :128] + aq_ref[...]) * (1.0 / RQ)).astype(BF16)
        gq_ref[s, :, 128:] = (gq[:, 128:] * (1.0 / RQ)).astype(BF16)
        gk = fold(tk_ref[...], rank_tile(KA, (KPAD, RK * 128)))
        gv = fold(tv_ref[...], rank_tile(KCOLS + KA, (KPAD, RK * 128)))
        gkv = gk + gv
        one = ((gkv[:, :128] + ak_ref[...]) * (1.0 / RK)).astype(BF16)
        two = ((gkv[:, 128:256] + av_ref[...]) * (1.0 / RK)).astype(BF16)
        three = (gkv[:, 256:] * (1.0 / RK)).astype(BF16)
        gkp_ref[s] = jnp.zeros_like(gkp_ref[s])
        for i in range(nblk):
            rows = slice(i * own, (i + 1) * own)
            slot = slot_for(me, first + i)
            gkp_ref[s, slot, :, :128] = one[rows]
            gkp_ref[s, slot, :, 128:256] = two[rows]
            gkp_ref[s, slot, :, 256:] = three[rows]

    def emit(s):
        crosses[s].wait()
        total = hm_ref[s] + (ok_ref[s].astype(F32) + ox_ref[s].astype(F32))
        out_ref[s] = total.astype(BF16)

    named = {"F%d%d" % key: part for key, part in sums.items()}
    named.update({"O%d" % g: part for g, part in enumerate(outs)})
    named.update({"K%d" % g: part for g, part in enumerate(facs)})

    def run(point):
        for name, k in AFTER_EVENTS.get(point, ()):
            if name == "cross":
                crosses[k].start()
            elif name == "emit":
                emit(k)
            elif name == "key":
                keys[k].cross()
            else:
                named[name].step(k)

    def step(t, carry):
        s = t // PAIRS
        pair = t % PAIRS
        slot = t % 2

        @pl.when(t < seqs * PAIRS - 1)
        def _():
            for copy in fetch(t + 1):
                copy.start()

        @pl.when(pair == 0)
        def _():
            bq_ref[...] = mm(qf_ref[s], rank_tile(QA, (QPAD, RQ * 128)))
            bk_ref[...] = mm(kvw_ref[s, :, :256], rank_tile(KA, (256, RK * 128)))
            bv_ref[...] = mm(kvw_ref[s, :, 128:384], rank_tile(KCOLS + KA - 128, (256, RK * 128)))
            fill_cap(me, first, dq_ref[s], dk_ref[s], cap_ref, nblk, own)
            for ref in (aq_ref, ak_ref, av_ref, tq_ref, tk_ref, tv_ref):
                ref[...] = jnp.zeros_like(ref)

        @pl.when(t == SECOND)
        def _():
            down.wait()
            dm_ref[1] += dx_ref[...].astype(F32)

        @pl.when((t == 0) | (t == SECOND))
        def _():
            mids(t // SECOND)

        @pl.when(t == SECOND)
        def _():
            second()

        for copy in fetch(t):
            copy.wait()
        q = q_ref[s, pair]
        k = kb_ref[slot]
        v = vb_ref[slot]
        qs = stacked(q)
        da = stacked(da_ref[s, pair])
        cap = cap_ref[...]
        st = jnp.minimum(mm(k, qs, NT), jnp.concatenate([cap, cap], axis=1))
        p = jnp.exp(st - lse_ref[s, pair])
        dp = mm(v, da, NT)
        delta = jnp.sum(p * dp, axis=0, keepdims=True)
        ds = (p * (dp - delta)).astype(BF16)
        dv = mm(p.astype(BF16), da)
        dk = mm(ds, qs)
        dq = unstacked(mm(k, ds, TN), own) * (DH ** (-0.5))

        eq = head_spread(pair, 0, RQ, (128, RQ * 128))
        qe = mm(qf_ref[s, :, :128], eq)
        dq6 = jnp.concatenate([dq] * RQ, axis=1)
        tq_ref[...] += dq6 * qe
        aq_ref[...] += mm((dq6 * bq_ref[...]).astype(BF16), eq, NT)
        ek = head_spread(pair, 0, RK, (128, RK * 128))
        ev = head_spread(pair, KCOLS - 128, RK, (128, RK * 128))
        ke = mm(kvw_ref[s, :, :128], ek)
        ve = mm(kvw_ref[s, :, 128:256], ev)
        dk2 = jnp.concatenate([dk] * RK, axis=1)
        dv2 = jnp.concatenate([dv] * RK, axis=1)
        tk_ref[...] += dk2 * ke
        tv_ref[...] += dv2 * ve
        ak_ref[...] += mm((dk2 * bk_ref[...]).astype(BF16), ek, NT)
        av_ref[...] += mm((dv2 * bv_ref[...]).astype(BF16), ev, NT)

        @pl.when(pair == PAIRS - 1)
        def _():
            finish(s)

        @pl.when(t == PAIRS - 1)
        def _():
            keys[0].core()

        for when in range(seqs * PAIRS):
            if when in AFTER_EVENTS:

                @pl.when(t == when)
                def _(when=when):
                    run(when)

        return carry

    lax.fori_loop(0, seqs * PAIRS, step, 0)
    keys[1].core()
    n1 = n1_ref[...].reshape(seqs * own, d)
    gq = gq_ref[...].reshape(seqs * own, QPAD)
    w = mm(gq, n1, TN).astype(BF16)
    for g in range(n_q):
        fb[g][...] = w[:, g * 512:(g + 1) * 512].reshape(32, 16, 512)
        facs[g].begin()
    dn1 = mm(gq[:, :QCOLS], wt_ref[:QCOLS, :])
    run("T0")
    keys[1].cross()
    run("T1")
    gkv0 = keys[0].total().astype(BF16)
    gkv = jnp.concatenate([gkv0, keys[1].total().astype(BF16)], axis=0)
    gf = mm(gkv, n1, TN)

    def spread(value, only):
        for g in only:
            for i in range(8):
                for j in range(d // K_LANES):
                    row = 16 * (8 * g + i)
                    piece = value[row:row + 16, j * K_LANES:(j + 1) * K_LANES]
                    fb[n_q + g][4 * i + j] = piece.astype(BF16)
            facs[n_q + g].begin()

    last = len(K_PARTS) - 1
    spread(gf, range(last))
    dn1 = dn1 + mm(gkv[:, :KV], wt_ref[QCOLS:, :])
    load_x.wait()
    hin = late_ref[...].reshape(seqs * own, d).astype(F32)
    r1 = lax.rsqrt(jnp.mean(hin * hin, axis=-1, keepdims=True) + EPS)
    z1 = dn1 * g1_ref[...]
    gain_one = jnp.sum(dn1 * hin * r1, axis=0, keepdims=True)
    gf = jnp.concatenate(
        [gf[:GAIN_ROW], gain_one, gain_ref[...], gf[GAIN_ROW + 2:]], axis=0
    )
    spread(gf, (last,))
    run("T2")
    grad = r1 * z1 - hin * (r1 * r1 * r1) * jnp.mean(z1 * hin, axis=-1, keepdims=True)
    ig_ref[...] = (dm_ref[...].reshape(seqs * own, d) + grad).astype(BF16).reshape(seqs, own, d)
    run("T3")


def after(nblk, gw, own_sums, dn, ds, ok, os, q, k, v, lse, dq, dk, qf, kvw, hm, c, wo, g1, g2, att, n1, x, wt):
    seqs, own, d = hm.shape
    win = nblk * own
    shape = jax.ShapeDtypeStruct
    far = (0, 2, 3, 5, 7, 8, 15, 21)
    results = [shape((32, 16, lanes), BF16) for _, lanes in attention_parts()]
    total = 3 * len(SPLITS) + len(results)
    args = (gw, own_sums, dn, ds, ok, os, q, k, v, lse, dq, dk, qf, kvw, hm, c, wo, g1, g2, att, n1, x, wt)
    res = pl.pallas_call(
        functools.partial(after_kernel, nblk),
        in_specs=[hbm() if i in far else vmem() for i in range(len(args))],
        out_specs=[vmem()] * (3 + len(results)),
        out_shape=[
            shape((seqs, own, d), BF16), shape((seqs, own, d), BF16),
            shape((2 * FFN_UNITS, 16, LANES), BF16),
        ] + results,
        scratch_shapes=[
            pltpu.VMEM((own, RQ * 128), F32),
            pltpu.VMEM((win, RK * 128), F32),
            pltpu.VMEM((win, RK * 128), F32),
            pltpu.VMEM((win, own), F32),
            pltpu.VMEM((seqs, PAIRS, own, 128), BF16),
            pltpu.VMEM((own, 128), F32),
            pltpu.VMEM((win, 128), F32),
            pltpu.VMEM((win, 128), F32),
            pltpu.VMEM((own, RQ * 128), F32),
            pltpu.VMEM((win, RK * 128), F32),
            pltpu.VMEM((win, RK * 128), F32),
            pltpu.VMEM((seqs, own, d), F32),
            pltpu.VMEM((seqs, own, d), BF16),
            pltpu.VMEM((seqs, own, QPAD), BF16),
            pltpu.VMEM((seqs, 4, own, KPAD), BF16),
            pltpu.VMEM((seqs, 2, own, KPAD), BF16),
            pltpu.VMEM((seqs, own, KPAD), BF16),
            pltpu.VMEM((seqs, own, d), BF16),
            pltpu.VMEM((2, win, 128), BF16),
            pltpu.VMEM((2, win, 128), BF16),
            pltpu.VMEM((own, d), BF16),
            pltpu.VMEM((1, d), F32),
        ]
        + [pltpu.VMEM((7 * chunk_units(EARLY), 16, LANES), BF16)] * 3
        + [pltpu.VMEM((4 * chunk_units(EARLY), 16, LANES), BF16)] * 3
        + [pltpu.VMEM((n, 16, 1024), BF16) for n in (32, 31, 16) for _ in OUT_PARTS]
        + [
            pltpu.VMEM((n, 16, lanes), BF16) for n in (32, 31, 16)
            for _, lanes in attention_parts()[len(OUT_PARTS):]
        ]
        + [
            pltpu.SemaphoreType.DMA((total, 10)),
            pltpu.SemaphoreType.DMA((total, 10)),
            pltpu.SemaphoreType.DMA((3,)),
            pltpu.SemaphoreType.DMA((5, 2)),
            pltpu.SemaphoreType.DMA((5, 2)),
            pltpu.SemaphoreType.DMA((2, 2)),
            pltpu.SemaphoreType.DMA((3,)),
        ],
        compiler_params=fused(2),
        cost_estimate=cost(60e9, 60e6),
        name="after",
    )(*args)
    n = 3 + len(OUT_PARTS)
    return res[0], res[1], res[2], res[3:n], res[n:]


def last_kernel(
    out_ref, ig_ref, gr_ref, o0_ref, o1_ref, q0_ref, q1_ref, k0_ref, k1_ref, k2_ref,
    output_ref, grad_ref, gate_ref, up_ref, down_ref, go_ref, gf_ref, gain_ref,
):
    step = pl.program_id(0)
    output_ref[...] = out_ref[...]
    grad_ref[...] = ig_ref[...]
    units = gr_ref.shape[2]
    for m, ref in enumerate((gate_ref, up_ref, down_ref)):
        for i in range(2):
            ref[:, i * LANES:(i + 1) * LANES] = gr_ref[i, m].reshape(16 * units, LANES).astype(F32)
    for g, ref in enumerate((o0_ref, o1_ref)):

        @pl.when(step // 2 == g)
        def _(ref=ref):
            half = pl.ds((step % 2) * 16, 16)
            go_ref[...] = ref[half].reshape(256, 1024).astype(F32)

    rows = pl.ds(pl.multiple_of(step * 128, 128), 128)
    for i, ref in enumerate((q0_ref, q1_ref)):
        gf_ref[rows, i * 512:(i + 1) * 512] = ref[pl.ds(step * 8, 8)].reshape(128, 512).astype(F32)

    @pl.when(step == 3)
    def _():
        for g, ref in enumerate((k0_ref, k1_ref, k2_ref)):
            count = min(KV - 128 * g, 128) // 16

            def rows(i, carry, g=g, ref=ref):
                at = pl.ds(pl.multiple_of(QCOLS + 128 * g + 16 * i, 16), 16)
                for j in range(1024 // K_LANES):
                    cols = slice(j * K_LANES, (j + 1) * K_LANES)
                    gf_ref[at, cols] = ref[4 * i + j].astype(F32)
                return carry

            lax.fori_loop(0, count, rows, 0)
        unit = (GAIN_ROW - 256) // 16
        for j in range(1024 // K_LANES):
            cols = slice(j * K_LANES, (j + 1) * K_LANES)
            gain_ref[:, cols] = k2_ref[4 * unit + j].astype(F32)[:8]


def finish_all(output, grad, gr, go, gf, cols):
    seqs, own, d = output.shape
    ff = 16 * gr.shape[0] // 6
    gr = gr.reshape(2, 3, ff // 16, 16, LANES)
    steps = 4
    shape = jax.ShapeDtypeStruct
    whole = lambda a: pl.BlockSpec(a.shape, lambda i, a=a: (0,) * len(a.shape))
    tokens = pl.BlockSpec((seqs, own // steps, d), lambda i: (0, i, 0))
    outs = [
        shape(output.shape, BF16), shape(output.shape, BF16), shape((ff, d), F32),
        shape((ff, d), F32), shape((ff, d), F32), shape((d, d), F32), shape((cols, d), F32),
        shape((8, d), F32),
    ]
    rows = lambda n: pl.BlockSpec((n // steps, d), lambda i: (i, 0))
    return pl.pallas_call(
        last_kernel,
        grid=(steps,),
        in_specs=[
            tokens, tokens,
            pl.BlockSpec((2, 3, ff // 16 // steps, 16, LANES), lambda i: (0, 0, i, 0, 0)),
        ] + [whole(a) for a in list(go) + list(gf)],
        out_specs=[tokens, tokens, rows(ff), rows(ff), rows(ff), rows(d), whole(outs[6]), whole(outs[7])],
        out_shape=outs,
        compiler_params=params(),
        cost_estimate=cost(1e6, 30e6),
        name="last",
    )(output, grad, gr, *go, *gf)


def fused_body(
    tokens, doc_ids, factor_weight, output_weight, norm_one, norm_two,
    gate_weight, up_weight, down_weight, cotangent,
):
    seqs, own, d = tokens.shape
    me = lax.axis_index("wide")
    nblk = -(-(MAX_DOC - 1) // own) + 1
    first = me // 3
    g1 = norm_one[None]
    g2 = norm_two[None]
    dq = lax.dynamic_slice_in_dim(doc_ids, me * own, own, 1)[:, None, :]
    dk = lax.dynamic_slice_in_dim(doc_ids, first * own, nblk * own, 1)[:, :, None]
    wt = factor_weight.T
    n1, qf, kvw, att, q, k, v, lse, hm, ng, cg = fore(
        nblk, tokens, wt, output_weight, g1, g2, dq, dk, cotangent
    )
    dn, ds, ok, os, gw, own_sums = middle(ng, cg, gate_weight.T, up_weight.T, down_weight)
    output, input_grad, gr, go, gf = after(
        nblk, gw, own_sums, dn, ds, ok, os, q, k, v, lse, dq, dk, qf, kvw, hm, cotangent, output_weight,
        g1, g2, att, n1, tokens, wt,
    )
    output, input_grad, gate, up, down, out, fac, gain = finish_all(
        output, input_grad, gr, go, gf, factor_weight.shape[1]
    )
    return output, input_grad, fac.T, out, gain[0], gain[1], gate.T, up.T, down


def swap(x, axis, size, bit):
    return lax.ppermute(x, axis, [(i, i ^ bit) for i in range(size)])


def steps_of(size):
    bits, b = [], size // 2
    while b:
        bits.append(b)
        b //= 2
    return bits


def gather(x, size):
    buf = x[None]
    for bit in steps_of(size):
        buf = jnp.concatenate([buf, swap(buf, "wide", size, bit)], axis=0)
    return buf


def order_of(size):
    order = [0]
    for bit in steps_of(size):
        order = order + [o ^ bit for o in order]
    return order


def scatter(parts, size):
    for bit in reversed(steps_of(size)):
        half = parts.shape[0] // 2
        got = swap(parts[half:], "wide", size, bit)
        total = parts[:half].astype(F32) + got.astype(F32)
        parts = total if half == 1 else total.astype(BF16)
    return parts[0]


def body(
    tokens, doc_ids, factor_weight, output_weight, norm_one, norm_two,
    gate_weight, up_weight, down_weight, cotangent,
):
    seqs, own, d = tokens.shape
    full_len = doc_ids.shape[1]
    size = full_len // own
    me = lax.axis_index("wide")
    left = min(-(-(MAX_DOC - 1) // own), size - 1)
    nblk = left + 1
    start = jnp.maximum(me - left, 0)
    order = order_of(size)
    slot_of = [order.index(j) for j in range(size)]
    slots = jnp.asarray(slot_of, jnp.int32)
    blocks = start + jnp.arange(nblk, dtype=jnp.int32)
    scalars = jnp.concatenate(
        [me[None].astype(jnp.int32), (me - blocks) * own, slots[me ^ blocks]]
    ).astype(jnp.int32)
    g1 = norm_one[None]
    g2 = norm_two[None]

    n1, qf, kvf = front(tokens.reshape(seqs * own, d), factor_weight, g1)
    qf = qf.reshape(seqs, own, QPAD)
    kvg = gather(kvf.reshape(seqs, own, KPAD), size)
    doc_query = lax.dynamic_slice_in_dim(doc_ids, me * own, own, 1)
    doc_key = lax.dynamic_slice_in_dim(doc_ids, start * own, nblk * own, 1)
    cots = [gather(cotangent[s], size) for s in range(seqs)]

    fwd = []
    for s in range(seqs):
        dq = doc_query[s][None, :]
        dk = doc_key[s][:, None]
        fwd.append(
            (dq, dk)
            + tuple(attend(nblk, scalars, qf[s], kvg[:, s], dq, dk, tokens[s], output_weight, g2))
        )
    prev = None
    outs, dns = [], []
    for s in range(seqs):
        n2 = gather(fwd[s][8], size)
        res = ffn(n2, cots[s], gate_weight, up_weight, down_weight, prev, s == seqs - 1)
        outs.append(res[0])
        dns.append(res[1])
        prev = res[2:]
    grads = [lax.psum(g, "rows").astype(F32) for g in prev]

    output, mids, lows, gain_two, gqs, gkvs = [], [], [], 0.0, [], []
    for s in range(seqs):
        dq, dk, att, q, k, v, lse, hm, n2, kvw = fwd[s]
        dn = scatter(dns[s], size)
        dm, low, gain, gq, gkv = back(
            nblk, size, scalars, q, k, v, lse, dq, dk, qf[s], kvw, dn, hm,
            cotangent[s], output_weight, g2,
        )
        output.append((hm + scatter(outs[s], size)).astype(BF16))
        mids.append(dm)
        lows.append(low)
        gqs.append(gq)
        gkvs.append(gkv)
        gain_two = gain_two + gain
    att_all = jnp.stack([f[2] for f in fwd]).reshape(seqs * own, d)
    grad_out = mm(att_all, jnp.stack(lows).reshape(seqs * own, d), TN)
    gkv = scatter(jnp.stack(gkvs, axis=1), size).astype(BF16)
    dfac = jnp.concatenate([jnp.stack(gqs)[..., :QCOLS], gkv[..., :KV]], axis=-1)
    dfac = dfac.reshape(seqs * own, -1)
    grad_factors = mm(n1, dfac, TN)
    dn1 = mm(dfac, factor_weight, NT)
    hin = tokens.reshape(seqs * own, d).astype(F32)
    r1 = lax.rsqrt(jnp.mean(hin * hin, axis=-1, keepdims=True) + EPS)
    z1 = dn1 * g1
    gain_one = jnp.sum(dn1 * hin * r1, axis=0)
    grad_norm = r1 * z1 - hin * (r1 * r1 * r1) * jnp.mean(z1 * hin, axis=-1, keepdims=True)
    input_grad = (jnp.stack(mids).reshape(seqs * own, d) + grad_norm).astype(BF16)
    parts = [grad_out, grad_factors.T, gain_one[None], gain_two]
    packed = jnp.concatenate([p.astype(BF16) for p in parts], axis=0)
    packed = lax.psum(packed, ("rows", "wide")).astype(F32)
    fac = grad_factors.shape[1]
    return (
        jnp.stack(output),
        input_grad.reshape(seqs, own, d),
        packed[d:d + fac].T,
        packed[:d],
        packed[d + fac],
        packed[d + fac + 1],
        grads[0],
        grads[1],
        grads[2],
    )


def solution(mesh):
    placed = (
        P("rows", "wide", None), P("rows", None), P(), P(), P(), P(),
        P(None, "wide"), P(None, "wide"), P("wide", None), P("rows", "wide", None),
    )
    small = mesh.shape["rows"] == 8 and mesh.shape["wide"] == 4
    return jax.shard_map(
        fused_body if small else body,
        mesh=mesh,
        in_specs=placed,
        out_specs=(
            P("rows", "wide", None), P("rows", "wide", None), P(), P(), P(), P(),
            P(None, "wide"), P(None, "wide"), P("wide", None),
        ),
        check_vma=False,
    )
```

```python
import functools

import jax
import jax.numpy as jnp
from jax import lax
from jax.experimental import pallas as pl
from jax.experimental.pallas import tpu as pltpu
from jax.sharding import PartitionSpec as P

H = 16
DH = 64
RQ = 6
RK = 2
MAX_DOC = 512
EPS = 1e-06
NEG = -1000000000.0
BIG = 3.0e38

QA = H * RQ
QCOLS = QA + RQ * DH
KA = H * RK
KCOLS = KA + RK * DH
KV = 2 * KCOLS
QPAD = 512
KPAD = 384
PAIRS = H // 2

F32 = jnp.float32
BF16 = jnp.bfloat16

NN = (((1,), (0,)), ((), ()))
NT = (((1,), (1,)), ((), ()))
TN = (((0,), (0,)), ((), ()))


def mm(a, b, dims=NN):
    return lax.dot_general(a, b, dims, preferred_element_type=F32)


def params(vmem_mb=60):
    return pltpu.CompilerParams(vmem_limit_bytes=vmem_mb << 20)


def cost(flops, nbytes):
    return pl.CostEstimate(flops=int(flops), bytes_accessed=int(nbytes), transcendentals=0)


def selection(shape, rule):
    row = lax.broadcasted_iota(jnp.int32, shape, 0)
    col = lax.broadcasted_iota(jnp.int32, shape, 1)
    return jnp.where(rule(row, col), 1.0, 0.0).astype(BF16)


def head_spread(pair, base, rank, shape):
    def rule(row, col):
        r = col // 128
        lane = col - r * 128
        head = 2 * pair + jnp.where(lane >= DH, 1, 0)
        return row == base + head * rank + r

    return selection(shape, rule)


def rank_tile(base, shape):
    def rule(row, col):
        r = col // 128
        lane = col - r * 128
        return row == base + r * DH + jnp.where(lane >= DH, lane - DH, lane)

    return selection(shape, rule)


def front_kernel(x_ref, w_ref, g_ref, n_ref, q_ref, kv_ref):
    x = x_ref[...].astype(F32)
    r = lax.rsqrt(jnp.mean(x * x, axis=-1, keepdims=True) + EPS)
    n = (x * r * g_ref[...]).astype(BF16)
    n_ref[...] = n
    f = mm(n, w_ref[...]).astype(BF16)
    q_ref[...] = f[:, :QPAD]
    kv_ref[:, :KV] = f[:, QCOLS:]
    kv_ref[:, KV:] = jnp.zeros((f.shape[0], KPAD - KV), BF16)


def front(x, w, gain):
    rows, d = x.shape
    blk = 256 if rows % 256 == 0 else rows
    return pl.pallas_call(
        front_kernel,
        grid=(rows // blk,),
        in_specs=[
            pl.BlockSpec((blk, d), lambda i: (i, 0)),
            pl.BlockSpec(w.shape, lambda i: (0, 0)),
            pl.BlockSpec((1, d), lambda i: (0, 0)),
        ],
        out_specs=[
            pl.BlockSpec((blk, d), lambda i: (i, 0)),
            pl.BlockSpec((blk, QPAD), lambda i: (i, 0)),
            pl.BlockSpec((blk, KPAD), lambda i: (i, 0)),
        ],
        out_shape=[
            jax.ShapeDtypeStruct((rows, d), BF16),
            jax.ShapeDtypeStruct((rows, QPAD), BF16),
            jax.ShapeDtypeStruct((rows, KPAD), BF16),
        ],
        compiler_params=params(),
        cost_estimate=cost(2 * rows * d * 800, rows * d * 6 + d * 1600),
        name="front",
    )(x, w, gain)


def make_cap(s_ref, dq_ref, dk_ref, cap_ref, nblk, own):
    dq = dq_ref[...]
    for i in range(nblk):
        rows = pl.ds(i * own, own)
        key = lax.broadcasted_iota(jnp.int32, (own, own), 0)
        query = lax.broadcasted_iota(jnp.int32, (own, own), 1) + s_ref[1 + i]
        ok = (dk_ref[rows, :] == dq) & (key <= query)
        cap_ref[rows, :] = jnp.where(ok, BIG, NEG)


def stacked(x):
    lane = lax.broadcasted_iota(jnp.int32, x.shape, 1)
    zero = jnp.zeros_like(x)
    return jnp.concatenate(
        [jnp.where(lane < DH, x, zero), jnp.where(lane >= DH, x, zero)], axis=0
    )


def unstacked(xt, own):
    pair = jnp.concatenate([xt[:DH, :own], xt[DH:, own:]], axis=0)
    return pair.T


def key_parts(kvf_ref, pair):
    ek = head_spread(pair, 0, RK, (128, RK * 128))
    ev = head_spread(pair, KCOLS - 128, RK, (128, RK * 128))
    ke = mm(kvf_ref[:, :128], ek)
    ve = mm(kvf_ref[:, 128:256], ev)
    return ke, ve


def tile_keys(kvf_ref, bk_ref, bv_ref):
    bk_ref[...] = mm(kvf_ref[:, :256], rank_tile(KA, (256, RK * 128)))
    bv_ref[...] = mm(kvf_ref[:, 128:384], rank_tile(KCOLS + KA - 128, (256, RK * 128)))


def attend_kernel(
    nblk, s_ref, qf_ref, kvg_ref, dq_ref, dk_ref, x_ref, wo_ref, g_ref,
    att_ref, q_ref, k_ref, v_ref, lse_ref, hm_ref, n_ref, kvw_ref,
    bq_ref, bk_ref, bv_ref, cap_ref, full_ref,
):
    pair = pl.program_id(0)
    own = qf_ref.shape[0]

    @pl.when(pair == 0)
    def _():
        for i in range(nblk):
            kvw_ref[pl.ds(i * own, own), :] = kvg_ref[s_ref[1 + nblk + i]]
        bq_ref[...] = mm(qf_ref[...], rank_tile(QA, (QPAD, RQ * 128)))
        tile_keys(kvw_ref, bk_ref, bv_ref)
        make_cap(s_ref, dq_ref, dk_ref, cap_ref, nblk, own)

    qe = mm(qf_ref[:, :128], head_spread(pair, 0, RQ, (128, RQ * 128)))
    qsum = qe[:, :128] * bq_ref[:, :128]
    for r in range(1, RQ):
        cols = slice(r * 128, (r + 1) * 128)
        qsum = qsum + qe[:, cols] * bq_ref[:, cols]
    q = (qsum * (1.0 / RQ)).astype(BF16)
    ke, ve = key_parts(kvw_ref, pair)
    k = ((ke[:, :128] * bk_ref[:, :128] + ke[:, 128:] * bk_ref[:, 128:]) * (1.0 / RK)).astype(BF16)
    v = ((ve[:, :128] * bv_ref[:, :128] + ve[:, 128:] * bv_ref[:, 128:]) * (1.0 / RK)).astype(BF16)
    q = q * jnp.asarray(DH ** (-0.5), BF16)
    q_ref[...] = q
    k_ref[...] = k
    v_ref[...] = v
    cap = cap_ref[...]
    st = jnp.minimum(mm(k, stacked(q), NT), jnp.concatenate([cap, cap], axis=1))
    top = jnp.max(st, axis=0, keepdims=True)
    e = jnp.exp(st - top)
    total = jnp.sum(e, axis=0, keepdims=True)
    p = (e * (1.0 / total)).astype(BF16)
    lse_ref[0] = top + jnp.log(total)
    att = unstacked(mm(v, p, TN), own).astype(BF16)
    att_ref[...] = att
    full_ref[pair] = att

    @pl.when(pair == pl.num_programs(0) - 1)
    def _():
        hm = x_ref[...].astype(F32)
        att_all = jnp.concatenate([full_ref[i] for i in range(PAIRS)], axis=1)
        hm = hm + mm(att_all, wo_ref[...])
        hm_ref[...] = hm
        r = lax.rsqrt(jnp.mean(hm * hm, axis=-1, keepdims=True) + EPS)
        n_ref[...] = (hm * r * g_ref[...]).astype(BF16)


def attend(nblk, scalars, qf, kvg, dq, dk, x, wo, gain):
    own, d = x.shape
    win = nblk * own
    whole = lambda a: pl.BlockSpec(a.shape, lambda p, a=a: (0,) * a.ndim)
    col = lambda rows: pl.BlockSpec((rows, 128), lambda p: (0, p))
    return pl.pallas_call(
        functools.partial(attend_kernel, nblk),
        grid=(PAIRS,),
        in_specs=[pl.BlockSpec(memory_space=pltpu.SMEM)]
        + [whole(a) for a in (qf, kvg, dq, dk, x, wo, gain)],
        out_specs=[
            col(own), col(own), col(win), col(win),
            pl.BlockSpec((1, 1, 2 * own), lambda p: (p, 0, 0)),
            pl.BlockSpec((own, d), lambda p: (0, 0)),
            pl.BlockSpec((own, d), lambda p: (0, 0)),
            pl.BlockSpec((win, KPAD), lambda p: (0, 0)),
        ],
        out_shape=[
            jax.ShapeDtypeStruct((own, d), BF16),
            jax.ShapeDtypeStruct((own, d), BF16),
            jax.ShapeDtypeStruct((win, d), BF16),
            jax.ShapeDtypeStruct((win, d), BF16),
            jax.ShapeDtypeStruct((PAIRS, 1, 2 * own), F32),
            jax.ShapeDtypeStruct((own, d), F32),
            jax.ShapeDtypeStruct((own, d), BF16),
            jax.ShapeDtypeStruct((win, KPAD), BF16),
        ],
        scratch_shapes=[
            pltpu.VMEM((own, RQ * 128), F32),
            pltpu.VMEM((win, RK * 128), F32),
            pltpu.VMEM((win, RK * 128), F32),
            pltpu.VMEM((win, own), F32),
            pltpu.VMEM((PAIRS, own, 128), BF16),
        ],
        compiler_params=params(),
        cost_estimate=cost(12e9, 12e6),
        name="attend",
    )(scalars, qf, kvg, dq, dk, x, wo, gain)


def ffn_kernel(has_prev, bf16_out, *refs):
    if has_prev:
        n_ref, c_ref, wg_ref, wu_ref, wd_ref, pg_ref, pu_ref, pd_ref = refs[:8]
        refs = refs[8:]
    else:
        n_ref, c_ref, wg_ref, wu_ref, wd_ref = refs[:5]
        refs = refs[5:]
    o_ref, dn_ref, og_ref, ou_ref, od_ref = refs[:5]
    if bf16_out:
        ag_ref, au_ref, ad_ref = refs[5:]
    else:
        ag_ref, au_ref, ad_ref = og_ref, ou_ref, od_ref
    step = pl.program_id(0)

    @pl.when(step == 0)
    def _():
        if has_prev:
            ag_ref[...] = pg_ref[...]
            au_ref[...] = pu_ref[...]
            ad_ref[...] = pd_ref[...]
        else:
            ag_ref[...] = jnp.zeros_like(ag_ref)
            au_ref[...] = jnp.zeros_like(au_ref)
            ad_ref[...] = jnp.zeros_like(ad_ref)

    n = n_ref[0]
    c = c_ref[0]
    wg, wu, wd = wg_ref[...], wu_ref[...], wd_ref[...]
    g = mm(n, wg)
    u = mm(n, wu)
    dh = mm(c, wd, NT)
    s = 1.0 / (1.0 + jnp.exp(-g))
    gs = g * s
    hid = (gs * u).astype(BF16)
    dg = (dh * u * (s * (1.0 + g * (1.0 - s)))).astype(BF16)
    du = (dh * gs).astype(BF16)
    o_ref[0] = mm(hid, wd).astype(BF16)
    dn_ref[0] = (mm(dg, wg, NT) + mm(du, wu, NT)).astype(BF16)
    ag_ref[...] += mm(n, dg, TN)
    au_ref[...] += mm(n, du, TN)
    ad_ref[...] += mm(hid, c, TN)
    if bf16_out:

        @pl.when(step == pl.num_programs(0) - 1)
        def _():
            og_ref[...] = ag_ref[...].astype(BF16)
            ou_ref[...] = au_ref[...].astype(BF16)
            od_ref[...] = ad_ref[...].astype(BF16)


def ffn(n, c, wg, wu, wd, prev, last):
    w, own, d = n.shape
    ff = wg.shape[1]
    one = lambda a: pl.BlockSpec(
        a.shape, lambda i, a=a: (0,) * a.ndim, pipeline_mode=pl.Buffered(1)
    )
    blk = pl.BlockSpec((1, own, d), lambda i: (i, 0, 0))
    dt = BF16 if last else F32
    args = [n, c, wg, wu, wd] + list(prev or [])
    shapes = [(d, ff), (d, ff), (ff, d)]
    return pl.pallas_call(
        functools.partial(ffn_kernel, bool(prev), last),
        grid=(w,),
        in_specs=[blk, blk] + [one(a) for a in args[2:]],
        out_specs=[blk, blk] + [
            pl.BlockSpec(s, lambda i: (0, 0), pipeline_mode=pl.Buffered(1)) for s in shapes
        ],
        out_shape=[jax.ShapeDtypeStruct(n.shape, BF16)] * 2
        + [jax.ShapeDtypeStruct(s, dt) for s in shapes],
        scratch_shapes=[pltpu.VMEM(s, F32) for s in shapes] if last else [],
        compiler_params=params(),
        cost_estimate=cost(18 * w * own * d * ff, 20 * w * own * d),
        name="ffn",
    )(*args)


def back_kernel(
    nblk, s_ref, q_ref, k_ref, v_ref, lse_ref, dq_ref, dk_ref, qf_ref, kvw_ref,
    dn_ref, hm_ref, c_ref, wo_ref, g_ref,
    dm_ref, dl_ref, gain_ref, gq_ref, gkv_ref,
    bq_ref, bk_ref, bv_ref, cap_ref, da_ref, aq_ref, ak_ref, av_ref, tq_ref, tk_ref, tv_ref,
):
    pair = pl.program_id(0)
    own = q_ref.shape[0]
    last = pl.num_programs(0) - 1

    @pl.when(pair == 0)
    def _():
        hm = hm_ref[...]
        dn = dn_ref[...].astype(F32)
        r = lax.rsqrt(jnp.mean(hm * hm, axis=-1, keepdims=True) + EPS)
        z = dn * g_ref[...]
        gain_ref[...] = jnp.sum(dn * hm * r, axis=0, keepdims=True)
        dm = (
            c_ref[...].astype(F32)
            + r * z
            - hm * (r * r * r) * jnp.mean(z * hm, axis=-1, keepdims=True)
        )
        dm_ref[...] = dm
        low = dm.astype(BF16)
        dl_ref[...] = low
        da = mm(low, wo_ref[...], NT).astype(BF16)
        for i in range(PAIRS):
            da_ref[i] = da[:, i * 128:(i + 1) * 128]
        bq_ref[...] = mm(qf_ref[...], rank_tile(QA, (QPAD, RQ * 128)))
        tile_keys(kvw_ref, bk_ref, bv_ref)
        make_cap(s_ref, dq_ref, dk_ref, cap_ref, nblk, own)
        for ref in (aq_ref, ak_ref, av_ref, tq_ref, tk_ref, tv_ref):
            ref[...] = jnp.zeros_like(ref)

    q = q_ref[...]
    k = k_ref[...]
    v = v_ref[...]
    qs = stacked(q)
    ds_ = stacked(da_ref[pair])
    cap = cap_ref[...]
    st = jnp.minimum(mm(k, qs, NT), jnp.concatenate([cap, cap], axis=1))
    p = jnp.exp(st - lse_ref[0])
    dp = mm(v, ds_, NT)
    delta = jnp.sum(p * dp, axis=0, keepdims=True)
    ds = (p * (dp - delta)).astype(BF16)
    dv = mm(p.astype(BF16), ds_)
    dk = mm(ds, qs)
    dq = unstacked(mm(k, ds, TN), own) * (DH ** (-0.5))

    eq = head_spread(pair, 0, RQ, (128, RQ * 128))
    qe = mm(qf_ref[:, :128], eq)
    dq6 = jnp.concatenate([dq] * RQ, axis=1)
    tq_ref[...] += dq6 * qe
    aq_ref[...] += mm((dq6 * bq_ref[...]).astype(BF16), eq, NT)
    ek = head_spread(pair, 0, RK, (128, RK * 128))
    ev = head_spread(pair, KCOLS - 128, RK, (128, RK * 128))
    ke = mm(kvw_ref[:, :128], ek)
    ve = mm(kvw_ref[:, 128:256], ev)
    dk2 = jnp.concatenate([dk] * RK, axis=1)
    dv2 = jnp.concatenate([dv] * RK, axis=1)
    tk_ref[...] += dk2 * ke
    tv_ref[...] += dv2 * ve
    ak_ref[...] += mm((dk2 * bk_ref[...]).astype(BF16), ek, NT)
    av_ref[...] += mm((dv2 * bv_ref[...]).astype(BF16), ev, NT)

    @pl.when(pair == last)
    def _():
        def fold(x, t):
            hi = x.astype(BF16)
            lo = (x - hi.astype(F32)).astype(BF16)
            return mm(hi, t, NT) + mm(lo, t, NT)

        gq = fold(tq_ref[...], rank_tile(QA, (QPAD, RQ * 128)))
        gq_ref[:, :128] = ((gq[:, :128] + aq_ref[...]) * (1.0 / RQ)).astype(BF16)
        gq_ref[:, 128:] = (gq[:, 128:] * (1.0 / RQ)).astype(BF16)
        gk = fold(tk_ref[...], rank_tile(KA, (KPAD, RK * 128)))
        gv = fold(tv_ref[...], rank_tile(KCOLS + KA, (KPAD, RK * 128)))
        gkv = gk + gv
        first = ((gkv[:, :128] + ak_ref[...]) * (1.0 / RK)).astype(BF16)
        second = ((gkv[:, 128:256] + av_ref[...]) * (1.0 / RK)).astype(BF16)
        third = (gkv[:, 256:] * (1.0 / RK)).astype(BF16)
        gkv_ref[...] = jnp.zeros_like(gkv_ref)
        for i in range(nblk):
            rows = slice(i * own, (i + 1) * own)
            slot = s_ref[1 + nblk + i]
            gkv_ref[slot, :, :128] = first[rows]
            gkv_ref[slot, :, 128:256] = second[rows]
            gkv_ref[slot, :, 256:] = third[rows]


def back(nblk, width, scalars, q, k, v, lse, dq, dk, qf, kvw, dn, hm, c, wo, gain):
    own, d = q.shape
    win = nblk * own
    whole = lambda a: pl.BlockSpec(a.shape, lambda p, a=a: (0,) * a.ndim)
    col = lambda rows: pl.BlockSpec((rows, 128), lambda p: (0, p))
    fixed = lambda *s: pl.BlockSpec(s, lambda p: (0,) * len(s))
    return pl.pallas_call(
        functools.partial(back_kernel, nblk),
        grid=(PAIRS,),
        in_specs=[
            pl.BlockSpec(memory_space=pltpu.SMEM), col(own), col(win), col(win),
            pl.BlockSpec((1, 1, 2 * own), lambda p: (p, 0, 0)),
        ] + [whole(a) for a in (dq, dk, qf, kvw, dn, hm, c, wo, gain)],
        out_specs=[
            fixed(own, d), fixed(own, d), fixed(1, d), fixed(own, QPAD),
            fixed(width, own, KPAD),
        ],
        out_shape=[
            jax.ShapeDtypeStruct((own, d), F32),
            jax.ShapeDtypeStruct((own, d), BF16),
            jax.ShapeDtypeStruct((1, d), F32),
            jax.ShapeDtypeStruct((own, QPAD), BF16),
            jax.ShapeDtypeStruct((width, own, KPAD), BF16),
        ],
        scratch_shapes=[
            pltpu.VMEM((own, RQ * 128), F32),
            pltpu.VMEM((win, RK * 128), F32),
            pltpu.VMEM((win, RK * 128), F32),
            pltpu.VMEM((win, own), F32),
            pltpu.VMEM((PAIRS, own, 128), BF16),
            pltpu.VMEM((own, 128), F32),
            pltpu.VMEM((win, 128), F32),
            pltpu.VMEM((win, 128), F32),
            pltpu.VMEM((own, RQ * 128), F32),
            pltpu.VMEM((win, RK * 128), F32),
            pltpu.VMEM((win, RK * 128), F32),
        ],
        compiler_params=params(),
        cost_estimate=cost(30e9, 15e6),
        name="back",
    )(scalars, q, k, v, lse, dq, dk, qf, kvw, dn, hm, c, wo, gain)


def flip(index, bit):
    digit = (index // bit) % 2
    return index + bit - 2 * bit * digit


AXES = {"c": ("wide", 1), "x": ("wide", 2), "y": ("rows", 1), "n": ("rows", 2), "f": ("rows", 4)}


def enter(names):
    barrier = pltpu.get_barrier_semaphore()
    for name in names:
        pl.semaphore_signal(
            barrier, inc=1, device_id=partner(name), device_id_type=pl.DeviceIdType.MESH
        )
    pl.semaphore_wait(barrier, len(names))


def partner(name):
    axis, bit = AXES[name]
    return {axis: flip(lax.axis_index(axis), bit)}


def digit(name):
    axis, bit = AXES[name]
    return (lax.axis_index(axis) // bit) % 2


def wide_digits(index):
    return index // 2, index % 2


def slot_for(me, block):
    mx, mc = wide_digits(me)
    bx, bc = wide_digits(block)
    return 2 * ((mc + bc) % 2) + (mx + bx) % 2


def send_to(name, src, dst, send, recv):
    return pltpu.make_async_remote_copy(
        src_ref=src, dst_ref=dst, send_sem=send, recv_sem=recv,
        device_id=partner(name), device_id_type=pl.DeviceIdType.MESH,
    )


class Gather:
    def __init__(self, ref, send, recv, rows=None):
        at = [ref.at[i] if rows is None else ref.at[i, rows] for i in range(4)]
        self.x = send_to("x", at[0], at[1], send.at[0], recv.at[0])
        self.c = send_to("c", at[0], at[2], send.at[1], recv.at[1])
        self.r = send_to("c", at[1], at[3], send.at[2], recv.at[2])

    def first(self):
        self.x.start()
        self.c.start()

    def relay(self):
        self.x.wait()
        self.r.start()

    def done(self):
        self.c.wait()
        self.r.wait()


class Scatter:
    def __init__(self, part, got, last, send, recv):
        self.part, self.got, self.last = part, got, last
        self.c = send_to("c", part.at[pl.ds(2, 2)], got, send.at[0], recv.at[0])
        if last is not None:
            self.x = send_to("x", part.at[1], last, send.at[1], recv.at[1])

    def core(self):
        self.c.start()

    def kept(self, i):
        return self.part[i].astype(F32) + self.got[i].astype(F32)

    def cross(self):
        self.c.wait()
        self.part[1] = self.kept(1).astype(BF16)
        self.x.start()
        self.part[0] = self.kept(0).astype(BF16)

    def total(self):
        self.x.wait()
        return self.part[0].astype(F32) + self.last[...].astype(F32)


class Sum:
    def __init__(self, names, unit, src, base, acc, got, res, rbase, send, recv,
                 local=None, top=None, flat=False):
        self.names, self.unit, self.n = names, unit, len(names)
        self.src, self.base, self.acc, self.got = src, base, acc, got
        self.res, self.rbase, self.send, self.recv = res, rbase, send, recv
        self.local, self.flat = local, flat
        self.top = unit * 2 ** (self.n - 1) if top is None else top

    def low(self, i, skip=0):
        total = 0
        for j in range(skip, i):
            total = total + digit(self.names[j]) * 2 ** (self.n - 1 - j)
        return total

    def span(self, ref, base, chunk, count):
        return ref.at[pl.ds(base + chunk * self.unit, count * self.unit)]

    def keep(self):
        half = 2 ** (self.n - 1)
        return pltpu.make_async_copy(
            self.span(self.src, self.base, self.low(1), half), self.acc, self.local
        )

    def halve(self, i):
        half = 2 ** (self.n - 1 - i)
        away = (1 - digit(self.names[i])) * half
        if i == 0:
            src = self.span(self.src, self.base, away, half)
        else:
            src = self.span(self.acc, 0, self.low(i, 1) + away, half)
        dst = self.span(self.got, 0, 2 ** self.n - 2 * half, half)
        return send_to(self.names[i], src, dst, self.send.at[i], self.recv.at[i])

    def begin(self):
        self.halve(0).start()
        if self.local is not None:
            self.keep().start()

    def place(self, i):
        if self.flat:
            return self.rbase
        return self.rbase + digit(self.names[0]) * self.top + self.low(i, 1) * self.unit

    def double(self, i):
        half = 2 ** (self.n - 1 - i)
        held = self.res.at[pl.ds(self.place(i + 1), half * self.unit)]
        k = self.n + i
        return send_to(self.names[i], held, held, self.send.at[k], self.recv.at[k])

    def resume(self, own, at):
        place = self.place(self.n)
        for j in range(self.unit):
            self.res[place + j] = own[at + j]
        self.double(self.n - 1).start()

    def add(self, i):
        half = 2 ** (self.n - 1 - i)
        offset = (2 ** self.n - 2 * half) * self.unit
        self.halve(i).wait()
        kept = self.low(i + 1, 1) * self.unit
        first = i == 0 and self.local is None
        if i == 0 and self.local is not None:
            self.keep().wait()
        own = self.base + self.low(1) * self.unit
        last = i == self.n - 1
        place = self.place(self.n)

        count = self.unit if self.unit > 1 else min(half, 4)

        def some(i, carry):
            j = i * count
            mine = self.src[pl.ds(own + j, count)] if first else self.acc[pl.ds(kept + j, count)]
            value = (mine.astype(F32) + self.got[pl.ds(offset + j, count)].astype(F32)).astype(BF16)
            if last:
                self.res[pl.ds(place + j, count)] = value
            else:
                self.acc[pl.ds(kept + j, count)] = value
            return carry

        lax.fori_loop(0, half * self.unit // count, some, 0)

    def step(self, k):
        n = self.n
        if k < n:
            self.add(k)
            if k < n - 1:
                self.halve(k + 1).start()
            elif not self.flat:
                self.double(n - 1).start()
        else:
            i = 2 * n - 1 - k
            self.double(i).wait()
            if i > 0:
                self.double(i - 1).start()


def fill_cap(me, first, dq, dk, cap_ref, nblk, own):
    for i in range(nblk):
        rows = pl.ds(i * own, own)
        key = lax.broadcasted_iota(jnp.int32, (own, own), 0)
        query = lax.broadcasted_iota(jnp.int32, (own, own), 1) + (me - first - i) * own
        ok = (dk[i * own:(i + 1) * own, :] == dq) & (key <= query)
        cap_ref[rows, :] = jnp.where(ok, BIG, NEG)


def fore_kernel(
    nblk, x_ref, wt_ref, wo_ref, g1_ref, g2_ref, dq_ref, dk_ref, c_ref,
    n1_ref, qf_ref, kvw_ref, att_ref, q_ref, k_ref, v_ref, lse_ref, hm_ref, ng_ref, nb_ref, cg_ref,
    kvg_ref, bq_ref, bk_ref, bv_ref, cap_ref, full_ref, send, recv,
):
    seqs, own, d = x_ref.shape
    me = lax.axis_index("wide")
    first = me // 3
    kvs = [Gather(kvg_ref.at[s], send.at[s], recv.at[s]) for s in range(seqs)]
    cots = [Gather(cg_ref.at[s], send.at[2 + s], recv.at[2 + s]) for s in range(seqs)]
    norm = Gather(ng_ref, send.at[4], recv.at[4])
    for s in range(seqs):
        cg_ref[s, 0] = c_ref[s]
    for s in range(seqs):
        x = x_ref[s].astype(F32)
        r = lax.rsqrt(jnp.mean(x * x, axis=-1, keepdims=True) + EPS)
        n = (x * r * g1_ref[...]).astype(BF16)
        n1_ref[s] = n
        f = mm(n, wt_ref[...], NT).astype(BF16)
        qf_ref[s] = f[:, :QPAD]
        kvg_ref[s, 0, :, :KV] = f[:, QCOLS:]
        kvg_ref[s, 0, :, KV:] = jnp.zeros((own, KPAD - KV), BF16)
        if s == 0:
            enter("cx")
        kvs[s].first()
    kvs[0].relay()
    for s in range(seqs):
        cots[s].first()
    kvs[0].done()

    def step(t, carry):
        s = t // PAIRS
        pair = t % PAIRS

        @pl.when(t == PAIRS)
        def _():
            kvs[1].done()

        @pl.when(pair == 0)
        def _():
            for i in range(nblk):
                kvw_ref[s, pl.ds(i * own, own), :] = kvg_ref[s, slot_for(me, first + i)]
            bq_ref[...] = mm(qf_ref[s], rank_tile(QA, (QPAD, RQ * 128)))
            bk_ref[...] = mm(kvw_ref[s, :, :256], rank_tile(KA, (256, RK * 128)))
            bv_ref[...] = mm(kvw_ref[s, :, 128:384], rank_tile(KCOLS + KA - 128, (256, RK * 128)))
            fill_cap(me, first, dq_ref[s], dk_ref[s], cap_ref, nblk, own)

        qe = mm(qf_ref[s, :, :128], head_spread(pair, 0, RQ, (128, RQ * 128)))
        qsum = qe[:, :128] * bq_ref[:, :128]
        for r in range(1, RQ):
            cols = slice(r * 128, (r + 1) * 128)
            qsum = qsum + qe[:, cols] * bq_ref[:, cols]
        q = (qsum * (1.0 / RQ)).astype(BF16)
        ke = mm(kvw_ref[s, :, :128], head_spread(pair, 0, RK, (128, RK * 128)))
        ve = mm(kvw_ref[s, :, 128:256], head_spread(pair, KCOLS - 128, RK, (128, RK * 128)))
        k = ((ke[:, :128] * bk_ref[:, :128] + ke[:, 128:] * bk_ref[:, 128:]) * (1.0 / RK)).astype(BF16)
        v = ((ve[:, :128] * bv_ref[:, :128] + ve[:, 128:] * bv_ref[:, 128:]) * (1.0 / RK)).astype(BF16)
        q = q * jnp.asarray(DH ** (-0.5), BF16)
        q_ref[s, pair] = q
        k_ref[s, pair] = k
        v_ref[s, pair] = v
        cap = cap_ref[...]
        st = jnp.minimum(mm(k, stacked(q), NT), jnp.concatenate([cap, cap], axis=1))
        top = jnp.max(st, axis=0, keepdims=True)
        e = jnp.exp(st - top)
        total = jnp.sum(e, axis=0, keepdims=True)
        p = (e * (1.0 / total)).astype(BF16)
        lse_ref[s, pair] = top + jnp.log(total)
        full_ref[pair] = unstacked(mm(v, p, TN), own).astype(BF16)

        @pl.when(pair == PAIRS - 1)
        def _():
            att = jnp.concatenate([full_ref[i] for i in range(PAIRS)], axis=1)
            att_ref[s] = att
            hm = x_ref[s].astype(F32) + mm(att, wo_ref[...])
            hm_ref[s] = hm
            r = lax.rsqrt(jnp.mean(hm * hm, axis=-1, keepdims=True) + EPS)
            n2 = (hm * r * g2_ref[...]).astype(BF16)

            @pl.when(s == 0)
            def _():
                ng_ref[0] = n2
                norm.first()

            @pl.when(s == 1)
            def _():
                nb_ref[...] = n2

        @pl.when(t == 2)
        def _():
            kvs[1].relay()

        @pl.when(t == 6)
        def _():
            cots[0].relay()

        @pl.when(t == 13)
        def _():
            cots[1].relay()

        return carry

    lax.fori_loop(0, seqs * PAIRS, step, 0)
    norm.relay()
    for each in cots + [norm]:
        each.done()


def vmem():
    return pl.BlockSpec(memory_space=pltpu.VMEM)


def hbm():
    return pl.BlockSpec(memory_space=pl.ANY)


def fused(ident, limit=63):
    return pltpu.CompilerParams(
        vmem_limit_bytes=limit << 20, collective_id=ident, has_side_effects=True
    )


def fore(nblk, x, wt, wo, g1, g2, dq, dk, c):
    seqs, own, d = x.shape
    win = nblk * own
    shape = jax.ShapeDtypeStruct
    return pl.pallas_call(
        functools.partial(fore_kernel, nblk),
        in_specs=[vmem()] * 8,
        out_specs=[vmem()] * 12,
        out_shape=[
            shape((seqs, own, d), BF16), shape((seqs, own, QPAD), BF16),
            shape((seqs, win, KPAD), BF16), shape((seqs, own, d), BF16),
            shape((seqs, PAIRS, own, 128), BF16), shape((seqs, PAIRS, win, 128), BF16),
            shape((seqs, PAIRS, win, 128), BF16), shape((seqs, PAIRS, 1, 2 * own), F32),
            shape((seqs, own, d), F32), shape((4, own, d), BF16), shape((own, d), BF16),
            shape((seqs, 4, own, d), BF16),
        ],
        scratch_shapes=[
            pltpu.VMEM((seqs, 4, own, KPAD), BF16),
            pltpu.VMEM((own, RQ * 128), F32),
            pltpu.VMEM((win, RK * 128), F32),
            pltpu.VMEM((win, RK * 128), F32),
            pltpu.VMEM((win, own), F32),
            pltpu.VMEM((PAIRS, own, 128), BF16),
            pltpu.SemaphoreType.DMA((5, 3)),
            pltpu.SemaphoreType.DMA((5, 3)),
        ],
        compiler_params=fused(0),
        cost_estimate=cost(30e9, 30e6),
        name="fore",
    )(x, wt, wo, g1, g2, dq, dk, c)


SPLITS = ((0, 192), (192, 256), (448, 256))
EARLY = len(SPLITS) - 2
LANES = 512
FFN_NAMES = (("ynf", "ynf", "nyf"), ("ynf", "nyf", "ynf"), ("ynf", "nyf", "ynf"))


def chunk_units(h):
    return SPLITS[h][1] // 16 * (1024 // LANES) // 8


def late_at(h):
    return 24 * sum(chunk_units(i) for i in range(EARLY, h))


def own_at(h, m):
    return 3 * sum(chunk_units(i) for i in range(h)) + m * chunk_units(h)


MIDDLE_EVENTS = {
    (1, "m0"): ((0, 0, 0),),
    (1, "m1"): ((0, 2, 0),),
    (1, "m2"): ((0, 1, 0), (0, 0, 1),),
    (2, 0): ((0, 2, 1),),
    (2, 1): ((0, 1, 1), (0, 0, 2),),
    (2, 2): ((0, 2, 2),),
    (2, 3): ((0, 1, 2),),
}


def middle_kernel(
    n_ref, nb_ref, c_ref, wg_ref, wu_ref, wd_ref,
    dn_ref, ds_ref, ok_ref, os_ref, gw_ref, own_ref,
    hid_ref, dg_ref, du_ref, oa_ref, da_ref, op_ref, dp_ref, xs_ref, oc_ref, dc_ref, dx_ref, nn_ref, *refs,
):
    seqs, size, own, d = c_ref.shape
    srcs, refs = refs[:EARLY], refs[EARLY:]
    accs, refs = refs[:3 * EARLY], refs[3 * EARLY:]
    gots, refs = refs[:3 * EARLY], refs[3 * EARLY:]
    send, recv, xsend, xrecv, nsend, nrecv = refs
    downs = [
        send_to("c", dp_ref.at[s], dc_ref.at[s], xsend.at[0, s], xrecv.at[0, s]) for s in range(seqs)
    ]
    ups = [
        send_to("c", op_ref.at[s], oc_ref.at[s], xsend.at[1, s], xrecv.at[1, s]) for s in range(seqs)
    ]
    cross = send_to("x", xs_ref, dx_ref, xsend.at[2, 0], xrecv.at[2, 0])
    parts = {}
    for h in range(EARLY):
        for m in range(3):
            i = 3 * h + m
            u = chunk_units(h)
            parts[h, m] = Sum(
                FFN_NAMES[h][m], u, srcs[h], 8 * u * m, accs[i], gots[i], own_ref, own_at(h, m),
                send.at[i], recv.at[i], flat=True,
            )
    norms = [
        Gather(nn_ref, nsend.at[i], nrecv.at[i], pl.ds(i * (own // 4), own // 4)) for i in range(4)
    ]
    nn_ref[0] = nb_ref[...]
    enter("cxynf")
    for norm in norms:
        norm.first()

    def run(point):
        for h, m, k in MIDDLE_EVENTS.get(point, ()):
            parts[h, m].step(k)

    def hidden(s, b, n, span):
        c = c_ref[s, b]
        g = mm(wg_ref[span, :], n, NT)
        u = mm(wu_ref[span, :], n, NT)
        dh = mm(wd_ref[span, :], c, NT)
        sg = 1.0 / (1.0 + jnp.exp(-g))
        gs = g * sg
        cols = pl.ds(pl.multiple_of((s * size + b) * own, 128), own)
        hid_ref[span, cols] = (gs * u).astype(BF16)
        dg_ref[span, cols] = (dh * u * (sg * (1.0 + g * (1.0 - sg)))).astype(BF16)
        du_ref[span, cols] = (dh * gs).astype(BF16)

    def project(s, b, t):
        cols = pl.ds(pl.multiple_of((s * size + b) * own, 128), own)
        o = mm(hid_ref[:, cols], wd_ref[...], TN)
        dn = mm(dg_ref[:, cols], wg_ref[...], TN) + mm(du_ref[:, cols], wu_ref[...], TN)

        @pl.when(b >= 2)
        def _():
            op_ref[s, b - 2] = o.astype(BF16)
            dp_ref[s, b - 2] = dn.astype(BF16)

        @pl.when(b < 2)
        def _():
            oa_ref[s, b] = o.astype(BF16)
            da_ref[s, b] = dn

        @pl.when(t == 1)
        def _():
            downs[s].start()
            ups[s].start()

    def one(t, carry):
        b = size - 1 - t
        hidden(0, b, n_ref[b], slice(0, wd_ref.shape[0]))
        project(0, b, t)

        @pl.when(t == 1)
        def _():
            norms[0].relay()

        @pl.when(t == 2)
        def _():
            norms[1].relay()
            norms[2].relay()

        return carry

    lax.fori_loop(0, size, one, 0)
    norms[3].relay()
    downs[0].wait()
    xs_ref[...] = (da_ref[0, 1] + dc_ref[0, 1].astype(F32)).astype(BF16)
    cross.start()
    for norm in norms:
        norm.done()
    half = size * own
    for h, (off, rows) in enumerate(SPLITS):
        last = h == len(SPLITS) - 1
        early = h < EARLY

        def two(t, carry, h=h, off=off, rows=rows, last=last):
            b = size - 1 - t
            hidden(1, b, nn_ref[b], slice(off, off + rows))
            if last:
                project(1, b, t)
            for j in range(size):
                if (h, j) in MIDDLE_EVENTS:

                    @pl.when(t == j)
                    def _(j=j):
                        run((h, j))

            return carry

        lax.fori_loop(0, size, two, 0)
        count = rows // 16
        span = slice(off, off + rows)
        for m, (a_ref, b_refs) in enumerate((
            (dg_ref, (n_ref, nn_ref)), (du_ref, (n_ref, nn_ref)),
            (hid_ref, (c_ref.at[0], c_ref.at[1])),
        )):
            w = mm(a_ref[span, :half], b_refs[0][...].reshape(half, d))
            w = (w + mm(a_ref[span, half:], b_refs[1][...].reshape(half, d))).astype(BF16)
            to, start = (srcs[h], 0) if early else (gw_ref, late_at(h))
            for i in range(d // LANES):
                at = start + (m * (d // LANES) + i) * count
                piece = w[:, i * LANES:(i + 1) * LANES]
                to[pl.ds(at, count)] = piece.reshape(count, 16, LANES)
            if early:
                parts[h, m].begin()
            run((h, "m%d" % m))
    for s in range(seqs):
        ups[s].wait()
        ok_ref[s] = (oa_ref[s, 0].astype(F32) + oc_ref[s, 0].astype(F32)).astype(BF16)
        os_ref[s] = (oa_ref[s, 1].astype(F32) + oc_ref[s, 1].astype(F32)).astype(BF16)
    downs[1].wait()
    dn_ref[1] = da_ref[1, 0] + dc_ref[1, 0].astype(F32)
    ds_ref[...] = (da_ref[1, 1] + dc_ref[1, 1].astype(F32)).astype(BF16)
    run("end")
    cross.wait()
    dn_ref[0] = da_ref[0, 0] + dc_ref[0, 0].astype(F32) + dx_ref[...].astype(F32)


def middle(n, nb, c, wg, wu, wd):
    seqs, size, own, d = c.shape
    shape = jax.ShapeDtypeStruct
    flat = (wd.shape[0], seqs * size * own)
    u = [chunk_units(h) for h in range(EARLY) for _ in range(3)]
    unit = lambda k: pltpu.VMEM((k, 16, LANES), BF16)
    return pl.pallas_call(
        middle_kernel,
        in_specs=[vmem()] * 6,
        out_specs=[vmem()] * 6,
        out_shape=[
            shape((seqs, own, d), F32), shape((own, d), BF16), shape((seqs, own, d), BF16),
            shape((seqs, own, d), BF16), shape((late_at(len(SPLITS)), 16, LANES), BF16),
            shape((own_at(EARLY, 0), 16, LANES), BF16),
        ],
        scratch_shapes=[pltpu.VMEM(flat, BF16)] * 3
        + [pltpu.VMEM((seqs, 2, own, d), BF16), pltpu.VMEM((seqs, 2, own, d), F32)]
        + [pltpu.VMEM((seqs, 2, own, d), BF16)] * 2
        + [pltpu.VMEM((own, d), BF16)]
        + [pltpu.VMEM((seqs, 2, own, d), BF16)] * 2
        + [pltpu.VMEM((own, d), BF16), pltpu.VMEM((size, own, d), BF16)]
        + [unit(24 * chunk_units(h)) for h in range(EARLY)]
        + [unit(4 * k) for k in u]
        + [unit(7 * k) for k in u]
        + [
            pltpu.SemaphoreType.DMA((3 * EARLY, 3)),
            pltpu.SemaphoreType.DMA((3 * EARLY, 3)),
            pltpu.SemaphoreType.DMA((3, seqs)),
            pltpu.SemaphoreType.DMA((3, seqs)),
            pltpu.SemaphoreType.DMA((4, 3)),
            pltpu.SemaphoreType.DMA((4, 3)),
        ],
        compiler_params=fused(1),
        cost_estimate=cost(27e9, 30e6),
        name="middle",
    )(n, nb, c, wg, wu, wd)


FFN_UNITS = 3 * sum(r for _, r in SPLITS) // 16
SECOND = 3
AFTER_EVENTS = {
    0: (("F00", 3), ("F01", 3), ("F10", 0),),
    1: (("F02", 3),),
    2: (("F11", 0), ("F12", 0), ("F21", 0), ("F20", 0),),
    3: (("F00", 4), ("O0", 0), ("F01", 4),),
    4: (("O1", 0), ("F22", 0), ("F10", 1), ("F02", 4),),
    5: (("cross", 0), ("F12", 1), ("F11", 1),),
    6: (("F20", 1), ("F10", 2), ("F21", 1), ("O1", 1), ("F22", 1),),
    7: (("F12", 2), ("F00", 5), ("F11", 2),),
    8: (("F02", 5), ("F20", 2), ("O0", 1),),
    9: (("cross", 1), ("key", 0), ("F10", 3), ("F01", 5), ("F21", 2), ("emit", 0),),
    10: (("O0", 2), ("O1", 2), ("F22", 2),),
    11: (("F12", 3), ("O1", 3),),
    12: (("F11", 3),),
    13: (("F20", 3), ("F10", 4), ("emit", 1),),
    14: (("F21", 3), ("O0", 3), ("F11", 4), ("F22", 3),),
    15: (("O1", 4), ("F12", 4), ("F10", 5), ("O0", 4), ("F20", 4),),
    "T0": (("F21", 4),),
    "T1": (("O1", 5), ("K0", 0), ("O0", 5), ("K1", 0), ("F11", 5), ("F12", 5), ("F22", 4),),
    "T2": (("K0", 1), ("K2", 0), ("F20", 5), ("K3", 0), ("O1", 6),),
    "T3": (("K4", 0), ("F21", 5), ("O0", 6), ("K2", 1), ("K1", 1), ("F22", 5), ("K0", 2), ("O0", 7), ("O1", 7), ("K3", 1), ("K2", 2), ("K4", 1), ("K0", 3), ("K1", 2), ("K3", 2), ("K2", 3), ("K4", 2), ("K0", 4), ("O1", 8), ("K1", 3), ("O0", 8), ("K4", 3), ("K3", 3), ("K2", 4), ("K0", 5), ("K1", 4), ("K4", 4), ("K3", 4), ("O1", 9), ("K2", 5), ("K0", 6), ("K4", 5), ("K1", 5), ("K3", 5), ("O0", 9), ("K2", 6), ("K4", 6), ("K0", 7), ("K1", 6), ("K2", 7), ("K3", 6), ("K4", 7), ("K1", 7), ("K3", 7), ("K0", 8), ("K2", 8), ("K4", 8), ("K0", 9), ("K3", 8), ("K2", 9), ("K4", 9), ("K1", 8), ("K3", 9), ("K1", 9),),
}
OUT_PARTS = ("cyxnf", "cxnyf")
Q_PARTS = ("cxynf", "cnyfx")
K_PARTS = ("cxynf", "cynfx", "cnfxy")
K_LANES = 256
GAIN_ROW = 352


def attention_parts():
    return [(n, 1024) for n in OUT_PARTS] + [(n, 512) for n in Q_PARTS] + [(n, K_LANES) for n in K_PARTS]


def after_kernel(
    nblk, gw_ref, own_ref, dn_ref, ds_ref, ok_ref, os_ref, q_ref, k_ref, v_ref, lse_ref, dq_ref, dk_ref,
    qf_ref, kvw_ref, hm_ref, c_ref, wo_ref, g1_ref, g2_ref, att_ref, n1_ref, x_ref, wt_ref,
    out_ref, ig_ref, gr_ref, *refs,
):
    n_out, n_q = len(OUT_PARTS), len(Q_PARTS)
    n_fac = n_q + len(K_PARTS)
    or_refs, refs = refs[:n_out], refs[n_out:]
    fr_refs, refs = refs[:n_fac], refs[n_fac:]
    (bq_ref, bk_ref, bv_ref, cap_ref, da_ref, aq_ref, ak_ref, av_ref, tq_ref, tk_ref, tv_ref,
     dm_ref, late_ref, gq_ref, gkp_ref, gkc_ref, gkx_ref, ox_ref, kb_ref, vb_ref, dx_ref, gain_ref) = refs[:22]
    refs = refs[22:]
    n_late = 3 * (len(SPLITS) - EARLY)
    gots, refs = refs[:n_late], refs[n_late:]
    accs, refs = refs[:n_late], refs[n_late:]
    ob, refs = refs[:n_out], refs[n_out:]
    og, refs = refs[:n_out], refs[n_out:]
    oa, refs = refs[:n_out], refs[n_out:]
    fb, refs = refs[:n_fac], refs[n_fac:]
    fg, refs = refs[:n_fac], refs[n_fac:]
    fa, refs = refs[:n_fac], refs[n_fac:]
    send, recv, loc, gs, gr, kvsem, wsem = refs
    seqs, own, d = hm_ref.shape
    me = lax.axis_index("wide")
    first = me // 3

    sums = {}
    half = gr_ref.shape[0] // 2
    for h, (off, rows) in enumerate(SPLITS):
        for m in range(3):
            i = 3 * h + m
            u = chunk_units(h)
            late = h >= EARLY
            j = i - 3 * EARLY
            sums[h, m] = Sum(
                FFN_NAMES[h][m], u, gw_ref if late else None, late_at(h) + 8 * u * m,
                accs[j] if late else None, gots[j] if late else None,
                gr_ref, m * (half // 3) + off // 16, send.at[i], recv.at[i],
                local=loc.at[j] if late else None, top=half,
            )
    k0 = len(sums)
    outs = [
        Sum(names, 1, ob[g], 0, oa[g], og[g], or_refs[g], 0, send.at[k0 + g], recv.at[k0 + g])
        for g, names in enumerate(OUT_PARTS)
    ]
    k1 = k0 + n_out
    facs = [
        Sum(names, 1, fb[g], 0, fa[g], fg[g], fr_refs[g], 0, send.at[k1 + g], recv.at[k1 + g])
        for g, names in enumerate(Q_PARTS + K_PARTS)
    ]
    keys = [
        Scatter(gkp_ref.at[s], gkc_ref.at[s], gkx_ref.at[s], gs.at[s], gr.at[s])
        for s in range(seqs)
    ]
    crosses = [
        send_to("x", os_ref.at[s], ox_ref.at[s], gs.at[2 + s, 0], gr.at[2 + s, 0])
        for s in range(seqs)
    ]

    def fetch(t):
        return [
            pltpu.make_async_copy(a.at[t // PAIRS, t % PAIRS], b.at[t % 2], kvsem.at[i, t % 2])
            for i, (a, b) in enumerate(((k_ref, kb_ref), (v_ref, vb_ref)))
        ]

    for copy in fetch(0):
        copy.start()
    loads = [
        pltpu.make_async_copy(dn_ref, dm_ref, wsem.at[0]),
        pltpu.make_async_copy(c_ref, late_ref, wsem.at[1]),
    ]
    for copy in loads:
        copy.start()
    enter("cxynf")
    for h, m in sums:
        if h >= EARLY:
            sums[h, m].begin()
        else:
            sums[h, m].resume(own_ref, own_at(h, m))

    for copy in loads:
        copy.wait()
    down = send_to("x", ds_ref, dx_ref, gs.at[4, 0], gr.at[4, 0])
    down.start()
    gain_ref[...] = jnp.zeros((1, d), F32)

    def mids(s):
        hm = hm_ref[s]
        dn = dm_ref[s]
        r = lax.rsqrt(jnp.mean(hm * hm, axis=-1, keepdims=True) + EPS)
        z = dn * g2_ref[...]
        gain_ref[...] += jnp.sum(dn * hm * r, axis=0, keepdims=True)
        dm = (
            late_ref[s].astype(F32)
            + r * z
            - hm * (r * r * r) * jnp.mean(z * hm, axis=-1, keepdims=True)
        )
        dm_ref[s] = dm
        low = dm.astype(BF16)
        late_ref[s] = low
        da = mm(low, wo_ref[...], NT).astype(BF16)
        for i in range(PAIRS):
            da_ref[s, i] = da[:, i * 128:(i + 1) * 128]

    load_x = pltpu.make_async_copy(x_ref, late_ref, wsem.at[2])

    def second():
        for g in range(n_out):

            def rows(j, carry, g=g):
                cols = pl.ds(pl.multiple_of(g * 512 + j * 256, 128), 256)
                a = att_ref[:, :, cols].reshape(seqs * own, 256)
                w = mm(a, late_ref[...].reshape(seqs * own, d), TN).astype(BF16)
                ob[g][pl.ds(j * 16, 16)] = w.reshape(16, 16, d)
                return carry

            lax.fori_loop(0, 2, rows, 0)
            outs[g].begin()
        load_x.start()

    def finish(s):
        def fold(x, t):
            hi = x.astype(BF16)
            lo = (x - hi.astype(F32)).astype(BF16)
            return mm(hi, t, NT) + mm(lo, t, NT)

        gq = fold(tq_ref[...], rank_tile(QA, (QPAD, RQ * 128)))
        gq_ref[s, :, :128] = ((gq[:, :128] + aq_ref[...]) * (1.0 / RQ)).astype(BF16)
        gq_ref[s, :, 128:] = (gq[:, 128:] * (1.0 / RQ)).astype(BF16)
        gk = fold(tk_ref[...], rank_tile(KA, (KPAD, RK * 128)))
        gv = fold(tv_ref[...], rank_tile(KCOLS + KA, (KPAD, RK * 128)))
        gkv = gk + gv
        one = ((gkv[:, :128] + ak_ref[...]) * (1.0 / RK)).astype(BF16)
        two = ((gkv[:, 128:256] + av_ref[...]) * (1.0 / RK)).astype(BF16)
        three = (gkv[:, 256:] * (1.0 / RK)).astype(BF16)
        gkp_ref[s] = jnp.zeros_like(gkp_ref[s])
        for i in range(nblk):
            rows = slice(i * own, (i + 1) * own)
            slot = slot_for(me, first + i)
            gkp_ref[s, slot, :, :128] = one[rows]
            gkp_ref[s, slot, :, 128:256] = two[rows]
            gkp_ref[s, slot, :, 256:] = three[rows]

    def emit(s):
        crosses[s].wait()
        total = hm_ref[s] + (ok_ref[s].astype(F32) + ox_ref[s].astype(F32))
        out_ref[s] = total.astype(BF16)

    named = {"F%d%d" % key: part for key, part in sums.items()}
    named.update({"O%d" % g: part for g, part in enumerate(outs)})
    named.update({"K%d" % g: part for g, part in enumerate(facs)})

    def run(point):
        for name, k in AFTER_EVENTS.get(point, ()):
            if name == "cross":
                crosses[k].start()
            elif name == "emit":
                emit(k)
            elif name == "key":
                keys[k].cross()
            else:
                named[name].step(k)

    def step(t, carry):
        s = t // PAIRS
        pair = t % PAIRS
        slot = t % 2

        @pl.when(t < seqs * PAIRS - 1)
        def _():
            for copy in fetch(t + 1):
                copy.start()

        @pl.when(pair == 0)
        def _():
            bq_ref[...] = mm(qf_ref[s], rank_tile(QA, (QPAD, RQ * 128)))
            bk_ref[...] = mm(kvw_ref[s, :, :256], rank_tile(KA, (256, RK * 128)))
            bv_ref[...] = mm(kvw_ref[s, :, 128:384], rank_tile(KCOLS + KA - 128, (256, RK * 128)))
            fill_cap(me, first, dq_ref[s], dk_ref[s], cap_ref, nblk, own)
            for ref in (aq_ref, ak_ref, av_ref, tq_ref, tk_ref, tv_ref):
                ref[...] = jnp.zeros_like(ref)

        @pl.when(t == SECOND)
        def _():
            down.wait()
            dm_ref[1] += dx_ref[...].astype(F32)

        @pl.when((t == 0) | (t == SECOND))
        def _():
            mids(t // SECOND)

        @pl.when(t == SECOND)
        def _():
            second()

        for copy in fetch(t):
            copy.wait()
        q = q_ref[s, pair]
        k = kb_ref[slot]
        v = vb_ref[slot]
        qs = stacked(q)
        da = stacked(da_ref[s, pair])
        cap = cap_ref[...]
        st = jnp.minimum(mm(k, qs, NT), jnp.concatenate([cap, cap], axis=1))
        p = jnp.exp(st - lse_ref[s, pair])
        dp = mm(v, da, NT)
        delta = jnp.sum(p * dp, axis=0, keepdims=True)
        ds = (p * (dp - delta)).astype(BF16)
        dv = mm(p.astype(BF16), da)
        dk = mm(ds, qs)
        dq = unstacked(mm(k, ds, TN), own) * (DH ** (-0.5))

        eq = head_spread(pair, 0, RQ, (128, RQ * 128))
        qe = mm(qf_ref[s, :, :128], eq)
        dq6 = jnp.concatenate([dq] * RQ, axis=1)
        tq_ref[...] += dq6 * qe
        aq_ref[...] += mm((dq6 * bq_ref[...]).astype(BF16), eq, NT)
        ek = head_spread(pair, 0, RK, (128, RK * 128))
        ev = head_spread(pair, KCOLS - 128, RK, (128, RK * 128))
        ke = mm(kvw_ref[s, :, :128], ek)
        ve = mm(kvw_ref[s, :, 128:256], ev)
        dk2 = jnp.concatenate([dk] * RK, axis=1)
        dv2 = jnp.concatenate([dv] * RK, axis=1)
        tk_ref[...] += dk2 * ke
        tv_ref[...] += dv2 * ve
        ak_ref[...] += mm((dk2 * bk_ref[...]).astype(BF16), ek, NT)
        av_ref[...] += mm((dv2 * bv_ref[...]).astype(BF16), ev, NT)

        @pl.when(pair == PAIRS - 1)
        def _():
            finish(s)

        @pl.when(t == PAIRS - 1)
        def _():
            keys[0].core()

        for when in range(seqs * PAIRS):
            if when in AFTER_EVENTS:

                @pl.when(t == when)
                def _(when=when):
                    run(when)

        return carry

    lax.fori_loop(0, seqs * PAIRS, step, 0)
    keys[1].core()
    n1 = n1_ref[...].reshape(seqs * own, d)
    gq = gq_ref[...].reshape(seqs * own, QPAD)
    w = mm(gq, n1, TN).astype(BF16)
    for g in range(n_q):
        fb[g][...] = w[:, g * 512:(g + 1) * 512].reshape(32, 16, 512)
        facs[g].begin()
    dn1 = mm(gq[:, :QCOLS], wt_ref[:QCOLS, :])
    run("T0")
    keys[1].cross()
    run("T1")
    gkv0 = keys[0].total().astype(BF16)
    gkv = jnp.concatenate([gkv0, keys[1].total().astype(BF16)], axis=0)
    gf = mm(gkv, n1, TN)

    def spread(value, only):
        for g in only:
            for i in range(8):
                for j in range(d // K_LANES):
                    row = 16 * (8 * g + i)
                    piece = value[row:row + 16, j * K_LANES:(j + 1) * K_LANES]
                    fb[n_q + g][4 * i + j] = piece.astype(BF16)
            facs[n_q + g].begin()

    last = len(K_PARTS) - 1
    spread(gf, range(last))
    dn1 = dn1 + mm(gkv[:, :KV], wt_ref[QCOLS:, :])
    load_x.wait()
    hin = late_ref[...].reshape(seqs * own, d).astype(F32)
    r1 = lax.rsqrt(jnp.mean(hin * hin, axis=-1, keepdims=True) + EPS)
    z1 = dn1 * g1_ref[...]
    gain_one = jnp.sum(dn1 * hin * r1, axis=0, keepdims=True)
    gf = jnp.concatenate(
        [gf[:GAIN_ROW], gain_one, gain_ref[...], gf[GAIN_ROW + 2:]], axis=0
    )
    spread(gf, (last,))
    run("T2")
    grad = r1 * z1 - hin * (r1 * r1 * r1) * jnp.mean(z1 * hin, axis=-1, keepdims=True)
    ig_ref[...] = (dm_ref[...].reshape(seqs * own, d) + grad).astype(BF16).reshape(seqs, own, d)
    run("T3")


def after(nblk, gw, own_sums, dn, ds, ok, os, q, k, v, lse, dq, dk, qf, kvw, hm, c, wo, g1, g2, att, n1, x, wt):
    seqs, own, d = hm.shape
    win = nblk * own
    shape = jax.ShapeDtypeStruct
    far = (0, 2, 3, 5, 7, 8, 15, 21)
    results = [shape((32, 16, lanes), BF16) for _, lanes in attention_parts()]
    total = 3 * len(SPLITS) + len(results)
    args = (gw, own_sums, dn, ds, ok, os, q, k, v, lse, dq, dk, qf, kvw, hm, c, wo, g1, g2, att, n1, x, wt)
    res = pl.pallas_call(
        functools.partial(after_kernel, nblk),
        in_specs=[hbm() if i in far else vmem() for i in range(len(args))],
        out_specs=[vmem()] * (3 + len(results)),
        out_shape=[
            shape((seqs, own, d), BF16), shape((seqs, own, d), BF16),
            shape((2 * FFN_UNITS, 16, LANES), BF16),
        ] + results,
        scratch_shapes=[
            pltpu.VMEM((own, RQ * 128), F32),
            pltpu.VMEM((win, RK * 128), F32),
            pltpu.VMEM((win, RK * 128), F32),
            pltpu.VMEM((win, own), F32),
            pltpu.VMEM((seqs, PAIRS, own, 128), BF16),
            pltpu.VMEM((own, 128), F32),
            pltpu.VMEM((win, 128), F32),
            pltpu.VMEM((win, 128), F32),
            pltpu.VMEM((own, RQ * 128), F32),
            pltpu.VMEM((win, RK * 128), F32),
            pltpu.VMEM((win, RK * 128), F32),
            pltpu.VMEM((seqs, own, d), F32),
            pltpu.VMEM((seqs, own, d), BF16),
            pltpu.VMEM((seqs, own, QPAD), BF16),
            pltpu.VMEM((seqs, 4, own, KPAD), BF16),
            pltpu.VMEM((seqs, 2, own, KPAD), BF16),
            pltpu.VMEM((seqs, own, KPAD), BF16),
            pltpu.VMEM((seqs, own, d), BF16),
            pltpu.VMEM((2, win, 128), BF16),
            pltpu.VMEM((2, win, 128), BF16),
            pltpu.VMEM((own, d), BF16),
            pltpu.VMEM((1, d), F32),
        ]
        + [
            pltpu.VMEM((n * chunk_units(h), 16, LANES), BF16)
            for n in (7, 4) for h in range(EARLY, len(SPLITS)) for _ in range(3)
        ]
        + [pltpu.VMEM((n, 16, 1024), BF16) for n in (32, 31, 16) for _ in OUT_PARTS]
        + [
            pltpu.VMEM((n, 16, lanes), BF16) for n in (32, 31, 16)
            for _, lanes in attention_parts()[len(OUT_PARTS):]
        ]
        + [
            pltpu.SemaphoreType.DMA((total, 10)),
            pltpu.SemaphoreType.DMA((total, 10)),
            pltpu.SemaphoreType.DMA((3 * (len(SPLITS) - EARLY),)),
            pltpu.SemaphoreType.DMA((5, 2)),
            pltpu.SemaphoreType.DMA((5, 2)),
            pltpu.SemaphoreType.DMA((2, 2)),
            pltpu.SemaphoreType.DMA((3,)),
        ],
        compiler_params=fused(2),
        cost_estimate=cost(60e9, 60e6),
        name="after",
    )(*args)
    n = 3 + len(OUT_PARTS)
    return res[0], res[1], res[2], res[3:n], res[n:]


def last_kernel(
    out_ref, ig_ref, gr_ref, o0_ref, o1_ref, q0_ref, q1_ref, k0_ref, k1_ref, k2_ref,
    output_ref, grad_ref, gate_ref, up_ref, down_ref, go_ref, gf_ref, gain_ref,
):
    step = pl.program_id(0)
    output_ref[...] = out_ref[...]
    grad_ref[...] = ig_ref[...]
    units = gr_ref.shape[2]
    for m, ref in enumerate((gate_ref, up_ref, down_ref)):
        for i in range(2):
            ref[:, i * LANES:(i + 1) * LANES] = gr_ref[i, m].reshape(16 * units, LANES).astype(F32)
    for g, ref in enumerate((o0_ref, o1_ref)):

        @pl.when(step // 2 == g)
        def _(ref=ref):
            half = pl.ds((step % 2) * 16, 16)
            go_ref[...] = ref[half].reshape(256, 1024).astype(F32)

    rows = pl.ds(pl.multiple_of(step * 128, 128), 128)
    for i, ref in enumerate((q0_ref, q1_ref)):
        gf_ref[rows, i * 512:(i + 1) * 512] = ref[pl.ds(step * 8, 8)].reshape(128, 512).astype(F32)

    @pl.when(step == 3)
    def _():
        for g, ref in enumerate((k0_ref, k1_ref, k2_ref)):
            count = min(KV - 128 * g, 128) // 16

            def rows(i, carry, g=g, ref=ref):
                at = pl.ds(pl.multiple_of(QCOLS + 128 * g + 16 * i, 16), 16)
                for j in range(1024 // K_LANES):
                    cols = slice(j * K_LANES, (j + 1) * K_LANES)
                    gf_ref[at, cols] = ref[4 * i + j].astype(F32)
                return carry

            lax.fori_loop(0, count, rows, 0)
        unit = (GAIN_ROW - 256) // 16
        for j in range(1024 // K_LANES):
            cols = slice(j * K_LANES, (j + 1) * K_LANES)
            gain_ref[:, cols] = k2_ref[4 * unit + j].astype(F32)[:8]


def finish_all(output, grad, gr, go, gf, cols):
    seqs, own, d = output.shape
    ff = 16 * gr.shape[0] // 6
    gr = gr.reshape(2, 3, ff // 16, 16, LANES)
    steps = 4
    shape = jax.ShapeDtypeStruct
    whole = lambda a: pl.BlockSpec(a.shape, lambda i, a=a: (0,) * len(a.shape))
    tokens = pl.BlockSpec((seqs, own // steps, d), lambda i: (0, i, 0))
    outs = [
        shape(output.shape, BF16), shape(output.shape, BF16), shape((ff, d), F32),
        shape((ff, d), F32), shape((ff, d), F32), shape((d, d), F32), shape((cols, d), F32),
        shape((8, d), F32),
    ]
    rows = lambda n: pl.BlockSpec((n // steps, d), lambda i: (i, 0))
    return pl.pallas_call(
        last_kernel,
        grid=(steps,),
        in_specs=[
            tokens, tokens,
            pl.BlockSpec((2, 3, ff // 16 // steps, 16, LANES), lambda i: (0, 0, i, 0, 0)),
        ] + [whole(a) for a in list(go) + list(gf)],
        out_specs=[tokens, tokens, rows(ff), rows(ff), rows(ff), rows(d), whole(outs[6]), whole(outs[7])],
        out_shape=outs,
        compiler_params=params(),
        cost_estimate=cost(1e6, 30e6),
        name="last",
    )(output, grad, gr, *go, *gf)


def fused_body(
    tokens, doc_ids, factor_weight, output_weight, norm_one, norm_two,
    gate_weight, up_weight, down_weight, cotangent,
):
    seqs, own, d = tokens.shape
    me = lax.axis_index("wide")
    nblk = -(-(MAX_DOC - 1) // own) + 1
    first = me // 3
    g1 = norm_one[None]
    g2 = norm_two[None]
    dq = lax.dynamic_slice_in_dim(doc_ids, me * own, own, 1)[:, None, :]
    dk = lax.dynamic_slice_in_dim(doc_ids, first * own, nblk * own, 1)[:, :, None]
    wt = factor_weight.T
    n1, qf, kvw, att, q, k, v, lse, hm, ng, nb, cg = fore(
        nblk, tokens, wt, output_weight, g1, g2, dq, dk, cotangent
    )
    dn, ds, ok, os, gw, own_sums = middle(ng, nb, cg, gate_weight.T, up_weight.T, down_weight)
    output, input_grad, gr, go, gf = after(
        nblk, gw, own_sums, dn, ds, ok, os, q, k, v, lse, dq, dk, qf, kvw, hm, cotangent, output_weight,
        g1, g2, att, n1, tokens, wt,
    )
    output, input_grad, gate, up, down, out, fac, gain = finish_all(
        output, input_grad, gr, go, gf, factor_weight.shape[1]
    )
    return output, input_grad, fac.T, out, gain[0], gain[1], gate.T, up.T, down


def swap(x, axis, size, bit):
    return lax.ppermute(x, axis, [(i, i ^ bit) for i in range(size)])


def steps_of(size):
    bits, b = [], size // 2
    while b:
        bits.append(b)
        b //= 2
    return bits


def gather(x, size):
    buf = x[None]
    for bit in steps_of(size):
        buf = jnp.concatenate([buf, swap(buf, "wide", size, bit)], axis=0)
    return buf


def order_of(size):
    order = [0]
    for bit in steps_of(size):
        order = order + [o ^ bit for o in order]
    return order


def scatter(parts, size):
    for bit in reversed(steps_of(size)):
        half = parts.shape[0] // 2
        got = swap(parts[half:], "wide", size, bit)
        total = parts[:half].astype(F32) + got.astype(F32)
        parts = total if half == 1 else total.astype(BF16)
    return parts[0]


def body(
    tokens, doc_ids, factor_weight, output_weight, norm_one, norm_two,
    gate_weight, up_weight, down_weight, cotangent,
):
    seqs, own, d = tokens.shape
    full_len = doc_ids.shape[1]
    size = full_len // own
    me = lax.axis_index("wide")
    left = min(-(-(MAX_DOC - 1) // own), size - 1)
    nblk = left + 1
    start = jnp.maximum(me - left, 0)
    order = order_of(size)
    slot_of = [order.index(j) for j in range(size)]
    slots = jnp.asarray(slot_of, jnp.int32)
    blocks = start + jnp.arange(nblk, dtype=jnp.int32)
    scalars = jnp.concatenate(
        [me[None].astype(jnp.int32), (me - blocks) * own, slots[me ^ blocks]]
    ).astype(jnp.int32)
    g1 = norm_one[None]
    g2 = norm_two[None]

    n1, qf, kvf = front(tokens.reshape(seqs * own, d), factor_weight, g1)
    qf = qf.reshape(seqs, own, QPAD)
    kvg = gather(kvf.reshape(seqs, own, KPAD), size)
    doc_query = lax.dynamic_slice_in_dim(doc_ids, me * own, own, 1)
    doc_key = lax.dynamic_slice_in_dim(doc_ids, start * own, nblk * own, 1)
    cots = [gather(cotangent[s], size) for s in range(seqs)]

    fwd = []
    for s in range(seqs):
        dq = doc_query[s][None, :]
        dk = doc_key[s][:, None]
        fwd.append(
            (dq, dk)
            + tuple(attend(nblk, scalars, qf[s], kvg[:, s], dq, dk, tokens[s], output_weight, g2))
        )
    prev = None
    outs, dns = [], []
    for s in range(seqs):
        n2 = gather(fwd[s][8], size)
        res = ffn(n2, cots[s], gate_weight, up_weight, down_weight, prev, s == seqs - 1)
        outs.append(res[0])
        dns.append(res[1])
        prev = res[2:]
    grads = [lax.psum(g, "rows").astype(F32) for g in prev]

    output, mids, lows, gain_two, gqs, gkvs = [], [], [], 0.0, [], []
    for s in range(seqs):
        dq, dk, att, q, k, v, lse, hm, n2, kvw = fwd[s]
        dn = scatter(dns[s], size)
        dm, low, gain, gq, gkv = back(
            nblk, size, scalars, q, k, v, lse, dq, dk, qf[s], kvw, dn, hm,
            cotangent[s], output_weight, g2,
        )
        output.append((hm + scatter(outs[s], size)).astype(BF16))
        mids.append(dm)
        lows.append(low)
        gqs.append(gq)
        gkvs.append(gkv)
        gain_two = gain_two + gain
    att_all = jnp.stack([f[2] for f in fwd]).reshape(seqs * own, d)
    grad_out = mm(att_all, jnp.stack(lows).reshape(seqs * own, d), TN)
    gkv = scatter(jnp.stack(gkvs, axis=1), size).astype(BF16)
    dfac = jnp.concatenate([jnp.stack(gqs)[..., :QCOLS], gkv[..., :KV]], axis=-1)
    dfac = dfac.reshape(seqs * own, -1)
    grad_factors = mm(n1, dfac, TN)
    dn1 = mm(dfac, factor_weight, NT)
    hin = tokens.reshape(seqs * own, d).astype(F32)
    r1 = lax.rsqrt(jnp.mean(hin * hin, axis=-1, keepdims=True) + EPS)
    z1 = dn1 * g1
    gain_one = jnp.sum(dn1 * hin * r1, axis=0)
    grad_norm = r1 * z1 - hin * (r1 * r1 * r1) * jnp.mean(z1 * hin, axis=-1, keepdims=True)
    input_grad = (jnp.stack(mids).reshape(seqs * own, d) + grad_norm).astype(BF16)
    parts = [grad_out, grad_factors.T, gain_one[None], gain_two]
    packed = jnp.concatenate([p.astype(BF16) for p in parts], axis=0)
    packed = lax.psum(packed, ("rows", "wide")).astype(F32)
    fac = grad_factors.shape[1]
    return (
        jnp.stack(output),
        input_grad.reshape(seqs, own, d),
        packed[d:d + fac].T,
        packed[:d],
        packed[d + fac],
        packed[d + fac + 1],
        grads[0],
        grads[1],
        grads[2],
    )


def solution(mesh):
    placed = (
        P("rows", "wide", None), P("rows", None), P(), P(), P(), P(),
        P(None, "wide"), P(None, "wide"), P("wide", None), P("rows", "wide", None),
    )
    small = mesh.shape["rows"] == 8 and mesh.shape["wide"] == 4
    return jax.shard_map(
        fused_body if small else body,
        mesh=mesh,
        in_specs=placed,
        out_specs=(
            P("rows", "wide", None), P("rows", "wide", None), P(), P(), P(), P(),
            P(None, "wide"), P(None, "wide"), P("wide", None),
        ),
        check_vma=False,
    )
```

```python
import functools

import jax
import jax.numpy as jnp
from jax import lax
from jax.experimental import pallas as pl
from jax.experimental.pallas import tpu as pltpu
from jax.sharding import PartitionSpec as P

H = 16
DH = 64
RQ = 6
RK = 2
MAX_DOC = 512
EPS = 1e-06
NEG = -1000000000.0
BIG = 3.0e38

QA = H * RQ
QCOLS = QA + RQ * DH
KA = H * RK
KCOLS = KA + RK * DH
KV = 2 * KCOLS
QPAD = 512
KPAD = 384
PAIRS = H // 2

F32 = jnp.float32
BF16 = jnp.bfloat16

NN = (((1,), (0,)), ((), ()))
NT = (((1,), (1,)), ((), ()))
TN = (((0,), (0,)), ((), ()))


def mm(a, b, dims=NN):
    return lax.dot_general(a, b, dims, preferred_element_type=F32)


def params(vmem_mb=60):
    return pltpu.CompilerParams(vmem_limit_bytes=vmem_mb << 20)


def cost(flops, nbytes):
    return pl.CostEstimate(flops=int(flops), bytes_accessed=int(nbytes), transcendentals=0)


def selection(shape, rule):
    row = lax.broadcasted_iota(jnp.int32, shape, 0)
    col = lax.broadcasted_iota(jnp.int32, shape, 1)
    return jnp.where(rule(row, col), 1.0, 0.0).astype(BF16)


def head_spread(pair, base, rank, shape):
    def rule(row, col):
        r = col // 128
        lane = col - r * 128
        head = 2 * pair + jnp.where(lane >= DH, 1, 0)
        return row == base + head * rank + r

    return selection(shape, rule)


def rank_tile(base, shape):
    def rule(row, col):
        r = col // 128
        lane = col - r * 128
        return row == base + r * DH + jnp.where(lane >= DH, lane - DH, lane)

    return selection(shape, rule)


def front_kernel(x_ref, w_ref, g_ref, n_ref, q_ref, kv_ref):
    x = x_ref[...].astype(F32)
    r = lax.rsqrt(jnp.mean(x * x, axis=-1, keepdims=True) + EPS)
    n = (x * r * g_ref[...]).astype(BF16)
    n_ref[...] = n
    f = mm(n, w_ref[...]).astype(BF16)
    q_ref[...] = f[:, :QPAD]
    kv_ref[:, :KV] = f[:, QCOLS:]
    kv_ref[:, KV:] = jnp.zeros((f.shape[0], KPAD - KV), BF16)


def front(x, w, gain):
    rows, d = x.shape
    blk = 256 if rows % 256 == 0 else rows
    return pl.pallas_call(
        front_kernel,
        grid=(rows // blk,),
        in_specs=[
            pl.BlockSpec((blk, d), lambda i: (i, 0)),
            pl.BlockSpec(w.shape, lambda i: (0, 0)),
            pl.BlockSpec((1, d), lambda i: (0, 0)),
        ],
        out_specs=[
            pl.BlockSpec((blk, d), lambda i: (i, 0)),
            pl.BlockSpec((blk, QPAD), lambda i: (i, 0)),
            pl.BlockSpec((blk, KPAD), lambda i: (i, 0)),
        ],
        out_shape=[
            jax.ShapeDtypeStruct((rows, d), BF16),
            jax.ShapeDtypeStruct((rows, QPAD), BF16),
            jax.ShapeDtypeStruct((rows, KPAD), BF16),
        ],
        compiler_params=params(),
        cost_estimate=cost(2 * rows * d * 800, rows * d * 6 + d * 1600),
        name="front",
    )(x, w, gain)


def make_cap(s_ref, dq_ref, dk_ref, cap_ref, nblk, own):
    dq = dq_ref[...]
    for i in range(nblk):
        rows = pl.ds(i * own, own)
        key = lax.broadcasted_iota(jnp.int32, (own, own), 0)
        query = lax.broadcasted_iota(jnp.int32, (own, own), 1) + s_ref[1 + i]
        ok = (dk_ref[rows, :] == dq) & (key <= query)
        cap_ref[rows, :] = jnp.where(ok, BIG, NEG)


def stacked(x):
    lane = lax.broadcasted_iota(jnp.int32, x.shape, 1)
    zero = jnp.zeros_like(x)
    return jnp.concatenate(
        [jnp.where(lane < DH, x, zero), jnp.where(lane >= DH, x, zero)], axis=0
    )


def unstacked(xt, own):
    pair = jnp.concatenate([xt[:DH, :own], xt[DH:, own:]], axis=0)
    return pair.T


def key_parts(kvf_ref, pair):
    ek = head_spread(pair, 0, RK, (128, RK * 128))
    ev = head_spread(pair, KCOLS - 128, RK, (128, RK * 128))
    ke = mm(kvf_ref[:, :128], ek)
    ve = mm(kvf_ref[:, 128:256], ev)
    return ke, ve


def tile_keys(kvf_ref, bk_ref, bv_ref):
    bk_ref[...] = mm(kvf_ref[:, :256], rank_tile(KA, (256, RK * 128)))
    bv_ref[...] = mm(kvf_ref[:, 128:384], rank_tile(KCOLS + KA - 128, (256, RK * 128)))


def attend_kernel(
    nblk, s_ref, qf_ref, kvg_ref, dq_ref, dk_ref, x_ref, wo_ref, g_ref,
    att_ref, q_ref, k_ref, v_ref, lse_ref, hm_ref, n_ref, kvw_ref,
    bq_ref, bk_ref, bv_ref, cap_ref, full_ref,
):
    pair = pl.program_id(0)
    own = qf_ref.shape[0]

    @pl.when(pair == 0)
    def _():
        for i in range(nblk):
            kvw_ref[pl.ds(i * own, own), :] = kvg_ref[s_ref[1 + nblk + i]]
        bq_ref[...] = mm(qf_ref[...], rank_tile(QA, (QPAD, RQ * 128)))
        tile_keys(kvw_ref, bk_ref, bv_ref)
        make_cap(s_ref, dq_ref, dk_ref, cap_ref, nblk, own)

    qe = mm(qf_ref[:, :128], head_spread(pair, 0, RQ, (128, RQ * 128)))
    qsum = qe[:, :128] * bq_ref[:, :128]
    for r in range(1, RQ):
        cols = slice(r * 128, (r + 1) * 128)
        qsum = qsum + qe[:, cols] * bq_ref[:, cols]
    q = (qsum * (1.0 / RQ)).astype(BF16)
    ke, ve = key_parts(kvw_ref, pair)
    k = ((ke[:, :128] * bk_ref[:, :128] + ke[:, 128:] * bk_ref[:, 128:]) * (1.0 / RK)).astype(BF16)
    v = ((ve[:, :128] * bv_ref[:, :128] + ve[:, 128:] * bv_ref[:, 128:]) * (1.0 / RK)).astype(BF16)
    q = q * jnp.asarray(DH ** (-0.5), BF16)
    q_ref[...] = q
    k_ref[...] = k
    v_ref[...] = v
    cap = cap_ref[...]
    st = jnp.minimum(mm(k, stacked(q), NT), jnp.concatenate([cap, cap], axis=1))
    top = jnp.max(st, axis=0, keepdims=True)
    e = jnp.exp(st - top)
    total = jnp.sum(e, axis=0, keepdims=True)
    p = (e * (1.0 / total)).astype(BF16)
    lse_ref[0] = top + jnp.log(total)
    att = unstacked(mm(v, p, TN), own).astype(BF16)
    att_ref[...] = att
    full_ref[pair] = att

    @pl.when(pair == pl.num_programs(0) - 1)
    def _():
        hm = x_ref[...].astype(F32)
        att_all = jnp.concatenate([full_ref[i] for i in range(PAIRS)], axis=1)
        hm = hm + mm(att_all, wo_ref[...])
        hm_ref[...] = hm
        r = lax.rsqrt(jnp.mean(hm * hm, axis=-1, keepdims=True) + EPS)
        n_ref[...] = (hm * r * g_ref[...]).astype(BF16)


def attend(nblk, scalars, qf, kvg, dq, dk, x, wo, gain):
    own, d = x.shape
    win = nblk * own
    whole = lambda a: pl.BlockSpec(a.shape, lambda p, a=a: (0,) * a.ndim)
    col = lambda rows: pl.BlockSpec((rows, 128), lambda p: (0, p))
    return pl.pallas_call(
        functools.partial(attend_kernel, nblk),
        grid=(PAIRS,),
        in_specs=[pl.BlockSpec(memory_space=pltpu.SMEM)]
        + [whole(a) for a in (qf, kvg, dq, dk, x, wo, gain)],
        out_specs=[
            col(own), col(own), col(win), col(win),
            pl.BlockSpec((1, 1, 2 * own), lambda p: (p, 0, 0)),
            pl.BlockSpec((own, d), lambda p: (0, 0)),
            pl.BlockSpec((own, d), lambda p: (0, 0)),
            pl.BlockSpec((win, KPAD), lambda p: (0, 0)),
        ],
        out_shape=[
            jax.ShapeDtypeStruct((own, d), BF16),
            jax.ShapeDtypeStruct((own, d), BF16),
            jax.ShapeDtypeStruct((win, d), BF16),
            jax.ShapeDtypeStruct((win, d), BF16),
            jax.ShapeDtypeStruct((PAIRS, 1, 2 * own), F32),
            jax.ShapeDtypeStruct((own, d), F32),
            jax.ShapeDtypeStruct((own, d), BF16),
            jax.ShapeDtypeStruct((win, KPAD), BF16),
        ],
        scratch_shapes=[
            pltpu.VMEM((own, RQ * 128), F32),
            pltpu.VMEM((win, RK * 128), F32),
            pltpu.VMEM((win, RK * 128), F32),
            pltpu.VMEM((win, own), F32),
            pltpu.VMEM((PAIRS, own, 128), BF16),
        ],
        compiler_params=params(),
        cost_estimate=cost(12e9, 12e6),
        name="attend",
    )(scalars, qf, kvg, dq, dk, x, wo, gain)


def ffn_kernel(has_prev, bf16_out, *refs):
    if has_prev:
        n_ref, c_ref, wg_ref, wu_ref, wd_ref, pg_ref, pu_ref, pd_ref = refs[:8]
        refs = refs[8:]
    else:
        n_ref, c_ref, wg_ref, wu_ref, wd_ref = refs[:5]
        refs = refs[5:]
    o_ref, dn_ref, og_ref, ou_ref, od_ref = refs[:5]
    if bf16_out:
        ag_ref, au_ref, ad_ref = refs[5:]
    else:
        ag_ref, au_ref, ad_ref = og_ref, ou_ref, od_ref
    step = pl.program_id(0)

    @pl.when(step == 0)
    def _():
        if has_prev:
            ag_ref[...] = pg_ref[...]
            au_ref[...] = pu_ref[...]
            ad_ref[...] = pd_ref[...]
        else:
            ag_ref[...] = jnp.zeros_like(ag_ref)
            au_ref[...] = jnp.zeros_like(au_ref)
            ad_ref[...] = jnp.zeros_like(ad_ref)

    n = n_ref[0]
    c = c_ref[0]
    wg, wu, wd = wg_ref[...], wu_ref[...], wd_ref[...]
    g = mm(n, wg)
    u = mm(n, wu)
    dh = mm(c, wd, NT)
    s = 1.0 / (1.0 + jnp.exp(-g))
    gs = g * s
    hid = (gs * u).astype(BF16)
    dg = (dh * u * (s * (1.0 + g * (1.0 - s)))).astype(BF16)
    du = (dh * gs).astype(BF16)
    o_ref[0] = mm(hid, wd).astype(BF16)
    dn_ref[0] = (mm(dg, wg, NT) + mm(du, wu, NT)).astype(BF16)
    ag_ref[...] += mm(n, dg, TN)
    au_ref[...] += mm(n, du, TN)
    ad_ref[...] += mm(hid, c, TN)
    if bf16_out:

        @pl.when(step == pl.num_programs(0) - 1)
        def _():
            og_ref[...] = ag_ref[...].astype(BF16)
            ou_ref[...] = au_ref[...].astype(BF16)
            od_ref[...] = ad_ref[...].astype(BF16)


def ffn(n, c, wg, wu, wd, prev, last):
    w, own, d = n.shape
    ff = wg.shape[1]
    one = lambda a: pl.BlockSpec(
        a.shape, lambda i, a=a: (0,) * a.ndim, pipeline_mode=pl.Buffered(1)
    )
    blk = pl.BlockSpec((1, own, d), lambda i: (i, 0, 0))
    dt = BF16 if last else F32
    args = [n, c, wg, wu, wd] + list(prev or [])
    shapes = [(d, ff), (d, ff), (ff, d)]
    return pl.pallas_call(
        functools.partial(ffn_kernel, bool(prev), last),
        grid=(w,),
        in_specs=[blk, blk] + [one(a) for a in args[2:]],
        out_specs=[blk, blk] + [
            pl.BlockSpec(s, lambda i: (0, 0), pipeline_mode=pl.Buffered(1)) for s in shapes
        ],
        out_shape=[jax.ShapeDtypeStruct(n.shape, BF16)] * 2
        + [jax.ShapeDtypeStruct(s, dt) for s in shapes],
        scratch_shapes=[pltpu.VMEM(s, F32) for s in shapes] if last else [],
        compiler_params=params(),
        cost_estimate=cost(18 * w * own * d * ff, 20 * w * own * d),
        name="ffn",
    )(*args)


def back_kernel(
    nblk, s_ref, q_ref, k_ref, v_ref, lse_ref, dq_ref, dk_ref, qf_ref, kvw_ref,
    dn_ref, hm_ref, c_ref, wo_ref, g_ref,
    dm_ref, dl_ref, gain_ref, gq_ref, gkv_ref,
    bq_ref, bk_ref, bv_ref, cap_ref, da_ref, aq_ref, ak_ref, av_ref, tq_ref, tk_ref, tv_ref,
):
    pair = pl.program_id(0)
    own = q_ref.shape[0]
    last = pl.num_programs(0) - 1

    @pl.when(pair == 0)
    def _():
        hm = hm_ref[...]
        dn = dn_ref[...].astype(F32)
        r = lax.rsqrt(jnp.mean(hm * hm, axis=-1, keepdims=True) + EPS)
        z = dn * g_ref[...]
        gain_ref[...] = jnp.sum(dn * hm * r, axis=0, keepdims=True)
        dm = (
            c_ref[...].astype(F32)
            + r * z
            - hm * (r * r * r) * jnp.mean(z * hm, axis=-1, keepdims=True)
        )
        dm_ref[...] = dm
        low = dm.astype(BF16)
        dl_ref[...] = low
        da = mm(low, wo_ref[...], NT).astype(BF16)
        for i in range(PAIRS):
            da_ref[i] = da[:, i * 128:(i + 1) * 128]
        bq_ref[...] = mm(qf_ref[...], rank_tile(QA, (QPAD, RQ * 128)))
        tile_keys(kvw_ref, bk_ref, bv_ref)
        make_cap(s_ref, dq_ref, dk_ref, cap_ref, nblk, own)
        for ref in (aq_ref, ak_ref, av_ref, tq_ref, tk_ref, tv_ref):
            ref[...] = jnp.zeros_like(ref)

    q = q_ref[...]
    k = k_ref[...]
    v = v_ref[...]
    qs = stacked(q)
    ds_ = stacked(da_ref[pair])
    cap = cap_ref[...]
    st = jnp.minimum(mm(k, qs, NT), jnp.concatenate([cap, cap], axis=1))
    p = jnp.exp(st - lse_ref[0])
    dp = mm(v, ds_, NT)
    delta = jnp.sum(p * dp, axis=0, keepdims=True)
    ds = (p * (dp - delta)).astype(BF16)
    dv = mm(p.astype(BF16), ds_)
    dk = mm(ds, qs)
    dq = unstacked(mm(k, ds, TN), own) * (DH ** (-0.5))

    eq = head_spread(pair, 0, RQ, (128, RQ * 128))
    qe = mm(qf_ref[:, :128], eq)
    dq6 = jnp.concatenate([dq] * RQ, axis=1)
    tq_ref[...] += dq6 * qe
    aq_ref[...] += mm((dq6 * bq_ref[...]).astype(BF16), eq, NT)
    ek = head_spread(pair, 0, RK, (128, RK * 128))
    ev = head_spread(pair, KCOLS - 128, RK, (128, RK * 128))
    ke = mm(kvw_ref[:, :128], ek)
    ve = mm(kvw_ref[:, 128:256], ev)
    dk2 = jnp.concatenate([dk] * RK, axis=1)
    dv2 = jnp.concatenate([dv] * RK, axis=1)
    tk_ref[...] += dk2 * ke
    tv_ref[...] += dv2 * ve
    ak_ref[...] += mm((dk2 * bk_ref[...]).astype(BF16), ek, NT)
    av_ref[...] += mm((dv2 * bv_ref[...]).astype(BF16), ev, NT)

    @pl.when(pair == last)
    def _():
        def fold(x, t):
            hi = x.astype(BF16)
            lo = (x - hi.astype(F32)).astype(BF16)
            return mm(hi, t, NT) + mm(lo, t, NT)

        gq = fold(tq_ref[...], rank_tile(QA, (QPAD, RQ * 128)))
        gq_ref[:, :128] = ((gq[:, :128] + aq_ref[...]) * (1.0 / RQ)).astype(BF16)
        gq_ref[:, 128:] = (gq[:, 128:] * (1.0 / RQ)).astype(BF16)
        gk = fold(tk_ref[...], rank_tile(KA, (KPAD, RK * 128)))
        gv = fold(tv_ref[...], rank_tile(KCOLS + KA, (KPAD, RK * 128)))
        gkv = gk + gv
        first = ((gkv[:, :128] + ak_ref[...]) * (1.0 / RK)).astype(BF16)
        second = ((gkv[:, 128:256] + av_ref[...]) * (1.0 / RK)).astype(BF16)
        third = (gkv[:, 256:] * (1.0 / RK)).astype(BF16)
        gkv_ref[...] = jnp.zeros_like(gkv_ref)
        for i in range(nblk):
            rows = slice(i * own, (i + 1) * own)
            slot = s_ref[1 + nblk + i]
            gkv_ref[slot, :, :128] = first[rows]
            gkv_ref[slot, :, 128:256] = second[rows]
            gkv_ref[slot, :, 256:] = third[rows]


def back(nblk, width, scalars, q, k, v, lse, dq, dk, qf, kvw, dn, hm, c, wo, gain):
    own, d = q.shape
    win = nblk * own
    whole = lambda a: pl.BlockSpec(a.shape, lambda p, a=a: (0,) * a.ndim)
    col = lambda rows: pl.BlockSpec((rows, 128), lambda p: (0, p))
    fixed = lambda *s: pl.BlockSpec(s, lambda p: (0,) * len(s))
    return pl.pallas_call(
        functools.partial(back_kernel, nblk),
        grid=(PAIRS,),
        in_specs=[
            pl.BlockSpec(memory_space=pltpu.SMEM), col(own), col(win), col(win),
            pl.BlockSpec((1, 1, 2 * own), lambda p: (p, 0, 0)),
        ] + [whole(a) for a in (dq, dk, qf, kvw, dn, hm, c, wo, gain)],
        out_specs=[
            fixed(own, d), fixed(own, d), fixed(1, d), fixed(own, QPAD),
            fixed(width, own, KPAD),
        ],
        out_shape=[
            jax.ShapeDtypeStruct((own, d), F32),
            jax.ShapeDtypeStruct((own, d), BF16),
            jax.ShapeDtypeStruct((1, d), F32),
            jax.ShapeDtypeStruct((own, QPAD), BF16),
            jax.ShapeDtypeStruct((width, own, KPAD), BF16),
        ],
        scratch_shapes=[
            pltpu.VMEM((own, RQ * 128), F32),
            pltpu.VMEM((win, RK * 128), F32),
            pltpu.VMEM((win, RK * 128), F32),
            pltpu.VMEM((win, own), F32),
            pltpu.VMEM((PAIRS, own, 128), BF16),
            pltpu.VMEM((own, 128), F32),
            pltpu.VMEM((win, 128), F32),
            pltpu.VMEM((win, 128), F32),
            pltpu.VMEM((own, RQ * 128), F32),
            pltpu.VMEM((win, RK * 128), F32),
            pltpu.VMEM((win, RK * 128), F32),
        ],
        compiler_params=params(),
        cost_estimate=cost(30e9, 15e6),
        name="back",
    )(scalars, q, k, v, lse, dq, dk, qf, kvw, dn, hm, c, wo, gain)


def flip(index, bit):
    digit = (index // bit) % 2
    return index + bit - 2 * bit * digit


AXES = {"c": ("wide", 1), "x": ("wide", 2), "y": ("rows", 1), "n": ("rows", 2), "f": ("rows", 4)}


def enter(names):
    barrier = pltpu.get_barrier_semaphore()
    for name in names:
        pl.semaphore_signal(
            barrier, inc=1, device_id=partner(name), device_id_type=pl.DeviceIdType.MESH
        )
    pl.semaphore_wait(barrier, len(names))


def partner(name):
    axis, bit = AXES[name]
    return {axis: flip(lax.axis_index(axis), bit)}


def digit(name):
    axis, bit = AXES[name]
    return (lax.axis_index(axis) // bit) % 2


def wide_digits(index):
    return index // 2, index % 2


def slot_for(me, block):
    mx, mc = wide_digits(me)
    bx, bc = wide_digits(block)
    return 2 * ((mc + bc) % 2) + (mx + bx) % 2


def send_to(name, src, dst, send, recv):
    return pltpu.make_async_remote_copy(
        src_ref=src, dst_ref=dst, send_sem=send, recv_sem=recv,
        device_id=partner(name), device_id_type=pl.DeviceIdType.MESH,
    )


class Gather:
    def __init__(self, ref, send, recv, rows=None):
        at = [ref.at[i] if rows is None else ref.at[i, rows] for i in range(4)]
        self.x = send_to("x", at[0], at[1], send.at[0], recv.at[0])
        self.c = send_to("c", at[0], at[2], send.at[1], recv.at[1])
        self.r = send_to("c", at[1], at[3], send.at[2], recv.at[2])

    def first(self):
        self.x.start()
        self.c.start()

    def relay(self):
        self.x.wait()
        self.r.start()

    def done(self):
        self.c.wait()
        self.r.wait()


class Scatter:
    def __init__(self, part, got, last, send, recv):
        self.part, self.got, self.last = part, got, last
        self.c = send_to("c", part.at[pl.ds(2, 2)], got, send.at[0], recv.at[0])
        if last is not None:
            self.x = send_to("x", part.at[1], last, send.at[1], recv.at[1])

    def core(self):
        self.c.start()

    def kept(self, i):
        return self.part[i].astype(F32) + self.got[i].astype(F32)

    def cross(self):
        self.c.wait()
        self.part[1] = self.kept(1).astype(BF16)
        self.x.start()
        self.part[0] = self.kept(0).astype(BF16)

    def total(self):
        self.x.wait()
        return self.part[0].astype(F32) + self.last[...].astype(F32)


class Sum:
    def __init__(self, names, unit, src, base, acc, got, res, rbase, send, recv,
                 local=None, top=None, flat=False):
        self.names, self.unit, self.n = names, unit, len(names)
        self.src, self.base, self.acc, self.got = src, base, acc, got
        self.res, self.rbase, self.send, self.recv = res, rbase, send, recv
        self.local, self.flat = local, flat
        self.top = unit * 2 ** (self.n - 1) if top is None else top

    def low(self, i, skip=0):
        total = 0
        for j in range(skip, i):
            total = total + digit(self.names[j]) * 2 ** (self.n - 1 - j)
        return total

    def span(self, ref, base, chunk, count):
        return ref.at[pl.ds(base + chunk * self.unit, count * self.unit)]

    def keep(self):
        half = 2 ** (self.n - 1)
        return pltpu.make_async_copy(
            self.span(self.src, self.base, self.low(1), half), self.acc, self.local
        )

    def halve(self, i):
        half = 2 ** (self.n - 1 - i)
        away = (1 - digit(self.names[i])) * half
        if i == 0:
            src = self.span(self.src, self.base, away, half)
        else:
            src = self.span(self.acc, 0, self.low(i, 1) + away, half)
        dst = self.span(self.got, 0, 2 ** self.n - 2 * half, half)
        return send_to(self.names[i], src, dst, self.send.at[i], self.recv.at[i])

    def begin(self):
        self.halve(0).start()
        if self.local is not None:
            self.keep().start()

    def place(self, i):
        if self.flat:
            return self.rbase
        return self.rbase + digit(self.names[0]) * self.top + self.low(i, 1) * self.unit

    def double(self, i):
        half = 2 ** (self.n - 1 - i)
        held = self.res.at[pl.ds(self.place(i + 1), half * self.unit)]
        k = self.n + i
        return send_to(self.names[i], held, held, self.send.at[k], self.recv.at[k])

    def resume(self, own, at):
        place = self.place(self.n)
        for j in range(self.unit):
            self.res[place + j] = own[at + j]
        self.double(self.n - 1).start()

    def add(self, i):
        half = 2 ** (self.n - 1 - i)
        offset = (2 ** self.n - 2 * half) * self.unit
        self.halve(i).wait()
        kept = self.low(i + 1, 1) * self.unit
        first = i == 0 and self.local is None
        if i == 0 and self.local is not None:
            self.keep().wait()
        own = self.base + self.low(1) * self.unit
        last = i == self.n - 1
        place = self.place(self.n)

        count = self.unit if self.unit > 1 else min(half, 4)

        def some(i, carry):
            j = i * count
            mine = self.src[pl.ds(own + j, count)] if first else self.acc[pl.ds(kept + j, count)]
            value = (mine.astype(F32) + self.got[pl.ds(offset + j, count)].astype(F32)).astype(BF16)
            if last:
                self.res[pl.ds(place + j, count)] = value
            else:
                self.acc[pl.ds(kept + j, count)] = value
            return carry

        lax.fori_loop(0, half * self.unit // count, some, 0)

    def step(self, k):
        n = self.n
        if k < n:
            self.add(k)
            if k < n - 1:
                self.halve(k + 1).start()
            elif not self.flat:
                self.double(n - 1).start()
        else:
            i = 2 * n - 1 - k
            self.double(i).wait()
            if i > 0:
                self.double(i - 1).start()


def fill_cap(me, first, dq, dk, cap_ref, nblk, own):
    for i in range(nblk):
        rows = pl.ds(i * own, own)
        key = lax.broadcasted_iota(jnp.int32, (own, own), 0)
        query = lax.broadcasted_iota(jnp.int32, (own, own), 1) + (me - first - i) * own
        ok = (dk[i * own:(i + 1) * own, :] == dq) & (key <= query)
        cap_ref[rows, :] = jnp.where(ok, BIG, NEG)


def fore_kernel(
    nblk, x_ref, wt_ref, wo_ref, g1_ref, g2_ref, dq_ref, dk_ref, c_ref,
    n1_ref, qf_ref, kvw_ref, att_ref, q_ref, k_ref, v_ref, lse_ref, hm_ref, ng_ref, nb_ref, cg_ref,
    kvg_ref, bq_ref, bk_ref, bv_ref, cap_ref, full_ref, send, recv,
):
    seqs, own, d = x_ref.shape
    me = lax.axis_index("wide")
    first = me // 3
    kvs = [Gather(kvg_ref.at[s], send.at[s], recv.at[s]) for s in range(seqs)]
    cots = [Gather(cg_ref.at[s], send.at[2 + s], recv.at[2 + s]) for s in range(seqs)]
    norms = [
        Gather(ng_ref, send.at[4 + i], recv.at[4 + i], pl.ds(i * (own // 4), own // 4))
        for i in range(4)
    ]
    for s in range(seqs):
        cg_ref[s, 0] = c_ref[s]
    for s in range(seqs):
        x = x_ref[s].astype(F32)
        r = lax.rsqrt(jnp.mean(x * x, axis=-1, keepdims=True) + EPS)
        n = (x * r * g1_ref[...]).astype(BF16)
        n1_ref[s] = n
        f = mm(n, wt_ref[...], NT).astype(BF16)
        qf_ref[s] = f[:, :QPAD]
        kvg_ref[s, 0, :, :KV] = f[:, QCOLS:]
        kvg_ref[s, 0, :, KV:] = jnp.zeros((own, KPAD - KV), BF16)
        if s == 0:
            enter("cx")
        kvs[s].first()
    kvs[0].relay()
    for s in range(seqs):
        cots[s].first()
    kvs[0].done()

    def step(t, carry):
        s = t // PAIRS
        pair = t % PAIRS

        @pl.when(t == PAIRS)
        def _():
            kvs[1].done()

        @pl.when(pair == 0)
        def _():
            for i in range(nblk):
                kvw_ref[s, pl.ds(i * own, own), :] = kvg_ref[s, slot_for(me, first + i)]
            bq_ref[...] = mm(qf_ref[s], rank_tile(QA, (QPAD, RQ * 128)))
            bk_ref[...] = mm(kvw_ref[s, :, :256], rank_tile(KA, (256, RK * 128)))
            bv_ref[...] = mm(kvw_ref[s, :, 128:384], rank_tile(KCOLS + KA - 128, (256, RK * 128)))
            fill_cap(me, first, dq_ref[s], dk_ref[s], cap_ref, nblk, own)

        qe = mm(qf_ref[s, :, :128], head_spread(pair, 0, RQ, (128, RQ * 128)))
        qsum = qe[:, :128] * bq_ref[:, :128]
        for r in range(1, RQ):
            cols = slice(r * 128, (r + 1) * 128)
            qsum = qsum + qe[:, cols] * bq_ref[:, cols]
        q = (qsum * (1.0 / RQ)).astype(BF16)
        ke = mm(kvw_ref[s, :, :128], head_spread(pair, 0, RK, (128, RK * 128)))
        ve = mm(kvw_ref[s, :, 128:256], head_spread(pair, KCOLS - 128, RK, (128, RK * 128)))
        k = ((ke[:, :128] * bk_ref[:, :128] + ke[:, 128:] * bk_ref[:, 128:]) * (1.0 / RK)).astype(BF16)
        v = ((ve[:, :128] * bv_ref[:, :128] + ve[:, 128:] * bv_ref[:, 128:]) * (1.0 / RK)).astype(BF16)
        q = q * jnp.asarray(DH ** (-0.5), BF16)
        q_ref[s, pair] = q
        k_ref[s, pair] = k
        v_ref[s, pair] = v
        cap = cap_ref[...]
        st = jnp.minimum(mm(k, stacked(q), NT), jnp.concatenate([cap, cap], axis=1))
        top = jnp.max(st, axis=0, keepdims=True)
        e = jnp.exp(st - top)
        total = jnp.sum(e, axis=0, keepdims=True)
        p = (e * (1.0 / total)).astype(BF16)
        lse_ref[s, pair] = top + jnp.log(total)
        full_ref[pair] = unstacked(mm(v, p, TN), own).astype(BF16)

        @pl.when(pair == PAIRS - 1)
        def _():
            att = jnp.concatenate([full_ref[i] for i in range(PAIRS)], axis=1)
            att_ref[s] = att
            hm = x_ref[s].astype(F32) + mm(att, wo_ref[...])
            hm_ref[s] = hm
            r = lax.rsqrt(jnp.mean(hm * hm, axis=-1, keepdims=True) + EPS)
            n2 = (hm * r * g2_ref[...]).astype(BF16)

            @pl.when(s == 0)
            def _():
                ng_ref[0] = n2
                for norm in norms:
                    norm.first()

            @pl.when(s == 1)
            def _():
                nb_ref[...] = n2

        @pl.when(t == 2)
        def _():
            kvs[1].relay()

        @pl.when(t == 6)
        def _():
            cots[0].relay()

        @pl.when(t == 13)
        def _():
            cots[1].relay()

        return carry

    lax.fori_loop(0, seqs * PAIRS, step, 0)
    for norm in norms:
        norm.relay()
    for each in cots + norms:
        each.done()


def vmem():
    return pl.BlockSpec(memory_space=pltpu.VMEM)


def hbm():
    return pl.BlockSpec(memory_space=pl.ANY)


def fused(ident, limit=63):
    return pltpu.CompilerParams(
        vmem_limit_bytes=limit << 20, collective_id=ident, has_side_effects=True
    )


def fore(nblk, x, wt, wo, g1, g2, dq, dk, c):
    seqs, own, d = x.shape
    win = nblk * own
    shape = jax.ShapeDtypeStruct
    return pl.pallas_call(
        functools.partial(fore_kernel, nblk),
        in_specs=[vmem()] * 8,
        out_specs=[vmem()] * 12,
        out_shape=[
            shape((seqs, own, d), BF16), shape((seqs, own, QPAD), BF16),
            shape((seqs, win, KPAD), BF16), shape((seqs, own, d), BF16),
            shape((seqs, PAIRS, own, 128), BF16), shape((seqs, PAIRS, win, 128), BF16),
            shape((seqs, PAIRS, win, 128), BF16), shape((seqs, PAIRS, 1, 2 * own), F32),
            shape((seqs, own, d), F32), shape((4, own, d), BF16), shape((own, d), BF16),
            shape((seqs, 4, own, d), BF16),
        ],
        scratch_shapes=[
            pltpu.VMEM((seqs, 4, own, KPAD), BF16),
            pltpu.VMEM((own, RQ * 128), F32),
            pltpu.VMEM((win, RK * 128), F32),
            pltpu.VMEM((win, RK * 128), F32),
            pltpu.VMEM((win, own), F32),
            pltpu.VMEM((PAIRS, own, 128), BF16),
            pltpu.SemaphoreType.DMA((8, 3)),
            pltpu.SemaphoreType.DMA((8, 3)),
        ],
        compiler_params=fused(0),
        cost_estimate=cost(30e9, 30e6),
        name="fore",
    )(x, wt, wo, g1, g2, dq, dk, c)


SPLITS = ((0, 192), (192, 256), (448, 256))
EARLY = len(SPLITS) - 2
LANES = 512
FFN_NAMES = (("ynf", "ynf", "nyf"), ("ynf", "nyf", "ynf"), ("ynf", "nyf", "ynf"))


def chunk_units(h):
    return SPLITS[h][1] // 16 * (1024 // LANES) // 8


def late_at(h):
    return 24 * sum(chunk_units(i) for i in range(EARLY, h))


def own_at(h, m):
    return 3 * sum(chunk_units(i) for i in range(h)) + m * chunk_units(h)


MIDDLE_EVENTS = {
    (1, "m0"): ((0, 0, 0),),
    (1, "m1"): ((0, 2, 0),),
    (1, "m2"): ((0, 1, 0), (0, 0, 1),),
    (2, 0): ((0, 2, 1),),
    (2, 1): ((0, 1, 1), (0, 0, 2),),
    (2, 2): ((0, 2, 2),),
    (2, 3): ((0, 1, 2),),
}


def middle_kernel(
    n_ref, nb_ref, c_ref, wg_ref, wu_ref, wd_ref,
    dn_ref, ds_ref, ok_ref, os_ref, gw_ref, own_ref,
    hid_ref, dg_ref, du_ref, oa_ref, da_ref, op_ref, dp_ref, xs_ref, oc_ref, dc_ref, dx_ref, nn_ref, *refs,
):
    seqs, size, own, d = c_ref.shape
    srcs, refs = refs[:EARLY], refs[EARLY:]
    accs, refs = refs[:3 * EARLY], refs[3 * EARLY:]
    gots, refs = refs[:3 * EARLY], refs[3 * EARLY:]
    send, recv, xsend, xrecv, nsend, nrecv = refs
    downs = [
        send_to("c", dp_ref.at[s], dc_ref.at[s], xsend.at[0, s], xrecv.at[0, s]) for s in range(seqs)
    ]
    ups = [
        send_to("c", op_ref.at[s], oc_ref.at[s], xsend.at[1, s], xrecv.at[1, s]) for s in range(seqs)
    ]
    cross = send_to("x", xs_ref, dx_ref, xsend.at[2, 0], xrecv.at[2, 0])
    parts = {}
    for h in range(EARLY):
        for m in range(3):
            i = 3 * h + m
            u = chunk_units(h)
            parts[h, m] = Sum(
                FFN_NAMES[h][m], u, srcs[h], 8 * u * m, accs[i], gots[i], own_ref, own_at(h, m),
                send.at[i], recv.at[i], flat=True,
            )
    norms = [
        Gather(nn_ref, nsend.at[i], nrecv.at[i], pl.ds(i * (own // 4), own // 4)) for i in range(4)
    ]
    nn_ref[0] = nb_ref[...]
    enter("cxynf")
    for norm in norms:
        norm.first()

    def run(point):
        for h, m, k in MIDDLE_EVENTS.get(point, ()):
            parts[h, m].step(k)

    def hidden(s, b, n, span):
        c = c_ref[s, b]
        g = mm(wg_ref[span, :], n, NT)
        u = mm(wu_ref[span, :], n, NT)
        dh = mm(wd_ref[span, :], c, NT)
        sg = 1.0 / (1.0 + jnp.exp(-g))
        gs = g * sg
        cols = pl.ds(pl.multiple_of((s * size + b) * own, 128), own)
        hid_ref[span, cols] = (gs * u).astype(BF16)
        dg_ref[span, cols] = (dh * u * (sg * (1.0 + g * (1.0 - sg)))).astype(BF16)
        du_ref[span, cols] = (dh * gs).astype(BF16)

    def project(s, b, t):
        cols = pl.ds(pl.multiple_of((s * size + b) * own, 128), own)
        o = mm(hid_ref[:, cols], wd_ref[...], TN)
        dn = mm(dg_ref[:, cols], wg_ref[...], TN) + mm(du_ref[:, cols], wu_ref[...], TN)

        @pl.when(b >= 2)
        def _():
            op_ref[s, b - 2] = o.astype(BF16)
            dp_ref[s, b - 2] = dn.astype(BF16)

        @pl.when(b < 2)
        def _():
            oa_ref[s, b] = o.astype(BF16)
            da_ref[s, b] = dn

        @pl.when(t == 1)
        def _():
            downs[s].start()
            ups[s].start()

    def one(t, carry):
        b = size - 1 - t
        hidden(0, b, n_ref[b], slice(0, wd_ref.shape[0]))
        project(0, b, t)

        @pl.when(t == 1)
        def _():
            norms[0].relay()

        @pl.when(t == 2)
        def _():
            norms[1].relay()
            norms[2].relay()

        return carry

    lax.fori_loop(0, size, one, 0)
    norms[3].relay()
    downs[0].wait()
    xs_ref[...] = (da_ref[0, 1] + dc_ref[0, 1].astype(F32)).astype(BF16)
    cross.start()
    for norm in norms:
        norm.done()
    half = size * own
    for h, (off, rows) in enumerate(SPLITS):
        last = h == len(SPLITS) - 1
        early = h < EARLY

        def two(t, carry, h=h, off=off, rows=rows, last=last):
            b = size - 1 - t
            hidden(1, b, nn_ref[b], slice(off, off + rows))
            if last:
                project(1, b, t)
            for j in range(size):
                if (h, j) in MIDDLE_EVENTS:

                    @pl.when(t == j)
                    def _(j=j):
                        run((h, j))

            return carry

        lax.fori_loop(0, size, two, 0)
        count = rows // 16
        span = slice(off, off + rows)
        for m, (a_ref, b_refs) in enumerate((
            (dg_ref, (n_ref, nn_ref)), (du_ref, (n_ref, nn_ref)),
            (hid_ref, (c_ref.at[0], c_ref.at[1])),
        )):
            w = mm(a_ref[span, :half], b_refs[0][...].reshape(half, d))
            w = (w + mm(a_ref[span, half:], b_refs[1][...].reshape(half, d))).astype(BF16)
            to, start = (srcs[h], 0) if early else (gw_ref, late_at(h))
            for i in range(d // LANES):
                at = start + (m * (d // LANES) + i) * count
                piece = w[:, i * LANES:(i + 1) * LANES]
                to[pl.ds(at, count)] = piece.reshape(count, 16, LANES)
            if early:
                parts[h, m].begin()
            run((h, "m%d" % m))
    for s in range(seqs):
        ups[s].wait()
        ok_ref[s] = (oa_ref[s, 0].astype(F32) + oc_ref[s, 0].astype(F32)).astype(BF16)
        os_ref[s] = (oa_ref[s, 1].astype(F32) + oc_ref[s, 1].astype(F32)).astype(BF16)
    downs[1].wait()
    dn_ref[1] = da_ref[1, 0] + dc_ref[1, 0].astype(F32)
    ds_ref[...] = (da_ref[1, 1] + dc_ref[1, 1].astype(F32)).astype(BF16)
    run("end")
    cross.wait()
    dn_ref[0] = da_ref[0, 0] + dc_ref[0, 0].astype(F32) + dx_ref[...].astype(F32)


def middle(n, nb, c, wg, wu, wd):
    seqs, size, own, d = c.shape
    shape = jax.ShapeDtypeStruct
    flat = (wd.shape[0], seqs * size * own)
    u = [chunk_units(h) for h in range(EARLY) for _ in range(3)]
    unit = lambda k: pltpu.VMEM((k, 16, LANES), BF16)
    return pl.pallas_call(
        middle_kernel,
        in_specs=[vmem()] * 6,
        out_specs=[vmem()] * 6,
        out_shape=[
            shape((seqs, own, d), F32), shape((own, d), BF16), shape((seqs, own, d), BF16),
            shape((seqs, own, d), BF16), shape((late_at(len(SPLITS)), 16, LANES), BF16),
            shape((own_at(EARLY, 0), 16, LANES), BF16),
        ],
        scratch_shapes=[pltpu.VMEM(flat, BF16)] * 3
        + [pltpu.VMEM((seqs, 2, own, d), BF16), pltpu.VMEM((seqs, 2, own, d), F32)]
        + [pltpu.VMEM((seqs, 2, own, d), BF16)] * 2
        + [pltpu.VMEM((own, d), BF16)]
        + [pltpu.VMEM((seqs, 2, own, d), BF16)] * 2
        + [pltpu.VMEM((own, d), BF16), pltpu.VMEM((size, own, d), BF16)]
        + [unit(24 * chunk_units(h)) for h in range(EARLY)]
        + [unit(4 * k) for k in u]
        + [unit(7 * k) for k in u]
        + [
            pltpu.SemaphoreType.DMA((3 * EARLY, 3)),
            pltpu.SemaphoreType.DMA((3 * EARLY, 3)),
            pltpu.SemaphoreType.DMA((3, seqs)),
            pltpu.SemaphoreType.DMA((3, seqs)),
            pltpu.SemaphoreType.DMA((4, 3)),
            pltpu.SemaphoreType.DMA((4, 3)),
        ],
        compiler_params=fused(1),
        cost_estimate=cost(27e9, 30e6),
        name="middle",
    )(n, nb, c, wg, wu, wd)


FFN_UNITS = 3 * sum(r for _, r in SPLITS) // 16
SECOND = 3
AFTER_EVENTS = {
    0: (("F00", 3), ("F01", 3), ("F10", 0),),
    1: (("F02", 3),),
    2: (("F11", 0), ("F12", 0), ("F21", 0), ("F20", 0),),
    3: (("F00", 4), ("O0", 0), ("F01", 4),),
    4: (("O1", 0), ("F22", 0), ("F10", 1), ("F02", 4),),
    5: (("cross", 0), ("F12", 1), ("F11", 1),),
    6: (("F20", 1), ("F10", 2), ("F21", 1), ("O1", 1), ("F22", 1),),
    7: (("F12", 2), ("F00", 5), ("F11", 2),),
    8: (("F02", 5), ("F20", 2), ("O0", 1),),
    9: (("cross", 1), ("key", 0), ("F10", 3), ("F01", 5), ("F21", 2), ("emit", 0),),
    10: (("O0", 2), ("O1", 2), ("F22", 2),),
    11: (("F12", 3), ("O1", 3),),
    12: (("F11", 3),),
    13: (("F20", 3), ("F10", 4), ("emit", 1),),
    14: (("F21", 3), ("O0", 3), ("F11", 4), ("F22", 3),),
    15: (("O1", 4), ("F12", 4), ("F10", 5), ("O0", 4), ("F20", 4),),
    "T0": (("F21", 4),),
    "T1": (("O1", 5), ("K0", 0), ("O0", 5), ("K1", 0), ("F11", 5), ("F12", 5), ("F22", 4),),
    "T2": (("K0", 1), ("K2", 0), ("F20", 5), ("K3", 0), ("O1", 6),),
    "T3": (("K4", 0), ("F21", 5), ("O0", 6), ("K2", 1), ("K1", 1), ("F22", 5), ("K0", 2), ("O0", 7), ("O1", 7), ("K3", 1), ("K2", 2), ("K4", 1), ("K0", 3), ("K1", 2), ("K3", 2), ("K2", 3), ("K4", 2), ("K0", 4), ("O1", 8), ("K1", 3), ("O0", 8), ("K4", 3), ("K3", 3), ("K2", 4), ("K0", 5), ("K1", 4), ("K4", 4), ("K3", 4), ("O1", 9), ("K2", 5), ("K0", 6), ("K4", 5), ("K1", 5), ("K3", 5), ("O0", 9), ("K2", 6), ("K4", 6), ("K0", 7), ("K1", 6), ("K2", 7), ("K3", 6), ("K4", 7), ("K1", 7), ("K3", 7), ("K0", 8), ("K2", 8), ("K4", 8), ("K0", 9), ("K3", 8), ("K2", 9), ("K4", 9), ("K1", 8), ("K3", 9), ("K1", 9),),
}
OUT_PARTS = ("cyxnf", "cxnyf")
Q_PARTS = ("cxynf", "cnyfx")
K_PARTS = ("cxynf", "cynfx", "cnfxy")
K_LANES = 256
GAIN_ROW = 352


def attention_parts():
    return [(n, 1024) for n in OUT_PARTS] + [(n, 512) for n in Q_PARTS] + [(n, K_LANES) for n in K_PARTS]


def after_kernel(
    nblk, gw_ref, own_ref, dn_ref, ds_ref, ok_ref, os_ref, q_ref, k_ref, v_ref, lse_ref, dq_ref, dk_ref,
    qf_ref, kvw_ref, hm_ref, c_ref, wo_ref, g1_ref, g2_ref, att_ref, n1_ref, x_ref, wt_ref,
    out_ref, ig_ref, gr_ref, *refs,
):
    n_out, n_q = len(OUT_PARTS), len(Q_PARTS)
    n_fac = n_q + len(K_PARTS)
    or_refs, refs = refs[:n_out], refs[n_out:]
    fr_refs, refs = refs[:n_fac], refs[n_fac:]
    (bq_ref, bk_ref, bv_ref, cap_ref, da_ref, aq_ref, ak_ref, av_ref, tq_ref, tk_ref, tv_ref,
     dm_ref, late_ref, gq_ref, gkp_ref, gkc_ref, gkx_ref, ox_ref, kb_ref, vb_ref, dx_ref, gain_ref) = refs[:22]
    refs = refs[22:]
    n_late = 3 * (len(SPLITS) - EARLY)
    gots, refs = refs[:n_late], refs[n_late:]
    accs, refs = refs[:n_late], refs[n_late:]
    ob, refs = refs[:n_out], refs[n_out:]
    og, refs = refs[:n_out], refs[n_out:]
    oa, refs = refs[:n_out], refs[n_out:]
    fb, refs = refs[:n_fac], refs[n_fac:]
    fg, refs = refs[:n_fac], refs[n_fac:]
    fa, refs = refs[:n_fac], refs[n_fac:]
    send, recv, loc, gs, gr, kvsem, wsem = refs
    seqs, own, d = hm_ref.shape
    me = lax.axis_index("wide")
    first = me // 3

    sums = {}
    half = gr_ref.shape[0] // 2
    for h, (off, rows) in enumerate(SPLITS):
        for m in range(3):
            i = 3 * h + m
            u = chunk_units(h)
            late = h >= EARLY
            j = i - 3 * EARLY
            sums[h, m] = Sum(
                FFN_NAMES[h][m], u, gw_ref if late else None, late_at(h) + 8 * u * m,
                accs[j] if late else None, gots[j] if late else None,
                gr_ref, m * (half // 3) + off // 16, send.at[i], recv.at[i],
                local=loc.at[j] if late else None, top=half,
            )
    k0 = len(sums)
    outs = [
        Sum(names, 1, ob[g], 0, oa[g], og[g], or_refs[g], 0, send.at[k0 + g], recv.at[k0 + g])
        for g, names in enumerate(OUT_PARTS)
    ]
    k1 = k0 + n_out
    facs = [
        Sum(names, 1, fb[g], 0, fa[g], fg[g], fr_refs[g], 0, send.at[k1 + g], recv.at[k1 + g])
        for g, names in enumerate(Q_PARTS + K_PARTS)
    ]
    keys = [
        Scatter(gkp_ref.at[s], gkc_ref.at[s], gkx_ref.at[s], gs.at[s], gr.at[s])
        for s in range(seqs)
    ]
    crosses = [
        send_to("x", os_ref.at[s], ox_ref.at[s], gs.at[2 + s, 0], gr.at[2 + s, 0])
        for s in range(seqs)
    ]

    def fetch(t):
        return [
            pltpu.make_async_copy(a.at[t // PAIRS, t % PAIRS], b.at[t % 2], kvsem.at[i, t % 2])
            for i, (a, b) in enumerate(((k_ref, kb_ref), (v_ref, vb_ref)))
        ]

    for copy in fetch(0):
        copy.start()
    loads = [
        pltpu.make_async_copy(dn_ref, dm_ref, wsem.at[0]),
        pltpu.make_async_copy(c_ref, late_ref, wsem.at[1]),
    ]
    for copy in loads:
        copy.start()
    enter("cxynf")
    for h, m in sums:
        if h >= EARLY:
            sums[h, m].begin()
        else:
            sums[h, m].resume(own_ref, own_at(h, m))

    for copy in loads:
        copy.wait()
    down = send_to("x", ds_ref, dx_ref, gs.at[4, 0], gr.at[4, 0])
    down.start()
    gain_ref[...] = jnp.zeros((1, d), F32)

    def mids(s):
        hm = hm_ref[s]
        dn = dm_ref[s]
        r = lax.rsqrt(jnp.mean(hm * hm, axis=-1, keepdims=True) + EPS)
        z = dn * g2_ref[...]
        gain_ref[...] += jnp.sum(dn * hm * r, axis=0, keepdims=True)
        dm = (
            late_ref[s].astype(F32)
            + r * z
            - hm * (r * r * r) * jnp.mean(z * hm, axis=-1, keepdims=True)
        )
        dm_ref[s] = dm
        low = dm.astype(BF16)
        late_ref[s] = low
        da = mm(low, wo_ref[...], NT).astype(BF16)
        for i in range(PAIRS):
            da_ref[s, i] = da[:, i * 128:(i + 1) * 128]

    load_x = pltpu.make_async_copy(x_ref, late_ref, wsem.at[2])

    def second():
        for g in range(n_out):

            def rows(j, carry, g=g):
                cols = pl.ds(pl.multiple_of(g * 512 + j * 256, 128), 256)
                a = att_ref[:, :, cols].reshape(seqs * own, 256)
                w = mm(a, late_ref[...].reshape(seqs * own, d), TN).astype(BF16)
                ob[g][pl.ds(j * 16, 16)] = w.reshape(16, 16, d)
                return carry

            lax.fori_loop(0, 2, rows, 0)
            outs[g].begin()
        load_x.start()

    def finish(s):
        def fold(x, t):
            hi = x.astype(BF16)
            lo = (x - hi.astype(F32)).astype(BF16)
            return mm(hi, t, NT) + mm(lo, t, NT)

        gq = fold(tq_ref[...], rank_tile(QA, (QPAD, RQ * 128)))
        gq_ref[s, :, :128] = ((gq[:, :128] + aq_ref[...]) * (1.0 / RQ)).astype(BF16)
        gq_ref[s, :, 128:] = (gq[:, 128:] * (1.0 / RQ)).astype(BF16)
        gk = fold(tk_ref[...], rank_tile(KA, (KPAD, RK * 128)))
        gv = fold(tv_ref[...], rank_tile(KCOLS + KA, (KPAD, RK * 128)))
        gkv = gk + gv
        one = ((gkv[:, :128] + ak_ref[...]) * (1.0 / RK)).astype(BF16)
        two = ((gkv[:, 128:256] + av_ref[...]) * (1.0 / RK)).astype(BF16)
        three = (gkv[:, 256:] * (1.0 / RK)).astype(BF16)
        gkp_ref[s] = jnp.zeros_like(gkp_ref[s])
        for i in range(nblk):
            rows = slice(i * own, (i + 1) * own)
            slot = slot_for(me, first + i)
            gkp_ref[s, slot, :, :128] = one[rows]
            gkp_ref[s, slot, :, 128:256] = two[rows]
            gkp_ref[s, slot, :, 256:] = three[rows]

    def emit(s):
        crosses[s].wait()
        total = hm_ref[s] + (ok_ref[s].astype(F32) + ox_ref[s].astype(F32))
        out_ref[s] = total.astype(BF16)

    named = {"F%d%d" % key: part for key, part in sums.items()}
    named.update({"O%d" % g: part for g, part in enumerate(outs)})
    named.update({"K%d" % g: part for g, part in enumerate(facs)})

    def run(point):
        for name, k in AFTER_EVENTS.get(point, ()):
            if name == "cross":
                crosses[k].start()
            elif name == "emit":
                emit(k)
            elif name == "key":
                keys[k].cross()
            else:
                named[name].step(k)

    def step(t, carry):
        s = t // PAIRS
        pair = t % PAIRS
        slot = t % 2

        @pl.when(t < seqs * PAIRS - 1)
        def _():
            for copy in fetch(t + 1):
                copy.start()

        @pl.when(pair == 0)
        def _():
            bq_ref[...] = mm(qf_ref[s], rank_tile(QA, (QPAD, RQ * 128)))
            bk_ref[...] = mm(kvw_ref[s, :, :256], rank_tile(KA, (256, RK * 128)))
            bv_ref[...] = mm(kvw_ref[s, :, 128:384], rank_tile(KCOLS + KA - 128, (256, RK * 128)))
            fill_cap(me, first, dq_ref[s], dk_ref[s], cap_ref, nblk, own)
            for ref in (aq_ref, ak_ref, av_ref, tq_ref, tk_ref, tv_ref):
                ref[...] = jnp.zeros_like(ref)

        @pl.when(t == SECOND)
        def _():
            down.wait()
            dm_ref[1] += dx_ref[...].astype(F32)

        @pl.when((t == 0) | (t == SECOND))
        def _():
            mids(t // SECOND)

        @pl.when(t == SECOND)
        def _():
            second()

        for copy in fetch(t):
            copy.wait()
        q = q_ref[s, pair]
        k = kb_ref[slot]
        v = vb_ref[slot]
        qs = stacked(q)
        da = stacked(da_ref[s, pair])
        cap = cap_ref[...]
        st = jnp.minimum(mm(k, qs, NT), jnp.concatenate([cap, cap], axis=1))
        p = jnp.exp(st - lse_ref[s, pair])
        dp = mm(v, da, NT)
        delta = jnp.sum(p * dp, axis=0, keepdims=True)
        ds = (p * (dp - delta)).astype(BF16)
        dv = mm(p.astype(BF16), da)
        dk = mm(ds, qs)
        dq = unstacked(mm(k, ds, TN), own) * (DH ** (-0.5))

        eq = head_spread(pair, 0, RQ, (128, RQ * 128))
        qe = mm(qf_ref[s, :, :128], eq)
        dq6 = jnp.concatenate([dq] * RQ, axis=1)
        tq_ref[...] += dq6 * qe
        aq_ref[...] += mm((dq6 * bq_ref[...]).astype(BF16), eq, NT)
        ek = head_spread(pair, 0, RK, (128, RK * 128))
        ev = head_spread(pair, KCOLS - 128, RK, (128, RK * 128))
        ke = mm(kvw_ref[s, :, :128], ek)
        ve = mm(kvw_ref[s, :, 128:256], ev)
        dk2 = jnp.concatenate([dk] * RK, axis=1)
        dv2 = jnp.concatenate([dv] * RK, axis=1)
        tk_ref[...] += dk2 * ke
        tv_ref[...] += dv2 * ve
        ak_ref[...] += mm((dk2 * bk_ref[...]).astype(BF16), ek, NT)
        av_ref[...] += mm((dv2 * bv_ref[...]).astype(BF16), ev, NT)

        @pl.when(pair == PAIRS - 1)
        def _():
            finish(s)

        @pl.when(t == PAIRS - 1)
        def _():
            keys[0].core()

        for when in range(seqs * PAIRS):
            if when in AFTER_EVENTS:

                @pl.when(t == when)
                def _(when=when):
                    run(when)

        return carry

    lax.fori_loop(0, seqs * PAIRS, step, 0)
    keys[1].core()
    n1 = n1_ref[...].reshape(seqs * own, d)
    gq = gq_ref[...].reshape(seqs * own, QPAD)
    w = mm(gq, n1, TN).astype(BF16)
    for g in range(n_q):
        fb[g][...] = w[:, g * 512:(g + 1) * 512].reshape(32, 16, 512)
        facs[g].begin()
    dn1 = mm(gq[:, :QCOLS], wt_ref[:QCOLS, :])
    run("T0")
    keys[1].cross()
    run("T1")
    gkv0 = keys[0].total().astype(BF16)
    gkv = jnp.concatenate([gkv0, keys[1].total().astype(BF16)], axis=0)
    gf = mm(gkv, n1, TN)

    def spread(value, only):
        for g in only:
            for i in range(8):
                for j in range(d // K_LANES):
                    row = 16 * (8 * g + i)
                    piece = value[row:row + 16, j * K_LANES:(j + 1) * K_LANES]
                    fb[n_q + g][4 * i + j] = piece.astype(BF16)
            facs[n_q + g].begin()

    last = len(K_PARTS) - 1
    spread(gf, range(last))
    dn1 = dn1 + mm(gkv[:, :KV], wt_ref[QCOLS:, :])
    load_x.wait()
    hin = late_ref[...].reshape(seqs * own, d).astype(F32)
    r1 = lax.rsqrt(jnp.mean(hin * hin, axis=-1, keepdims=True) + EPS)
    z1 = dn1 * g1_ref[...]
    gain_one = jnp.sum(dn1 * hin * r1, axis=0, keepdims=True)
    gf = jnp.concatenate(
        [gf[:GAIN_ROW], gain_one, gain_ref[...], gf[GAIN_ROW + 2:]], axis=0
    )
    spread(gf, (last,))
    run("T2")
    grad = r1 * z1 - hin * (r1 * r1 * r1) * jnp.mean(z1 * hin, axis=-1, keepdims=True)
    ig_ref[...] = (dm_ref[...].reshape(seqs * own, d) + grad).astype(BF16).reshape(seqs, own, d)
    run("T3")


def after(nblk, gw, own_sums, dn, ds, ok, os, q, k, v, lse, dq, dk, qf, kvw, hm, c, wo, g1, g2, att, n1, x, wt):
    seqs, own, d = hm.shape
    win = nblk * own
    shape = jax.ShapeDtypeStruct
    far = (0, 2, 3, 5, 7, 8, 15, 21)
    results = [shape((32, 16, lanes), BF16) for _, lanes in attention_parts()]
    total = 3 * len(SPLITS) + len(results)
    args = (gw, own_sums, dn, ds, ok, os, q, k, v, lse, dq, dk, qf, kvw, hm, c, wo, g1, g2, att, n1, x, wt)
    res = pl.pallas_call(
        functools.partial(after_kernel, nblk),
        in_specs=[hbm() if i in far else vmem() for i in range(len(args))],
        out_specs=[vmem()] * (3 + len(results)),
        out_shape=[
            shape((seqs, own, d), BF16), shape((seqs, own, d), BF16),
            shape((2 * FFN_UNITS, 16, LANES), BF16),
        ] + results,
        scratch_shapes=[
            pltpu.VMEM((own, RQ * 128), F32),
            pltpu.VMEM((win, RK * 128), F32),
            pltpu.VMEM((win, RK * 128), F32),
            pltpu.VMEM((win, own), F32),
            pltpu.VMEM((seqs, PAIRS, own, 128), BF16),
            pltpu.VMEM((own, 128), F32),
            pltpu.VMEM((win, 128), F32),
            pltpu.VMEM((win, 128), F32),
            pltpu.VMEM((own, RQ * 128), F32),
            pltpu.VMEM((win, RK * 128), F32),
            pltpu.VMEM((win, RK * 128), F32),
            pltpu.VMEM((seqs, own, d), F32),
            pltpu.VMEM((seqs, own, d), BF16),
            pltpu.VMEM((seqs, own, QPAD), BF16),
            pltpu.VMEM((seqs, 4, own, KPAD), BF16),
            pltpu.VMEM((seqs, 2, own, KPAD), BF16),
            pltpu.VMEM((seqs, own, KPAD), BF16),
            pltpu.VMEM((seqs, own, d), BF16),
            pltpu.VMEM((2, win, 128), BF16),
            pltpu.VMEM((2, win, 128), BF16),
            pltpu.VMEM((own, d), BF16),
            pltpu.VMEM((1, d), F32),
        ]
        + [
            pltpu.VMEM((n * chunk_units(h), 16, LANES), BF16)
            for n in (7, 4) for h in range(EARLY, len(SPLITS)) for _ in range(3)
        ]
        + [pltpu.VMEM((n, 16, 1024), BF16) for n in (32, 31, 16) for _ in OUT_PARTS]
        + [
            pltpu.VMEM((n, 16, lanes), BF16) for n in (32, 31, 16)
            for _, lanes in attention_parts()[len(OUT_PARTS):]
        ]
        + [
            pltpu.SemaphoreType.DMA((total, 10)),
            pltpu.SemaphoreType.DMA((total, 10)),
            pltpu.SemaphoreType.DMA((3 * (len(SPLITS) - EARLY),)),
            pltpu.SemaphoreType.DMA((5, 2)),
            pltpu.SemaphoreType.DMA((5, 2)),
            pltpu.SemaphoreType.DMA((2, 2)),
            pltpu.SemaphoreType.DMA((3,)),
        ],
        compiler_params=fused(2),
        cost_estimate=cost(60e9, 60e6),
        name="after",
    )(*args)
    n = 3 + len(OUT_PARTS)
    return res[0], res[1], res[2], res[3:n], res[n:]


def last_kernel(
    out_ref, ig_ref, gr_ref, o0_ref, o1_ref, q0_ref, q1_ref, k0_ref, k1_ref, k2_ref,
    output_ref, grad_ref, gate_ref, up_ref, down_ref, go_ref, gf_ref, gain_ref,
):
    step = pl.program_id(0)
    output_ref[...] = out_ref[...]
    grad_ref[...] = ig_ref[...]
    units = gr_ref.shape[2]
    for m, ref in enumerate((gate_ref, up_ref, down_ref)):
        for i in range(2):
            ref[:, i * LANES:(i + 1) * LANES] = gr_ref[i, m].reshape(16 * units, LANES).astype(F32)
    for g, ref in enumerate((o0_ref, o1_ref)):

        @pl.when(step // 2 == g)
        def _(ref=ref):
            go_ref[...] = ref[...].reshape(256, 1024).astype(F32)

    rows = pl.ds(pl.multiple_of(step * 128, 128), 128)
    for i, ref in enumerate((q0_ref, q1_ref)):
        gf_ref[rows, i * 512:(i + 1) * 512] = ref[pl.ds(step * 8, 8)].reshape(128, 512).astype(F32)

    @pl.when(step == 3)
    def _():
        for g, ref in enumerate((k0_ref, k1_ref, k2_ref)):
            count = min(KV - 128 * g, 128) // 16

            def rows(i, carry, g=g, ref=ref):
                at = pl.ds(pl.multiple_of(QCOLS + 128 * g + 16 * i, 16), 16)
                for j in range(1024 // K_LANES):
                    cols = slice(j * K_LANES, (j + 1) * K_LANES)
                    gf_ref[at, cols] = ref[4 * i + j].astype(F32)
                return carry

            lax.fori_loop(0, count, rows, 0)
        unit = (GAIN_ROW - 256) // 16
        for j in range(1024 // K_LANES):
            cols = slice(j * K_LANES, (j + 1) * K_LANES)
            gain_ref[:, cols] = k2_ref[4 * unit + j].astype(F32)[:8]


def finish_all(output, grad, gr, go, gf, cols):
    seqs, own, d = output.shape
    ff = 16 * gr.shape[0] // 6
    gr = gr.reshape(2, 3, ff // 16, 16, LANES)
    steps = 4
    shape = jax.ShapeDtypeStruct
    whole = lambda a: pl.BlockSpec(a.shape, lambda i, a=a: (0,) * len(a.shape))
    tokens = pl.BlockSpec((seqs, own // steps, d), lambda i: (0, i, 0))
    outs = [
        shape(output.shape, BF16), shape(output.shape, BF16), shape((ff, d), F32),
        shape((ff, d), F32), shape((ff, d), F32), shape((d, d), F32), shape((cols, d), F32),
        shape((8, d), F32),
    ]
    rows = lambda n: pl.BlockSpec((n // steps, d), lambda i: (i, 0))
    return pl.pallas_call(
        last_kernel,
        grid=(steps,),
        in_specs=[
            tokens, tokens,
            pl.BlockSpec((2, 3, ff // 16 // steps, 16, LANES), lambda i: (0, 0, i, 0, 0)),
            pl.BlockSpec((16, 16, d), lambda i: (jnp.minimum(i, 1), 0, 0)),
            pl.BlockSpec((16, 16, d), lambda i: (jnp.maximum(i - 2, 0), 0, 0)),
        ] + [whole(a) for a in gf],
        out_specs=[tokens, tokens, rows(ff), rows(ff), rows(ff), rows(d), whole(outs[6]), whole(outs[7])],
        out_shape=outs,
        compiler_params=params(),
        cost_estimate=cost(1e6, 30e6),
        name="last",
    )(output, grad, gr, *go, *gf)


def fused_body(
    tokens, doc_ids, factor_weight, output_weight, norm_one, norm_two,
    gate_weight, up_weight, down_weight, cotangent,
):
    seqs, own, d = tokens.shape
    me = lax.axis_index("wide")
    nblk = -(-(MAX_DOC - 1) // own) + 1
    first = me // 3
    g1 = norm_one[None]
    g2 = norm_two[None]
    dq = lax.dynamic_slice_in_dim(doc_ids, me * own, own, 1)[:, None, :]
    dk = lax.dynamic_slice_in_dim(doc_ids, first * own, nblk * own, 1)[:, :, None]
    wt = factor_weight.T
    n1, qf, kvw, att, q, k, v, lse, hm, ng, nb, cg = fore(
        nblk, tokens, wt, output_weight, g1, g2, dq, dk, cotangent
    )
    dn, ds, ok, os, gw, own_sums = middle(ng, nb, cg, gate_weight.T, up_weight.T, down_weight)
    output, input_grad, gr, go, gf = after(
        nblk, gw, own_sums, dn, ds, ok, os, q, k, v, lse, dq, dk, qf, kvw, hm, cotangent, output_weight,
        g1, g2, att, n1, tokens, wt,
    )
    output, input_grad, gate, up, down, out, fac, gain = finish_all(
        output, input_grad, gr, go, gf, factor_weight.shape[1]
    )
    return output, input_grad, fac.T, out, gain[0], gain[1], gate.T, up.T, down


def swap(x, axis, size, bit):
    return lax.ppermute(x, axis, [(i, i ^ bit) for i in range(size)])


def steps_of(size):
    bits, b = [], size // 2
    while b:
        bits.append(b)
        b //= 2
    return bits


def gather(x, size):
    buf = x[None]
    for bit in steps_of(size):
        buf = jnp.concatenate([buf, swap(buf, "wide", size, bit)], axis=0)
    return buf


def order_of(size):
    order = [0]
    for bit in steps_of(size):
        order = order + [o ^ bit for o in order]
    return order


def scatter(parts, size):
    for bit in reversed(steps_of(size)):
        half = parts.shape[0] // 2
        got = swap(parts[half:], "wide", size, bit)
        total = parts[:half].astype(F32) + got.astype(F32)
        parts = total if half == 1 else total.astype(BF16)
    return parts[0]


def body(
    tokens, doc_ids, factor_weight, output_weight, norm_one, norm_two,
    gate_weight, up_weight, down_weight, cotangent,
):
    seqs, own, d = tokens.shape
    full_len = doc_ids.shape[1]
    size = full_len // own
    me = lax.axis_index("wide")
    left = min(-(-(MAX_DOC - 1) // own), size - 1)
    nblk = left + 1
    start = jnp.maximum(me - left, 0)
    order = order_of(size)
    slot_of = [order.index(j) for j in range(size)]
    slots = jnp.asarray(slot_of, jnp.int32)
    blocks = start + jnp.arange(nblk, dtype=jnp.int32)
    scalars = jnp.concatenate(
        [me[None].astype(jnp.int32), (me - blocks) * own, slots[me ^ blocks]]
    ).astype(jnp.int32)
    g1 = norm_one[None]
    g2 = norm_two[None]

    n1, qf, kvf = front(tokens.reshape(seqs * own, d), factor_weight, g1)
    qf = qf.reshape(seqs, own, QPAD)
    kvg = gather(kvf.reshape(seqs, own, KPAD), size)
    doc_query = lax.dynamic_slice_in_dim(doc_ids, me * own, own, 1)
    doc_key = lax.dynamic_slice_in_dim(doc_ids, start * own, nblk * own, 1)
    cots = [gather(cotangent[s], size) for s in range(seqs)]

    fwd = []
    for s in range(seqs):
        dq = doc_query[s][None, :]
        dk = doc_key[s][:, None]
        fwd.append(
            (dq, dk)
            + tuple(attend(nblk, scalars, qf[s], kvg[:, s], dq, dk, tokens[s], output_weight, g2))
        )
    prev = None
    outs, dns = [], []
    for s in range(seqs):
        n2 = gather(fwd[s][8], size)
        res = ffn(n2, cots[s], gate_weight, up_weight, down_weight, prev, s == seqs - 1)
        outs.append(res[0])
        dns.append(res[1])
        prev = res[2:]
    grads = [lax.psum(g, "rows").astype(F32) for g in prev]

    output, mids, lows, gain_two, gqs, gkvs = [], [], [], 0.0, [], []
    for s in range(seqs):
        dq, dk, att, q, k, v, lse, hm, n2, kvw = fwd[s]
        dn = scatter(dns[s], size)
        dm, low, gain, gq, gkv = back(
            nblk, size, scalars, q, k, v, lse, dq, dk, qf[s], kvw, dn, hm,
            cotangent[s], output_weight, g2,
        )
        output.append((hm + scatter(outs[s], size)).astype(BF16))
        mids.append(dm)
        lows.append(low)
        gqs.append(gq)
        gkvs.append(gkv)
        gain_two = gain_two + gain
    att_all = jnp.stack([f[2] for f in fwd]).reshape(seqs * own, d)
    grad_out = mm(att_all, jnp.stack(lows).reshape(seqs * own, d), TN)
    gkv = scatter(jnp.stack(gkvs, axis=1), size).astype(BF16)
    dfac = jnp.concatenate([jnp.stack(gqs)[..., :QCOLS], gkv[..., :KV]], axis=-1)
    dfac = dfac.reshape(seqs * own, -1)
    grad_factors = mm(n1, dfac, TN)
    dn1 = mm(dfac, factor_weight, NT)
    hin = tokens.reshape(seqs * own, d).astype(F32)
    r1 = lax.rsqrt(jnp.mean(hin * hin, axis=-1, keepdims=True) + EPS)
    z1 = dn1 * g1
    gain_one = jnp.sum(dn1 * hin * r1, axis=0)
    grad_norm = r1 * z1 - hin * (r1 * r1 * r1) * jnp.mean(z1 * hin, axis=-1, keepdims=True)
    input_grad = (jnp.stack(mids).reshape(seqs * own, d) + grad_norm).astype(BF16)
    parts = [grad_out, grad_factors.T, gain_one[None], gain_two]
    packed = jnp.concatenate([p.astype(BF16) for p in parts], axis=0)
    packed = lax.psum(packed, ("rows", "wide")).astype(F32)
    fac = grad_factors.shape[1]
    return (
        jnp.stack(output),
        input_grad.reshape(seqs, own, d),
        packed[d:d + fac].T,
        packed[:d],
        packed[d + fac],
        packed[d + fac + 1],
        grads[0],
        grads[1],
        grads[2],
    )


def solution(mesh):
    placed = (
        P("rows", "wide", None), P("rows", None), P(), P(), P(), P(),
        P(None, "wide"), P(None, "wide"), P("wide", None), P("rows", "wide", None),
    )
    small = mesh.shape["rows"] == 8 and mesh.shape["wide"] == 4
    return jax.shard_map(
        fused_body if small else body,
        mesh=mesh,
        in_specs=placed,
        out_specs=(
            P("rows", "wide", None), P("rows", "wide", None), P(), P(), P(), P(),
            P(None, "wide"), P(None, "wide"), P("wide", None),
        ),
        check_vma=False,
    )
```
